32 devices in a mesh: dp: 8 (over y, x, core), tensor: 4 (over z).
Axes of the slice: x: 2, y: 2, z: 4, core: 2. Of those that a mesh axis runs over, the one named last changes fastest.
Arguments:
- hidden_in: bfloat16 [8192, 768], P(('dp', 'tensor')), may hold values from -6 to 6
- segment_ids: int32 [8, 1024], P('dp'), may hold values from 0 to 7, never falling along the last dimension, each value on 1 to 512 neighbouring positions
- norm1_gain: bfloat16 [768], replicated, may hold values from 0.25 to 1.75
- query_weight: bfloat16 [768, 768], P(None, 'tensor'), may hold values from -0.21875 to 0.21875
- key_weight: bfloat16 [768, 768], P(None, 'tensor'), may hold values from -0.21875 to 0.21875
- value_weight: bfloat16 [768, 768], P(None, 'tensor'), may hold values from -0.21875 to 0.21875
- out_weight: bfloat16 [768, 768], P('tensor'), may hold values from -0.875 to 0.875
- bias_table: bfloat16 [32, 12], P(None, 'tensor'), may hold values from -3 to 3
- norm2_gain: bfloat16 [768], replicated, may hold values from 0.25 to 1.75
- gate_weight: bfloat16 [768, 2048], P(None, 'tensor'), may hold values from -0.21875 to 0.21875
- up_weight: bfloat16 [768, 2048], P(None, 'tensor'), may hold values from -0.21875 to 0.21875
- down_weight: bfloat16 [2048, 768], P('tensor'), may hold values from -0.125 to 0.125
- out_cotangent: bfloat16 [8192, 768], P(('dp', 'tensor')), may hold values from -6 to 6
Outputs:
- output: bfloat16 [8192, 768], P(('dp', 'tensor'))
- input_grad: bfloat16 [8192, 768], P(('dp', 'tensor'))
- norm1_gain_grad: float32 [768], replicated
- query_weight_grad: float32 [768, 768], P(None, 'tensor')
- key_weight_grad: float32 [768, 768], P(None, 'tensor')
- value_weight_grad: float32 [768, 768], P(None, 'tensor')
- out_weight_grad: float32 [768, 768], P('tensor')
- bias_table_grad: float32 [32, 12], P(None, 'tensor')
- norm2_gain_grad: float32 [768], replicated
- gate_weight_grad: float32 [768, 2048], P(None, 'tensor')
- up_weight_grad: float32 [768, 2048], P(None, 'tensor')
- down_weight_grad: float32 [2048, 768], P('tensor')
The draws below stay inside these ranges and needn't reach their ends.
Inputs may be any that keep to these rules, and one draw needn't show every extreme that they name: `segment_ids`: within each row the ids never fall; each of the 8 documents has 1 to 512 positions, and one has exactly 512.
All inputs are finite; a program needn't handle non-finite values.
Results may differ from the reference program's by a relative error of at most 0.019.
Values may be sent and summed in bfloat16 or wider, within the bound.
A program may use at most 256 MiB of HBM per device.

```python
import math
from functools import partial
import jax
import jax.numpy as jnp
import numpy as np
from jax import lax

D = 768
HEADS = 12
HEAD_DIM = 64
FF = 2048
BUCKETS = 32
LEN = 1024
SEGS = 8
SEG_MOST = 512
SEQ_DEV = 1
HD = 768
ROWS = 8
TOKENS = 8192


def block_scale(own_key, shape, cuts, smallest, high):
    loudness = 1.0
    for axis_at, shards_of in cuts:
        draws = jax.random.uniform(jax.random.fold_in(jax.random.fold_in(own_key, 6), axis_at), (shards_of,), jnp.float32, smallest / len(cuts), high / len(cuts))
        loudness = loudness * jnp.repeat(jnp.exp(draws), shape[axis_at] // shards_of).reshape((-1,) + (1,) * (len(shape) - 1 - axis_at))
    return loudness


def profile(count, total, limit, slope):
    loads = [(1 << 20) // math.isqrt(grade ** slope) + 1 for grade in range(2, count + 1)]
    spare, given = total - limit - (count - 1), [1] * (count - 1)
    while spare > 0:
        movable = [i for i in range(count - 1) if given[i] < limit]
        whole, left = sum([loads[i] for i in movable]), spare
        for i in movable:
            addition = min(limit - given[i], max(1, left * loads[i] // whole), spare)
            given[i] = given[i] + addition
            spare = spare - addition
    return np.array([limit] + given)


def ragged_sizes(rng, number_of, total, limit, lean):
    if number_of == 2:
        one = jax.random.randint(rng, (), max(1, total - limit), min(limit, total - 1) + 1)
        return jnp.stack([one, total - one])
    lengths = jnp.asarray(profile(number_of, total, limit, lean), jnp.int32)
    pairs = (number_of - 1) // 2
    source_of, receiver = lengths[1:1 + 2 * pairs:2], lengths[2:2 + 2 * pairs:2]
    room = jnp.minimum(source_of - 1, limit - receiver)
    moved = jax.random.randint(jax.random.fold_in(rng, 1), (pairs,), 0, 1 << 20) % (room + 1)
    lengths = lengths.at[1:1 + 2 * pairs:2].set(source_of - moved).at[2:2 + 2 * pairs:2].set(receiver + moved)
    return lengths[jax.random.permutation(jax.random.fold_in(rng, 2), number_of)]


def normal_values(own_key, extent, scale, most, split=(), kind=jnp.bfloat16):
    gain = block_scale(own_key, extent, split, -0.22, 0.18) if split else 1.0
    values = jax.random.normal(own_key, extent, jnp.float32) * scale * gain
    return jnp.minimum(jnp.maximum(values, -most), most).astype(kind)


def setup_inputs(seed: int = 0) -> dict:
    key_of = jax.random.split(jax.random.key(seed), 14)
    return {
        "hidden_in": normal_values(key_of[0], (TOKENS, D), 1.0, 6.0, ((0, 32),)),
        "segment_ids": jax.vmap(lambda own: jnp.searchsorted(jnp.cumsum(ragged_sizes(own, SEGS, LEN, SEG_MOST, 2)), jnp.arange(LEN), side="right"))(jax.random.split(key_of[1], ROWS)).reshape((ROWS, LEN)).astype(jnp.int32),
        "norm1_gain": jnp.clip(1.0 + 0.15 * jax.random.normal(key_of[2], (D,), jnp.float32), 0.25, 1.75).astype(jnp.bfloat16),
        "query_weight": normal_values(key_of[3], (D, HD), D ** -0.5, 0.21875, ((1, 4),)),
        "key_weight": normal_values(key_of[4], (D, HD), D ** -0.5, 0.21875, ((1, 4),)),
        "value_weight": normal_values(key_of[5], (D, HD), D ** -0.5, 0.21875, ((1, 4),)),
        "out_weight": normal_values(key_of[6], (HD, D), (HD // 16) ** -0.5, 0.875, ((0, 4),)),
        "bias_table": normal_values(key_of[7], (BUCKETS, HEADS), 1.0, 3.0, ((1, 4),)),
        "norm2_gain": jnp.clip(1.0 + 0.15 * jax.random.normal(key_of[8], (D,), jnp.float32), 0.25, 1.75).astype(jnp.bfloat16),
        "gate_weight": normal_values(key_of[9], (D, FF), D ** -0.5, 0.21875, ((1, 4),)),
        "up_weight": normal_values(key_of[10], (D, FF), D ** -0.5, 0.21875, ((1, 4),)),
        "down_weight": normal_values(key_of[11], (FF, D), FF ** -0.5, 0.125, ((0, 4),)),
        "out_cotangent": normal_values(key_of[12], (TOKENS, D), 1.0, 6.0, ((0, 32),)),
    }


far_marks = (12, 16, 23, 32, 46, 64, 91)
norm_eps = 1e-06
highest = lax.Precision.HIGHEST

@jax.custom_vjp
def low(v):
    return lax.optimization_barrier(v.astype(jnp.bfloat16)).astype(jnp.float32)

@jax.custom_vjp
def low_back(v):
    return v

def low_keep(v):
    return (low(v), None)

def low_pass(kept, grad):
    return (grad,)

def back_keep(v):
    return (v, None)

def back_low(kept, grad):
    return (low(grad),)
low.defvjp(low_keep, low_pass)
low_back.defvjp(back_keep, back_low)

def bucket_of(offset):
    magnitude = jnp.abs(offset)
    within = jnp.minimum(magnitude, 8)
    for far_mark in far_marks:
        within = within + (magnitude >= far_mark).astype(jnp.int32)
    return within + jnp.where(offset > 0, 16, 0).astype(jnp.int32)

def rms_scale(row_values, gain_value):
    return row_values * lax.rsqrt(lax.optimization_barrier(jnp.mean(row_values * row_values, axis=-1, keepdims=True)) + norm_eps) * gain_value

def attend_row(bias_full, row_parts):
    queries, key_rows, value_rows, segments = row_parts
    length = queries.shape[0]
    query_heads = queries.reshape(length, HEADS, HEAD_DIM)
    key_heads = key_rows.reshape(length, HEADS, HEAD_DIM)
    value_heads = value_rows.reshape(length, HEADS, HEAD_DIM)
    raw_scores = jnp.einsum('qhd,khd->hqk', query_heads, key_heads, precision=highest) * HEAD_DIM ** (-0.5) + bias_full
    scores = low_back(raw_scores)
    same_doc = segments[:, None] == segments[None, :]
    scores = jnp.where(same_doc[None], scores, -1000000000.0)
    probs = low(jax.nn.softmax(scores, axis=-1))
    mixed_rows = jnp.einsum('hqk,khd->qhd', probs, value_heads, precision=highest).reshape(length, HEADS * HEAD_DIM)
    return low(low_back(mixed_rows))

def forward(segments, hidden_in, norm1_gain, query_weight, key_weight, value_weight, out_weight, bias_table, norm2_gain, gate_weight, up_weight, down_weight):
    length = segments.shape[1]
    normed_first = low(rms_scale(hidden_in, norm1_gain))
    queries = low(low_back(jnp.einsum('gld,de->gle', normed_first, query_weight, precision=highest)))
    key_rows = low(low_back(jnp.einsum('gld,de->gle', normed_first, key_weight, precision=highest)))
    value_rows = low(low_back(jnp.einsum('gld,de->gle', normed_first, value_weight, precision=highest)))
    places = jnp.arange(length, dtype=jnp.int32)
    offsets = places[None, :] - places[:, None]
    bias_full = jnp.transpose(bias_table[bucket_of(offsets)], (2, 0, 1))
    mixed = lax.map(jax.checkpoint(partial(attend_row, bias_full)), (queries, key_rows, value_rows, segments))
    attention = jnp.einsum('gle,ed->gld', mixed, out_weight, precision=highest)
    residual = hidden_in + low_back(attention)
    normed_second = low(rms_scale(residual, norm2_gain))
    gate_value = low_back(jnp.einsum('gld,df->glf', normed_second, gate_weight, precision=highest))
    up_value = low_back(jnp.einsum('gld,df->glf', normed_second, up_weight, precision=highest))
    hidden = low(jax.nn.gelu(gate_value, approximate=True) * up_value)
    return residual + low_back(jnp.einsum('glf,fd->gld', hidden, down_weight, precision=highest))

def reference(hidden_in, segment_ids, norm1_gain, query_weight, key_weight, value_weight, out_weight, bias_table, norm2_gain, gate_weight, up_weight, down_weight, out_cotangent):
    row_number = segment_ids.shape[0]
    length = segment_ids.shape[1]
    width = hidden_in.shape[1]
    group_rows = SEQ_DEV
    group_count = row_number // group_rows
    weight_values = tuple((weight_item.astype(jnp.float32) for weight_item in (norm1_gain, query_weight, key_weight, value_weight, out_weight, bias_table, norm2_gain, gate_weight, up_weight, down_weight)))
    inputs = hidden_in.astype(jnp.float32).reshape(group_count, group_rows, length, width)
    cotangents = out_cotangent.astype(jnp.float32).reshape(group_count, group_rows, length, width)
    segments = segment_ids.reshape(group_count, group_rows, length)

    def one_group(running, group_parts):
        input_group, cot_group, seg_group = group_parts

        def apply_layer(input_value, *layer_weights):
            return forward(seg_group, input_value, *layer_weights)
        output_group, pullback = jax.vjp(apply_layer, input_group, *weight_values)
        gradients = pullback(cot_group)
        updated = tuple((total_value + grad_value for total_value, grad_value in zip(running, gradients[1:])))
        return (updated, (output_group.astype(jnp.bfloat16), gradients[0].astype(jnp.bfloat16)))
    zeros_start = tuple((jnp.zeros_like(weight_item) for weight_item in weight_values))
    sums, (outputs, input_grads) = lax.scan(one_group, zeros_start, (inputs, cotangents, segments))
    return (outputs.reshape(-1, width), input_grads.reshape(-1, width), sums[0], sums[1], sums[2], sums[3], sums[4], sums[5], sums[6], sums[7], sums[8], sums[9])
```

```python
from functools import partial

import jax
import jax.numpy as jnp
from jax import lax
from jax.experimental import pallas as pl
from jax.experimental.pallas import tpu as pltpu
from jax.sharding import PartitionSpec as P

HEAD_DIM = 64
BUCKETS = 32
far_marks = (12, 16, 23, 32, 46, 64, 91)
norm_eps = 1e-06
far_score = 2.0**30
BLK = 256
f32 = jnp.float32
bf16 = jnp.bfloat16


def bucket_of(offset):
    magnitude = jnp.abs(offset)
    within = jnp.minimum(magnitude, 8)
    for far_mark in far_marks:
        within = within + (magnitude >= far_mark).astype(jnp.int32)
    return within + jnp.where(offset > 0, 16, 0).astype(jnp.int32)


def key_range(block, count):
    return range(max(0, block - 2), min(count, block + 3))


def contract(lhs, rhs, left, right):
    return lax.dot_general(
        lhs, rhs, (((left,), (right,)), ((), ())), preferred_element_type=f32
    )


def attend_kernel(
    normed_ref, wq_ref, wk_ref, wv_ref, seg_ref, table_ref,
    mixed_ref, probs_ref, q_ref, k_ref, v_ref, inv_ref,
    w_s, kt_s, bias_s, score_s, first_s,
):
    head = pl.program_id(0)
    length = normed_ref.shape[0]
    count = length // BLK
    lane = lax.broadcasted_iota(jnp.int32, (BLK, 128), 1)
    low_half = lane < HEAD_DIM

    @pl.when(head == 0)
    def _():
        w_s[...] = jnp.zeros_like(w_s)
        for place, ref in enumerate((wq_ref, wk_ref, wv_ref)):
            w_s[:, 256 * place : 256 * place + 192] = ref[...]
        row8 = lax.broadcasted_iota(jnp.int32, (8, 128), 0)
        lane8 = lax.broadcasted_iota(jnp.int32, (8, 128), 1)
        spread = jnp.where((lane8 % HEAD_DIM) == row8, 1.0, 0.0).astype(bf16)

        def project(step, carry):
            rows = pl.ds(pl.multiple_of(step * BLK, BLK), BLK)
            seg_row = seg_ref[:, rows]
            kinds = lax.broadcasted_iota(jnp.int32, (8, BLK), 0)
            hot = jnp.where(
                jnp.broadcast_to(seg_row, (8, BLK)) == kinds, 1.0, 0.0
            ).astype(bf16)
            same = contract(hot, spread, 0, 0)
            in_aug = (lane % HEAD_DIM) < 8
            aug_q = jnp.where(in_aug, same, 0.0)
            aug_k = jnp.where(in_aug, (same - 1.0) * far_score, 0.0)
            rows_in = normed_ref[rows, :]
            q = jnp.dot(rows_in, w_s[:, 0:256], preferred_element_type=f32)
            k = jnp.dot(rows_in, w_s[:, 256:512], preferred_element_type=f32)
            v = jnp.dot(rows_in, w_s[:, 512:768], preferred_element_type=f32)
            scale = HEAD_DIM ** (-0.5)
            for h, (cols, mine) in enumerate(
                ((slice(0, 128), low_half), (slice(0, 128), ~low_half), (slice(128, 256), low_half))
            ):
                q_ref[h, rows, :] = jnp.where(mine, q[:, cols] * scale, aug_q).astype(bf16)
                k_h = jnp.where(mine, k[:, cols], aug_k).astype(bf16)
                k_ref[h, rows, :] = k_h
                v_ref[h, rows, :] = jnp.where(mine, v[:, cols], 1.0).astype(bf16)
                kt_s[h, :, rows] = k_h.T
            return carry

        lax.fori_loop(0, count, project, 0)

    offset = lax.broadcasted_iota(jnp.int32, (BUCKETS, length), 1)
    offset = jnp.where(offset >= length // 2, offset - length, offset)
    hot_bucket = jnp.where(
        bucket_of(offset) == lax.broadcasted_iota(jnp.int32, (BUCKETS, length), 0), 1.0, 0.0
    ).astype(bf16)
    by_offset = contract(table_ref[head], hot_bucket, 1, 0)[0:1]
    spread_rows = jnp.broadcast_to(by_offset, (BLK, length))
    bias_s[...] = pltpu.roll(spread_rows, 0, 1, stride=1, stride_axis=0)

    for block in range(count):
        rows = slice(block * BLK, (block + 1) * BLK)
        q_h = q_ref[head, rows, :]
        top = None
        for key in key_range(block, count):
            part = jnp.dot(
                q_h, kt_s[head, :, key * BLK : (key + 1) * BLK], preferred_element_type=f32
            )
            delta = key - block
            at = (delta * BLK) % length
            part = part + bias_s[:, at : at + BLK]
            score_s[:, key * BLK : (key + 1) * BLK] = part
            top = part if top is None else jnp.maximum(top, part)
        top = jnp.max(jnp.maximum(top[:, :128], top[:, 128:]), axis=1, keepdims=True)
        total = jnp.zeros((BLK, 128), f32)
        for key in key_range(block, count):
            cols = slice(key * BLK, (key + 1) * BLK)
            part = jnp.exp(score_s[:, cols] - top).astype(bf16)
            probs_ref[0, rows, cols] = part
            total = total + jnp.dot(part, v_ref[head, cols, :], preferred_element_type=f32)
        sums = pltpu.roll(total, HEAD_DIM, 1)
        inverse = 1.0 / sums
        out = total * inverse

        @pl.when(head == 0)
        def _():
            first_s[rows, 0:128] = out
            first_s[rows, 128:256] = inverse

        @pl.when(head == 1)
        def _():
            mixed_ref[rows, 0:128] = jnp.where(low_half, first_s[rows, 0:128], out).astype(bf16)
            inv_ref[rows, 0:128] = jnp.where(low_half, first_s[rows, 128:256], inverse)

        @pl.when(head == 2)
        def _():
            mixed_ref[rows, 128:192] = out[:, 0:HEAD_DIM].astype(bf16)
            inv_ref[rows, 128:256] = inverse


def attend(normed, wq, wk, wv, segments, bias_table):
    length, width = normed.shape
    heads = bias_table.shape[1]
    inner = heads * HEAD_DIM
    table = jnp.broadcast_to(bias_table.T[:, None, :], (heads, 8, BUCKETS))
    whole = lambda *dims: pl.BlockSpec(dims, lambda h: (0,) * len(dims))
    return pl.pallas_call(
        attend_kernel,
        grid=(heads,),
        name="attend",
        out_shape=(
            jax.ShapeDtypeStruct((length, inner), bf16),
            jax.ShapeDtypeStruct((heads, length, length), bf16),
            jax.ShapeDtypeStruct((heads, length, 128), bf16),
            jax.ShapeDtypeStruct((heads, length, 128), bf16),
            jax.ShapeDtypeStruct((heads, length, 128), bf16),
            jax.ShapeDtypeStruct((length, 256), f32),
        ),
        in_specs=[
            whole(length, width),
            whole(width, inner),
            whole(width, inner),
            whole(width, inner),
            whole(1, length),
            whole(heads, 8, BUCKETS),
        ],
        out_specs=(
            whole(length, inner),
            pl.BlockSpec((1, length, length), lambda h: (h, 0, 0)),
            whole(heads, length, 128),
            whole(heads, length, 128),
            whole(heads, length, 128),
            whole(length, 256),
        ),
        scratch_shapes=[
            pltpu.VMEM((width, 768), bf16),
            pltpu.VMEM((heads, 128, length), bf16),
            pltpu.VMEM((BLK, length), f32),
            pltpu.VMEM((BLK, length), f32),
            pltpu.VMEM((length, 256), f32),
        ],
        compiler_params=pltpu.CompilerParams(
            dimension_semantics=("arbitrary",), vmem_limit_bytes=48 << 20
        ),
        cost_estimate=pl.CostEstimate(flops=3 << 30, bytes_accessed=12 << 20, transcendentals=3 << 20),
    )(normed, wq, wk, wv, segments, table)


def attend_back_kernel(
    mixed_grad_ref, mixed_ref, inv_ref, probs_ref, q_ref, k_ref, v_ref, normed_ref,
    wq_ref, wk_ref, wv_ref,
    normed_grad_ref, weight_grad_ref, table_grad_ref,
    w_s, dot_s, dott_s, qt_s, vt_s, grad_s, joined_s, near_s, far_s, dkt_s, dvt_s,
):
    head = pl.program_id(0)
    length = normed_ref.shape[0]
    count = length // BLK
    lane = lax.broadcasted_iota(jnp.int32, (BLK, 128), 1)
    low_half = lane < HEAD_DIM
    heads = 3

    @pl.when(head == 0)
    def _():
        w_s[...] = jnp.zeros_like(w_s)
        for place, ref in enumerate((wq_ref, wk_ref, wv_ref)):
            w_s[:, 256 * place : 256 * place + 192] = ref[...]

        def prepare(step, carry):
            rows = pl.ds(pl.multiple_of(step * BLK, BLK), BLK)
            for h in range(heads):
                cols = slice(0, 128) if h < 2 else slice(128, 256)
                mine = ~low_half if h == 1 else low_half
                if h < 2:
                    grad = mixed_grad_ref[rows, 0:128].astype(f32)
                    mix = mixed_ref[rows, 0:128].astype(f32)
                else:
                    fill = jnp.zeros((BLK, HEAD_DIM), f32)
                    grad = jnp.concatenate(
                        (mixed_grad_ref[rows, 128:192].astype(f32), fill), axis=1
                    )
                    mix = jnp.concatenate((mixed_ref[rows, 128:192].astype(f32), fill), axis=1)
                inverse = inv_ref[rows, cols]
                grad = jnp.where(mine, grad * inverse, 0.0)
                centre = -jnp.sum(grad * mix, axis=1, keepdims=True)
                high = centre.astype(bf16).astype(f32)
                base = 0 if h == 1 else HEAD_DIM
                grad = jnp.where(lane == base, high, grad)
                grad = jnp.where(lane == base + 1, centre - high, grad)
                low = grad.astype(bf16)
                dot_s[h, rows, :] = low
                dott_s[h, :, rows] = low.T
                qt_s[h, :, rows] = q_ref[h, rows, :].T
                vt_s[h, :, rows] = v_ref[h, rows, :].T
            return carry

        lax.fori_loop(0, count, prepare, 0)

    near_s[...] = jnp.zeros_like(near_s)
    far_s[...] = jnp.zeros_like(far_s)
    dkt_s[...] = jnp.zeros_like(dkt_s)
    dvt_s[...] = jnp.zeros_like(dvt_s)
    for block in range(count):
        rows = slice(block * BLK, (block + 1) * BLK)
        d_h = dot_s[head, rows, :]
        dt_h = dott_s[head, :, rows]
        qt_h = qt_s[head, :, rows]
        query_grad = jnp.zeros((BLK, 128), f32)
        for key in key_range(block, count):
            cols = slice(key * BLK, (key + 1) * BLK)
            probs = probs_ref[0, rows, cols]
            slope = jnp.dot(d_h, vt_s[head, :, cols], preferred_element_type=f32)
            grad = probs.astype(f32) * slope
            low = grad.astype(bf16)
            delta = key - block
            if abs(delta) == 2:
                side = 0 if delta < 0 else 1
                far_s[side] += grad[:, :128] + grad[:, 128:]
            else:
                near_s[:, (delta + 1) * BLK : (delta + 2) * BLK] += grad
            query_grad = query_grad + jnp.dot(low, k_ref[head, cols, :], preferred_element_type=f32)
            dkt_s[:, cols] += jnp.dot(qt_h, low, preferred_element_type=f32)
            dvt_s[:, cols] += jnp.dot(dt_h, probs, preferred_element_type=f32)
        grad_s[rows, 0:128] = query_grad * HEAD_DIM ** (-0.5)
    for block in range(count):
        rows = slice(block * BLK, (block + 1) * BLK)
        grad_s[rows, 128:256] = dkt_s[:, rows].T
        grad_s[rows, 256:384] = dvt_s[:, rows].T

    place = lax.broadcasted_iota(jnp.int32, (BLK, 3 * BLK), 1) - BLK
    place = place - lax.broadcasted_iota(jnp.int32, (BLK, 3 * BLK), 0)
    bucket = bucket_of(place)
    near = near_s[...]
    sub = lax.broadcasted_iota(jnp.int32, (BUCKETS, 128), 0)
    table = jnp.zeros((BUCKETS, 128), f32)
    for b in range(BUCKETS):
        if b == 16:
            continue
        part = jnp.sum(jnp.where(bucket == b, near, 0.0), axis=0, keepdims=True)
        folded = part[:, 0:128]
        for at in range(1, 6):
            folded = folded + part[:, at * 128 : (at + 1) * 128]
        if b in (15, 31):
            folded = folded + jnp.sum(far_s[0 if b == 15 else 1], axis=0, keepdims=True)
        table = jnp.where(sub == b, folded, table)
    table_grad_ref[0] = table

    @pl.when(head == 0)
    def _():
        for at in range(3):
            joined_s[:, 256 * at : 256 * at + 128] = grad_s[:, 128 * at : 128 * at + 128].astype(bf16)

    @pl.when(head == 1)
    def _():
        lanes = lax.broadcasted_iota(jnp.int32, (length, 128), 1)
        for at in range(3):
            joined_s[:, 256 * at : 256 * at + 128] = jnp.where(
                lanes < HEAD_DIM,
                joined_s[:, 256 * at : 256 * at + 128].astype(f32),
                grad_s[:, 128 * at : 128 * at + 128],
            ).astype(bf16)

    @pl.when(head == 2)
    def _():
        lanes = lax.broadcasted_iota(jnp.int32, (length, 128), 1)
        for at in range(3):
            joined_s[:, 256 * at + 128 : 256 * at + 256] = jnp.where(
                lanes < HEAD_DIM, grad_s[:, 128 * at : 128 * at + 128], 0.0
            ).astype(bf16)
        for block in range(count):
            rows = slice(block * BLK, (block + 1) * BLK)
            normed_grad_ref[rows, :] = contract(joined_s[rows, :], w_s[...], 1, 1).astype(bf16)
        for at in range(3):
            part = contract(normed_ref[...], joined_s[:, 256 * at : 256 * at + 256], 0, 0)
            weight_grad_ref[at] = part[:, 0:192].astype(bf16)


def attend_back(mixed_grad, mixed, inverse, probs, q, k, v, normed, wq, wk, wv):
    length, width = normed.shape
    heads = q.shape[0]
    inner = heads * HEAD_DIM
    whole = lambda *dims: pl.BlockSpec(dims, lambda h: (0,) * len(dims))
    return pl.pallas_call(
        attend_back_kernel,
        grid=(heads,),
        name="attend_back",
        out_shape=(
            jax.ShapeDtypeStruct((length, width), bf16),
            jax.ShapeDtypeStruct((3, width, inner), bf16),
            jax.ShapeDtypeStruct((heads, BUCKETS, 128), f32),
        ),
        in_specs=[
            whole(length, inner),
            whole(length, inner),
            whole(length, 256),
            pl.BlockSpec((1, length, length), lambda h: (h, 0, 0)),
            whole(heads, length, 128),
            whole(heads, length, 128),
            whole(heads, length, 128),
            whole(length, width),
            whole(width, inner),
            whole(width, inner),
            whole(width, inner),
        ],
        out_specs=(
            whole(length, width),
            whole(3, width, inner),
            pl.BlockSpec((1, BUCKETS, 128), lambda h: (h, 0, 0)),
        ),
        scratch_shapes=[
            pltpu.VMEM((width, 768), bf16),
            pltpu.VMEM((heads, length, 128), bf16),
            pltpu.VMEM((heads, 128, length), bf16),
            pltpu.VMEM((heads, 128, length), bf16),
            pltpu.VMEM((heads, 128, length), bf16),
            pltpu.VMEM((length, 384), f32),
            pltpu.VMEM((length, 768), bf16),
            pltpu.VMEM((BLK, 3 * BLK), f32),
            pltpu.VMEM((2, BLK, 128), f32),
            pltpu.VMEM((128, length), f32),
            pltpu.VMEM((128, length), f32),
        ],
        compiler_params=pltpu.CompilerParams(
            dimension_semantics=("arbitrary",), vmem_limit_bytes=56 << 20
        ),
        cost_estimate=pl.CostEstimate(flops=6 << 30, bytes_accessed=16 << 20, transcendentals=0),
    )(mixed_grad, mixed, inverse, probs, q, k, v, normed, wq, wk, wv)


def mean_square_scale(rows):
    return lax.rsqrt(jnp.mean(rows * rows, axis=-1, keepdims=True) + norm_eps)


def unit_kernel(
    mixed_ref, hidden_ref, cot_ref, out_w_ref, gate_w_ref, up_w_ref, down_w_ref, gain_ref,
    output_ref, residual_grad_ref, mixed_grad_ref, gain_grad_ref,
    out_wg_ref, gate_wg_ref, up_wg_ref, down_wg_ref,
    residual_s, normed_s, sum_s, back_s,
):
    step = pl.program_id(0)
    parts = pl.num_programs(0)
    groups = mixed_ref.shape[0]
    tokens = residual_s.shape[0]

    @pl.when(step == 0)
    def _():
        mixed = jnp.concatenate([mixed_ref[g] for g in range(groups)], axis=1)
        out_w = jnp.concatenate([out_w_ref[g] for g in range(groups)], axis=0)
        residual = hidden_ref[...].astype(f32) + jnp.dot(mixed, out_w, preferred_element_type=f32)
        residual_s[...] = residual
        normed_s[...] = (residual * mean_square_scale(residual) * gain_ref[...].astype(f32)).astype(bf16)
        sum_s[...] = jnp.zeros_like(sum_s)
        back_s[...] = jnp.zeros_like(back_s)

    normed = normed_s[...]
    cot = cot_ref[...]
    gate = jnp.dot(normed, gate_w_ref[0], preferred_element_type=f32)
    up = jnp.dot(normed, up_w_ref[0], preferred_element_type=f32)
    hidden_grad = contract(cot, down_w_ref[0], 1, 1)
    c0 = 0.7978845608028654
    square = gate * gate
    bend = jnp.tanh(gate * (c0 + (c0 * 0.044715) * square))
    half = 0.5 + 0.5 * bend
    act = gate * half
    slope = half + 0.5 * gate * (1.0 - bend * bend) * (c0 + (3.0 * c0 * 0.044715) * square)
    hidden = (act * up).astype(bf16)
    gate_grad = (hidden_grad * up * slope).astype(bf16)
    up_grad = (hidden_grad * act).astype(bf16)
    sum_s[...] += jnp.dot(hidden, down_w_ref[0], preferred_element_type=f32)
    back_s[...] += contract(gate_grad, gate_w_ref[0], 1, 1) + contract(up_grad, up_w_ref[0], 1, 1)
    down_wg_ref[0] = contract(hidden, cot, 0, 0).astype(bf16)
    gate_wg_ref[0] = contract(normed, gate_grad, 0, 0).astype(bf16)
    up_wg_ref[0] = contract(normed, up_grad, 0, 0).astype(bf16)

    @pl.when(step == parts - 1)
    def _():
        residual = residual_s[...]
        output_ref[...] = (residual + sum_s[...]).astype(bf16)
        back = back_s[...]
        r = mean_square_scale(residual)
        gain_grad_ref[...] = jnp.sum(back * residual * r, axis=0, keepdims=True)
        g = back * gain_ref[...].astype(f32)
        centre = jnp.mean(g * residual, axis=-1, keepdims=True)
        residual_grad = cot_ref[...].astype(f32) + r * g - (r * r * r * centre) * residual
        residual_grad_ref[...] = residual_grad
        low = residual_grad.astype(bf16)
        for g_at in range(groups):
            mixed_grad_ref[g_at] = contract(low, out_w_ref[g_at], 1, 1).astype(bf16)
            out_wg_ref[g_at] = contract(mixed_ref[g_at], low, 0, 0).astype(bf16)


def unit(mixed, hidden_in, cot, out_w, gate_w, up_w, down_w, gain):
    groups, tokens, part = mixed.shape
    width = hidden_in.shape[1]
    units = gate_w.shape[2]
    whole = lambda *dims: pl.BlockSpec(dims, lambda s: (0,) * len(dims))
    each = lambda *dims: pl.BlockSpec((1,) + dims, lambda s: (s, 0, 0))
    return pl.pallas_call(
        unit_kernel,
        grid=(groups,),
        name="unit",
        out_shape=(
            jax.ShapeDtypeStruct((tokens, width), bf16),
            jax.ShapeDtypeStruct((tokens, width), f32),
            jax.ShapeDtypeStruct((groups, tokens, part), bf16),
            jax.ShapeDtypeStruct((1, width), f32),
            jax.ShapeDtypeStruct((groups, part, width), bf16),
            jax.ShapeDtypeStruct((groups, width, units), bf16),
            jax.ShapeDtypeStruct((groups, width, units), bf16),
            jax.ShapeDtypeStruct((groups, units, width), bf16),
        ),
        in_specs=[
            whole(groups, tokens, part),
            whole(tokens, width),
            whole(tokens, width),
            whole(groups, part, width),
            each(width, units),
            each(width, units),
            each(units, width),
            whole(1, width),
        ],
        out_specs=(
            whole(tokens, width),
            whole(tokens, width),
            whole(groups, tokens, part),
            whole(1, width),
            whole(groups, part, width),
            each(width, units),
            each(width, units),
            each(units, width),
        ),
        scratch_shapes=[
            pltpu.VMEM((tokens, width), f32),
            pltpu.VMEM((tokens, width), bf16),
            pltpu.VMEM((tokens, width), f32),
            pltpu.VMEM((tokens, width), f32),
        ],
        compiler_params=pltpu.CompilerParams(
            dimension_semantics=("arbitrary",), vmem_limit_bytes=48 << 20
        ),
        cost_estimate=pl.CostEstimate(flops=9 << 30, bytes_accessed=26 << 20, transcendentals=1 << 20),
    )(mixed, hidden_in, cot, out_w, gate_w, up_w, down_w, gain)


def shards(
    hidden_in, segment_ids, norm1_gain, query_weight, key_weight, value_weight, out_weight,
    bias_table, norm2_gain, gate_weight, up_weight, down_weight, out_cotangent,
):
    rows_here, width = hidden_in.shape
    length = segment_ids.shape[1]
    assert segment_ids.shape[0] == 1
    groups = length // rows_here
    input_rows = hidden_in.astype(f32)
    first_gain = norm1_gain.astype(f32)
    r1 = mean_square_scale(input_rows)
    normed_here = (input_rows * r1 * first_gain).astype(bf16)
    normed = lax.all_gather(normed_here, "tensor", axis=0, tiled=True)
    gate_w, up_w, down_w, out_w = (
        lax.all_gather(w, "tensor", axis=0) for w in (gate_weight, up_weight, down_weight, out_weight)
    )
    mixed, probs, q, k, v, inverse = attend(
        normed, query_weight, key_weight, value_weight, segment_ids, bias_table
    )
    swap = lambda blocks: lax.all_to_all(blocks, "tensor", 0, 0)
    mixed_here = swap(mixed.reshape(groups, rows_here, -1))
    output, residual_grad, mixed_grad_here, gain2, out_wg, gate_wg, up_wg, down_wg = unit(
        mixed_here, hidden_in, out_cotangent, out_w, gate_w, up_w, down_w, norm2_gain[None]
    )
    mixed_grad = swap(mixed_grad_here).reshape(length, -1)
    normed_grad, qkv_wg, table_grad = attend_back(
        mixed_grad, mixed, inverse, probs, q, k, v, normed, query_weight, key_weight, value_weight
    )
    back = lax.psum_scatter(normed_grad, "tensor", scatter_dimension=0, tiled=True).astype(f32)
    gain1 = jnp.sum(back * input_rows * r1, axis=0)
    g1 = back * first_gain
    centre = jnp.mean(g1 * input_rows, axis=-1, keepdims=True)
    input_grad = (residual_grad + r1 * g1 - (r1 * r1 * r1 * centre) * input_rows).astype(bf16)
    table_part = jnp.sum(table_grad, axis=-1).T
    scatter = lambda wg: lax.psum_scatter(wg, "tensor", scatter_dimension=0)
    wgs = tuple(scatter(wg) for wg in (out_wg, gate_wg, up_wg, down_wg))
    sums = lax.psum((qkv_wg,) + wgs, "dp")
    sums = tuple(s.astype(f32) for s in sums)
    gains = lax.psum(jnp.stack((gain1, gain2[0])), ("dp", "tensor"))
    table_sum = lax.psum(table_part, "dp")
    return (
        output, input_grad, gains[0], sums[0][0], sums[0][1], sums[0][2], sums[1], table_sum,
        gains[1], sums[2], sums[3], sums[4],
    )


def solution(mesh):
    in_specs = (
        P(("dp", "tensor"), None), P("dp", None), P(),
        P(None, "tensor"), P(None, "tensor"), P(None, "tensor"), P("tensor", None),
        P(None, "tensor"), P(), P(None, "tensor"), P(None, "tensor"), P("tensor", None),
        P(("dp", "tensor"), None),
    )
    out_specs = (
        P(("dp", "tensor"), None), P(("dp", "tensor"), None), P(),
        P(None, "tensor"), P(None, "tensor"), P(None, "tensor"), P("tensor", None),
        P(None, "tensor"), P(), P(None, "tensor"), P(None, "tensor"), P("tensor", None),
    )
    return jax.shard_map(shards, mesh=mesh, in_specs=in_specs, out_specs=out_specs, check_vma=False)
```

```python
import functools

import jax
import jax.numpy as jnp
from jax import lax
from jax.experimental import pallas as pl
from jax.experimental.pallas import tpu as pltpu
from jax.sharding import PartitionSpec as P

HEAD_DIM = 64
BUCKETS = 32
far_marks = (12, 16, 23, 32, 46, 64, 91)
norm_eps = 1e-06
far_score = 2.0**30
BLK = 256
f32 = jnp.float32
bf16 = jnp.bfloat16


def bucket_of(offset):
    magnitude = jnp.abs(offset)
    within = jnp.minimum(magnitude, 8)
    for far_mark in far_marks:
        within = within + (magnitude >= far_mark).astype(jnp.int32)
    return within + jnp.where(offset > 0, 16, 0).astype(jnp.int32)


def key_range(block, count):
    return range(max(0, block - 2), min(count, block + 3))


def contract(lhs, rhs, left, right):
    return lax.dot_general(
        lhs, rhs, (((left,), (right,)), ((), ())), preferred_element_type=f32
    )


def attend_kernel(
    normed_ref, wq_ref, wk_ref, wv_ref, seg_ref, table_ref,
    mixed_ref, probs_ref, q_ref, k_ref, v_ref, inv_ref,
    w_s, kt_s, bias_s, score_s, first_s,
):
    head = pl.program_id(0)
    length = normed_ref.shape[0]
    count = length // BLK
    lane = lax.broadcasted_iota(jnp.int32, (BLK, 128), 1)
    low_half = lane < HEAD_DIM

    @pl.when(head == 0)
    def _():
        w_s[...] = jnp.zeros_like(w_s)
        for place, ref in enumerate((wq_ref, wk_ref, wv_ref)):
            w_s[:, 256 * place : 256 * place + 192] = ref[...]
        row8 = lax.broadcasted_iota(jnp.int32, (8, 128), 0)
        lane8 = lax.broadcasted_iota(jnp.int32, (8, 128), 1)
        spread = jnp.where((lane8 % HEAD_DIM) == row8, 1.0, 0.0).astype(bf16)

        def project(step, carry):
            rows = pl.ds(pl.multiple_of(step * BLK, BLK), BLK)
            seg_row = seg_ref[:, rows]
            kinds = lax.broadcasted_iota(jnp.int32, (8, BLK), 0)
            hot = jnp.where(
                jnp.broadcast_to(seg_row, (8, BLK)) == kinds, 1.0, 0.0
            ).astype(bf16)
            same = contract(hot, spread, 0, 0)
            in_aug = (lane % HEAD_DIM) < 8
            aug_q = jnp.where(in_aug, same, 0.0)
            aug_k = jnp.where(in_aug, (same - 1.0) * far_score, 0.0)
            rows_in = normed_ref[rows, :]
            q = jnp.dot(rows_in, w_s[:, 0:256], preferred_element_type=f32)
            k = jnp.dot(rows_in, w_s[:, 256:512], preferred_element_type=f32)
            v = jnp.dot(rows_in, w_s[:, 512:768], preferred_element_type=f32)
            scale = HEAD_DIM ** (-0.5)
            for h, (cols, mine) in enumerate(
                ((slice(0, 128), low_half), (slice(0, 128), ~low_half), (slice(128, 256), low_half))
            ):
                q_ref[h, rows, :] = jnp.where(mine, q[:, cols] * scale, aug_q).astype(bf16)
                k_h = jnp.where(mine, k[:, cols], aug_k).astype(bf16)
                k_ref[h, rows, :] = k_h
                v_ref[h, rows, :] = jnp.where(mine, v[:, cols], 1.0).astype(bf16)
                kt_s[h, :, rows] = k_h.T
            return carry

        lax.fori_loop(0, count, project, 0)

    offset = lax.broadcasted_iota(jnp.int32, (BUCKETS, length), 1)
    offset = jnp.where(offset >= length // 2, offset - length, offset)
    hot_bucket = jnp.where(
        bucket_of(offset) == lax.broadcasted_iota(jnp.int32, (BUCKETS, length), 0), 1.0, 0.0
    ).astype(bf16)
    by_offset = contract(table_ref[head], hot_bucket, 1, 0)[0:1]
    spread_rows = jnp.broadcast_to(by_offset, (BLK, length))
    bias_s[...] = pltpu.roll(spread_rows, 0, 1, stride=1, stride_axis=0)

    for block in range(count):
        rows = slice(block * BLK, (block + 1) * BLK)
        q_h = q_ref[head, rows, :]
        top = None
        for key in key_range(block, count):
            part = jnp.dot(
                q_h, kt_s[head, :, key * BLK : (key + 1) * BLK], preferred_element_type=f32
            )
            delta = key - block
            at = (delta * BLK) % length
            part = part + bias_s[:, at : at + BLK]
            score_s[:, key * BLK : (key + 1) * BLK] = part
            top = part if top is None else jnp.maximum(top, part)
        top = jnp.max(jnp.maximum(top[:, :128], top[:, 128:]), axis=1, keepdims=True)
        total = jnp.zeros((BLK, 128), f32)
        for key in key_range(block, count):
            cols = slice(key * BLK, (key + 1) * BLK)
            part = jnp.exp(score_s[:, cols] - top).astype(bf16)
            probs_ref[0, rows, cols] = part
            total = total + jnp.dot(part, v_ref[head, cols, :], preferred_element_type=f32)
        sums = pltpu.roll(total, HEAD_DIM, 1)
        inverse = 1.0 / sums
        out = total * inverse

        @pl.when(head == 0)
        def _():
            first_s[rows, 0:128] = out
            first_s[rows, 128:256] = inverse

        @pl.when(head == 1)
        def _():
            mixed_ref[rows, 0:128] = jnp.where(low_half, first_s[rows, 0:128], out).astype(bf16)
            inv_ref[rows, 0:128] = jnp.where(low_half, first_s[rows, 128:256], inverse)

        @pl.when(head == 2)
        def _():
            mixed_ref[rows, 128:192] = out[:, 0:HEAD_DIM].astype(bf16)
            inv_ref[rows, 128:256] = inverse


def attend(normed, wq, wk, wv, segments, bias_table):
    length, width = normed.shape
    heads = bias_table.shape[1]
    inner = heads * HEAD_DIM
    table = jnp.broadcast_to(bias_table.T[:, None, :], (heads, 8, BUCKETS))
    whole = lambda *dims: pl.BlockSpec(dims, lambda h: (0,) * len(dims))
    return pl.pallas_call(
        attend_kernel,
        grid=(heads,),
        name="attend",
        out_shape=(
            jax.ShapeDtypeStruct((length, inner), bf16),
            jax.ShapeDtypeStruct((heads, length, length), bf16),
            jax.ShapeDtypeStruct((heads, length, 128), bf16),
            jax.ShapeDtypeStruct((heads, length, 128), bf16),
            jax.ShapeDtypeStruct((heads, length, 128), bf16),
            jax.ShapeDtypeStruct((length, 256), f32),
        ),
        in_specs=[
            whole(length, width),
            whole(width, inner),
            whole(width, inner),
            whole(width, inner),
            whole(1, length),
            whole(heads, 8, BUCKETS),
        ],
        out_specs=(
            whole(length, inner),
            pl.BlockSpec((1, length, length), lambda h: (h, 0, 0)),
            whole(heads, length, 128),
            whole(heads, length, 128),
            whole(heads, length, 128),
            whole(length, 256),
        ),
        scratch_shapes=[
            pltpu.VMEM((width, 768), bf16),
            pltpu.VMEM((heads, 128, length), bf16),
            pltpu.VMEM((BLK, length), f32),
            pltpu.VMEM((BLK, length), f32),
            pltpu.VMEM((length, 256), f32),
        ],
        compiler_params=pltpu.CompilerParams(
            dimension_semantics=("arbitrary",), vmem_limit_bytes=48 << 20
        ),
        cost_estimate=pl.CostEstimate(flops=3 << 30, bytes_accessed=12 << 20, transcendentals=3 << 20),
    )(normed, wq, wk, wv, segments, table)


def attend_back_kernel(
    mixed_grad_ref, mixed_ref, inv_ref, probs_ref, q_ref, k_ref, v_ref, normed_ref,
    wq_ref, wk_ref, wv_ref, gain1_ref, gain2_grad_ref,
    normed_grad_ref, weight_grad_ref, small_ref,
    w_s, dot_s, dott_s, qt_s, vt_s, grad_s, joined_s, near_s, far_s, dkt_s, dvt_s,
):
    head = pl.program_id(0)
    length = normed_ref.shape[0]
    count = length // BLK
    lane = lax.broadcasted_iota(jnp.int32, (BLK, 128), 1)
    low_half = lane < HEAD_DIM
    heads = 3

    @pl.when(head == 0)
    def _():
        small_ref[...] = jnp.zeros_like(small_ref)
        small_ref[1:2, :] = gain2_grad_ref[...]
        w_s[...] = jnp.zeros_like(w_s)
        for place, ref in enumerate((wq_ref, wk_ref, wv_ref)):
            w_s[:, 256 * place : 256 * place + 192] = ref[...]

        def prepare(step, carry):
            rows = pl.ds(pl.multiple_of(step * BLK, BLK), BLK)
            for h in range(heads):
                cols = slice(0, 128) if h < 2 else slice(128, 256)
                mine = ~low_half if h == 1 else low_half
                if h < 2:
                    grad = mixed_grad_ref[rows, 0:128].astype(f32)
                    mix = mixed_ref[rows, 0:128].astype(f32)
                else:
                    fill = jnp.zeros((BLK, HEAD_DIM), f32)
                    grad = jnp.concatenate(
                        (mixed_grad_ref[rows, 128:192].astype(f32), fill), axis=1
                    )
                    mix = jnp.concatenate((mixed_ref[rows, 128:192].astype(f32), fill), axis=1)
                inverse = inv_ref[rows, cols]
                grad = jnp.where(mine, grad * inverse, 0.0)
                centre = -jnp.sum(grad * mix, axis=1, keepdims=True)
                high = centre.astype(bf16).astype(f32)
                base = 0 if h == 1 else HEAD_DIM
                grad = jnp.where(lane == base, high, grad)
                grad = jnp.where(lane == base + 1, centre - high, grad)
                low = grad.astype(bf16)
                dot_s[h, rows, :] = low
                dott_s[h, :, rows] = low.T
                qt_s[h, :, rows] = q_ref[h, rows, :].T
                vt_s[h, :, rows] = v_ref[h, rows, :].T
            return carry

        lax.fori_loop(0, count, prepare, 0)

    near_s[...] = jnp.zeros_like(near_s)
    far_s[...] = jnp.zeros_like(far_s)
    dkt_s[...] = jnp.zeros_like(dkt_s)
    dvt_s[...] = jnp.zeros_like(dvt_s)
    for block in range(count):
        rows = slice(block * BLK, (block + 1) * BLK)
        d_h = dot_s[head, rows, :]
        dt_h = dott_s[head, :, rows]
        qt_h = qt_s[head, :, rows]
        query_grad = jnp.zeros((BLK, 128), f32)
        for key in key_range(block, count):
            cols = slice(key * BLK, (key + 1) * BLK)
            probs = probs_ref[0, rows, cols]
            slope = jnp.dot(d_h, vt_s[head, :, cols], preferred_element_type=f32)
            grad = probs.astype(f32) * slope
            low = grad.astype(bf16)
            delta = key - block
            if abs(delta) == 2:
                side = 0 if delta < 0 else 1
                far_s[side] += grad[:, :128] + grad[:, 128:]
            else:
                near_s[:, (delta + 1) * BLK : (delta + 2) * BLK] += grad
            query_grad = query_grad + jnp.dot(low, k_ref[head, cols, :], preferred_element_type=f32)
            dkt_s[:, cols] += jnp.dot(qt_h, low, preferred_element_type=f32)
            dvt_s[:, cols] += jnp.dot(dt_h, probs, preferred_element_type=f32)
        grad_s[rows, 0:128] = query_grad * HEAD_DIM ** (-0.5)
    for block in range(count):
        rows = slice(block * BLK, (block + 1) * BLK)
        grad_s[rows, 128:256] = dkt_s[:, rows].T
        grad_s[rows, 256:384] = dvt_s[:, rows].T

    place = lax.broadcasted_iota(jnp.int32, (BLK, 3 * BLK), 1) - BLK
    place = place - lax.broadcasted_iota(jnp.int32, (BLK, 3 * BLK), 0)
    bucket = bucket_of(place)
    near = near_s[...]
    sub = lax.broadcasted_iota(jnp.int32, (BUCKETS, 128), 0)
    table = jnp.zeros((BUCKETS, 128), f32)
    for b in range(BUCKETS):
        if b == 16:
            continue
        part = jnp.sum(jnp.where(bucket == b, near, 0.0), axis=0, keepdims=True)
        folded = part[:, 0:128]
        for at in range(1, 6):
            folded = folded + part[:, at * 128 : (at + 1) * 128]
        if b in (15, 31):
            folded = folded + jnp.sum(far_s[0 if b == 15 else 1], axis=0, keepdims=True)
        table = jnp.where(sub == b, folded, table)
    flat = lax.dot_general(
        jnp.ones((8, 128), f32), table, (((1,), (1,)), ((), ())),
        preferred_element_type=f32, precision=lax.Precision.HIGHEST,
    )
    for h in range(heads):
        @pl.when(head == h)
        def _(h=h):
            small_ref[8 + h : 9 + h, 0:BUCKETS] = flat[0:1]

    @pl.when(head == 0)
    def _():
        for at in range(3):
            joined_s[:, 256 * at : 256 * at + 128] = grad_s[:, 128 * at : 128 * at + 128].astype(bf16)

    @pl.when(head == 1)
    def _():
        lanes = lax.broadcasted_iota(jnp.int32, (length, 128), 1)
        for at in range(3):
            joined_s[:, 256 * at : 256 * at + 128] = jnp.where(
                lanes < HEAD_DIM,
                joined_s[:, 256 * at : 256 * at + 128].astype(f32),
                grad_s[:, 128 * at : 128 * at + 128],
            ).astype(bf16)

    @pl.when(head == 2)
    def _():
        lanes = lax.broadcasted_iota(jnp.int32, (length, 128), 1)
        for at in range(3):
            joined_s[:, 256 * at + 128 : 256 * at + 256] = jnp.where(
                lanes < HEAD_DIM, grad_s[:, 128 * at : 128 * at + 128], 0.0
            ).astype(bf16)
        gain1_grad = jnp.zeros((1, normed_ref.shape[1]), f32)
        for block in range(count):
            rows = slice(block * BLK, (block + 1) * BLK)
            part = contract(joined_s[rows, :], w_s[...], 1, 1)
            normed_grad_ref[rows, :] = part.astype(bf16)
            gain1_grad = gain1_grad + jnp.sum(part * normed_ref[rows, :].astype(f32), axis=0, keepdims=True)
        small_ref[0:1, :] = gain1_grad / gain1_ref[...].astype(f32)
        for at in range(3):
            width = normed_ref.shape[1]
            part = contract(normed_ref[...], joined_s[:, 256 * at : 256 * at + 256], 0, 0)
            weight_grad_ref[at * width : (at + 1) * width, :] = part[:, 0:192].astype(bf16)


def attend_back(mixed_grad, mixed, inverse, probs, q, k, v, normed, wq, wk, wv, gain1, gain2_grad):
    length, width = normed.shape
    heads = q.shape[0]
    inner = heads * HEAD_DIM
    whole = lambda *dims: pl.BlockSpec(dims, lambda h: (0,) * len(dims))
    return pl.pallas_call(
        attend_back_kernel,
        grid=(heads,),
        name="attend_back",
        out_shape=(
            jax.ShapeDtypeStruct((length, width), bf16),
            jax.ShapeDtypeStruct((3 * width, inner), bf16),
            jax.ShapeDtypeStruct((16, width), f32),
        ),
        in_specs=[
            whole(length, inner),
            whole(length, inner),
            whole(length, 256),
            pl.BlockSpec((1, length, length), lambda h: (h, 0, 0)),
            whole(heads, length, 128),
            whole(heads, length, 128),
            whole(heads, length, 128),
            whole(length, width),
            whole(width, inner),
            whole(width, inner),
            whole(width, inner),
            whole(1, width),
            whole(1, width),
        ],
        out_specs=(
            whole(length, width),
            whole(3 * width, inner),
            whole(16, width),
        ),
        scratch_shapes=[
            pltpu.VMEM((width, 768), bf16),
            pltpu.VMEM((heads, length, 128), bf16),
            pltpu.VMEM((heads, 128, length), bf16),
            pltpu.VMEM((heads, 128, length), bf16),
            pltpu.VMEM((heads, 128, length), bf16),
            pltpu.VMEM((length, 384), f32),
            pltpu.VMEM((length, 768), bf16),
            pltpu.VMEM((BLK, 3 * BLK), f32),
            pltpu.VMEM((2, BLK, 128), f32),
            pltpu.VMEM((128, length), f32),
            pltpu.VMEM((128, length), f32),
        ],
        compiler_params=pltpu.CompilerParams(
            dimension_semantics=("arbitrary",), vmem_limit_bytes=56 << 20
        ),
        cost_estimate=pl.CostEstimate(flops=6 << 30, bytes_accessed=16 << 20, transcendentals=0),
    )(mixed_grad, mixed, inverse, probs, q, k, v, normed, wq, wk, wv, gain1, gain2_grad)


def mean_square_scale(rows):
    return lax.rsqrt(jnp.mean(rows * rows, axis=-1, keepdims=True) + norm_eps)


def unit_kernel(
    mixed_ref, hidden_ref, cot_ref, out_w_ref, gate_w_ref, up_w_ref, down_w_ref, gain_ref,
    output_ref, residual_grad_ref, mixed_grad_ref, gain_grad_ref,
    out_wg_ref, gate_wg_ref, up_wg_ref, down_wg_ref,
    residual_s, normed_s, sum_s, back_s,
):
    step = pl.program_id(0)
    parts = pl.num_programs(0)
    groups = mixed_ref.shape[0]
    tokens = residual_s.shape[0]

    @pl.when(step == 0)
    def _():
        mixed = jnp.concatenate([mixed_ref[g] for g in range(groups)], axis=1)
        out_w = jnp.concatenate([out_w_ref[g] for g in range(groups)], axis=0)
        residual = hidden_ref[...].astype(f32) + jnp.dot(mixed, out_w, preferred_element_type=f32)
        residual_s[...] = residual
        normed_s[...] = (residual * mean_square_scale(residual) * gain_ref[...].astype(f32)).astype(bf16)
        sum_s[...] = jnp.zeros_like(sum_s)
        back_s[...] = jnp.zeros_like(back_s)

    normed = normed_s[...]
    cot = cot_ref[...]
    gate = jnp.dot(normed, gate_w_ref[0], preferred_element_type=f32)
    up = jnp.dot(normed, up_w_ref[0], preferred_element_type=f32)
    hidden_grad = contract(cot, down_w_ref[0], 1, 1)
    c0 = 0.7978845608028654
    square = gate * gate
    bend = jnp.tanh(gate * (c0 + (c0 * 0.044715) * square))
    half = 0.5 + 0.5 * bend
    act = gate * half
    slope = half + 0.5 * gate * (1.0 - bend * bend) * (c0 + (3.0 * c0 * 0.044715) * square)
    hidden = (act * up).astype(bf16)
    gate_grad = (hidden_grad * up * slope).astype(bf16)
    up_grad = (hidden_grad * act).astype(bf16)
    sum_s[...] += jnp.dot(hidden, down_w_ref[0], preferred_element_type=f32)
    back_s[...] += contract(gate_grad, gate_w_ref[0], 1, 1) + contract(up_grad, up_w_ref[0], 1, 1)
    down_wg_ref[0] = contract(hidden, cot, 0, 0).astype(bf16)
    gate_wg_ref[0] = contract(normed, gate_grad, 0, 0).astype(bf16)
    up_wg_ref[0] = contract(normed, up_grad, 0, 0).astype(bf16)

    @pl.when(step == parts - 1)
    def _():
        residual = residual_s[...]
        output_ref[...] = (residual + sum_s[...]).astype(bf16)
        back = back_s[...]
        r = mean_square_scale(residual)
        gain_grad_ref[...] = jnp.sum(back * residual * r, axis=0, keepdims=True)
        g = back * gain_ref[...].astype(f32)
        centre = jnp.mean(g * residual, axis=-1, keepdims=True)
        residual_grad = cot_ref[...].astype(f32) + r * g - (r * r * r * centre) * residual
        residual_grad_ref[...] = residual_grad
        low = residual_grad.astype(bf16)
        for g_at in range(groups):
            mixed_grad_ref[g_at] = contract(low, out_w_ref[g_at], 1, 1).astype(bf16)
            out_wg_ref[g_at] = contract(mixed_ref[g_at], low, 0, 0).astype(bf16)


def unit(mixed, hidden_in, cot, out_w, gate_w, up_w, down_w, gain):
    groups, tokens, part = mixed.shape
    width = hidden_in.shape[1]
    units = gate_w.shape[2]
    whole = lambda *dims: pl.BlockSpec(dims, lambda s: (0,) * len(dims))
    each = lambda *dims: pl.BlockSpec((1,) + dims, lambda s: (s, 0, 0))
    return pl.pallas_call(
        unit_kernel,
        grid=(groups,),
        name="unit",
        out_shape=(
            jax.ShapeDtypeStruct((tokens, width), bf16),
            jax.ShapeDtypeStruct((tokens, width), f32),
            jax.ShapeDtypeStruct((groups, tokens, part), bf16),
            jax.ShapeDtypeStruct((1, width), f32),
            jax.ShapeDtypeStruct((groups, part, width), bf16),
            jax.ShapeDtypeStruct((groups, width, units), bf16),
            jax.ShapeDtypeStruct((groups, width, units), bf16),
            jax.ShapeDtypeStruct((groups, units, width), bf16),
        ),
        in_specs=[
            whole(groups, tokens, part),
            whole(tokens, width),
            whole(tokens, width),
            whole(groups, part, width),
            each(width, units),
            each(width, units),
            each(units, width),
            whole(1, width),
        ],
        out_specs=(
            whole(tokens, width),
            whole(tokens, width),
            whole(groups, tokens, part),
            whole(1, width),
            whole(groups, part, width),
            each(width, units),
            each(width, units),
            each(units, width),
        ),
        scratch_shapes=[
            pltpu.VMEM((tokens, width), f32),
            pltpu.VMEM((tokens, width), bf16),
            pltpu.VMEM((tokens, width), f32),
            pltpu.VMEM((tokens, width), f32),
        ],
        compiler_params=pltpu.CompilerParams(
            dimension_semantics=("arbitrary",), vmem_limit_bytes=48 << 20
        ),
        cost_estimate=pl.CostEstimate(flops=9 << 30, bytes_accessed=26 << 20, transcendentals=1 << 20),
    )(mixed, hidden_in, cot, out_w, gate_w, up_w, down_w, gain)


MESH_IDS = pl.DeviceIdType.MESH


def places():
    dp = lax.axis_index("dp")
    line = lax.axis_index("tensor")
    core = lax.rem(dp, 2)
    x = lax.rem(dp // 2, 2)
    y = dp // 4
    flips = (dp + 1 - 2 * core, dp + 2 - 4 * x, dp + 4 - 8 * y)
    return dp, line, core, x, y, flips


def nearest(line, k):
    upper = line // 2
    inner = line * (1 - upper) + (3 - line) * upper
    block = k + 1 - inner if k == 0 else k + 1
    block = block * (1 - upper) + (3 - block) * upper
    way = (1 if k == 0 else -1) * (1 - 2 * upper)
    return block, way


class Item:
    def __init__(self, place, base, rows, flipped, by_columns=False):
        self.place, self.base, self.rows = place, base, rows
        self.flipped, self.by_columns = flipped, by_columns

    def bits(self, x, y):
        return (y, x) if self.flipped else (x, y)

    def partner(self, level, flips):
        if level == 0:
            return flips[0]
        return flips[1 + ((level - 1) ^ int(self.flipped))]

    def window(self, ref, lead, level, core, first, second):
        width = ref.shape[-1]
        if self.by_columns:
            size = self.rows // (1, 2, 4)[level - 1]
            start = self.base + 0 * core
            if level > 1:
                start = start + first * (self.rows // 2)
            if level > 2:
                start = start + second * (self.rows // 4)
            cols = pl.ds(pl.multiple_of(core * (width // 2), 128), width // 2)
        else:
            size = self.rows // (2, 4, 8)[level - 1]
            start = self.base + core * (self.rows // 2)
            if level > 1:
                start = start + first * (self.rows // 4)
            if level > 2:
                start = start + second * (self.rows // 8)
            cols = pl.ds(0, width)
        rows = pl.ds(pl.multiple_of(start, 16), size)
        if lead is None:
            return ref.at[rows, cols]
        return ref.at[lead, rows, cols]


def weight_items(units, part, width):
    return (
        Item(0, 0, width, False),
        Item(1, 0, width, True),
        Item(2, 0, units // 2, False),
        Item(2, units // 2, units // 2, True),
        Item(3, 0, part, False, by_columns=True),
    )


def gather_kernel(
    normed_ref, gate_ref, up_ref, down_ref, out_ref,
    normed_all, gate_all, up_all, down_all, out_all,
    z_send, z_recv, p_send, p_recv, own_sem,
    hold_gate, hold_up, hold_down, hold_out, hold_normed,
):
    dp, line, core, x, y, flips = places()
    upper = line // 2
    inner = line * (1 - upper) + (3 - line) * upper
    own = (gate_ref, up_ref, down_ref, out_ref)
    full = (gate_all, up_all, down_all, out_all)
    units, width = down_ref.shape
    items = weight_items(units, out_ref.shape[0], width)
    count = len(items)

    barrier = pltpu.get_barrier_semaphore()
    for flip in flips:
        pl.semaphore_signal(barrier, inc=1, device_id=(flip, line), device_id_type=MESH_IDS)

    @pl.when(line > 0)
    def _():
        pl.semaphore_signal(barrier, inc=1, device_id=(dp, line - 1), device_id_type=MESH_IDS)

    @pl.when(line < 3)
    def _():
        pl.semaphore_signal(barrier, inc=1, device_id=(dp, line + 1), device_id_type=MESH_IDS)

    pl.semaphore_wait(barrier, 4 + inner)

    def eighth(i, ref, lead):
        item = items[i]
        first, second = item.bits(x, y)
        return item.window(ref, lead, 3, core, first, second)

    def along(i, block, target, side, first_hop):
        if i == count:
            src = normed_ref if first_hop else normed_all.at[block]
            dst = normed_all.at[block]
        else:
            dst = eighth(i, full[items[i].place], block)
            src = eighth(i, own[items[i].place], None) if first_hop else dst
        return pltpu.make_async_remote_copy(
            src_ref=src, dst_ref=dst, send_sem=z_send.at[i, block, side], recv_sem=z_recv.at[i, block],
            device_id=(dp, target), device_id_type=MESH_IDS,
        )

    def send_own(i):
        @pl.when(line > 0)
        def _():
            along(i, line, line - 1, 0, True).start()

        @pl.when(line < 3)
        def _():
            along(i, line, line + 1, 1, True).start()

    def arrive(i, k):
        block, way = nearest(line, k)
        along(i, block, line, 0, False).wait_recv()

        @pl.when(inner == 1)
        def _():
            along(i, block, line + way, 0, False).start()

    def spread(i, k, stage):
        block, _ = nearest(line, k)
        item = items[i]
        first, second = item.bits(x, y)
        window = item.window(full[item.place], block, 3 - stage, core, first, second)
        return pltpu.make_async_remote_copy(
            src_ref=window, dst_ref=window, send_sem=p_send.at[stage, i, k], recv_sem=p_recv.at[stage, i, k],
            device_id=(item.partner(2 - stage, flips), line), device_id_type=MESH_IDS,
        )

    for i in range(count):
        send_own(i)
    holds = (hold_gate, hold_up, hold_down, hold_out, hold_normed)
    loads = []
    stores = []
    for place, ref in enumerate(own + (normed_ref,)):
        target = (full + (normed_all,))[place].at[line]
        loads.append(pltpu.make_async_copy(ref, holds[place], own_sem.at[0, place]))
        stores.append(pltpu.make_async_copy(holds[place], target, own_sem.at[1, place]))
    for load in loads:
        load.start()
    for load, store in zip(loads, stores):
        load.wait()
        store.start()

    def advance(k, stage):
        for i in range(count):
            if stage > 0:
                spread(i, k, stage - 1).wait_recv()
            spread(i, k, stage).start()

    for k in range(3):
        for i in range(count):
            arrive(i, k)
            spread(i, k, 0).start()
        if k == 2:
            send_own(count)
        if k >= 1:
            advance(k - 1, 1)
        if k >= 2:
            advance(k - 2, 2)
    advance(2, 1)
    arrive(count, 0)
    advance(1, 2)
    arrive(count, 1)
    advance(2, 2)
    arrive(count, 2)

    for store in stores:
        store.wait()
    for i in range(count + 1):
        @pl.when(line > 0)
        def _(i=i):
            along(i, line, line - 1, 0, True).wait_send()

        @pl.when(line < 3)
        def _(i=i):
            along(i, line, line + 1, 1, True).wait_send()

        @pl.when(inner == 1)
        def _(i=i):
            for k in range(3):
                block, way = nearest(line, k)
                along(i, block, line + way, 0, False).wait_send()

    for k in range(3):
        for i in range(count):
            spread(i, k, 2).wait_recv()
            for stage in range(3):
                spread(i, k, stage).wait_send()


def gather(normed, gate, up, down, out):
    rows, width = normed.shape
    units, part = gate.shape[1], out.shape[0]
    anywhere = pl.BlockSpec(memory_space=pl.ANY)
    return pl.pallas_call(
        gather_kernel,
        name="gather",
        out_shape=(
            jax.ShapeDtypeStruct((4, rows, width), bf16),
            jax.ShapeDtypeStruct((4, width, units), bf16),
            jax.ShapeDtypeStruct((4, width, units), bf16),
            jax.ShapeDtypeStruct((4, units, width), bf16),
            jax.ShapeDtypeStruct((4, part, width), bf16),
        ),
        in_specs=[anywhere] * 5,
        out_specs=(anywhere,) * 5,
        scratch_shapes=[
            pltpu.SemaphoreType.DMA((6, 4, 2)),
            pltpu.SemaphoreType.DMA((6, 4)),
            pltpu.SemaphoreType.DMA((3, 5, 3)),
            pltpu.SemaphoreType.DMA((3, 5, 3)),
            pltpu.SemaphoreType.DMA((2, 5)),
            pltpu.VMEM(gate.shape, bf16),
            pltpu.VMEM(up.shape, bf16),
            pltpu.VMEM(down.shape, bf16),
            pltpu.VMEM(out.shape, bf16),
            pltpu.VMEM(normed.shape, bf16),
        ],
        compiler_params=pltpu.CompilerParams(collective_id=1, has_side_effects=True),
    )(normed, gate, up, down, out)


def swap_kernel(mine_ref, theirs_ref, send_sem, recv_sem, own_sem):
    dp, line, _, _, _, _ = places()
    barrier = pltpu.get_barrier_semaphore()
    others = [lax.rem(line + i, 4) for i in (1, 2, 3)]
    for other in others:
        pl.semaphore_signal(barrier, inc=1, device_id=(dp, other), device_id_type=MESH_IDS)
    pl.semaphore_wait(barrier, 3)
    copies = [
        pltpu.make_async_remote_copy(
            src_ref=mine_ref.at[other], dst_ref=theirs_ref.at[line], send_sem=send_sem.at[i], recv_sem=recv_sem.at[2 - i],
            device_id=(dp, other), device_id_type=MESH_IDS,
        )
        for i, other in enumerate(others)
    ]
    for copy in copies:
        copy.start()
    keep = pltpu.make_async_copy(mine_ref.at[line], theirs_ref.at[line], own_sem)
    keep.start()
    for i, other in enumerate(others):
        copies[i].wait_send()
        pltpu.make_async_remote_copy(
            src_ref=mine_ref.at[other], dst_ref=theirs_ref.at[other], send_sem=send_sem.at[i], recv_sem=recv_sem.at[i],
            device_id=(dp, other), device_id_type=MESH_IDS,
        ).wait_recv()
    keep.wait()


def swap(blocks):
    anywhere = pl.BlockSpec(memory_space=pl.ANY)
    return pl.pallas_call(
        swap_kernel,
        name="swap",
        out_shape=jax.ShapeDtypeStruct(blocks.shape, blocks.dtype),
        in_specs=[anywhere],
        out_specs=anywhere,
        scratch_shapes=[
            pltpu.SemaphoreType.DMA((3,)),
            pltpu.SemaphoreType.DMA((3,)),
            pltpu.SemaphoreType.DMA,
        ],
        compiler_params=pltpu.CompilerParams(collective_id=2, has_side_effects=True),
    )(blocks)


class Chunk:
    def __init__(self, item, block, acc, from_core, from_first, from_second, from_left, from_right, number):
        self.item, self.block, self.number = item, block, number
        self.acc, self.from_core, self.from_first = acc, from_core, from_first
        self.from_second, self.from_left, self.from_right = from_second, from_left, from_right


def add_rows(target, start, size, source):
    rows = pl.ds(start, size)
    target[rows, :] = (target[rows, :].astype(f32) + source[...].astype(f32)).astype(bf16)


def reduce_kernel(
    back_ref, out_ref, gate_ref, up_ref, down_ref, qkv_ref, small_ref,
    back_sum, out_sum, gate_sum, up_sum, down_sum, qkv_sum, small_sum,
    *scratch,
):
    dp, line, core, x, y, flips = places()
    upper = line // 2
    inner = line * (1 - upper) + (3 - line) * upper
    units, width = down_ref.shape[1:]
    part = out_ref.shape[1]
    grads = (gate_ref, up_ref, down_ref, out_ref)
    sums = (gate_sum, up_sum, down_sum, out_sum)
    items = weight_items(units, part, width)
    count = len(items)
    scratch = list(scratch)
    take = lambda: scratch.pop(0)
    halves, cores, firsts, seconds, lefts, rights = ([take() for _ in range(count)] for _ in range(6))
    qkv_half, qkv_core, qkv_first, qkv_second = (take() for _ in range(4))
    back_acc, back_left, back_right = (take() for _ in range(3))
    small_got = take()
    load_sem, core_send, core_recv, pair_send, pair_recv = (take() for _ in range(5))
    line_send, left_recv, right_recv, spread_send, spread_recv = (take() for _ in range(5))
    back_load, back_send, back_left_recv, back_right_recv, small_send, small_recv = (take() for _ in range(6))

    barrier = pltpu.get_barrier_semaphore()
    across = lax.rem(line + 2, 4)
    for flip in flips:
        pl.semaphore_signal(barrier, inc=1, device_id=(flip, line), device_id_type=MESH_IDS)
    pl.semaphore_signal(barrier, inc=1, device_id=(dp, across), device_id_type=MESH_IDS)

    @pl.when(line > 0)
    def _():
        pl.semaphore_signal(barrier, inc=1, device_id=(dp, line - 1), device_id_type=MESH_IDS)

    @pl.when(line < 3)
    def _():
        pl.semaphore_signal(barrier, inc=1, device_id=(dp, line + 1), device_id_type=MESH_IDS)

    pl.semaphore_wait(barrier, 5 + inner)

    def remote(src, dst, send, recv, target):
        return pltpu.make_async_remote_copy(
            src_ref=src, dst_ref=dst, send_sem=send, recv_sem=recv, device_id=target, device_id_type=MESH_IDS
        )

    chunks = []
    qkv_item = Item(4, 0, qkv_ref.shape[0], True)
    chunks.append(Chunk(qkv_item, None, qkv_half, qkv_core, qkv_first, qkv_second, None, None, 0))
    for i, item in enumerate(items):
        for block in (0, 3, 1, 2):
            chunks.append(
                Chunk(
                    item, block, halves[i].at[block], cores[i].at[block], firsts[i].at[block],
                    seconds[i].at[block], lefts[i].at[block], rights[i].at[block], len(chunks),
                )
            )

    def source(chunk):
        return qkv_ref if chunk.block is None else grads[chunk.item.place]

    def result(chunk):
        return qkv_sum if chunk.block is None else sums[chunk.item.place]

    def load_copy(chunk):
        window = chunk.item.window(source(chunk), chunk.block, 1, core, 0, 0)
        return pltpu.make_async_copy(window, chunk.acc, load_sem.at[chunk.number])

    def core_copy(chunk):
        window = chunk.item.window(source(chunk), chunk.block, 1, 1 - core, 0, 0)
        n = chunk.number
        return remote(window, chunk.from_core, core_send.at[n], core_recv.at[n], (flips[0], line))

    def pair_copy(chunk, stage):
        half = chunk.acc.shape[0]
        first, second = chunk.item.bits(x, y)
        n = chunk.number
        if stage == 0:
            size, start, target = half // 2, (1 - first) * (half // 2), chunk.from_first
        else:
            size = half // 4
            start, target = first * (half // 2) + (1 - second) * (half // 4), chunk.from_second
        window = chunk.acc.at[pl.ds(pl.multiple_of(start, 16), size), :]
        partner = chunk.item.partner(1 + stage, flips)
        return remote(window, target, pair_send.at[stage, n], pair_recv.at[stage, n], (partner, line))

    def eighth(chunk):
        half = chunk.acc.shape[0]
        first, second = chunk.item.bits(x, y)
        start = pl.multiple_of(first * (half // 2) + second * (half // 4), 16)
        return start, half // 4

    def mine(chunk):
        start, size = eighth(chunk)
        return chunk.acc.at[pl.ds(start, size), :]

    def hop_copy(chunk, at, right):
        n = chunk.number
        if right:
            return remote(mine(chunk), chunk.from_left, line_send.at[n], left_recv.at[n], (dp, at + 1))
        return remote(mine(chunk), chunk.from_right, line_send.at[n], right_recv.at[n], (dp, at - 1))

    def spread_copy(chunk, stage):
        item = chunk.item
        first, second = item.bits(x, y)
        window = item.window(result(chunk), None, 3 - stage, core, first, second)
        src = mine(chunk) if stage == 0 else window
        n = chunk.number
        return remote(
            src, window, spread_send.at[stage, n], spread_recv.at[stage, n], (item.partner(2 - stage, flips), line)
        )

    def keep_copy(chunk):
        first, second = chunk.item.bits(x, y)
        window = chunk.item.window(result(chunk), None, 3, core, first, second)
        return pltpu.make_async_copy(mine(chunk), window, load_sem.at[chunk.number])

    def from_left(chunk, at):
        hop_copy(chunk, at, True).wait_recv()

    def on_plane(chunk, act):
        if chunk.block is None:
            act()
        else:
            pl.when(line == chunk.block)(act)

    def step_core(chunk):
        load_copy(chunk).wait()
        core_copy(chunk).wait_recv()
        half = chunk.acc.shape[0]
        add_rows(chunk.acc, 0, half, chunk.from_core)
        pair_copy(chunk, 0).start()

    def step_first(chunk):
        pair_copy(chunk, 0).wait_recv()
        half = chunk.acc.shape[0]
        first, _ = chunk.item.bits(x, y)
        add_rows(chunk.acc, pl.multiple_of(first * (half // 2), 16), half // 2, chunk.from_first)
        pair_copy(chunk, 1).start()

    def step_second(chunk):
        pair_copy(chunk, 1).wait_recv()
        start, size = eighth(chunk)
        add_rows(chunk.acc, start, size, chunk.from_second)

    def step_hop(chunk, hop):
        if chunk.block is None:
            return
        start, size = eighth(chunk)
        if chunk.block > hop:
            @pl.when(line == hop)
            def _():
                if hop > 0:
                    hop_copy(chunk, hop, True).wait_recv()
                    add_rows(chunk.acc, start, size, chunk.from_left)
                hop_copy(chunk, hop, True).start()
        at = 3 - hop
        if chunk.block < at:
            @pl.when(line == at)
            def _():
                if hop > 0:
                    hop_copy(chunk, at, False).wait_recv()
                    add_rows(chunk.acc, start, size, chunk.from_right)
                hop_copy(chunk, at, False).start()

    def step_last(chunk):
        def act():
            if chunk.block is not None:
                start, size = eighth(chunk)
                if chunk.block > 0:
                    hop_copy(chunk, chunk.block, True).wait_recv()
                    add_rows(chunk.acc, start, size, chunk.from_left)
                if chunk.block < 3:
                    hop_copy(chunk, chunk.block, False).wait_recv()
                    add_rows(chunk.acc, start, size, chunk.from_right)
            spread_copy(chunk, 0).start()
            keep_copy(chunk).start()

        on_plane(chunk, act)

    def step_spread(chunk, stage):
        def act():
            if stage == 1:
                keep_copy(chunk).wait()
            spread_copy(chunk, stage - 1).wait_recv()
            if stage < 3:
                spread_copy(chunk, stage).start()

        on_plane(chunk, act)

    parts = back_acc.shape[1]
    back_rows = back_acc.shape[2]

    def back_load_copy():
        return pltpu.make_async_copy(back_ref, back_acc, back_load)

    def back_hop_copy(block, part_at, at, right):
        src = back_acc.at[block, part_at]
        if right:
            return remote(
                src, back_left.at[block, part_at], back_send.at[block, part_at], back_left_recv.at[block, part_at],
                (dp, at + 1),
            )
        return remote(
            src, back_right.at[block, part_at], back_send.at[block, part_at], back_right_recv.at[block, part_at],
            (dp, at - 1),
        )

    def back_hop(hop, part_at):
        at = 3 - hop

        @pl.when(line == hop)
        def _():
            for block in range(3, hop, -1):
                if hop > 0:
                    back_hop_copy(block, part_at, hop, True).wait_recv()
                    acc = back_acc.at[block, part_at]
                    add_rows(acc, 0, back_rows, back_left.at[block, part_at])
                back_hop_copy(block, part_at, hop, True).start()

        @pl.when(line == at)
        def _():
            for block in range(0, at):
                if hop > 0:
                    back_hop_copy(block, part_at, at, False).wait_recv()
                    acc = back_acc.at[block, part_at]
                    add_rows(acc, 0, back_rows, back_right.at[block, part_at])
                back_hop_copy(block, part_at, at, False).start()

    def back_last(part_at):
        for block in range(4):
            @pl.when(line == block)
            def _(block=block):
                total = back_acc[block, part_at].astype(f32)
                if block > 0:
                    back_hop_copy(block, part_at, block, True).wait_recv()
                    total = total + back_left[block, part_at].astype(f32)
                if block < 3:
                    back_hop_copy(block, part_at, block, False).wait_recv()
                    total = total + back_right[block, part_at].astype(f32)
                back_sum[part_at * back_rows : (part_at + 1) * back_rows, :] = total

    def small_copy(stage):
        partner = (flips[stage], line) if stage < 3 else (dp, line + 1 - 2 * lax.rem(line, 2))
        if stage == 4:
            partner = (dp, across)
        return remote(small_sum, small_got.at[stage], small_send.at[stage], small_recv.at[stage], partner)

    def small_step(stage):
        if stage > 0:
            small_copy(stage - 1).wait()
            rows = lax.broadcasted_iota(jnp.int32, small_sum.shape, 0)
            got = small_got[stage - 1]
            if stage > 3:
                got = jnp.where(rows < 8, got, 0.0)
            small_sum[...] = small_sum[...] + got
        else:
            small_sum[...] = small_ref[...]
        if stage < 5:
            small_copy(stage).start()

    loaded = back_load_copy()
    loaded.start()
    for chunk in chunks:
        core_copy(chunk).start()
        load_copy(chunk).start()
    loaded.wait()
    for part_at in range(parts):
        back_hop(0, part_at)
    lags = (0, 2, 4, 6, 8, 10, 12, 14, 16)
    extra = {3: [lambda: small_step(0)]}
    for stage in range(1, 6):
        extra.setdefault(3 + 3 * stage, []).append(lambda stage=stage: small_step(stage))
    for hop in (1, 2):
        for part_at in range(parts):
            extra.setdefault(4 * hop - 2 + 2 * part_at, []).append(
                lambda hop=hop, part_at=part_at: back_hop(hop, part_at)
            )
    for part_at in range(parts):
        extra.setdefault(12 + 2 * part_at, []).append(lambda part_at=part_at: back_last(part_at))

    for slot in range(len(chunks) + lags[-1]):
        def at_lag(i):
            n = slot - lags[i]
            return chunks[n] if 0 <= n < len(chunks) else None

        for i, act in enumerate(
            (
                step_core, step_first, step_second,
                lambda c: step_hop(c, 1), lambda c: step_hop(c, 2), step_last,
                lambda c: step_spread(c, 1), lambda c: step_spread(c, 2), lambda c: step_spread(c, 3),
            )
        ):
            chunk = at_lag(i)
            if chunk is not None:
                act(chunk)
                if i == 2:
                    step_hop(chunk, 0)
        for act in extra.get(slot, ()):
            act()

    for chunk in chunks:
        core_copy(chunk).wait_send()
        pair_copy(chunk, 0).wait_send()
        pair_copy(chunk, 1).wait_send()

        def sent(chunk=chunk):
            for stage in range(3):
                spread_copy(chunk, stage).wait_send()

        on_plane(chunk, sent)
        if chunk.block is not None:
            pl.when(line < chunk.block)(lambda chunk=chunk: hop_copy(chunk, line, True).wait_send())
            pl.when(line > chunk.block)(lambda chunk=chunk: hop_copy(chunk, line, False).wait_send())
    for block in range(4):
        for part_at in range(parts):
            copy = functools.partial(back_hop_copy, block, part_at, line)
            pl.when(line < block)(lambda copy=copy: copy(True).wait_send())
            pl.when(line > block)(lambda copy=copy: copy(False).wait_send())


def reduce_all(back, out_wg, gate_wg, up_wg, down_wg, qkv_wg, small):
    groups, rows, width = back.shape[0], back.shape[1], back.shape[2]
    units, part = down_wg.shape[1], out_wg.shape[1]
    parts = 2
    items = weight_items(units, part, width)
    shapes = []
    for item in items:
        cols = (units, units, width, width)[item.place]
        shapes.append((item.rows, cols // 2) if item.by_columns else (item.rows // 2, cols))
    scratch = []
    for divide in (1, 1, 2, 4, 4, 4):
        scratch += [pltpu.VMEM((groups, r // divide, c), bf16) for r, c in shapes]
    qkv_half = (qkv_wg.shape[0] // 2, qkv_wg.shape[1])
    scratch += [pltpu.VMEM((qkv_half[0] // d, qkv_half[1]), bf16) for d in (1, 1, 2, 4)]
    scratch += [pltpu.VMEM((groups, parts, rows // parts, width), bf16)] * 3
    scratch += [pltpu.VMEM((5,) + small.shape, f32)]
    n = 1 + groups * len(items)
    dma = pltpu.SemaphoreType.DMA
    scratch += [dma((n,)), dma((n,)), dma((n,)), dma((2, n)), dma((2, n))]
    scratch += [dma((n,)), dma((n,)), dma((n,)), dma((3, n)), dma((3, n))]
    scratch += [dma, dma((groups, parts)), dma((groups, parts)), dma((groups, parts)), dma((5,)), dma((5,))]
    anywhere = pl.BlockSpec(memory_space=pl.ANY)
    inside = pl.BlockSpec(memory_space=pltpu.VMEM)
    return pl.pallas_call(
        reduce_kernel,
        name="reduce_all",
        out_shape=(
            jax.ShapeDtypeStruct((rows, width), f32),
            jax.ShapeDtypeStruct((part, width), bf16),
            jax.ShapeDtypeStruct((width, units), bf16),
            jax.ShapeDtypeStruct((width, units), bf16),
            jax.ShapeDtypeStruct((units, width), bf16),
            jax.ShapeDtypeStruct(qkv_wg.shape, bf16),
            jax.ShapeDtypeStruct(small.shape, f32),
        ),
        in_specs=[anywhere] * 6 + [inside],
        out_specs=(inside,) * 7,
        scratch_shapes=scratch,
        compiler_params=pltpu.CompilerParams(
            collective_id=3, has_side_effects=True, vmem_limit_bytes=50 << 20
        ),
    )(back.reshape(groups, parts, rows // parts, width), out_wg, gate_wg, up_wg, down_wg, qkv_wg, small)


def gather_by_axis(normed, gate, up, down, out):
    return tuple(lax.all_gather(part, "tensor", axis=0) for part in (normed, gate, up, down, out))


def swap_by_axis(blocks):
    return lax.all_to_all(blocks, "tensor", 0, 0)


def reduce_by_axis(back, out_wg, gate_wg, up_wg, down_wg, qkv_wg, small):
    back_sum = lax.psum_scatter(back, "tensor", scatter_dimension=0).astype(f32)
    parts = tuple(
        lax.psum_scatter(wg, "tensor", scatter_dimension=0) for wg in (out_wg, gate_wg, up_wg, down_wg)
    )
    sums = lax.psum(parts + (qkv_wg,), "dp")
    small_sum = lax.psum(small, "dp")
    gains = lax.psum(small_sum[:8], "tensor")
    return (back_sum,) + tuple(sums) + (jnp.concatenate((gains, small_sum[8:])),)


def shards(
    by_kernel,
    hidden_in, segment_ids, norm1_gain, query_weight, key_weight, value_weight, out_weight,
    bias_table, norm2_gain, gate_weight, up_weight, down_weight, out_cotangent,
):
    gather_parts = gather if by_kernel else gather_by_axis
    swap_parts = swap if by_kernel else swap_by_axis
    reduce_parts = reduce_all if by_kernel else reduce_by_axis
    rows_here, width = hidden_in.shape
    length = segment_ids.shape[1]
    assert segment_ids.shape[0] == 1
    groups = length // rows_here
    heads = bias_table.shape[1]
    input_rows = hidden_in.astype(f32)
    first_gain = norm1_gain.astype(f32)
    r1 = mean_square_scale(input_rows)
    normed_here = (input_rows * r1 * first_gain).astype(bf16)
    normed, gate_w, up_w, down_w, out_w = gather_parts(
        normed_here, gate_weight, up_weight, down_weight, out_weight
    )
    normed = normed.reshape(length, width)
    mixed, probs, q, k, v, inverse = attend(
        normed, query_weight, key_weight, value_weight, segment_ids, bias_table
    )
    mixed_here = swap_parts(mixed.reshape(groups, rows_here, -1))
    output, residual_grad, mixed_grad_here, gain2, out_wg, gate_wg, up_wg, down_wg = unit(
        mixed_here, hidden_in, out_cotangent, out_w, gate_w, up_w, down_w, norm2_gain[None]
    )
    mixed_grad = swap_parts(mixed_grad_here).reshape(length, -1)
    normed_grad, qkv_wg, small = attend_back(
        mixed_grad, mixed, inverse, probs, q, k, v, normed, query_weight, key_weight, value_weight,
        norm1_gain[None], gain2,
    )
    back, out_sum, gate_sum, up_sum, down_sum, qkv_sum, small_sum = reduce_parts(
        normed_grad.reshape(groups, rows_here, width), out_wg, gate_wg, up_wg, down_wg, qkv_wg, small
    )
    g1 = back * first_gain
    centre = jnp.mean(g1 * input_rows, axis=-1, keepdims=True)
    input_grad = (residual_grad + r1 * g1 - (r1 * r1 * r1 * centre) * input_rows).astype(bf16)
    qkv = qkv_sum.astype(f32)
    return (
        output, input_grad, small_sum[0], qkv[:width], qkv[width : 2 * width], qkv[2 * width :],
        out_sum.astype(f32), small_sum[8 : 8 + heads, :BUCKETS].T,
        small_sum[1], gate_sum.astype(f32), up_sum.astype(f32), down_sum.astype(f32),
    )


def solution(mesh):
    in_specs = (
        P(("dp", "tensor"), None), P("dp", None), P(),
        P(None, "tensor"), P(None, "tensor"), P(None, "tensor"), P("tensor", None),
        P(None, "tensor"), P(), P(None, "tensor"), P(None, "tensor"), P("tensor", None),
        P(("dp", "tensor"), None),
    )
    out_specs = (
        P(("dp", "tensor"), None), P(("dp", "tensor"), None), P(),
        P(None, "tensor"), P(None, "tensor"), P(None, "tensor"), P("tensor", None),
        P(None, "tensor"), P(), P(None, "tensor"), P(None, "tensor"), P("tensor", None),
    )
    by_kernel = mesh.shape["dp"] == 8 and mesh.shape["tensor"] == 4
    return jax.shard_map(
        functools.partial(shards, by_kernel), mesh=mesh, in_specs=in_specs, out_specs=out_specs, check_vma=False
    )
```

```python
import functools

import jax
import jax.numpy as jnp
from jax import lax
from jax.experimental import pallas as pl
from jax.experimental.pallas import tpu as pltpu
from jax.sharding import PartitionSpec as P

HEAD_DIM = 64
BUCKETS = 32
far_marks = (12, 16, 23, 32, 46, 64, 91)
norm_eps = 1e-06
far_score = 2.0**30
BLK = 256
f32 = jnp.float32
bf16 = jnp.bfloat16


def bucket_of(offset):
    magnitude = jnp.abs(offset)
    within = jnp.minimum(magnitude, 8)
    for far_mark in far_marks:
        within = within + (magnitude >= far_mark).astype(jnp.int32)
    return within + jnp.where(offset > 0, 16, 0).astype(jnp.int32)


def key_range(block, count):
    return range(max(0, block - 2), min(count, block + 3))


def contract(lhs, rhs, left, right):
    return lax.dot_general(
        lhs, rhs, (((left,), (right,)), ((), ())), preferred_element_type=f32
    )


def attend_kernel(
    normed_ref, wq_ref, wk_ref, wv_ref, seg_ref, table_ref,
    mixed_ref, probs_ref, q_ref, k_ref, v_ref, inv_ref,
    w_s, kt_s, bias_s, score_s, first_s,
):
    head = pl.program_id(0)
    length = normed_ref.shape[0]
    count = length // BLK
    lane = lax.broadcasted_iota(jnp.int32, (BLK, 128), 1)
    low_half = lane < HEAD_DIM

    @pl.when(head == 0)
    def _():
        w_s[...] = jnp.zeros_like(w_s)
        for place, ref in enumerate((wq_ref, wk_ref, wv_ref)):
            w_s[256 * place : 256 * place + 192, :] = ref[...]
        row8 = lax.broadcasted_iota(jnp.int32, (8, 128), 0)
        lane8 = lax.broadcasted_iota(jnp.int32, (8, 128), 1)
        spread = jnp.where((lane8 % HEAD_DIM) == row8, 1.0, 0.0).astype(bf16)

        def project(step, carry):
            rows = pl.ds(pl.multiple_of(step * BLK, BLK), BLK)
            seg_row = seg_ref[:, rows]
            kinds = lax.broadcasted_iota(jnp.int32, (8, BLK), 0)
            hot = jnp.where(
                jnp.broadcast_to(seg_row, (8, BLK)) == kinds, 1.0, 0.0
            ).astype(bf16)
            same = contract(hot, spread, 0, 0)
            in_aug = (lane % HEAD_DIM) < 8
            aug_q = jnp.where(in_aug, same, 0.0)
            aug_k = jnp.where(in_aug, (same - 1.0) * far_score, 0.0)
            rows_in = normed_ref[rows, :]
            q = contract(rows_in, w_s[0:256, :], 1, 1)
            k = contract(rows_in, w_s[256:512, :], 1, 1)
            v = contract(rows_in, w_s[512:768, :], 1, 1)
            scale = HEAD_DIM ** (-0.5)
            for h, (cols, mine) in enumerate(
                ((slice(0, 128), low_half), (slice(0, 128), ~low_half), (slice(128, 256), low_half))
            ):
                q_ref[h, rows, :] = jnp.where(mine, q[:, cols] * scale, aug_q).astype(bf16)
                k_h = jnp.where(mine, k[:, cols], aug_k).astype(bf16)
                k_ref[h, rows, :] = k_h
                v_ref[h, rows, :] = jnp.where(mine, v[:, cols], 1.0).astype(bf16)
                kt_s[h, :, rows] = k_h.T
            return carry

        lax.fori_loop(0, count, project, 0)

    offset = lax.broadcasted_iota(jnp.int32, (BUCKETS, length), 1)
    offset = jnp.where(offset >= length // 2, offset - length, offset)
    hot_bucket = jnp.where(
        bucket_of(offset) == lax.broadcasted_iota(jnp.int32, (BUCKETS, length), 0), 1.0, 0.0
    ).astype(bf16)
    by_offset = contract(table_ref[head], hot_bucket, 1, 0)[0:1]
    spread_rows = jnp.broadcast_to(by_offset, (BLK, length))
    bias_s[...] = pltpu.roll(spread_rows, 0, 1, stride=1, stride_axis=0)

    for block in range(count):
        rows = slice(block * BLK, (block + 1) * BLK)
        q_h = q_ref[head, rows, :]
        top = None
        for key in key_range(block, count):
            part = jnp.dot(
                q_h, kt_s[head, :, key * BLK : (key + 1) * BLK], preferred_element_type=f32
            )
            delta = key - block
            at = (delta * BLK) % length
            part = part + bias_s[:, at : at + BLK]
            score_s[:, key * BLK : (key + 1) * BLK] = part
            top = part if top is None else jnp.maximum(top, part)
        top = jnp.max(jnp.maximum(top[:, :128], top[:, 128:]), axis=1, keepdims=True)
        total = jnp.zeros((BLK, 128), f32)
        for key in key_range(block, count):
            cols = slice(key * BLK, (key + 1) * BLK)
            part = jnp.exp(score_s[:, cols] - top).astype(bf16)
            probs_ref[0, rows, cols] = part
            total = total + jnp.dot(part, v_ref[head, cols, :], preferred_element_type=f32)
        sums = pltpu.roll(total, HEAD_DIM, 1)
        inverse = 1.0 / sums
        out = total * inverse

        @pl.when(head == 0)
        def _():
            first_s[rows, 0:128] = out
            first_s[rows, 128:256] = inverse

        @pl.when(head == 1)
        def _():
            mixed_ref[rows, 0:128] = jnp.where(low_half, first_s[rows, 0:128], out).astype(bf16)
            inv_ref[rows, 0:128] = jnp.where(low_half, first_s[rows, 128:256], inverse)

        @pl.when(head == 2)
        def _():
            mixed_ref[rows, 128:192] = out[:, 0:HEAD_DIM].astype(bf16)
            inv_ref[rows, 128:256] = inverse


def attend(normed, wq, wk, wv, segments, bias_table):
    length, width = normed.shape
    heads = bias_table.shape[1]
    inner = heads * HEAD_DIM
    table = jnp.broadcast_to(bias_table.T[:, None, :], (heads, 8, BUCKETS))
    whole = lambda *dims: pl.BlockSpec(dims, lambda h: (0,) * len(dims))
    return pl.pallas_call(
        attend_kernel,
        grid=(heads,),
        name="attend",
        out_shape=(
            jax.ShapeDtypeStruct((length, inner), bf16),
            jax.ShapeDtypeStruct((heads, length, length), bf16),
            jax.ShapeDtypeStruct((heads, length, 128), bf16),
            jax.ShapeDtypeStruct((heads, length, 128), bf16),
            jax.ShapeDtypeStruct((heads, length, 128), bf16),
            jax.ShapeDtypeStruct((length, 256), f32),
        ),
        in_specs=[
            whole(length, width),
            whole(inner, width),
            whole(inner, width),
            whole(inner, width),
            whole(1, length),
            whole(heads, 8, BUCKETS),
        ],
        out_specs=(
            whole(length, inner),
            pl.BlockSpec((1, length, length), lambda h: (h, 0, 0)),
            whole(heads, length, 128),
            whole(heads, length, 128),
            whole(heads, length, 128),
            whole(length, 256),
        ),
        scratch_shapes=[
            pltpu.VMEM((768, width), bf16),
            pltpu.VMEM((heads, 128, length), bf16),
            pltpu.VMEM((BLK, length), f32),
            pltpu.VMEM((BLK, length), f32),
            pltpu.VMEM((length, 256), f32),
        ],
        compiler_params=pltpu.CompilerParams(
            dimension_semantics=("arbitrary",), vmem_limit_bytes=48 << 20
        ),
        cost_estimate=pl.CostEstimate(flops=3 << 30, bytes_accessed=12 << 20, transcendentals=3 << 20),
    )(normed, wq, wk, wv, segments, table)


def mean_square_scale(rows):
    return lax.rsqrt(jnp.mean(rows * rows, axis=-1, keepdims=True) + norm_eps)


def unit_kernel(
    mixed_ref, hidden_ref, cot_ref, out_w_ref, gate_w_ref, up_w_ref, down_w_ref, gain_ref,
    output_ref, residual_grad_ref, mixed_grad_ref, gain_grad_ref,
    out_wg_ref, gate_wg_ref, up_wg_ref, down_wg_ref,
    residual_s, normed_s, sum_s, back_s,
):
    step = pl.program_id(0)
    parts = pl.num_programs(0)
    groups = mixed_ref.shape[0]
    tokens = residual_s.shape[0]

    @pl.when(step == 0)
    def _():
        mixed = jnp.concatenate([mixed_ref[g] for g in range(groups)], axis=1)
        out_w = jnp.concatenate([out_w_ref[g] for g in range(groups)], axis=0)
        residual = hidden_ref[...].astype(f32) + jnp.dot(mixed, out_w, preferred_element_type=f32)
        residual_s[...] = residual
        normed_s[...] = (residual * mean_square_scale(residual) * gain_ref[...].astype(f32)).astype(bf16)
        sum_s[...] = jnp.zeros_like(sum_s)
        back_s[...] = jnp.zeros_like(back_s)

    normed = normed_s[...]
    cot = cot_ref[...]
    gate = jnp.dot(normed, gate_w_ref[0], preferred_element_type=f32)
    up = jnp.dot(normed, up_w_ref[0], preferred_element_type=f32)
    hidden_grad = contract(cot, down_w_ref[0], 1, 1)
    c0 = 0.7978845608028654
    square = gate * gate
    bend = jnp.tanh(gate * (c0 + (c0 * 0.044715) * square))
    half = 0.5 + 0.5 * bend
    act = gate * half
    slope = half + 0.5 * gate * (1.0 - bend * bend) * (c0 + (3.0 * c0 * 0.044715) * square)
    hidden = (act * up).astype(bf16)
    gate_grad = (hidden_grad * up * slope).astype(bf16)
    up_grad = (hidden_grad * act).astype(bf16)
    sum_s[...] += jnp.dot(hidden, down_w_ref[0], preferred_element_type=f32)
    back_s[...] += contract(gate_grad, gate_w_ref[0], 1, 1) + contract(up_grad, up_w_ref[0], 1, 1)
    down_wg_ref[0] = contract(hidden, cot, 0, 0).astype(bf16)
    gate_wg_ref[0] = contract(normed, gate_grad, 0, 0).astype(bf16)
    up_wg_ref[0] = contract(normed, up_grad, 0, 0).astype(bf16)

    @pl.when(step == parts - 1)
    def _():
        residual = residual_s[...]
        output_ref[...] = (residual + sum_s[...]).astype(bf16)
        back = back_s[...]
        r = mean_square_scale(residual)
        gain_grad_ref[...] = jnp.sum(back * residual * r, axis=0, keepdims=True)
        g = back * gain_ref[...].astype(f32)
        centre = jnp.mean(g * residual, axis=-1, keepdims=True)
        residual_grad = cot_ref[...].astype(f32) + r * g - (r * r * r * centre) * residual
        residual_grad_ref[...] = residual_grad
        low = residual_grad.astype(bf16)
        for g_at in range(groups):
            mixed_grad_ref[g_at] = contract(low, out_w_ref[g_at], 1, 1).astype(bf16)
            out_wg_ref[g_at] = contract(mixed_ref[g_at], low, 0, 0).astype(bf16)


def unit(mixed, hidden_in, cot, out_w, gate_w, up_w, down_w, gain):
    groups, tokens, part = mixed.shape
    width = hidden_in.shape[1]
    units = gate_w.shape[2]
    whole = lambda *dims: pl.BlockSpec(dims, lambda s: (0,) * len(dims))
    each = lambda *dims: pl.BlockSpec((1,) + dims, lambda s: (s, 0, 0))
    return pl.pallas_call(
        unit_kernel,
        grid=(groups,),
        name="unit",
        out_shape=(
            jax.ShapeDtypeStruct((tokens, width), bf16),
            jax.ShapeDtypeStruct((tokens, width), f32),
            jax.ShapeDtypeStruct((groups, tokens, part), bf16),
            jax.ShapeDtypeStruct((1, width), f32),
            jax.ShapeDtypeStruct((groups, part, width), bf16),
            jax.ShapeDtypeStruct((groups, width, units), bf16),
            jax.ShapeDtypeStruct((groups, width, units), bf16),
            jax.ShapeDtypeStruct((groups, units, width), bf16),
        ),
        in_specs=[
            whole(groups, tokens, part),
            whole(tokens, width),
            whole(tokens, width),
            whole(groups, part, width),
            each(width, units),
            each(width, units),
            each(units, width),
            whole(1, width),
        ],
        out_specs=(
            whole(tokens, width),
            whole(tokens, width),
            whole(groups, tokens, part),
            whole(1, width),
            whole(groups, part, width),
            each(width, units),
            each(width, units),
            each(units, width),
        ),
        scratch_shapes=[
            pltpu.VMEM((tokens, width), f32),
            pltpu.VMEM((tokens, width), bf16),
            pltpu.VMEM((tokens, width), f32),
            pltpu.VMEM((tokens, width), f32),
        ],
        compiler_params=pltpu.CompilerParams(
            dimension_semantics=("arbitrary",), vmem_limit_bytes=48 << 20
        ),
        cost_estimate=pl.CostEstimate(flops=9 << 30, bytes_accessed=26 << 20, transcendentals=1 << 20),
    )(mixed, hidden_in, cot, out_w, gate_w, up_w, down_w, gain)


MESH_IDS = pl.DeviceIdType.MESH


def places():
    dp = lax.axis_index("dp")
    line = lax.axis_index("tensor")
    core = lax.rem(dp, 2)
    x = lax.rem(dp // 2, 2)
    y = dp // 4
    flips = (dp + 1 - 2 * core, dp + 2 - 4 * x, dp + 4 - 8 * y)
    return dp, line, core, x, y, flips


def nearest(line, k):
    upper = line // 2
    inner = line * (1 - upper) + (3 - line) * upper
    block = k + 1 - inner if k == 0 else k + 1
    block = block * (1 - upper) + (3 - block) * upper
    way = (1 if k == 0 else -1) * (1 - 2 * upper)
    return block, way


class Item:
    def __init__(self, place, base, rows, flipped, by_columns=False):
        self.place, self.base, self.rows = place, base, rows
        self.flipped, self.by_columns = flipped, by_columns

    def bits(self, x, y):
        return (y, x) if self.flipped else (x, y)

    def partner(self, level, flips):
        if level == 0:
            return flips[0]
        return flips[1 + ((level - 1) ^ int(self.flipped))]

    def window(self, ref, lead, level, core, first, second):
        width = ref.shape[-1]
        if self.by_columns:
            size = self.rows // (1, 2, 4)[level - 1]
            start = self.base + 0 * core
            if level > 1:
                start = start + first * (self.rows // 2)
            if level > 2:
                start = start + second * (self.rows // 4)
            cols = pl.ds(pl.multiple_of(core * (width // 2), 128), width // 2)
        else:
            size = self.rows // (2, 4, 8)[level - 1]
            start = self.base + core * (self.rows // 2)
            if level > 1:
                start = start + first * (self.rows // 4)
            if level > 2:
                start = start + second * (self.rows // 8)
            cols = pl.ds(0, width)
        rows = pl.ds(pl.multiple_of(start, 16), size)
        if lead is None:
            return ref.at[rows, cols]
        return ref.at[lead, rows, cols]


def weight_items(units, part, width):
    return (
        Item(0, 0, width, False),
        Item(1, 0, width, True),
        Item(2, 0, units // 2, False),
        Item(2, units // 2, units // 2, True),
        Item(3, 0, part, False, by_columns=True),
    )


def gather_kernel(
    normed_ref, gate_ref, up_ref, down_ref, out_ref,
    normed_all, gate_all, up_all, down_all, out_all,
    z_send, z_recv, p_send, p_recv, own_sem,
    hold_gate, hold_up, hold_down, hold_out, hold_normed,
):
    dp, line, core, x, y, flips = places()
    upper = line // 2
    inner = line * (1 - upper) + (3 - line) * upper
    own = (gate_ref, up_ref, down_ref, out_ref)
    full = (gate_all, up_all, down_all, out_all)
    units, width = down_ref.shape
    items = weight_items(units, out_ref.shape[0], width)
    count = len(items)

    barrier = pltpu.get_barrier_semaphore()
    for flip in flips:
        pl.semaphore_signal(barrier, inc=1, device_id=(flip, line), device_id_type=MESH_IDS)

    @pl.when(line > 0)
    def _():
        pl.semaphore_signal(barrier, inc=1, device_id=(dp, line - 1), device_id_type=MESH_IDS)

    @pl.when(line < 3)
    def _():
        pl.semaphore_signal(barrier, inc=1, device_id=(dp, line + 1), device_id_type=MESH_IDS)

    pl.semaphore_wait(barrier, 4 + inner)

    def eighth(i, ref, lead):
        item = items[i]
        first, second = item.bits(x, y)
        return item.window(ref, lead, 3, core, first, second)

    def along(i, block, target, side, first_hop):
        if i == count:
            src = normed_ref if first_hop else normed_all.at[block]
            dst = normed_all.at[block]
        else:
            dst = eighth(i, full[items[i].place], block)
            src = eighth(i, own[items[i].place], None) if first_hop else dst
        return pltpu.make_async_remote_copy(
            src_ref=src, dst_ref=dst, send_sem=z_send.at[i, block, side], recv_sem=z_recv.at[i, block],
            device_id=(dp, target), device_id_type=MESH_IDS,
        )

    def send_own(i):
        @pl.when(line > 0)
        def _():
            along(i, line, line - 1, 0, True).start()

        @pl.when(line < 3)
        def _():
            along(i, line, line + 1, 1, True).start()

    def arrive(i, k):
        block, way = nearest(line, k)
        along(i, block, line, 0, False).wait_recv()

        @pl.when(inner == 1)
        def _():
            along(i, block, line + way, 0, False).start()

    def spread(i, k, stage):
        block, _ = nearest(line, k)
        item = items[i]
        first, second = item.bits(x, y)
        window = item.window(full[item.place], block, 3 - stage, core, first, second)
        return pltpu.make_async_remote_copy(
            src_ref=window, dst_ref=window, send_sem=p_send.at[stage, i, k], recv_sem=p_recv.at[stage, i, k],
            device_id=(item.partner(2 - stage, flips), line), device_id_type=MESH_IDS,
        )

    for i in range(count):
        send_own(i)
    holds = (hold_gate, hold_up, hold_down, hold_out, hold_normed)
    loads = []
    stores = []
    for place, ref in enumerate(own + (normed_ref,)):
        target = (full + (normed_all,))[place].at[line]
        loads.append(pltpu.make_async_copy(ref, holds[place], own_sem.at[0, place]))
        stores.append(pltpu.make_async_copy(holds[place], target, own_sem.at[1, place]))
    for load in loads:
        load.start()
    for load, store in zip(loads, stores):
        load.wait()
        store.start()

    def advance(k, stage):
        for i in range(count):
            if stage > 0:
                spread(i, k, stage - 1).wait_recv()
            spread(i, k, stage).start()

    for k in range(3):
        for i in range(count):
            arrive(i, k)
            spread(i, k, 0).start()
        if k == 2:
            send_own(count)
        if k >= 1:
            advance(k - 1, 1)
        if k >= 2:
            advance(k - 2, 2)
    advance(2, 1)
    arrive(count, 0)
    advance(1, 2)
    arrive(count, 1)
    advance(2, 2)
    arrive(count, 2)

    for store in stores:
        store.wait()
    for i in range(count + 1):
        @pl.when(line > 0)
        def _(i=i):
            along(i, line, line - 1, 0, True).wait_send()

        @pl.when(line < 3)
        def _(i=i):
            along(i, line, line + 1, 1, True).wait_send()

        @pl.when(inner == 1)
        def _(i=i):
            for k in range(3):
                block, way = nearest(line, k)
                along(i, block, line + way, 0, False).wait_send()

    for k in range(3):
        for i in range(count):
            spread(i, k, 2).wait_recv()
            for stage in range(3):
                spread(i, k, stage).wait_send()


def gather(normed, gate, up, down, out):
    rows, width = normed.shape
    units, part = gate.shape[1], out.shape[0]
    anywhere = pl.BlockSpec(memory_space=pl.ANY)
    return pl.pallas_call(
        gather_kernel,
        name="gather",
        out_shape=(
            jax.ShapeDtypeStruct((4, rows, width), bf16),
            jax.ShapeDtypeStruct((4, width, units), bf16),
            jax.ShapeDtypeStruct((4, width, units), bf16),
            jax.ShapeDtypeStruct((4, units, width), bf16),
            jax.ShapeDtypeStruct((4, part, width), bf16),
        ),
        in_specs=[anywhere] * 5,
        out_specs=(anywhere,) * 5,
        scratch_shapes=[
            pltpu.SemaphoreType.DMA((6, 4, 2)),
            pltpu.SemaphoreType.DMA((6, 4)),
            pltpu.SemaphoreType.DMA((3, 5, 3)),
            pltpu.SemaphoreType.DMA((3, 5, 3)),
            pltpu.SemaphoreType.DMA((2, 5)),
            pltpu.VMEM(gate.shape, bf16),
            pltpu.VMEM(up.shape, bf16),
            pltpu.VMEM(down.shape, bf16),
            pltpu.VMEM(out.shape, bf16),
            pltpu.VMEM(normed.shape, bf16),
        ],
        compiler_params=pltpu.CompilerParams(collective_id=1, has_side_effects=True),
    )(normed, gate, up, down, out)


def swap_kernel(mine_ref, theirs_ref, send_sem, recv_sem, own_sem):
    dp, line, _, _, _, _ = places()
    barrier = pltpu.get_barrier_semaphore()
    others = [lax.rem(line + i, 4) for i in (1, 2, 3)]
    for other in others:
        pl.semaphore_signal(barrier, inc=1, device_id=(dp, other), device_id_type=MESH_IDS)
    pl.semaphore_wait(barrier, 3)
    copies = [
        pltpu.make_async_remote_copy(
            src_ref=mine_ref.at[other], dst_ref=theirs_ref.at[line], send_sem=send_sem.at[i], recv_sem=recv_sem.at[2 - i],
            device_id=(dp, other), device_id_type=MESH_IDS,
        )
        for i, other in enumerate(others)
    ]
    for copy in copies:
        copy.start()
    keep = pltpu.make_async_copy(mine_ref.at[line], theirs_ref.at[line], own_sem)
    keep.start()
    for i, other in enumerate(others):
        copies[i].wait_send()
        pltpu.make_async_remote_copy(
            src_ref=mine_ref.at[other], dst_ref=theirs_ref.at[other], send_sem=send_sem.at[i], recv_sem=recv_sem.at[i],
            device_id=(dp, other), device_id_type=MESH_IDS,
        ).wait_recv()
    keep.wait()


def swap(blocks):
    anywhere = pl.BlockSpec(memory_space=pl.ANY)
    return pl.pallas_call(
        swap_kernel,
        name="swap",
        out_shape=jax.ShapeDtypeStruct(blocks.shape, blocks.dtype),
        in_specs=[anywhere],
        out_specs=anywhere,
        scratch_shapes=[
            pltpu.SemaphoreType.DMA((3,)),
            pltpu.SemaphoreType.DMA((3,)),
            pltpu.SemaphoreType.DMA,
        ],
        compiler_params=pltpu.CompilerParams(collective_id=2, has_side_effects=True),
    )(blocks)


class Chunk:
    def __init__(self, item, block, acc, from_core, from_first, from_second, from_left, from_right, number):
        self.item, self.block, self.number = item, block, number
        self.acc, self.from_core, self.from_first = acc, from_core, from_first
        self.from_second, self.from_left, self.from_right = from_second, from_left, from_right


class Named:
    def __init__(self, names, refs):
        for name, ref in zip(names, refs):
            setattr(self, name, ref)


def add_rows(target, start, size, source):
    rows = pl.ds(start, size)
    target[rows, :] = (target[rows, :].astype(f32) + source[...].astype(f32)).astype(bf16)


def remote(src, dst, send, recv, target):
    return pltpu.make_async_remote_copy(
        src_ref=src, dst_ref=dst, send_sem=send, recv_sem=recv, device_id=target, device_id_type=MESH_IDS
    )


def greet(dp, line, flips):
    barrier = pltpu.get_barrier_semaphore()
    for flip in flips:
        pl.semaphore_signal(barrier, inc=1, device_id=(flip, line), device_id_type=MESH_IDS)
    for i in (1, 2, 3):
        pl.semaphore_signal(
            barrier, inc=1, device_id=(dp, lax.rem(line + i, 4)), device_id_type=MESH_IDS
        )
    pl.semaphore_wait(barrier, 6)


def attention_back_tasks(s, r):
    heads, length = s.dot.shape[0], s.dot.shape[1]
    count = length // BLK
    lane = lax.broadcasted_iota(jnp.int32, (BLK, 128), 1)
    low_half = lane < HEAD_DIM
    width = r.normed.shape[1]
    tasks = []

    def load_weights():
        s.w[...] = jnp.zeros_like(s.w)
        for place, ref in enumerate((r.wq, r.wk, r.wv)):
            s.w[256 * place : 256 * place + 192, :] = ref[...]

    tasks.append(load_weights)

    def prepare():
        def body(step, carry):
            rows = pl.ds(pl.multiple_of(step * BLK, BLK), BLK)
            for h in range(heads):
                cols = slice(0, 128) if h < 2 else slice(128, 256)
                mine = ~low_half if h == 1 else low_half
                if h < 2:
                    grad = s.mixed_grad[step, :, 0:128].astype(f32)
                    mix = r.mixed[rows, 0:128].astype(f32)
                else:
                    fill = jnp.zeros((BLK, HEAD_DIM), f32)
                    grad = jnp.concatenate((s.mixed_grad[step, :, 128:192].astype(f32), fill), axis=1)
                    mix = jnp.concatenate((r.mixed[rows, 128:192].astype(f32), fill), axis=1)
                grad = jnp.where(mine, grad * r.inverse[rows, cols], 0.0)
                centre = -jnp.sum(grad * mix, axis=1, keepdims=True)
                high = centre.astype(bf16).astype(f32)
                base = 0 if h == 1 else HEAD_DIM
                grad = jnp.where(lane == base, high, grad)
                grad = jnp.where(lane == base + 1, centre - high, grad)
                low = grad.astype(bf16)
                s.dot[h, rows, :] = low
                s.dott[h, :, rows] = low.T
                s.qt[h, :, rows] = r.q[h, rows, :].T
                s.vt[h, :, rows] = r.v[h, rows, :].T
            return carry

        lax.fori_loop(0, count, body, 0)

    tasks.append(prepare)

    def clear(h):
        s.probs_copy(h).wait()
        s.near[...] = jnp.zeros_like(s.near)
        s.far[...] = jnp.zeros_like(s.far)
        s.dkt[...] = jnp.zeros_like(s.dkt)
        s.dvt[...] = jnp.zeros_like(s.dvt)

    def block_step(h, block):
        if block == 0:
            clear(h)
        rows = slice(block * BLK, (block + 1) * BLK)
        d_h = s.dot[h, rows, :]
        dt_h = s.dott[h, :, rows]
        qt_h = s.qt[h, :, rows]
        query_grad = jnp.zeros((BLK, 128), f32)
        for key in key_range(block, count):
            cols = slice(key * BLK, (key + 1) * BLK)
            probs = s.probs[h % 2, rows, cols]
            slope = jnp.dot(d_h, s.vt[h, :, cols], preferred_element_type=f32)
            grad = probs.astype(f32) * slope
            low = grad.astype(bf16)
            delta = key - block
            if abs(delta) == 2:
                s.far[0 if delta < 0 else 1] += grad[:, :128] + grad[:, 128:]
            else:
                s.near[:, (delta + 1) * BLK : (delta + 2) * BLK] += grad
            query_grad = query_grad + jnp.dot(low, r.k[h, cols, :], preferred_element_type=f32)
            s.dkt[:, cols] += jnp.dot(qt_h, low, preferred_element_type=f32)
            s.dvt[:, cols] += jnp.dot(dt_h, probs, preferred_element_type=f32)
        s.grad[rows, 0:128] = query_grad * HEAD_DIM ** (-0.5)

    def head_end(h):
        if h + 2 < heads:
            s.probs_copy(h + 2).start()
        for block in range(count):
            rows = slice(block * BLK, (block + 1) * BLK)
            s.grad[rows, 128:256] = s.dkt[:, rows].T
            s.grad[rows, 256:384] = s.dvt[:, rows].T
            for at in range(3):
                part = s.grad[rows, 128 * at : 128 * at + 128]
                if h == 0:
                    s.joined[rows, 256 * at : 256 * at + 128] = part.astype(bf16)
                elif h == 1:
                    before = s.joined[rows, 256 * at : 256 * at + 128].astype(f32)
                    s.joined[rows, 256 * at : 256 * at + 128] = jnp.where(low_half, before, part).astype(bf16)
                else:
                    s.joined[rows, 256 * at + 128 : 256 * at + 256] = jnp.where(low_half, part, 0.0).astype(bf16)
        place = lax.broadcasted_iota(jnp.int32, (BLK, 3 * BLK), 1) - BLK
        place = place - lax.broadcasted_iota(jnp.int32, (BLK, 3 * BLK), 0)
        bucket = bucket_of(place)
        near = s.near[...]
        sub = lax.broadcasted_iota(jnp.int32, (BUCKETS, 128), 0)
        table = jnp.zeros((BUCKETS, 128), f32)
        for b in range(BUCKETS):
            if b == 16:
                continue
            part = jnp.sum(jnp.where(bucket == b, near, 0.0), axis=0, keepdims=True)
            folded = part[:, 0:128]
            for at in range(1, 6):
                folded = folded + part[:, at * 128 : (at + 1) * 128]
            if b in (15, 31):
                folded = folded + jnp.sum(s.far[0 if b == 15 else 1], axis=0, keepdims=True)
            table = jnp.where(sub == b, folded, table)
        flat = lax.dot_general(
            jnp.ones((8, 128), f32), table, (((1,), (1,)), ((), ())),
            preferred_element_type=f32, precision=lax.Precision.HIGHEST,
        )
        s.small_mine[8 + h : 9 + h, 0:BUCKETS] = flat[0:1]

    for h in range(heads):
        for block in range(count):
            tasks.append(functools.partial(block_step, h, block))
        tasks.append(functools.partial(head_end, h))

    def rows_grad(block):
        rows = slice(block * BLK, (block + 1) * BLK)
        part = jnp.dot(s.joined[rows, :], s.w[...], preferred_element_type=f32)
        half = BLK // 2
        s.back_acc[block, 0] = part[:half].astype(bf16)
        s.back_acc[block, 1] = part[half:].astype(bf16)
        s.gain[...] += jnp.sum(part * r.normed[rows, :].astype(f32), axis=0, keepdims=True)

    def weights_grad(at):
        part = contract(s.joined[:, 256 * at : 256 * at + 256], r.normed[...], 0, 0)
        s.qkv_wg[192 * at : 192 * at + 192, :] = part[0:192].astype(bf16)

    return tasks, rows_grad, weights_grad


BACK_OPERANDS = (
    "grad_here", "out_wg", "gate_wg", "up_wg", "down_wg", "probs_all", "mixed", "inverse", "q", "k", "v",
    "normed", "wq", "wk", "wv", "gain1", "gain2_grad",
)
BACK_RESULTS = ("back_sum", "out_sum", "gate_sum", "up_sum", "down_sum", "qkv_sum", "small_sum")


def back_kernel(names, *refs):
    r = Named(BACK_OPERANDS + BACK_RESULTS, refs)
    s = Named(names, refs[len(BACK_OPERANDS) + len(BACK_RESULTS) :])
    dp, line, core, x, y, flips = places()
    units, width = r.down_wg.shape[1:]
    part = r.out_wg.shape[1]
    grads = (r.gate_wg, r.up_wg, r.down_wg, r.out_wg, s.qkv_wg)
    sums = (r.gate_sum, r.up_sum, r.down_sum, r.out_sum, r.qkv_sum)
    items = weight_items(units, part, width)
    across = lax.rem(line + 2, 4)

    s.probs_copy = lambda h: pltpu.make_async_copy(r.probs_all.at[h], s.probs.at[h % 2], s.probs_sem.at[h])
    for h in range(2):
        s.probs_copy(h).start()
    greet(dp, line, flips)

    def swap_out(i):
        other = lax.rem(line + i, 4)
        return remote(
            r.grad_here.at[other], s.mixed_grad.at[line], s.swap_send.at[i - 1], s.swap_recv.at[3 - i], (dp, other)
        )

    def swap_in(i):
        other = lax.rem(line + i, 4)
        return remote(
            r.grad_here.at[other], s.mixed_grad.at[other], s.swap_send.at[i - 1], s.swap_recv.at[i - 1], (dp, other)
        )

    swap_keep = pltpu.make_async_copy(r.grad_here.at[line], s.mixed_grad.at[line], s.swap_keep)
    for i in (2, 1, 3):
        swap_out(i).start()
    swap_keep.start()

    chunks = []
    for i, block in CHUNK_ORDER:
        item = items[i]
        if item.by_columns:
            item = Item(item.place, item.base, item.rows, block > 1, True)
        stages = (getattr(s, stage + str(i)) for stage in ("half", "core", "first", "second", "left", "right"))
        chunks.append(Chunk(item, block, *(ref.at[block] for ref in stages), len(chunks)))
    for turn in range(3):
        item = Item(4, turn * part, part, turn % 2 == 0, True)
        stages = (s.qkv_half, s.qkv_core, s.qkv_first, s.qkv_second)
        chunks.append(Chunk(item, None, *(ref.at[turn] for ref in stages), None, None, len(chunks)))

    def load_copy(chunk):
        window = chunk.item.window(grads[chunk.item.place], chunk.block, 1, core, 0, 0)
        return pltpu.make_async_copy(window, chunk.acc, s.load_sem.at[chunk.number])

    def core_copy(chunk):
        window = chunk.item.window(grads[chunk.item.place], chunk.block, 1, 1 - core, 0, 0)
        n = chunk.number
        return remote(window, chunk.from_core, s.core_send.at[n], s.core_recv.at[n], (flips[0], line))

    def begin(chunk):
        core_copy(chunk).start()
        load_copy(chunk).start()

    def pair_copy(chunk, stage):
        half = chunk.acc.shape[0]
        first, second = chunk.item.bits(x, y)
        n = chunk.number
        if stage == 0:
            size, start, target = half // 2, (1 - first) * (half // 2), chunk.from_first
        else:
            size = half // 4
            start, target = first * (half // 2) + (1 - second) * (half // 4), chunk.from_second
        window = chunk.acc.at[pl.ds(pl.multiple_of(start, 16), size), :]
        partner = chunk.item.partner(1 + stage, flips)
        return remote(window, target, s.pair_send.at[stage, n], s.pair_recv.at[stage, n], (partner, line))

    def eighth(chunk):
        half = chunk.acc.shape[0]
        first, second = chunk.item.bits(x, y)
        return pl.multiple_of(first * (half // 2) + second * (half // 4), 16), half // 4

    def mine(chunk):
        start, size = eighth(chunk)
        return chunk.acc.at[pl.ds(start, size), :]

    def hop_copy(chunk, at, right):
        n = chunk.number
        if right:
            return remote(mine(chunk), chunk.from_left, s.line_send.at[n], s.left_recv.at[n], (dp, at + 1))
        return remote(mine(chunk), chunk.from_right, s.line_send.at[n], s.right_recv.at[n], (dp, at - 1))

    def spread_copy(chunk, stage):
        item = chunk.item
        first, second = item.bits(x, y)
        window = item.window(sums[item.place], None, 3 - stage, core, first, second)
        src = mine(chunk) if stage == 0 else window
        n = chunk.number
        return remote(
            src, window, s.spread_send.at[stage, n], s.spread_recv.at[stage, n],
            (item.partner(2 - stage, flips), line),
        )

    def keep_copy(chunk):
        first, second = chunk.item.bits(x, y)
        window = chunk.item.window(sums[chunk.item.place], None, 3, core, first, second)
        return pltpu.make_async_copy(mine(chunk), window, s.load_sem.at[chunk.number])

    def on_plane(chunk, act):
        if chunk.block is None:
            act()
        else:
            pl.when(line == chunk.block)(act)

    def step_core(chunk):
        load_copy(chunk).wait()
        core_copy(chunk).wait_recv()
        add_rows(chunk.acc, 0, chunk.acc.shape[0], chunk.from_core)
        pair_copy(chunk, 0).start()

    def step_first(chunk):
        pair_copy(chunk, 0).wait_recv()
        half = chunk.acc.shape[0]
        first, _ = chunk.item.bits(x, y)
        add_rows(chunk.acc, pl.multiple_of(first * (half // 2), 16), half // 2, chunk.from_first)
        pair_copy(chunk, 1).start()

    def step_hop(chunk, hop):
        if chunk.block is None:
            return
        start, size = eighth(chunk)
        if chunk.block > hop:
            @pl.when(line == hop)
            def _():
                if hop > 0:
                    hop_copy(chunk, hop, True).wait_recv()
                    add_rows(chunk.acc, start, size, chunk.from_left)
                hop_copy(chunk, hop, True).start()
        at = 3 - hop
        if chunk.block < at:
            @pl.when(line == at)
            def _():
                if hop > 0:
                    hop_copy(chunk, at, False).wait_recv()
                    add_rows(chunk.acc, start, size, chunk.from_right)
                hop_copy(chunk, at, False).start()

    def step_second(chunk):
        pair_copy(chunk, 1).wait_recv()
        start, size = eighth(chunk)
        add_rows(chunk.acc, start, size, chunk.from_second)
        if chunk.block is None:
            step_last(chunk)
        else:
            step_hop(chunk, 0)

    def step_last(chunk):
        def act():
            if chunk.block is not None:
                start, size = eighth(chunk)
                if chunk.block > 0:
                    hop_copy(chunk, chunk.block, True).wait_recv()
                    add_rows(chunk.acc, start, size, chunk.from_left)
                if chunk.block < 3:
                    hop_copy(chunk, chunk.block, False).wait_recv()
                    add_rows(chunk.acc, start, size, chunk.from_right)
            spread_copy(chunk, 0).start()
            keep_copy(chunk).start()

        on_plane(chunk, act)

    def step_spread(chunk, stage):
        def act():
            if stage == 1:
                keep_copy(chunk).wait()
            spread_copy(chunk, stage - 1).wait_recv()
            if stage < 3:
                spread_copy(chunk, stage).start()

        on_plane(chunk, act)

    parts = s.back_acc.shape[1]
    back_rows = s.back_acc.shape[2]

    def back_hop_copy(block, part_at, at, right):
        src = s.back_acc.at[block, part_at]
        send = s.back_send.at[block, part_at]
        if right:
            return remote(
                src, s.back_left.at[block, part_at], send, s.back_left_recv.at[block, part_at], (dp, at + 1)
            )
        return remote(
            src, s.back_right.at[block, part_at], send, s.back_right_recv.at[block, part_at], (dp, at - 1)
        )

    def back_hop(hop, part_at):
        at = 3 - hop

        @pl.when(line == hop)
        def _():
            for block in range(3, hop, -1):
                if hop > 0:
                    back_hop_copy(block, part_at, hop, True).wait_recv()
                    add_rows(s.back_acc.at[block, part_at], 0, back_rows, s.back_left.at[block, part_at])
                back_hop_copy(block, part_at, hop, True).start()

        @pl.when(line == at)
        def _():
            for block in range(0, at):
                if hop > 0:
                    back_hop_copy(block, part_at, at, False).wait_recv()
                    add_rows(s.back_acc.at[block, part_at], 0, back_rows, s.back_right.at[block, part_at])
                back_hop_copy(block, part_at, at, False).start()

    def back_last(part_at):
        for block in range(4):
            @pl.when(line == block)
            def _(block=block):
                total = s.back_acc[block, part_at].astype(f32)
                if block > 0:
                    back_hop_copy(block, part_at, block, True).wait_recv()
                    total = total + s.back_left[block, part_at].astype(f32)
                if block < 3:
                    back_hop_copy(block, part_at, block, False).wait_recv()
                    total = total + s.back_right[block, part_at].astype(f32)
                r.back_sum[part_at * back_rows : (part_at + 1) * back_rows, :] = total

    def small_copy(stage):
        partner = (flips[stage], line) if stage < 3 else (dp, line + 1 - 2 * lax.rem(line, 2))
        if stage == 4:
            partner = (dp, across)
        return remote(r.small_sum, s.small_got.at[stage], s.small_send.at[stage], s.small_recv.at[stage], partner)

    def small_step(stage):
        if stage > 0:
            small_copy(stage - 1).wait()
            rows = lax.broadcasted_iota(jnp.int32, r.small_sum.shape, 0)
            got = s.small_got[stage - 1]
            if stage > 3:
                got = jnp.where(rows < 8, got, 0.0)
            r.small_sum[...] = r.small_sum[...] + got
        else:
            s.small_mine[0:1, :] = s.gain[...] / r.gain1[...].astype(f32)
            s.small_mine[1:2, :] = r.gain2_grad[...]
            r.small_sum[...] = s.small_mine[...]
        if stage < 5:
            small_copy(stage).start()

    ahead = 4
    first_of_qkv = len(chunks) - 3
    lags = LAGS
    extra = {}

    def run_slot(slot):
        if slot + ahead < first_of_qkv:
            begin(chunks[slot + ahead])
        for i, act in enumerate(
            (
                step_core, step_first, step_second,
                lambda c: step_hop(c, 1), lambda c: step_hop(c, 2),
                lambda c: None if c.block is None else step_last(c),
                lambda c: None if c.block is None else step_spread(c, 1),
                lambda c: None if c.block is None else step_spread(c, 2),
                lambda c: None if c.block is None else step_spread(c, 3),
            )
        ):
            n = slot - lags[i]
            if 0 <= n < len(chunks):
                act(chunks[n])
        for i in range(3):
            n = slot - (lags[2] + QKV_LAG * (1 + i))
            if first_of_qkv <= n < len(chunks):
                step_spread(chunks[n], i + 1)
        for act in extra.get(slot, ()):
            act()

    for chunk in chunks[:ahead]:
        begin(chunk)
    s.small_mine[...] = jnp.zeros_like(s.small_mine)
    s.gain[...] = jnp.zeros_like(s.gain)
    tasks, rows_grad, weights_grad = attention_back_tasks(s, r)
    slot = 0
    tasks.pop(0)()
    for _ in range(SLOTS_BEFORE):
        run_slot(slot)
        slot += 1
    for i in (1, 2, 3):
        swap_in(i).wait_recv()
        swap_out(i).wait_send()
    swap_keep.wait()
    for number, task in enumerate(tasks):
        task()
        if number in SLOTS_AFTER:
            run_slot(slot)
            slot += 1
    for block in (0, 3, 1, 2):
        rows_grad(block)
    for part_at in range(parts):
        back_hop(0, part_at)
    for turn in range(3):
        weights_grad(turn)
        begin(chunks[first_of_qkv + turn])
    assert slot <= first_of_qkv
    extra.setdefault(slot, []).append(lambda: small_step(0))
    for stage in range(1, 6):
        extra.setdefault(slot + 2 * stage, []).append(lambda stage=stage: small_step(stage))
    for part_at in range(parts):
        for hop in (1, 2):
            extra.setdefault(slot + 4 * hop - 2 + 2 * part_at, []).append(functools.partial(back_hop, hop, part_at))
        extra.setdefault(slot + 10 + 2 * part_at, []).append(functools.partial(back_last, part_at))
    last = max(max(extra) + 1, len(chunks) + lags[2] + 3 * QKV_LAG, first_of_qkv + lags[-1])
    while slot < last:
        run_slot(slot)
        slot += 1

    for chunk in chunks:
        core_copy(chunk).wait_send()
        pair_copy(chunk, 0).wait_send()
        pair_copy(chunk, 1).wait_send()

        def sent(chunk=chunk):
            for stage in range(3):
                spread_copy(chunk, stage).wait_send()

        on_plane(chunk, sent)
        if chunk.block is not None:
            pl.when(line < chunk.block)(lambda chunk=chunk: hop_copy(chunk, line, True).wait_send())
            pl.when(line > chunk.block)(lambda chunk=chunk: hop_copy(chunk, line, False).wait_send())
    for block in range(4):
        for part_at in range(parts):
            copy = functools.partial(back_hop_copy, block, part_at, line)
            pl.when(line < block)(lambda copy=copy: copy(True).wait_send())
            pl.when(line > block)(lambda copy=copy: copy(False).wait_send())


CHUNK_ORDER = tuple(
    ((2 * pair + at % 2), block)
    for pair in (0, 1)
    for at, block in enumerate((0, 3, 1, 2, 3, 0, 2, 1))
) + ((4, 0), (4, 3), (4, 1), (4, 2))
LAGS = (0, 4, 8, 11, 14, 17, 20, 23, 26)
QKV_LAG = 2
SLOTS_BEFORE = 5
SLOTS_AFTER = tuple(range(1, 16))


def back_all(
    grad_here, out_wg, gate_wg, up_wg, down_wg, probs, mixed, inverse, q, k, v, normed, wq, wk, wv, gain1, gain2_grad
):
    groups, rows, inner = grad_here.shape
    heads, length = q.shape[0], q.shape[1]
    width = normed.shape[1]
    units, part = down_wg.shape[1], out_wg.shape[1]
    parts = 2
    items = weight_items(units, part, width)
    n = 3 + groups * len(items)
    dma = pltpu.SemaphoreType.DMA
    scratch = {}
    for stage, divide in (("half", 1), ("core", 1), ("first", 2), ("second", 4), ("left", 4), ("right", 4)):
        for i, item in enumerate(items):
            cols = (units, units, width, width)[item.place]
            shape = (item.rows, cols // 2) if item.by_columns else (item.rows // 2, cols)
            scratch[stage + str(i)] = pltpu.VMEM((groups, shape[0] // divide, shape[1]), bf16)
    for stage, divide in (("half", 1), ("core", 1), ("first", 2), ("second", 4)):
        scratch["qkv_" + stage] = pltpu.VMEM((3, part // divide, width // 2), bf16)
    for name in ("back_acc", "back_left", "back_right"):
        scratch[name] = pltpu.VMEM((groups, parts, rows // parts, width), bf16)
    scratch.update(
        small_got=pltpu.VMEM((5, 16, width), f32),
        small_mine=pltpu.VMEM((16, width), f32),
        mixed_grad=pltpu.VMEM((groups, rows, inner), bf16),
        qkv_wg=pltpu.VMEM((3 * part, width), bf16),
        load_sem=dma((n,)), core_send=dma((n,)), core_recv=dma((n,)),
        pair_send=dma((2, n)), pair_recv=dma((2, n)),
        line_send=dma((n,)), left_recv=dma((n,)), right_recv=dma((n,)),
        spread_send=dma((3, n)), spread_recv=dma((3, n)),
        back_send=dma((groups, parts)), back_left_recv=dma((groups, parts)), back_right_recv=dma((groups, parts)),
        small_send=dma((5,)), small_recv=dma((5,)),
        swap_send=dma((3,)), swap_recv=dma((3,)), swap_keep=dma,
    )
    scratch.update(attention_scratch(heads, length, width))
    anywhere = pl.BlockSpec(memory_space=pl.ANY)
    inside = pl.BlockSpec(memory_space=pltpu.VMEM)
    return pl.pallas_call(
        functools.partial(back_kernel, tuple(scratch)),
        name="back_all",
        out_shape=(
            jax.ShapeDtypeStruct((rows, width), f32),
            jax.ShapeDtypeStruct((part, width), bf16),
            jax.ShapeDtypeStruct((width, units), bf16),
            jax.ShapeDtypeStruct((width, units), bf16),
            jax.ShapeDtypeStruct((units, width), bf16),
            jax.ShapeDtypeStruct((3 * part, width), bf16),
            jax.ShapeDtypeStruct((16, width), f32),
        ),
        in_specs=[anywhere] * 6 + [inside] * 11,
        out_specs=(inside,) * 7,
        scratch_shapes=list(scratch.values()),
        compiler_params=pltpu.CompilerParams(
            collective_id=3, has_side_effects=True, vmem_limit_bytes=58 << 20
        ),
    )(grad_here, out_wg, gate_wg, up_wg, down_wg, probs, mixed, inverse, q, k, v, normed, wq, wk, wv, gain1, gain2_grad)


def back_local_kernel(names, *refs):
    operands = BACK_OPERANDS[5:] + ("mixed_grad", "back_out", "qkv_out", "small_out")
    r = Named(operands, refs)
    s = Named(names, refs[len(operands) :])
    s.mixed_grad, s.qkv_wg, s.small_mine, s.back_acc = r.mixed_grad, r.qkv_out, r.small_out, r.back_out
    s.probs_copy = lambda h: pltpu.make_async_copy(r.probs_all.at[h], s.probs.at[h % 2], s.probs_sem.at[h])
    for h in range(2):
        s.probs_copy(h).start()
    s.small_mine[...] = jnp.zeros_like(s.small_mine)
    s.gain[...] = jnp.zeros_like(s.gain)
    tasks, rows_grad, weights_grad = attention_back_tasks(s, r)
    for task in tasks:
        task()
    for block in range(r.back_out.shape[0]):
        rows_grad(block)
    for turn in range(3):
        weights_grad(turn)
    s.small_mine[0:1, :] = s.gain[...] / r.gain1[...].astype(f32)
    s.small_mine[1:2, :] = r.gain2_grad[...]


def attention_scratch(heads, length, width):
    return dict(
        gain=pltpu.VMEM((1, width), f32),
        probs=pltpu.VMEM((2, length, length), bf16),
        w=pltpu.VMEM((768, width), bf16),
        dot=pltpu.VMEM((heads, length, 128), bf16),
        dott=pltpu.VMEM((heads, 128, length), bf16),
        qt=pltpu.VMEM((heads, 128, length), bf16),
        vt=pltpu.VMEM((heads, 128, length), bf16),
        grad=pltpu.VMEM((length, 384), f32),
        joined=pltpu.VMEM((length, 768), bf16),
        near=pltpu.VMEM((BLK, 3 * BLK), f32),
        far=pltpu.VMEM((2, BLK, 128), f32),
        dkt=pltpu.VMEM((128, length), f32),
        dvt=pltpu.VMEM((128, length), f32),
        probs_sem=pltpu.SemaphoreType.DMA((heads,)),
    )


def back_by_axis(
    grad_here, out_wg, gate_wg, up_wg, down_wg, probs, mixed, inverse, q, k, v, normed, wq, wk, wv, gain1, gain2_grad
):
    groups, rows, inner = grad_here.shape
    heads, length = q.shape[0], q.shape[1]
    width = normed.shape[1]
    mixed_grad = lax.all_to_all(grad_here, "tensor", 0, 0)
    scratch = attention_scratch(heads, length, width)
    anywhere = pl.BlockSpec(memory_space=pl.ANY)
    inside = pl.BlockSpec(memory_space=pltpu.VMEM)
    back, qkv_wg, small = pl.pallas_call(
        functools.partial(back_local_kernel, tuple(scratch)),
        name="back_local",
        out_shape=(
            jax.ShapeDtypeStruct((groups, 2, rows // 2, width), bf16),
            jax.ShapeDtypeStruct((3 * inner, width), bf16),
            jax.ShapeDtypeStruct((16, width), f32),
        ),
        in_specs=[anywhere] + [inside] * 12,
        out_specs=(inside,) * 3,
        scratch_shapes=list(scratch.values()),
        compiler_params=pltpu.CompilerParams(vmem_limit_bytes=56 << 20),
    )(probs, mixed, inverse, q, k, v, normed, wq, wk, wv, gain1, gain2_grad, mixed_grad)
    back_sum = lax.psum_scatter(back.reshape(groups, rows, width), "tensor", scatter_dimension=0)
    parts = tuple(lax.psum_scatter(wg, "tensor", scatter_dimension=0) for wg in (out_wg, gate_wg, up_wg, down_wg))
    sums = lax.psum(parts + (qkv_wg,), "dp")
    small_sum = lax.psum(small, "dp")
    gains = lax.psum(small_sum[:8], "tensor")
    return (back_sum.astype(f32),) + tuple(sums) + (jnp.concatenate((gains, small_sum[8:])),)


def gather_by_axis(normed, gate, up, down, out):
    return tuple(lax.all_gather(part, "tensor", axis=0) for part in (normed, gate, up, down, out))


def swap_by_axis(blocks):
    return lax.all_to_all(blocks, "tensor", 0, 0)


def shards(
    by_kernel,
    hidden_in, segment_ids, norm1_gain, query_weight, key_weight, value_weight, out_weight,
    bias_table, norm2_gain, gate_weight, up_weight, down_weight, out_cotangent,
):
    gather_parts = gather if by_kernel else gather_by_axis
    swap_parts = swap if by_kernel else swap_by_axis
    back_parts = back_all if by_kernel else back_by_axis
    rows_here, width = hidden_in.shape
    length = segment_ids.shape[1]
    assert segment_ids.shape[0] == 1
    groups = length // rows_here
    heads = bias_table.shape[1]
    input_rows = hidden_in.astype(f32)
    first_gain = norm1_gain.astype(f32)
    r1 = mean_square_scale(input_rows)
    normed_here = (input_rows * r1 * first_gain).astype(bf16)
    normed, gate_w, up_w, down_w, out_w = gather_parts(
        normed_here, gate_weight, up_weight, down_weight, out_weight
    )
    normed = normed.reshape(length, width)
    query_weight, key_weight, value_weight = query_weight.T, key_weight.T, value_weight.T
    mixed, probs, q, k, v, inverse = attend(
        normed, query_weight, key_weight, value_weight, segment_ids, bias_table
    )
    mixed_here = swap_parts(mixed.reshape(groups, rows_here, -1))
    output, residual_grad, mixed_grad_here, gain2, out_wg, gate_wg, up_wg, down_wg = unit(
        mixed_here, hidden_in, out_cotangent, out_w, gate_w, up_w, down_w, norm2_gain[None]
    )
    back, out_sum, gate_sum, up_sum, down_sum, qkv_sum, small_sum = back_parts(
        mixed_grad_here, out_wg, gate_wg, up_wg, down_wg, probs, mixed, inverse, q, k, v, normed,
        query_weight, key_weight, value_weight, norm1_gain[None], gain2,
    )
    g1 = back * first_gain
    centre = jnp.mean(g1 * input_rows, axis=-1, keepdims=True)
    input_grad = (residual_grad + r1 * g1 - (r1 * r1 * r1 * centre) * input_rows).astype(bf16)
    qkv = qkv_sum.astype(f32)
    inner = heads * HEAD_DIM
    return (
        output, input_grad, small_sum[0], qkv[:inner].T, qkv[inner : 2 * inner].T, qkv[2 * inner :].T,
        out_sum.astype(f32), small_sum[8 : 8 + heads, :BUCKETS].T,
        small_sum[1], gate_sum.astype(f32), up_sum.astype(f32), down_sum.astype(f32),
    )


def solution(mesh):
    in_specs = (
        P(("dp", "tensor"), None), P("dp", None), P(),
        P(None, "tensor"), P(None, "tensor"), P(None, "tensor"), P("tensor", None),
        P(None, "tensor"), P(), P(None, "tensor"), P(None, "tensor"), P("tensor", None),
        P(("dp", "tensor"), None),
    )
    out_specs = (
        P(("dp", "tensor"), None), P(("dp", "tensor"), None), P(),
        P(None, "tensor"), P(None, "tensor"), P(None, "tensor"), P("tensor", None),
        P(None, "tensor"), P(), P(None, "tensor"), P(None, "tensor"), P("tensor", None),
    )
    by_kernel = mesh.shape["dp"] == 8 and mesh.shape["tensor"] == 4
    return jax.shard_map(
        functools.partial(shards, by_kernel), mesh=mesh, in_specs=in_specs, out_specs=out_specs, check_vma=False
    )
```

```python
import functools

import jax
import jax.numpy as jnp
from jax import lax
from jax.experimental import pallas as pl
from jax.experimental.pallas import tpu as pltpu
from jax.sharding import PartitionSpec as P

HEAD_DIM = 64
BUCKETS = 32
far_marks = (12, 16, 23, 32, 46, 64, 91)
norm_eps = 1e-06
far_score = 2.0**30
BLK = 256
f32 = jnp.float32
bf16 = jnp.bfloat16


def bucket_of(offset):
    magnitude = jnp.abs(offset)
    within = jnp.minimum(magnitude, 8)
    for far_mark in far_marks:
        within = within + (magnitude >= far_mark).astype(jnp.int32)
    return within + jnp.where(offset > 0, 16, 0).astype(jnp.int32)


def key_range(block, count):
    return range(max(0, block - 2), min(count, block + 3))


def contract(lhs, rhs, left, right):
    return lax.dot_general(
        lhs, rhs, (((left,), (right,)), ((), ())), preferred_element_type=f32
    )


def attend_kernel(
    normed_ref, wq_ref, wk_ref, wv_ref, seg_ref, table_ref,
    mixed_ref, probs_ref, qt_ref, k_ref, vt_ref, inv_ref,
    w_s, kt_s, bias_s, score_s, first_s, q_s, v_s,
):
    head = pl.program_id(0)
    length = normed_ref.shape[0]
    count = length // BLK
    lane = lax.broadcasted_iota(jnp.int32, (BLK, 128), 1)
    low_half = lane < HEAD_DIM

    @pl.when(head == 0)
    def _():
        w_s[...] = jnp.zeros_like(w_s)
        for place, ref in enumerate((wq_ref, wk_ref, wv_ref)):
            w_s[256 * place : 256 * place + 192, :] = ref[...]
        row8 = lax.broadcasted_iota(jnp.int32, (8, 128), 0)
        lane8 = lax.broadcasted_iota(jnp.int32, (8, 128), 1)
        spread = jnp.where((lane8 % HEAD_DIM) == row8, 1.0, 0.0).astype(bf16)

        def project(step, carry):
            rows = pl.ds(pl.multiple_of(step * BLK, BLK), BLK)
            seg_row = seg_ref[:, rows]
            kinds = lax.broadcasted_iota(jnp.int32, (8, BLK), 0)
            hot = jnp.where(
                jnp.broadcast_to(seg_row, (8, BLK)) == kinds, 1.0, 0.0
            ).astype(bf16)
            same = contract(hot, spread, 0, 0)
            in_aug = (lane % HEAD_DIM) < 8
            aug_q = jnp.where(in_aug, same, 0.0)
            aug_k = jnp.where(in_aug, (same - 1.0) * far_score, 0.0)
            rows_in = normed_ref[rows, :]
            q = contract(rows_in, w_s[0:256, :], 1, 1)
            k = contract(rows_in, w_s[256:512, :], 1, 1)
            v = contract(rows_in, w_s[512:768, :], 1, 1)
            scale = HEAD_DIM ** (-0.5)
            for h, (cols, mine) in enumerate(
                ((slice(0, 128), low_half), (slice(0, 128), ~low_half), (slice(128, 256), low_half))
            ):
                q_h = jnp.where(mine, q[:, cols] * scale, aug_q).astype(bf16)
                q_s[h, rows, :] = q_h
                qt_ref[h, :, rows] = q_h.T
                k_h = jnp.where(mine, k[:, cols], aug_k).astype(bf16)
                k_ref[h, rows, :] = k_h
                v_h = jnp.where(mine, v[:, cols], 1.0).astype(bf16)
                v_s[h, rows, :] = v_h
                vt_ref[h, :, rows] = v_h.T
                kt_s[h, :, rows] = k_h.T
            return carry

        lax.fori_loop(0, count, project, 0)

    offset = lax.broadcasted_iota(jnp.int32, (BUCKETS, length), 1)
    offset = jnp.where(offset >= length // 2, offset - length, offset)
    hot_bucket = jnp.where(
        bucket_of(offset) == lax.broadcasted_iota(jnp.int32, (BUCKETS, length), 0), 1.0, 0.0
    ).astype(bf16)
    by_offset = contract(table_ref[head], hot_bucket, 1, 0)[0:1]
    spread_rows = jnp.broadcast_to(by_offset, (BLK, length))
    bias_s[...] = pltpu.roll(spread_rows, 0, 1, stride=1, stride_axis=0)

    for block in range(count):
        rows = slice(block * BLK, (block + 1) * BLK)
        q_h = q_s[head, rows, :]
        top = None
        for key in key_range(block, count):
            part = jnp.dot(
                q_h, kt_s[head, :, key * BLK : (key + 1) * BLK], preferred_element_type=f32
            )
            delta = key - block
            at = (delta * BLK) % length
            part = part + bias_s[:, at : at + BLK]
            score_s[:, key * BLK : (key + 1) * BLK] = part
            top = part if top is None else jnp.maximum(top, part)
        top = jnp.max(jnp.maximum(top[:, :128], top[:, 128:]), axis=1, keepdims=True)
        total = jnp.zeros((BLK, 128), f32)
        for key in key_range(block, count):
            cols = slice(key * BLK, (key + 1) * BLK)
            part = jnp.exp(score_s[:, cols] - top).astype(bf16)
            probs_ref[0, rows, cols] = part
            total = total + jnp.dot(part, v_s[head, cols, :], preferred_element_type=f32)
        sums = pltpu.roll(total, HEAD_DIM, 1)
        inverse = 1.0 / sums
        out = total * inverse

        @pl.when(head == 0)
        def _():
            first_s[rows, 0:128] = out
            first_s[rows, 128:256] = inverse

        @pl.when(head == 1)
        def _():
            mixed_ref[rows, 0:128] = jnp.where(low_half, first_s[rows, 0:128], out).astype(bf16)
            inv_ref[rows, 0:128] = jnp.where(low_half, first_s[rows, 128:256], inverse)

        @pl.when(head == 2)
        def _():
            mixed_ref[rows, 128:192] = out[:, 0:HEAD_DIM].astype(bf16)
            inv_ref[rows, 128:256] = inverse


def attend(normed, wq, wk, wv, segments, bias_table):
    length, width = normed.shape
    heads = bias_table.shape[1]
    inner = heads * HEAD_DIM
    table = jnp.broadcast_to(bias_table.T[:, None, :], (heads, 8, BUCKETS))
    whole = lambda *dims: pl.BlockSpec(dims, lambda h: (0,) * len(dims))
    return pl.pallas_call(
        attend_kernel,
        grid=(heads,),
        name="attend",
        out_shape=(
            jax.ShapeDtypeStruct((length, inner), bf16),
            jax.ShapeDtypeStruct((heads, length, length), bf16),
            jax.ShapeDtypeStruct((heads, 128, length), bf16),
            jax.ShapeDtypeStruct((heads, length, 128), bf16),
            jax.ShapeDtypeStruct((heads, 128, length), bf16),
            jax.ShapeDtypeStruct((length, 256), f32),
        ),
        in_specs=[
            whole(length, width),
            whole(inner, width),
            whole(inner, width),
            whole(inner, width),
            whole(1, length),
            whole(heads, 8, BUCKETS),
        ],
        out_specs=(
            whole(length, inner),
            pl.BlockSpec((1, length, length), lambda h: (h, 0, 0)),
            whole(heads, 128, length),
            whole(heads, length, 128),
            whole(heads, 128, length),
            whole(length, 256),
        ),
        scratch_shapes=[
            pltpu.VMEM((768, width), bf16),
            pltpu.VMEM((heads, 128, length), bf16),
            pltpu.VMEM((BLK, length), f32),
            pltpu.VMEM((BLK, length), f32),
            pltpu.VMEM((length, 256), f32),
            pltpu.VMEM((heads, length, 128), bf16),
            pltpu.VMEM((heads, length, 128), bf16),
        ],
        compiler_params=pltpu.CompilerParams(
            dimension_semantics=("arbitrary",), vmem_limit_bytes=48 << 20
        ),
        cost_estimate=pl.CostEstimate(flops=3 << 30, bytes_accessed=12 << 20, transcendentals=3 << 20),
    )(normed, wq, wk, wv, segments, table)


def mean_square_scale(rows):
    return lax.rsqrt(jnp.mean(rows * rows, axis=-1, keepdims=True) + norm_eps)


MESH_IDS = pl.DeviceIdType.MESH


def places():
    dp = lax.axis_index("dp")
    line = lax.axis_index("tensor")
    core = lax.rem(dp, 2)
    x = lax.rem(dp // 2, 2)
    y = dp // 4
    flips = (dp + 1 - 2 * core, dp + 2 - 4 * x, dp + 4 - 8 * y)
    return dp, line, core, x, y, flips


def nearest(line, k):
    upper = line // 2
    inner = line * (1 - upper) + (3 - line) * upper
    block = k + 1 - inner if k == 0 else k + 1
    block = block * (1 - upper) + (3 - block) * upper
    way = (1 if k == 0 else -1) * (1 - 2 * upper)
    return block, way


class Item:
    def __init__(self, place, base, rows, flipped, by_columns=False):
        self.place, self.base, self.rows = place, base, rows
        self.flipped, self.by_columns = flipped, by_columns

    def bits(self, x, y):
        return (y, x) if self.flipped else (x, y)

    def partner(self, level, flips):
        if level == 0:
            return flips[0]
        return flips[1 + ((level - 1) ^ int(self.flipped))]

    def window(self, ref, lead, level, core, first, second):
        width = ref.shape[-1]
        if self.by_columns:
            size = self.rows // (1, 2, 4)[level - 1]
            start = self.base + 0 * core
            if level > 1:
                start = start + first * (self.rows // 2)
            if level > 2:
                start = start + second * (self.rows // 4)
            cols = pl.ds(pl.multiple_of(core * (width // 2), 128), width // 2)
        else:
            size = self.rows // (2, 4, 8)[level - 1]
            start = self.base + core * (self.rows // 2)
            if level > 1:
                start = start + first * (self.rows // 4)
            if level > 2:
                start = start + second * (self.rows // 8)
            cols = pl.ds(0, width)
        rows = pl.ds(pl.multiple_of(start, 16), size)
        if lead is None:
            return ref.at[rows, cols]
        return ref.at[lead, rows, cols]


def weight_items(units, part, width):
    return (
        Item(0, 0, width, False),
        Item(1, 0, width, True),
        Item(2, 0, units // 2, False),
        Item(2, units // 2, units // 2, True),
        Item(3, 0, part, False, by_columns=True),
    )


def gather_kernel(
    normed_ref, gate_ref, up_ref, down_ref, out_ref,
    normed_all, gate_all, up_all, down_all, out_all,
    z_send, z_recv, p_send, p_recv, own_sem,
    hold_gate, hold_up, hold_down, hold_out, hold_normed,
):
    dp, line, core, x, y, flips = places()
    upper = line // 2
    inner = line * (1 - upper) + (3 - line) * upper
    own = (gate_ref, up_ref, down_ref, out_ref)
    full = (gate_all, up_all, down_all, out_all)
    units, width = down_ref.shape
    items = weight_items(units, out_ref.shape[0], width)
    count = len(items)

    barrier = pltpu.get_barrier_semaphore()
    for flip in flips:
        pl.semaphore_signal(barrier, inc=1, device_id=(flip, line), device_id_type=MESH_IDS)

    @pl.when(line > 0)
    def _():
        pl.semaphore_signal(barrier, inc=1, device_id=(dp, line - 1), device_id_type=MESH_IDS)

    @pl.when(line < 3)
    def _():
        pl.semaphore_signal(barrier, inc=1, device_id=(dp, line + 1), device_id_type=MESH_IDS)

    pl.semaphore_wait(barrier, 4 + inner)

    def eighth(i, ref, lead):
        item = items[i]
        first, second = item.bits(x, y)
        return item.window(ref, lead, 3, core, first, second)

    def along(i, block, target, side, first_hop):
        if i == count:
            src = normed_ref if first_hop else normed_all.at[block]
            dst = normed_all.at[block]
        else:
            dst = eighth(i, full[items[i].place], block)
            src = eighth(i, own[items[i].place], None) if first_hop else dst
        return pltpu.make_async_remote_copy(
            src_ref=src, dst_ref=dst, send_sem=z_send.at[i, block, side], recv_sem=z_recv.at[i, block],
            device_id=(dp, target), device_id_type=MESH_IDS,
        )

    def send_own(i):
        @pl.when(line > 0)
        def _():
            along(i, line, line - 1, 0, True).start()

        @pl.when(line < 3)
        def _():
            along(i, line, line + 1, 1, True).start()

    def arrive(i, k):
        block, way = nearest(line, k)
        along(i, block, line, 0, False).wait_recv()

        @pl.when(inner == 1)
        def _():
            along(i, block, line + way, 0, False).start()

    def spread(i, k, stage):
        block, _ = nearest(line, k)
        item = items[i]
        first, second = item.bits(x, y)
        window = item.window(full[item.place], block, 3 - stage, core, first, second)
        return pltpu.make_async_remote_copy(
            src_ref=window, dst_ref=window, send_sem=p_send.at[stage, i, k], recv_sem=p_recv.at[stage, i, k],
            device_id=(item.partner(2 - stage, flips), line), device_id_type=MESH_IDS,
        )

    for i in range(count):
        send_own(i)
    holds = (hold_gate, hold_up, hold_down, hold_out, hold_normed)
    loads = []
    stores = []
    for place, ref in enumerate(own + (normed_ref,)):
        target = (full + (normed_all,))[place].at[line]
        loads.append(pltpu.make_async_copy(ref, holds[place], own_sem.at[0, place]))
        stores.append(pltpu.make_async_copy(holds[place], target, own_sem.at[1, place]))
    for load in loads:
        load.start()
    for load, store in zip(loads, stores):
        load.wait()
        store.start()

    def advance(k, stage):
        for i in range(count):
            if stage > 0:
                spread(i, k, stage - 1).wait_recv()
            spread(i, k, stage).start()

    for k in range(3):
        for i in range(count):
            arrive(i, k)
            spread(i, k, 0).start()
        if k == 2:
            send_own(count)
        if k >= 1:
            advance(k - 1, 1)
        if k >= 2:
            advance(k - 2, 2)
    advance(2, 1)
    arrive(count, 0)
    advance(1, 2)
    arrive(count, 1)
    advance(2, 2)
    arrive(count, 2)

    for store in stores:
        store.wait()
    for i in range(count + 1):
        @pl.when(line > 0)
        def _(i=i):
            along(i, line, line - 1, 0, True).wait_send()

        @pl.when(line < 3)
        def _(i=i):
            along(i, line, line + 1, 1, True).wait_send()

        @pl.when(inner == 1)
        def _(i=i):
            for k in range(3):
                block, way = nearest(line, k)
                along(i, block, line + way, 0, False).wait_send()

    for k in range(3):
        for i in range(count):
            spread(i, k, 2).wait_recv()
            for stage in range(3):
                spread(i, k, stage).wait_send()


def gather(normed, gate, up, down, out):
    rows, width = normed.shape
    units, part = gate.shape[1], out.shape[0]
    anywhere = pl.BlockSpec(memory_space=pl.ANY)
    return pl.pallas_call(
        gather_kernel,
        name="gather",
        out_shape=(
            jax.ShapeDtypeStruct((4, rows, width), bf16),
            jax.ShapeDtypeStruct((4, width, units), bf16),
            jax.ShapeDtypeStruct((4, width, units), bf16),
            jax.ShapeDtypeStruct((4, units, width), bf16),
            jax.ShapeDtypeStruct((4, part, width), bf16),
        ),
        in_specs=[anywhere] * 5,
        out_specs=(anywhere,) * 5,
        scratch_shapes=[
            pltpu.SemaphoreType.DMA((6, 4, 2)),
            pltpu.SemaphoreType.DMA((6, 4)),
            pltpu.SemaphoreType.DMA((3, 5, 3)),
            pltpu.SemaphoreType.DMA((3, 5, 3)),
            pltpu.SemaphoreType.DMA((2, 5)),
            pltpu.VMEM(gate.shape, bf16),
            pltpu.VMEM(up.shape, bf16),
            pltpu.VMEM(down.shape, bf16),
            pltpu.VMEM(out.shape, bf16),
            pltpu.VMEM(normed.shape, bf16),
        ],
        compiler_params=pltpu.CompilerParams(collective_id=1, has_side_effects=True),
    )(normed, gate, up, down, out)


def swap_kernel(mine_ref, theirs_ref, send_sem, recv_sem, own_sem):
    dp, line, _, _, _, _ = places()
    barrier = pltpu.get_barrier_semaphore()
    others = [lax.rem(line + i, 4) for i in (1, 2, 3)]
    for other in others:
        pl.semaphore_signal(barrier, inc=1, device_id=(dp, other), device_id_type=MESH_IDS)
    pl.semaphore_wait(barrier, 3)
    copies = [
        pltpu.make_async_remote_copy(
            src_ref=mine_ref.at[other], dst_ref=theirs_ref.at[line], send_sem=send_sem.at[i], recv_sem=recv_sem.at[2 - i],
            device_id=(dp, other), device_id_type=MESH_IDS,
        )
        for i, other in enumerate(others)
    ]
    for copy in copies:
        copy.start()
    keep = pltpu.make_async_copy(mine_ref.at[line], theirs_ref.at[line], own_sem)
    keep.start()
    for i, other in enumerate(others):
        copies[i].wait_send()
        pltpu.make_async_remote_copy(
            src_ref=mine_ref.at[other], dst_ref=theirs_ref.at[other], send_sem=send_sem.at[i], recv_sem=recv_sem.at[i],
            device_id=(dp, other), device_id_type=MESH_IDS,
        ).wait_recv()
    keep.wait()


def swap(blocks):
    anywhere = pl.BlockSpec(memory_space=pl.ANY)
    return pl.pallas_call(
        swap_kernel,
        name="swap",
        out_shape=jax.ShapeDtypeStruct(blocks.shape, blocks.dtype),
        in_specs=[anywhere],
        out_specs=anywhere,
        scratch_shapes=[
            pltpu.SemaphoreType.DMA((3,)),
            pltpu.SemaphoreType.DMA((3,)),
            pltpu.SemaphoreType.DMA,
        ],
        compiler_params=pltpu.CompilerParams(collective_id=2, has_side_effects=True),
    )(blocks)


class Named:
    def __init__(self, names, refs):
        for name, ref in zip(names, refs):
            setattr(self, name, ref)


def remote(src, dst, send, recv, target):
    return pltpu.make_async_remote_copy(
        src_ref=src, dst_ref=dst, send_sem=send, recv_sem=recv, device_id=target, device_id_type=MESH_IDS
    )


def greet(dp, line, flips):
    barrier = pltpu.get_barrier_semaphore()
    for flip in flips:
        pl.semaphore_signal(barrier, inc=1, device_id=(flip, line), device_id_type=MESH_IDS)
    for i in (1, 2, 3):
        pl.semaphore_signal(
            barrier, inc=1, device_id=(dp, lax.rem(line + i, 4)), device_id_type=MESH_IDS
        )
    pl.semaphore_wait(barrier, 6)


def unit_parts(s, r):
    groups = r.mixed_here.shape[0]

    def begin():
        mixed = jnp.concatenate([r.mixed_here[g] for g in range(groups)], axis=1)
        out_w = jnp.concatenate([s.out_w[g] for g in range(groups)], axis=0)
        residual = r.hidden_in[...].astype(f32) + jnp.dot(mixed, out_w, preferred_element_type=f32)
        s.residual[...] = residual
        s.normed2[...] = (residual * mean_square_scale(residual) * r.gain2[...].astype(f32)).astype(bf16)
        s.ahead[...] = residual
        s.behind[...] = jnp.zeros_like(s.behind)

    def block(b, slot):
        normed = s.normed2[...]
        cot = r.cot[...]
        gate_w, up_w, down_w = s.gate_w[slot], s.up_w[slot], s.down_w[slot]
        gate = jnp.dot(normed, gate_w, preferred_element_type=f32)
        up = jnp.dot(normed, up_w, preferred_element_type=f32)
        hidden_grad = contract(cot, down_w, 1, 1)
        c0 = 0.7978845608028654
        square = gate * gate
        bend = jnp.tanh(gate * (c0 + (c0 * 0.044715) * square))
        half = 0.5 + 0.5 * bend
        act = gate * half
        slope = half + 0.5 * gate * (1.0 - bend * bend) * (c0 + (3.0 * c0 * 0.044715) * square)
        hidden = (act * up).astype(bf16)
        gate_grad = (hidden_grad * up * slope).astype(bf16)
        up_grad = (hidden_grad * act).astype(bf16)
        s.ahead[...] += jnp.dot(hidden, down_w, preferred_element_type=f32)
        s.behind[...] += contract(gate_grad, gate_w, 1, 1) + contract(up_grad, up_w, 1, 1)
        s.down_wg[b] = contract(hidden, cot, 0, 0).astype(bf16)
        s.gate_wg[b] = contract(normed, gate_grad, 0, 0).astype(bf16)
        s.up_wg[b] = contract(normed, up_grad, 0, 0).astype(bf16)

    def end():
        residual = s.residual[...]
        r.output[...] = s.ahead[...].astype(bf16)
        back = s.behind[...]
        scale = mean_square_scale(residual)
        s.small_mine[1:2, :] = jnp.sum(back * residual * scale, axis=0, keepdims=True)
        g = back * r.gain2[...].astype(f32)
        centre = jnp.mean(g * residual, axis=-1, keepdims=True)
        residual_grad = r.cot[...].astype(f32) + scale * g - (scale * scale * scale * centre) * residual
        low = residual_grad.astype(bf16)
        s.behind[...] = residual_grad
        for g_at in range(groups):
            s.grad_here[g_at] = contract(low, s.out_w[g_at], 1, 1).astype(bf16)

    def out_grad():
        low = s.behind[...].astype(bf16)
        for g_at in range(groups):
            s.out_wg[g_at] = contract(r.mixed_here[g_at], low, 0, 0).astype(bf16)

    return begin, block, end, out_grad


def attention_back_tasks(s, r):
    heads, length = s.dot.shape[0], s.dot.shape[1]
    count = length // BLK
    lane = lax.broadcasted_iota(jnp.int32, (BLK, 128), 1)
    low_half = lane < HEAD_DIM
    tasks = []

    def probs_copy(h, block):
        at = (h * count + block) % 2
        rows = pl.ds(block * BLK, BLK)
        return pltpu.make_async_copy(r.probs_all.at[h, rows, :], s.probs.at[at], s.probs_sem.at[at])

    def prepare():
        probs_copy(0, 0).start()
        probs_copy(0, 1).start()

        def body(step, carry):
            rows = pl.ds(pl.multiple_of(step * BLK, BLK), BLK)
            for h in range(heads):
                cols = slice(0, 128) if h < 2 else slice(128, 256)
                mine = ~low_half if h == 1 else low_half
                if h < 2:
                    grad = s.mixed_grad[step, :, 0:128].astype(f32)
                    mix = r.mixed[rows, 0:128].astype(f32)
                else:
                    fill = jnp.zeros((BLK, HEAD_DIM), f32)
                    grad = jnp.concatenate((s.mixed_grad[step, :, 128:192].astype(f32), fill), axis=1)
                    mix = jnp.concatenate((r.mixed[rows, 128:192].astype(f32), fill), axis=1)
                grad = jnp.where(mine, grad * r.inverse[rows, cols], 0.0)
                centre = -jnp.sum(grad * mix, axis=1, keepdims=True)
                high = centre.astype(bf16).astype(f32)
                base = 0 if h == 1 else HEAD_DIM
                grad = jnp.where(lane == base, high, grad)
                grad = jnp.where(lane == base + 1, centre - high, grad)
                low = grad.astype(bf16)
                s.dot[h, rows, :] = low
                s.dott[h, :, rows] = low.T
            return carry

        lax.fori_loop(0, count, body, 0)

    tasks.append(prepare)

    def block_step(h, block):
        if block == 0:
            s.near[...] = jnp.zeros_like(s.near)
            s.far[...] = jnp.zeros_like(s.far)
            s.dkt[...] = jnp.zeros_like(s.dkt)
            s.dvt[...] = jnp.zeros_like(s.dvt)
        probs_copy(h, block).wait()
        at = (h * count + block) % 2
        rows = slice(block * BLK, (block + 1) * BLK)
        d_h = s.dot[h, rows, :]
        dt_h = s.dott[h, :, rows]
        qt_h = r.qt[h, :, rows]
        query_grad = jnp.zeros((BLK, 128), f32)
        for key in key_range(block, count):
            cols = slice(key * BLK, (key + 1) * BLK)
            probs = s.probs[at, :, cols]
            slope = jnp.dot(d_h, r.vt[h, :, cols], preferred_element_type=f32)
            grad = probs.astype(f32) * slope
            low = grad.astype(bf16)
            delta = key - block
            if abs(delta) == 2:
                s.far[0 if delta < 0 else 1] += grad[:, :128] + grad[:, 128:]
            else:
                s.near[:, (delta + 1) * BLK : (delta + 2) * BLK] += grad
            query_grad = query_grad + jnp.dot(low, r.k[h, cols, :], preferred_element_type=f32)
            s.dkt[:, cols] += jnp.dot(qt_h, low, preferred_element_type=f32)
            s.dvt[:, cols] += jnp.dot(dt_h, probs, preferred_element_type=f32)
        s.grad[rows, 0:128] = query_grad * HEAD_DIM ** (-0.5)
        turn = h * count + block + 2
        if turn < heads * count:
            probs_copy(turn // count, turn % count).start()

    def head_end(h):
        def body(step, carry):
            rows = pl.ds(pl.multiple_of(step * BLK, BLK), BLK)
            s.grad[rows, 128:256] = s.dkt[:, rows].T
            s.grad[rows, 256:384] = s.dvt[:, rows].T
            for at in range(3):
                part = s.grad[rows, 128 * at : 128 * at + 128]
                if h == 0:
                    s.joined[rows, 256 * at : 256 * at + 128] = part.astype(bf16)
                elif h == 1:
                    before = s.joined[rows, 256 * at : 256 * at + 128].astype(f32)
                    s.joined[rows, 256 * at : 256 * at + 128] = jnp.where(low_half, before, part).astype(bf16)
                else:
                    s.joined[rows, 256 * at + 128 : 256 * at + 256] = jnp.where(low_half, part, 0.0).astype(bf16)
            return carry

        lax.fori_loop(0, count, body, 0)
        place = lax.broadcasted_iota(jnp.int32, (BLK, 3 * BLK), 1) - BLK
        place = place - lax.broadcasted_iota(jnp.int32, (BLK, 3 * BLK), 0)
        s.bucket[...] = bucket_of(place)
        s.table[...] = jnp.zeros_like(s.table)

        def count_bucket(b, carry):
            part = jnp.sum(jnp.where(s.bucket[...] == b, s.near[...], 0.0), axis=0, keepdims=True)
            folded = part[:, 0:128]
            for at in range(1, 6):
                folded = folded + part[:, at * 128 : (at + 1) * 128]
            s.table[pl.ds(b, 1), :] = folded
            return carry

        lax.fori_loop(0, BUCKETS, count_bucket, 0)
        for side, b in ((0, 15), (1, 31)):
            s.table[b : b + 1, :] += jnp.sum(s.far[side], axis=0, keepdims=True)
        flat = lax.dot_general(
            jnp.ones((8, 128), f32), s.table[...], (((1,), (1,)), ((), ())),
            preferred_element_type=f32, precision=lax.Precision.HIGHEST,
        )
        s.small_mine[8 + h : 9 + h, 0:BUCKETS] = flat[0:1]

    for h in range(heads):
        for block in range(count):
            tasks.append(functools.partial(block_step, h, block))
        tasks.append(functools.partial(head_end, h))

    def rows_grad(block):
        rows = slice(block * BLK, (block + 1) * BLK)
        part = jnp.dot(s.joined[rows, :], s.w[...], preferred_element_type=f32)
        s.back_acc[block] = part.astype(bf16)
        s.gain[...] += jnp.sum(part * r.normed[rows, :].astype(f32), axis=0, keepdims=True)

    def weights_grad(at):
        part = contract(s.joined[:, 256 * at : 256 * at + 256], r.normed[...], 0, 0)
        s.qkv_wg[192 * at : 192 * at + 192, :] = part[0:192].astype(bf16)

    return tasks, rows_grad, weights_grad


REST_OPERANDS = (
    "gate_all", "up_all", "down_all", "out_all", "probs_all", "wq", "wk", "wv",
    "mixed_here", "hidden_in", "cot", "gain1", "gain2", "mixed", "inverse", "qt", "k", "vt", "normed",
)
REST_RESULTS = (
    "output", "input_grad", "small_sum", "out_sum", "gate_sum", "up_sum", "down_sum", "qkv_sum",
)


def load_weights(s, r, b, slot):
    pairs = ((r.gate_all, s.gate_w), (r.up_all, s.up_w), (r.down_all, s.down_w))
    return [
        pltpu.make_async_copy(src.at[b], dst.at[slot], s.weight_sem.at[i, slot]) for i, (src, dst) in enumerate(pairs)
    ]


def load_small(s, r):
    copies = [pltpu.make_async_copy(r.out_all, s.out_w, s.first_sem.at[0])]
    for place, ref in enumerate((r.wq, r.wk, r.wv)):
        part = ref.shape[0]
        copies.append(pltpu.make_async_copy(ref, s.w.at[pl.ds(256 * place, part), :], s.first_sem.at[1 + place]))
    return copies


def start_all(s, r):
    groups = s.out_w.shape[0]
    for copy in load_small(s, r) + load_weights(s, r, 0, 0):
        copy.start()
    s.small_mine[...] = jnp.zeros_like(s.small_mine)
    s.gain[...] = jnp.zeros_like(s.gain)
    for place in range(3):
        s.w[256 * place + 192 : 256 * place + 256, :] = jnp.zeros((64, s.w.shape[1]), bf16)
    return groups


def input_grad_rows(s, r, back):
    rows = r.hidden_in[...].astype(f32)
    scale = mean_square_scale(rows)
    g = back * r.gain1[...].astype(f32)
    centre = jnp.mean(g * rows, axis=-1, keepdims=True)
    r.input_grad[...] = (s.behind[...] + scale * g - (scale * scale * scale * centre) * rows).astype(bf16)


def add_rows(target, start, size, source):
    step = 32 if size % 32 == 0 else 16

    def body(i, carry):
        at = pl.multiple_of(i * step, step)
        rows = pl.ds(pl.multiple_of(start + at, 16), step)
        target[rows, :] = (target[rows, :].astype(f32) + source[pl.ds(at, step), :].astype(f32)).astype(bf16)
        return carry

    lax.fori_loop(0, size // step, body, 0)


def rest_kernel(names, *refs):
    r = Named(REST_OPERANDS + REST_RESULTS, refs)
    s = Named(names, refs[len(REST_OPERANDS) + len(REST_RESULTS) :])
    dp, line, core, x, y, flips = places()
    units, width = s.down_wg.shape[1:]
    part = s.out_wg.shape[1]
    items = weight_items(units, part, width)
    item_count = len(items)
    grads = (s.gate_wg, s.up_wg, s.down_wg, s.out_wg, s.qkv_wg)
    sums = (r.gate_sum, r.up_sum, r.down_sum, r.out_sum, r.qkv_sum)
    begin_unit, unit_block, end_unit, out_grad = unit_parts(s, r)
    tasks, rows_grad, weights_grad = attention_back_tasks(s, r)
    groups = start_all(s, r)
    greet(dp, line, flips)

    def item_of(i, block):
        if i < item_count - 1:
            return items[i]
        if i == item_count - 1:
            return Item(3, 0, part, block > 1, True)
        turn = i - item_count
        return Item(4, turn * part, part, turn % 2 == 0, True)

    def lead(i, block):
        return block if i < item_count else None

    def number(i, block):
        return i * groups + block if i < item_count else (item_count - 1) * groups + i - 1

    def at_block(ref, i, block):
        return ref.at[block] if i < item_count else ref

    def arrival(stage, i, block):
        return at_block(getattr(s, stage + str(i)), i, block)

    def held(i, block):
        item = item_of(i, block)
        if item.by_columns:
            return arrival("half", i, block), 0, item.rows
        return grads[item.place].at[block], item.base + core * (item.rows // 2), item.rows // 2

    def load_copy(i, block):
        item = item_of(i, block)
        window = item.window(grads[item.place], lead(i, block), 1, core, 0, 0)
        return pltpu.make_async_copy(window, arrival("half", i, block), s.load_sem.at[number(i, block)])

    def core_copy(i, block):
        item, n = item_of(i, block), number(i, block)
        window = item.window(grads[item.place], lead(i, block), 1, 1 - core, 0, 0)
        return remote(window, arrival("core", i, block), s.core_send.at[n], s.core_recv.at[n], (flips[0], line))

    def begin(i, block):
        core_copy(i, block).start()
        if item_of(i, block).by_columns:
            load_copy(i, block).start()

    def pair_copy(i, block, stage):
        ref, base, half = held(i, block)
        item, n = item_of(i, block), number(i, block)
        first, second = item.bits(x, y)
        if stage == 0:
            size, start, target = half // 2, (1 - first) * (half // 2), arrival("first", i, block)
        else:
            size = half // 4
            start, target = first * (half // 2) + (1 - second) * (half // 4), arrival("second", i, block)
        window = ref.at[pl.ds(pl.multiple_of(base + start, 16), size), :]
        partner = item.partner(1 + stage, flips)
        return remote(window, target, s.pair_send.at[stage, n], s.pair_recv.at[stage, n], (partner, line))

    def eighth(i, block):
        ref, base, half = held(i, block)
        first, second = item_of(i, block).bits(x, y)
        start = pl.multiple_of(base + first * (half // 2) + second * (half // 4), 16)
        return ref, start, half // 4

    def mine(i, block):
        ref, start, size = eighth(i, block)
        return ref.at[pl.ds(start, size), :]

    def line_copy(i, block, sender):
        target = getattr(s, "line" + str(i)).at[sender]
        return remote(
            mine(i, block), target, s.line_send.at[i, block], s.line_recv.at[i, sender], (dp, block)
        )

    def spread_copy(i, block, stage):
        item, n = item_of(i, block), number(i, block)
        first, second = item.bits(x, y)
        window = item.window(sums[item.place], None, 3 - stage, core, first, second)
        src = mine(i, block) if stage == 0 else window
        return remote(
            src, window, s.spread_send.at[stage, n], s.spread_recv.at[stage, n],
            (item.partner(2 - stage, flips), line),
        )

    def keep_copy(i, block):
        item = item_of(i, block)
        first, second = item.bits(x, y)
        window = item.window(sums[item.place], None, 3, core, first, second)
        return pltpu.make_async_copy(mine(i, block), window, s.load_sem.at[number(i, block)])

    def step_core(i, block, send=True):
        if item_of(i, block).by_columns:
            load_copy(i, block).wait()
        core_copy(i, block).wait_recv()
        ref, base, half = held(i, block)
        add_rows(ref, base, half, arrival("core", i, block))
        if send:
            pair_copy(i, block, 0).start()

    def step_first(i, block):
        pair_copy(i, block, 0).wait_recv()
        ref, base, half = held(i, block)
        first, _ = item_of(i, block).bits(x, y)
        add_rows(ref, base + first * (half // 2), half // 2, arrival("first", i, block))
        pair_copy(i, block, 1).start()

    def step_second(i, block):
        pair_copy(i, block, 1).wait_recv()
        ref, start, size = eighth(i, block)
        add_rows(ref, start, size, arrival("second", i, block))
        if i < item_count:
            pl.when(line != block)(lambda: line_copy(i, block, line).start())
        else:
            spread_copy(i, block, 0).start()
            keep_copy(i, block).start()

    def step_last(i, block):
        @pl.when(line == block)
        def _():
            ref, start, size = eighth(i, block)
            others = [o for o in range(groups) if o != block]
            for o in others:
                line_copy(i, block, o).wait_recv()
            arrived = getattr(s, "line" + str(i))
            total = ref[pl.ds(start, size), :].astype(f32)
            for o in others:
                total = total + arrived[o].astype(f32)
            ref[pl.ds(start, size), :] = total.astype(bf16)
            spread_copy(i, block, 0).start()
            keep_copy(i, block).start()

    def step_spread(i, block, stage):
        def act():
            if stage == 1:
                keep_copy(i, block).wait()
            spread_copy(i, block, stage - 1).wait_recv()
            if stage < 3:
                spread_copy(i, block, stage).start()

        if i < item_count:
            pl.when(line == block)(act)
        else:
            act()

    def swap_copy(i, sender_is_me):
        other = lax.rem(line + i, 4)
        if sender_is_me:
            return remote(
                s.grad_here.at[other], s.mixed_grad.at[line], s.swap_send.at[i - 1], s.swap_recv.at[3 - i], (dp, other)
            )
        return remote(
            s.grad_here.at[other], s.mixed_grad.at[other], s.swap_send.at[i - 1], s.swap_recv.at[i - 1], (dp, other)
        )

    def back_copy(block, at, right):
        src, send = s.back_acc.at[block], s.back_send.at[block]
        if right:
            return remote(src, s.back_left.at[block], send, s.back_left_recv.at[block], (dp, at + 1))
        return remote(src, s.back_right.at[block], send, s.back_right_recv.at[block], (dp, at - 1))

    def back_hop(hop, distance):
        @pl.when(line == hop)
        def _():
            block = hop + distance
            if block <= groups - 1:
                if hop > 0:
                    back_copy(block, hop, True).wait_recv()
                    add_rows(s.back_acc.at[block], 0, s.back_acc.shape[1], s.back_left.at[block])
                back_copy(block, hop, True).start()

        at = groups - 1 - hop

        @pl.when(line == at)
        def _():
            block = at - distance
            if block >= 0:
                if hop > 0:
                    back_copy(block, at, False).wait_recv()
                    add_rows(s.back_acc.at[block], 0, s.back_acc.shape[1], s.back_right.at[block])
                back_copy(block, at, False).start()

    def collect_rows():
        for block in range(groups):
            @pl.when(line == block)
            def _(block=block):
                total = s.back_acc[block].astype(f32)
                if block > 0:
                    back_copy(block, block, True).wait_recv()
                    total = total + s.back_left[block].astype(f32)
                if block < groups - 1:
                    back_copy(block, block, False).wait_recv()
                    total = total + s.back_right[block].astype(f32)
                input_grad_rows(s, r, total)

    def small_copy(stage):
        partner = (flips[stage], line) if stage < 3 else (dp, line + 1 - 2 * lax.rem(line, 2))
        if stage == 4:
            partner = (dp, lax.rem(line + 2, 4))
        return remote(s.small_mine, s.small_got.at[stage], s.small_send.at[stage], s.small_recv.at[stage], partner)

    def small_step(stage):
        if stage > 0:
            small_copy(stage - 1).wait()
            rows = lax.broadcasted_iota(jnp.int32, s.small_mine.shape, 0)
            got = s.small_got[stage - 1]
            if stage > 3:
                got = jnp.where(rows < 8, got, 0.0)
            s.small_mine[...] = s.small_mine[...] + got
        else:
            s.small_mine[0:1, :] = s.gain[...] / r.gain1[...].astype(f32)
        if stage < 5:
            small_copy(stage).start()
        else:
            r.small_sum[...] = s.small_mine[...]

    outer, inner = (0, groups - 1), tuple(range(1, groups - 1))
    teams = [[(i, block) for i in (0, 1)] for block in outer + inner]
    teams += [[(i, block) for block in pair for i in (2, 3)] for pair in (outer, inner)]
    teams.append([(item_count - 1, block) for block in range(groups)])
    teams.append([(item_count + turn, 0) for turn in range(3)])
    stage_acts = {
        "core": step_core,
        "first": step_first,
        "second": step_second,
        "last": step_last,
        "spread1": lambda i, block: step_spread(i, block, 1),
        "spread2": lambda i, block: step_spread(i, block, 2),
        "spread3": lambda i, block: step_spread(i, block, 3),
    }
    done = []

    def tend(moment):
        for name, team in WHEN.get(moment, ()):
            done.append((name, team))
            if name == "small":
                small_step(team)
            elif name == "rows":
                collect_rows()
            elif name == "hop":
                back_hop(*team)
            else:
                for i, block in teams[team]:
                    stage_acts[name](i, block)

    for copy in load_small(s, r):
        copy.wait()
    begin_unit()

    order = outer + inner
    for turn, block in enumerate(order):
        for copy in load_weights(s, r, block, turn % 2):
            copy.wait()
        if turn + 1 < groups:
            for copy in load_weights(s, r, order[turn + 1], (turn + 1) % 2):
                copy.start()
        unit_block(block, turn % 2)
        for i in range(item_count - 1):
            begin(i, block)
        tend("unit%d" % turn)
    end_unit()
    for i in (2, 1, 3):
        swap_copy(i, True).start()
    swap_keep = pltpu.make_async_copy(s.grad_here.at[line], s.mixed_grad.at[line], s.swap_keep)
    swap_keep.start()
    out_grad()
    for block in range(groups):
        begin(item_count - 1, block)
    tend("swap")
    for i in (1, 2, 3):
        swap_copy(i, False).wait_recv()
        swap_copy(i, True).wait_send()
    swap_keep.wait()
    for turn, task in enumerate(tasks):
        task()
        tend(turn)
    for block in range(groups):
        rows_grad(block)
    for distance in (3, 2, 1):
        back_hop(0, distance)
    for turn in range(3):
        weights_grad(turn)
        begin(item_count + turn, 0)
    small_step(0)

    for turn in range(len(WHEN)):
        tend("end%d" % turn)
    assert len(done) == len(set(done)) == 7 * 7 + 6 + 5 + 4
    for block in range(groups):
        pl.when(line < block)(lambda block=block: back_copy(block, line, True).wait_send())
        pl.when(line > block)(lambda block=block: back_copy(block, line, False).wait_send())
    for i, block in sum(teams, []):
        core_copy(i, block).wait_send()
        pair_copy(i, block, 0).wait_send()
        pair_copy(i, block, 1).wait_send()

        def sent(i=i, block=block):
            for stage in range(3):
                spread_copy(i, block, stage).wait_send()

        if i < item_count:
            pl.when(line == block)(sent)
            pl.when(line != block)(lambda i=i, block=block: line_copy(i, block, line).wait_send())
        else:
            sent()


WHEN = {
    "unit1": [("core", 0), ("core", 1)],
    "unit3": [("first", 0), ("core", 2)],
    "swap": [("first", 1), ("core", 3), ("second", 0)],
    0: [("first", 2), ("core", 4), ("second", 1)],
    3: [("first", 3), ("core", 5), ("second", 2)],
    5: [("last", 0)],
    7: [("first", 4), ("core", 6), ("second", 3), ("spread1", 0)],
    9: [("last", 1)],
    11: [("first", 5), ("second", 4), ("spread2", 0), ("spread1", 1)],
    13: [("last", 2)],
    14: [("first", 6), ("second", 5), ("spread2", 1), ("spread3", 0)],
    "end0": [("core", 7), ("second", 6), ("last", 3), ("spread1", 2), ("spread3", 1)],
    "end1": [("small", 1), ("first", 7), ("hop", (1, 2)), ("last", 4), ("spread1", 3), ("spread2", 2)],
    "end2": [("small", 2), ("second", 7), ("hop", (1, 1)), ("last", 5), ("last", 6), ("spread1", 4), ("spread2", 3)],
    "end3": [("small", 3), ("hop", (2, 1)), ("spread1", 7), ("spread1", 5), ("spread1", 6), ("spread3", 2)],
    "end4": [("small", 4), ("spread2", 7), ("spread2", 4), ("spread2", 5), ("spread2", 6), ("spread3", 3)],
    "end5": [("small", 5), ("spread3", 7), ("spread3", 4), ("spread3", 5), ("spread3", 6), ("rows", 0)],
}

def common_scratch(groups, rows, heads, length, width, units, part):
    dma = pltpu.SemaphoreType.DMA
    return dict(
        residual=pltpu.VMEM((rows, width), f32),
        normed2=pltpu.VMEM((rows, width), bf16),
        ahead=pltpu.VMEM((rows, width), f32),
        behind=pltpu.VMEM((rows, width), f32),
        out_w=pltpu.VMEM((groups, part, width), bf16),
        gate_w=pltpu.VMEM((2, width, units), bf16),
        up_w=pltpu.VMEM((2, width, units), bf16),
        down_w=pltpu.VMEM((2, units, width), bf16),
        gate_wg=pltpu.VMEM((groups, width, units), bf16),
        up_wg=pltpu.VMEM((groups, width, units), bf16),
        down_wg=pltpu.VMEM((groups, units, width), bf16),
        out_wg=pltpu.VMEM((groups, part, width), bf16),
        qkv_wg=pltpu.VMEM((3 * part, width), bf16),
        grad_here=pltpu.VMEM((groups, rows, part), bf16),
        mixed_grad=pltpu.VMEM((groups, rows, part), bf16),
        back_acc=pltpu.VMEM((groups, rows, width), bf16),
        small_mine=pltpu.VMEM((16, width), f32),
        gain=pltpu.VMEM((1, width), f32),
        probs=pltpu.VMEM((2, BLK, length), bf16),
        w=pltpu.VMEM((768, width), bf16),
        dot=pltpu.VMEM((heads, length, 128), bf16),
        dott=pltpu.VMEM((heads, 128, length), bf16),
        grad=pltpu.VMEM((length, 384), f32),
        joined=pltpu.VMEM((length, 768), bf16),
        near=pltpu.VMEM((BLK, 3 * BLK), f32),
        bucket=pltpu.VMEM((BLK, 3 * BLK), jnp.int32),
        table=pltpu.VMEM((BUCKETS, 128), f32),
        far=pltpu.VMEM((2, BLK, 128), f32),
        dkt=pltpu.VMEM((128, length), f32),
        dvt=pltpu.VMEM((128, length), f32),
        weight_sem=dma((3, 2)), first_sem=dma((4,)), probs_sem=dma((2,)),
    )


def result_shapes(rows, width, units, part):
    return (
        jax.ShapeDtypeStruct((rows, width), bf16),
        jax.ShapeDtypeStruct((rows, width), bf16),
        jax.ShapeDtypeStruct((16, width), f32),
        jax.ShapeDtypeStruct((part, width), bf16),
        jax.ShapeDtypeStruct((width, units), bf16),
        jax.ShapeDtypeStruct((width, units), bf16),
        jax.ShapeDtypeStruct((units, width), bf16),
        jax.ShapeDtypeStruct((3 * part, width), bf16),
    )


def rest_all(gate_all, up_all, down_all, out_all, probs, wq, wk, wv, mixed_here, hidden_in, cot, gain1, gain2,
             mixed, inverse, qt, k, vt, normed):
    groups, rows, part = mixed_here.shape
    heads, length = k.shape[0], k.shape[1]
    width = normed.shape[1]
    units = down_all.shape[1]
    items = weight_items(units, part, width)
    n = 3 + groups * len(items)
    dma = pltpu.SemaphoreType.DMA
    scratch = common_scratch(groups, rows, heads, length, width, units, part)
    for stage, divide in (("half", 1), ("core", 1), ("first", 2), ("second", 4), ("line", 4)):
        for i, item in enumerate(items):
            cols = (units, units, width, width)[item.place]
            shape = (item.rows, cols // 2) if item.by_columns else (item.rows // 2, cols)
            if stage != "half" or item.by_columns:
                scratch[stage + str(i)] = pltpu.VMEM((groups, shape[0] // divide, shape[1]), bf16)
        for turn in range(3):
            if stage != "line":
                scratch[stage + str(len(items) + turn)] = pltpu.VMEM((part // divide, width // 2), bf16)
    scratch.update(
        small_got=pltpu.VMEM((5, 16, width), f32),
        back_left=pltpu.VMEM((groups, rows, width), bf16),
        back_right=pltpu.VMEM((groups, rows, width), bf16),
        load_sem=dma((n,)), core_send=dma((n,)), core_recv=dma((n,)),
        pair_send=dma((2, n)), pair_recv=dma((2, n)),
        line_send=dma((len(items), groups)), line_recv=dma((len(items), groups)),
        spread_send=dma((3, n)), spread_recv=dma((3, n)),
        back_send=dma((groups,)), back_left_recv=dma((groups,)), back_right_recv=dma((groups,)),
        small_send=dma((5,)), small_recv=dma((5,)),
        swap_send=dma((3,)), swap_recv=dma((3,)), swap_keep=dma,
    )
    anywhere = pl.BlockSpec(memory_space=pl.ANY)
    inside = pl.BlockSpec(memory_space=pltpu.VMEM)
    return pl.pallas_call(
        functools.partial(rest_kernel, tuple(scratch)),
        name="rest_all",
        out_shape=result_shapes(rows, width, units, part),
        in_specs=[anywhere] * 8 + [inside] * 11,
        out_specs=(inside,) * 3 + (anywhere,) * 5,
        scratch_shapes=list(scratch.values()),
        compiler_params=pltpu.CompilerParams(
            collective_id=3, has_side_effects=True, vmem_limit_bytes=62 << 20
        ),
    )(gate_all, up_all, down_all, out_all, probs, wq, wk, wv, mixed_here, hidden_in, cot, gain1, gain2,
      mixed, inverse, qt, k, vt, normed)


UNIT_RESULTS = ("output", "residual_grad", "grads", "gain2_grad", "out_out", "gate_out", "up_out", "down_out")


def unit_local_kernel(names, *refs):
    operands = ("gate_all", "up_all", "down_all", "out_all", "mixed_here", "hidden_in", "cot", "gain2")
    r = Named(operands + UNIT_RESULTS, refs)
    s = Named(names, refs[len(operands) + len(UNIT_RESULTS) :])
    s.out_wg, s.gate_wg, s.up_wg, s.down_wg = r.out_out, r.gate_out, r.up_out, r.down_out
    s.behind, s.grad_here = r.residual_grad, r.grads
    begin, block, end, out_grad = unit_parts(s, r)
    groups = s.out_w.shape[0]
    first = [pltpu.make_async_copy(r.out_all, s.out_w, s.first_sem.at[0])] + load_weights(s, r, 0, 0)
    for copy in first:
        copy.start()
    first[0].wait()
    begin()

    def body(b, carry):
        slot = lax.rem(b, 2)
        for copy in load_weights(s, r, b, slot):
            copy.wait()

        @pl.when(b + 1 < groups)
        def _():
            for copy in load_weights(s, r, b + 1, 1 - slot):
                copy.start()

        block(b, slot)
        return carry

    lax.fori_loop(0, groups, body, 0)
    end()
    out_grad()
    r.gain2_grad[...] = s.small_mine[1:2, :]


def back_local_kernel(names, *refs):
    operands = ("probs_all", "mixed", "inverse", "qt", "k", "vt", "normed", "wq", "wk", "wv", "gain1", "mixed_grad")
    results = ("back_out", "qkv_out", "small_out")
    r = Named(operands + results, refs)
    s = Named(names, refs[len(operands) + len(results) :])
    s.mixed_grad, s.qkv_wg, s.small_mine, s.back_acc = r.mixed_grad, r.qkv_out, r.small_out, r.back_out
    tasks, rows_grad, weights_grad = attention_back_tasks(s, r)
    s.small_mine[...] = jnp.zeros_like(s.small_mine)
    s.gain[...] = jnp.zeros_like(s.gain)
    s.w[...] = jnp.zeros_like(s.w)
    for place, ref in enumerate((r.wq, r.wk, r.wv)):
        s.w[256 * place : 256 * place + ref.shape[0], :] = ref[...]
    for task in tasks:
        task()
    for block in range(r.back_out.shape[0]):
        rows_grad(block)
    for turn in range(3):
        weights_grad(turn)
    s.small_mine[0:1, :] = s.gain[...] / r.gain1[...].astype(f32)


def rest_by_axis(gate_all, up_all, down_all, out_all, probs, wq, wk, wv, mixed_here, hidden_in, cot, gain1, gain2,
                 mixed, inverse, qt, k, vt, normed):
    groups, rows, part = mixed_here.shape
    heads, length = k.shape[0], k.shape[1]
    width = normed.shape[1]
    units = down_all.shape[1]
    anywhere = pl.BlockSpec(memory_space=pl.ANY)
    inside = pl.BlockSpec(memory_space=pltpu.VMEM)
    every = common_scratch(groups, rows, heads, length, width, units, part)
    pick = lambda names: {name: every[name] for name in names}
    shape = jax.ShapeDtypeStruct
    scratch = pick(
        ("residual", "normed2", "ahead", "out_w", "gate_w", "up_w", "down_w", "small_mine", "weight_sem", "first_sem")
    )
    output, residual_grad, grads, gain2_grad, out_wg, gate_wg, up_wg, down_wg = pl.pallas_call(
        functools.partial(unit_local_kernel, tuple(scratch)),
        name="unit_local",
        out_shape=(
            shape((rows, width), bf16), shape((rows, width), f32), shape((groups, rows, part), bf16),
            shape((1, width), f32), shape((groups, part, width), bf16), shape((groups, width, units), bf16),
            shape((groups, width, units), bf16), shape((groups, units, width), bf16),
        ),
        in_specs=[anywhere] * 4 + [inside] * 4,
        out_specs=(inside,) * 8,
        scratch_shapes=list(scratch.values()),
        compiler_params=pltpu.CompilerParams(vmem_limit_bytes=56 << 20),
    )(gate_all, up_all, down_all, out_all, mixed_here, hidden_in, cot, gain2)
    mixed_grad = lax.all_to_all(grads, "tensor", 0, 0)
    scratch = pick(
        ("gain", "probs", "w", "dot", "dott", "grad", "joined", "near", "bucket", "table", "far", "dkt", "dvt",
         "probs_sem")
    )
    back, qkv_wg, small = pl.pallas_call(
        functools.partial(back_local_kernel, tuple(scratch)),
        name="back_local",
        out_shape=(
            shape((groups, rows, width), bf16), shape((3 * part, width), bf16), shape((16, width), f32),
        ),
        in_specs=[anywhere] + [inside] * 11,
        out_specs=(inside,) * 3,
        scratch_shapes=list(scratch.values()),
        compiler_params=pltpu.CompilerParams(vmem_limit_bytes=56 << 20),
    )(probs, mixed, inverse, qt, k, vt, normed, wq, wk, wv, gain1, mixed_grad)
    back_sum = lax.psum_scatter(back, "tensor", scatter_dimension=0).astype(f32)
    parts = tuple(lax.psum_scatter(wg, "tensor", scatter_dimension=0) for wg in (out_wg, gate_wg, up_wg, down_wg))
    sums = lax.psum(parts + (qkv_wg,), "dp")
    small = small.at[1].set(gain2_grad[0])
    small_sum = lax.psum(small, "dp")
    gains = lax.psum(small_sum[:8], "tensor")
    input_rows = hidden_in.astype(f32)
    r1 = mean_square_scale(input_rows)
    g1 = back_sum * gain1.astype(f32)
    centre = jnp.mean(g1 * input_rows, axis=-1, keepdims=True)
    input_grad = (residual_grad + r1 * g1 - (r1 * r1 * r1 * centre) * input_rows).astype(bf16)
    return (output, input_grad, jnp.concatenate((gains, small_sum[8:]))) + tuple(sums)


def gather_by_axis(normed, gate, up, down, out):
    return tuple(lax.all_gather(part, "tensor", axis=0) for part in (normed, gate, up, down, out))


def swap_by_axis(blocks):
    return lax.all_to_all(blocks, "tensor", 0, 0)


def shards(
    by_kernel,
    hidden_in, segment_ids, norm1_gain, query_weight, key_weight, value_weight, out_weight,
    bias_table, norm2_gain, gate_weight, up_weight, down_weight, out_cotangent,
):
    gather_parts = gather if by_kernel else gather_by_axis
    swap_parts = swap if by_kernel else swap_by_axis
    rest_parts = rest_all if by_kernel else rest_by_axis
    rows_here, width = hidden_in.shape
    length = segment_ids.shape[1]
    assert segment_ids.shape[0] == 1
    groups = length // rows_here
    heads = bias_table.shape[1]
    input_rows = hidden_in.astype(f32)
    normed_here = (input_rows * mean_square_scale(input_rows) * norm1_gain.astype(f32)).astype(bf16)
    normed, gate_w, up_w, down_w, out_w = gather_parts(
        normed_here, gate_weight, up_weight, down_weight, out_weight
    )
    normed = normed.reshape(length, width)
    query_weight, key_weight, value_weight = query_weight.T, key_weight.T, value_weight.T
    mixed, probs, qt, k, vt, inverse = attend(
        normed, query_weight, key_weight, value_weight, segment_ids, bias_table
    )
    mixed_here = swap_parts(mixed.reshape(groups, rows_here, -1))
    output, input_grad, small_sum, out_sum, gate_sum, up_sum, down_sum, qkv_sum = rest_parts(
        gate_w, up_w, down_w, out_w, probs, query_weight, key_weight, value_weight, mixed_here, hidden_in,
        out_cotangent, norm1_gain[None], norm2_gain[None], mixed, inverse, qt, k, vt, normed,
    )
    qkv = qkv_sum.astype(f32)
    inner = heads * HEAD_DIM
    return (
        output, input_grad, small_sum[0], qkv[:inner].T, qkv[inner : 2 * inner].T, qkv[2 * inner :].T,
        out_sum.astype(f32), small_sum[8 : 8 + heads, :BUCKETS].T,
        small_sum[1], gate_sum.astype(f32), up_sum.astype(f32), down_sum.astype(f32),
    )


def solution(mesh):
    in_specs = (
        P(("dp", "tensor"), None), P("dp", None), P(),
        P(None, "tensor"), P(None, "tensor"), P(None, "tensor"), P("tensor", None),
        P(None, "tensor"), P(), P(None, "tensor"), P(None, "tensor"), P("tensor", None),
        P(("dp", "tensor"), None),
    )
    out_specs = (
        P(("dp", "tensor"), None), P(("dp", "tensor"), None), P(),
        P(None, "tensor"), P(None, "tensor"), P(None, "tensor"), P("tensor", None),
        P(None, "tensor"), P(), P(None, "tensor"), P(None, "tensor"), P("tensor", None),
    )
    by_kernel = mesh.shape["dp"] == 8 and mesh.shape["tensor"] == 4
    return jax.shard_map(
        functools.partial(shards, by_kernel), mesh=mesh, in_specs=in_specs, out_specs=out_specs, check_vma=False
    )
```

```python
import functools

import jax
import jax.numpy as jnp
from jax import lax
from jax.experimental import pallas as pl
from jax.experimental.pallas import tpu as pltpu
from jax.sharding import PartitionSpec as P

HEAD_DIM = 64
BUCKETS = 32
far_marks = (12, 16, 23, 32, 46, 64, 91)
norm_eps = 1e-06
far_score = 2.0**30
BLK = 256
f32 = jnp.float32
bf16 = jnp.bfloat16


def bucket_of(offset):
    magnitude = jnp.abs(offset)
    within = jnp.minimum(magnitude, 8)
    for far_mark in far_marks:
        within = within + (magnitude >= far_mark).astype(jnp.int32)
    return within + jnp.where(offset > 0, 16, 0).astype(jnp.int32)


def key_range(block, count):
    return range(max(0, block - 2), min(count, block + 3))


def contract(lhs, rhs, left, right):
    return lax.dot_general(
        lhs, rhs, (((left,), (right,)), ((), ())), preferred_element_type=f32
    )


def attend_kernel(
    by_kernel, normed_ref, wq_ref, wk_ref, wv_ref, seg_ref, table_ref,
    mixed_ref, probs_ref, qt_ref, k_ref, vt_ref, inv_ref, here_ref,
    w_s, kt_s, bias_s, score_s, first_s, q_s, v_s, parts_s, send_sem, recv_sem, keep_sem,
):
    head = pl.program_id(0)
    length = normed_ref.shape[0]
    count = length // BLK
    lane = lax.broadcasted_iota(jnp.int32, (BLK, 128), 1)
    low_half = lane < HEAD_DIM

    if by_kernel:
        dp, line = lax.axis_index("dp"), lax.axis_index("tensor")
        others = [lax.rem(line + i, 4) for i in (1, 2, 3)]

        @pl.when(head == 0)
        def _():
            barrier = pltpu.get_barrier_semaphore()
            for other in others:
                pl.semaphore_signal(barrier, inc=1, device_id=(dp, other), device_id_type=MESH_IDS)
            pl.semaphore_wait(barrier, 3)

        def part_copy(half, i, sender_is_me):
            place = line if sender_is_me else others[i]
            return pltpu.make_async_remote_copy(
                src_ref=parts_s.at[half, others[i]], dst_ref=here_ref.at[half, place],
                send_sem=send_sem.at[half, i], recv_sem=recv_sem.at[half, 2 - i if sender_is_me else i],
                device_id=(dp, others[i]), device_id_type=MESH_IDS,
            )

        def own_copy(half):
            return pltpu.make_async_copy(parts_s.at[half, line], here_ref.at[half, line], keep_sem.at[half])

        def send_part(half):
            for i in (1, 0, 2):
                part_copy(half, i, True).start()
            own_copy(half).start()

    @pl.when(head == 0)
    def _():
        w_s[...] = jnp.zeros_like(w_s)
        for place, ref in enumerate((wq_ref, wk_ref, wv_ref)):
            w_s[256 * place : 256 * place + 192, :] = ref[...]
        row8 = lax.broadcasted_iota(jnp.int32, (8, 128), 0)
        lane8 = lax.broadcasted_iota(jnp.int32, (8, 128), 1)
        spread = jnp.where((lane8 % HEAD_DIM) == row8, 1.0, 0.0).astype(bf16)

        def project(step, carry):
            rows = pl.ds(pl.multiple_of(step * BLK, BLK), BLK)
            seg_row = seg_ref[:, rows]
            kinds = lax.broadcasted_iota(jnp.int32, (8, BLK), 0)
            hot = jnp.where(
                jnp.broadcast_to(seg_row, (8, BLK)) == kinds, 1.0, 0.0
            ).astype(bf16)
            same = contract(hot, spread, 0, 0)
            in_aug = (lane % HEAD_DIM) < 8
            aug_q = jnp.where(in_aug, same, 0.0)
            aug_k = jnp.where(in_aug, (same - 1.0) * far_score, 0.0)
            rows_in = normed_ref[rows, :]
            q = contract(rows_in, w_s[0:256, :], 1, 1)
            k = contract(rows_in, w_s[256:512, :], 1, 1)
            v = contract(rows_in, w_s[512:768, :], 1, 1)
            scale = HEAD_DIM ** (-0.5)
            for h, (cols, mine) in enumerate(
                ((slice(0, 128), low_half), (slice(0, 128), ~low_half), (slice(128, 256), low_half))
            ):
                q_h = jnp.where(mine, q[:, cols] * scale, aug_q).astype(bf16)
                q_s[h, rows, :] = q_h
                qt_ref[h, :, rows] = q_h.T
                k_h = jnp.where(mine, k[:, cols], aug_k).astype(bf16)
                k_ref[h, rows, :] = k_h
                v_h = jnp.where(mine, v[:, cols], 1.0).astype(bf16)
                v_s[h, rows, :] = v_h
                vt_ref[h, :, rows] = v_h.T
                kt_s[h, :, rows] = k_h.T
            return carry

        lax.fori_loop(0, count, project, 0)

    offset = lax.broadcasted_iota(jnp.int32, (BUCKETS, length), 1)
    offset = jnp.where(offset >= length // 2, offset - length, offset)
    hot_bucket = jnp.where(
        bucket_of(offset) == lax.broadcasted_iota(jnp.int32, (BUCKETS, length), 0), 1.0, 0.0
    ).astype(bf16)
    by_offset = contract(table_ref[head], hot_bucket, 1, 0)[0:1]
    spread_rows = jnp.broadcast_to(by_offset, (BLK, length))
    bias_s[...] = pltpu.roll(spread_rows, 0, 1, stride=1, stride_axis=0)

    for block in range(count):
        rows = slice(block * BLK, (block + 1) * BLK)
        q_h = q_s[head, rows, :]
        top = None
        for key in key_range(block, count):
            part = jnp.dot(
                q_h, kt_s[head, :, key * BLK : (key + 1) * BLK], preferred_element_type=f32
            )
            delta = key - block
            at = (delta * BLK) % length
            part = part + bias_s[:, at : at + BLK]
            score_s[:, key * BLK : (key + 1) * BLK] = part
            top = part if top is None else jnp.maximum(top, part)
        top = jnp.max(jnp.maximum(top[:, :128], top[:, 128:]), axis=1, keepdims=True)
        total = jnp.zeros((BLK, 128), f32)
        for key in key_range(block, count):
            cols = slice(key * BLK, (key + 1) * BLK)
            part = jnp.exp(score_s[:, cols] - top).astype(bf16)
            probs_ref[0, rows, cols] = part
            total = total + jnp.dot(part, v_s[head, cols, :], preferred_element_type=f32)
        sums = pltpu.roll(total, HEAD_DIM, 1)
        inverse = 1.0 / sums
        out = total * inverse

        @pl.when(head == 0)
        def _():
            first_s[rows, 0:128] = out
            first_s[rows, 128:256] = inverse

        @pl.when(head == 1)
        def _():
            pair = jnp.where(low_half, first_s[rows, 0:128], out).astype(bf16)
            mixed_ref[rows, 0:128] = pair
            parts_s[0, block] = pair
            inv_ref[rows, 0:128] = jnp.where(low_half, first_s[rows, 128:256], inverse)

        @pl.when(head == 2)
        def _():
            mixed_ref[rows, 128:192] = out[:, 0:HEAD_DIM].astype(bf16)
            inv_ref[rows, 128:256] = inverse
            parts_s[1, block] = out.astype(bf16)

    if by_kernel:
        @pl.when(head == 1)
        def _():
            send_part(0)

        @pl.when(head == 2)
        def _():
            send_part(1)
            for half in range(2):
                own_copy(half).wait()
                for i in range(3):
                    part_copy(half, i, True).wait_send()
                    part_copy(half, i, False).wait_recv()
    else:
        @pl.when(head == 2)
        def _():
            for half in range(2):
                keep = pltpu.make_async_copy(parts_s.at[half], here_ref.at[half], keep_sem.at[half])
                keep.start()
                keep.wait()


MESH_IDS = pl.DeviceIdType.MESH


def attend(by_kernel, normed, wq, wk, wv, segments, bias_table):
    length, width = normed.shape
    heads = bias_table.shape[1]
    inner = heads * HEAD_DIM
    table = jnp.broadcast_to(bias_table.T[:, None, :], (heads, 8, BUCKETS))
    whole = lambda *dims: pl.BlockSpec(dims, lambda h: (0,) * len(dims))
    return pl.pallas_call(
        functools.partial(attend_kernel, by_kernel),
        grid=(heads,),
        name="attend",
        out_shape=(
            jax.ShapeDtypeStruct((length, inner), bf16),
            jax.ShapeDtypeStruct((heads, length, length), bf16),
            jax.ShapeDtypeStruct((heads, 128, length), bf16),
            jax.ShapeDtypeStruct((heads, length, 128), bf16),
            jax.ShapeDtypeStruct((heads, 128, length), bf16),
            jax.ShapeDtypeStruct((length, 256), f32),
            jax.ShapeDtypeStruct((2, length // BLK, BLK, 128), bf16),
        ),
        in_specs=[
            whole(length, width),
            whole(inner, width),
            whole(inner, width),
            whole(inner, width),
            whole(1, length),
            whole(heads, 8, BUCKETS),
        ],
        out_specs=(
            whole(length, inner),
            pl.BlockSpec((1, length, length), lambda h: (h, 0, 0)),
            whole(heads, 128, length),
            whole(heads, length, 128),
            whole(heads, 128, length),
            whole(length, 256),
            pl.BlockSpec(memory_space=pl.ANY),
        ),
        scratch_shapes=[
            pltpu.VMEM((768, width), bf16),
            pltpu.VMEM((heads, 128, length), bf16),
            pltpu.VMEM((BLK, length), f32),
            pltpu.VMEM((BLK, length), f32),
            pltpu.VMEM((length, 256), f32),
            pltpu.VMEM((heads, length, 128), bf16),
            pltpu.VMEM((heads, length, 128), bf16),
            pltpu.VMEM((2, length // BLK, BLK, 128), bf16),
            pltpu.SemaphoreType.DMA((2, 3)),
            pltpu.SemaphoreType.DMA((2, 3)),
            pltpu.SemaphoreType.DMA((2,)),
        ],
        compiler_params=pltpu.CompilerParams(
            dimension_semantics=("arbitrary",), vmem_limit_bytes=60 << 20,
            **(dict(collective_id=2, has_side_effects=True) if by_kernel else {}),
        ),
        cost_estimate=pl.CostEstimate(flops=3 << 30, bytes_accessed=12 << 20, transcendentals=3 << 20),
    )(normed, wq, wk, wv, segments, table)


def mean_square_scale(rows):
    return lax.rsqrt(jnp.mean(rows * rows, axis=-1, keepdims=True) + norm_eps)


def places():
    dp = lax.axis_index("dp")
    line = lax.axis_index("tensor")
    core = lax.rem(dp, 2)
    x = lax.rem(dp // 2, 2)
    y = dp // 4
    flips = (dp + 1 - 2 * core, dp + 2 - 4 * x, dp + 4 - 8 * y)
    return dp, line, core, x, y, flips


def nearest(line, k):
    upper = line // 2
    inner = line * (1 - upper) + (3 - line) * upper
    block = k + 1 - inner if k == 0 else k + 1
    block = block * (1 - upper) + (3 - block) * upper
    way = (1 if k == 0 else -1) * (1 - 2 * upper)
    return block, way


class Item:
    def __init__(self, place, base, rows, flipped, by_columns=False):
        self.place, self.base, self.rows = place, base, rows
        self.flipped, self.by_columns = flipped, by_columns

    def bits(self, x, y):
        return (y, x) if self.flipped else (x, y)

    def partner(self, level, flips):
        if level == 0:
            return flips[0]
        return flips[1 + ((level - 1) ^ int(self.flipped))]

    def window(self, ref, lead, level, core, first, second):
        width = ref.shape[-1]
        if self.by_columns:
            size = self.rows // (1, 2, 4)[level - 1]
            start = self.base + 0 * core
            if level > 1:
                start = start + first * (self.rows // 2)
            if level > 2:
                start = start + second * (self.rows // 4)
            cols = pl.ds(pl.multiple_of(core * (width // 2), 128), width // 2)
        else:
            size = self.rows // (2, 4, 8)[level - 1]
            start = self.base + core * (self.rows // 2)
            if level > 1:
                start = start + first * (self.rows // 4)
            if level > 2:
                start = start + second * (self.rows // 8)
            cols = pl.ds(0, width)
        rows = pl.ds(pl.multiple_of(start, 16), size)
        if lead is None:
            return ref.at[rows, cols]
        return ref.at[lead, rows, cols]


def weight_items(units, part, width):
    return (
        Item(0, 0, width, False),
        Item(1, 0, width, True),
        Item(2, 0, units // 2, False),
        Item(2, units // 2, units // 2, True),
        Item(3, 0, part, False, by_columns=True),
    )


def gather_kernel(
    hidden_ref, gain_ref, gate_ref, up_ref, down_ref, out_ref,
    normed_all, gate_all, up_all, down_all, out_all,
    z_send, z_recv, p_send, p_recv, own_sem,
    hold_gate, hold_up, hold_down, hold_out, hold_normed,
):
    dp, line, core, x, y, flips = places()
    upper = line // 2
    inner = line * (1 - upper) + (3 - line) * upper
    normed_ref = hold_normed
    own = (gate_ref, up_ref, down_ref, out_ref)
    full = (gate_all, up_all, down_all, out_all)
    units, width = down_ref.shape
    items = weight_items(units, out_ref.shape[0], width)
    count = len(items)

    barrier = pltpu.get_barrier_semaphore()
    for flip in flips:
        pl.semaphore_signal(barrier, inc=1, device_id=(flip, line), device_id_type=MESH_IDS)

    @pl.when(line > 0)
    def _():
        pl.semaphore_signal(barrier, inc=1, device_id=(dp, line - 1), device_id_type=MESH_IDS)

    @pl.when(line < 3)
    def _():
        pl.semaphore_signal(barrier, inc=1, device_id=(dp, line + 1), device_id_type=MESH_IDS)

    pl.semaphore_wait(barrier, 4 + inner)

    def eighth(i, ref, lead):
        item = items[i]
        first, second = item.bits(x, y)
        return item.window(ref, lead, 3, core, first, second)

    def along(i, block, target, side, first_hop):
        if i == count:
            src = normed_ref if first_hop else normed_all.at[block]
            dst = normed_all.at[block]
        else:
            dst = eighth(i, full[items[i].place], block)
            src = eighth(i, own[items[i].place], None) if first_hop else dst
        return pltpu.make_async_remote_copy(
            src_ref=src, dst_ref=dst, send_sem=z_send.at[i, block, side], recv_sem=z_recv.at[i, block],
            device_id=(dp, target), device_id_type=MESH_IDS,
        )

    def send_own(i):
        @pl.when(line > 0)
        def _():
            along(i, line, line - 1, 0, True).start()

        @pl.when(line < 3)
        def _():
            along(i, line, line + 1, 1, True).start()

    def arrive(i, k):
        block, way = nearest(line, k)
        along(i, block, line, 0, False).wait_recv()

        @pl.when(inner == 1)
        def _():
            along(i, block, line + way, 0, False).start()

    def spread(i, k, stage):
        block, _ = nearest(line, k)
        item = items[i]
        first, second = item.bits(x, y)
        window = item.window(full[item.place], block, 3 - stage, core, first, second)
        return pltpu.make_async_remote_copy(
            src_ref=window, dst_ref=window, send_sem=p_send.at[stage, i, k], recv_sem=p_recv.at[stage, i, k],
            device_id=(item.partner(2 - stage, flips), line), device_id_type=MESH_IDS,
        )

    for i in range(count):
        send_own(i)
    holds = (hold_gate, hold_up, hold_down, hold_out)
    loads = []
    stores = []
    for place, ref in enumerate(own):
        loads.append(pltpu.make_async_copy(ref, holds[place], own_sem.at[0, place]))
        stores.append(pltpu.make_async_copy(holds[place], full[place].at[line], own_sem.at[1, place]))
    for load in loads:
        load.start()
    rows = hidden_ref[...].astype(f32)
    hold_normed[...] = (rows * mean_square_scale(rows) * gain_ref[0:1, :]).astype(bf16)
    keep = pltpu.make_async_copy(hold_normed, normed_all.at[line], own_sem.at[1, 4])
    keep.start()
    for load, store in zip(loads, stores):
        load.wait()
        store.start()

    def advance(k, stage):
        for i in range(count):
            if stage > 0:
                spread(i, k, stage - 1).wait_recv()
            spread(i, k, stage).start()

    for k in range(3):
        for i in range(count):
            arrive(i, k)
            spread(i, k, 0).start()
        if k == 2:
            send_own(count)
        if k >= 1:
            advance(k - 1, 1)
        if k >= 2:
            advance(k - 2, 2)
    advance(2, 1)
    arrive(count, 0)
    advance(1, 2)
    arrive(count, 1)
    advance(2, 2)
    arrive(count, 2)

    keep.wait()
    for store in stores:
        store.wait()
    for i in range(count + 1):
        @pl.when(line > 0)
        def _(i=i):
            along(i, line, line - 1, 0, True).wait_send()

        @pl.when(line < 3)
        def _(i=i):
            along(i, line, line + 1, 1, True).wait_send()

        @pl.when(inner == 1)
        def _(i=i):
            for k in range(3):
                block, way = nearest(line, k)
                along(i, block, line + way, 0, False).wait_send()

    for k in range(3):
        for i in range(count):
            spread(i, k, 2).wait_recv()
            for stage in range(3):
                spread(i, k, stage).wait_send()


def gather(hidden_in, gains, gate, up, down, out):
    rows, width = hidden_in.shape
    units, part = gate.shape[1], out.shape[0]
    anywhere = pl.BlockSpec(memory_space=pl.ANY)
    return pl.pallas_call(
        gather_kernel,
        name="gather",
        out_shape=(
            jax.ShapeDtypeStruct((4, rows, width), bf16),
            jax.ShapeDtypeStruct((4, width, units), bf16),
            jax.ShapeDtypeStruct((4, width, units), bf16),
            jax.ShapeDtypeStruct((4, units, width), bf16),
            jax.ShapeDtypeStruct((4, part, width), bf16),
        ),
        in_specs=[pl.BlockSpec(memory_space=pltpu.VMEM)] * 2 + [anywhere] * 4,
        out_specs=(anywhere,) * 5,
        scratch_shapes=[
            pltpu.SemaphoreType.DMA((6, 4, 2)),
            pltpu.SemaphoreType.DMA((6, 4)),
            pltpu.SemaphoreType.DMA((3, 5, 3)),
            pltpu.SemaphoreType.DMA((3, 5, 3)),
            pltpu.SemaphoreType.DMA((2, 5)),
            pltpu.VMEM(gate.shape, bf16),
            pltpu.VMEM(up.shape, bf16),
            pltpu.VMEM(down.shape, bf16),
            pltpu.VMEM(out.shape, bf16),
            pltpu.VMEM(hidden_in.shape, bf16),
        ],
        compiler_params=pltpu.CompilerParams(collective_id=1, has_side_effects=True),
    )(hidden_in, gains, gate, up, down, out)


class Named:
    def __init__(self, names, refs):
        for name, ref in zip(names, refs):
            setattr(self, name, ref)


def remote(src, dst, send, recv, target):
    return pltpu.make_async_remote_copy(
        src_ref=src, dst_ref=dst, send_sem=send, recv_sem=recv, device_id=target, device_id_type=MESH_IDS
    )


def greet(dp, line, flips):
    barrier = pltpu.get_barrier_semaphore()
    for flip in flips:
        pl.semaphore_signal(barrier, inc=1, device_id=(flip, line), device_id_type=MESH_IDS)
    for i in (1, 2, 3):
        pl.semaphore_signal(
            barrier, inc=1, device_id=(dp, lax.rem(line + i, 4)), device_id_type=MESH_IDS
        )
    pl.semaphore_wait(barrier, 6)


def unit_parts(s, r):
    groups = r.mixed_here.shape[1]

    def mixed_of(g):
        return jnp.concatenate((r.mixed_here[0, g], r.mixed_here[1, g][:, 0:HEAD_DIM]), axis=1)

    def begin():
        mixed = jnp.concatenate([mixed_of(g) for g in range(groups)], axis=1)
        out_w = jnp.concatenate([s.out_w[g] for g in range(groups)], axis=0)
        residual = r.hidden_in[...].astype(f32) + jnp.dot(mixed, out_w, preferred_element_type=f32)
        s.residual[...] = residual
        s.normed2[...] = (residual * mean_square_scale(residual) * r.gains[1:2, :]).astype(bf16)
        s.ahead[...] = residual
        s.behind[...] = jnp.zeros_like(s.behind)

    def block(b, slot):
        normed = s.normed2[...]
        cot = r.cot[...]
        gate_w, up_w, down_w = s.gate_w[slot], s.up_w[slot], s.down_w[slot]
        gate = jnp.dot(normed, gate_w, preferred_element_type=f32)
        up = jnp.dot(normed, up_w, preferred_element_type=f32)
        hidden_grad = contract(cot, down_w, 1, 1)
        c0 = 0.7978845608028654
        square = gate * gate
        bend = jnp.tanh(gate * (c0 + (c0 * 0.044715) * square))
        half = 0.5 + 0.5 * bend
        act = gate * half
        slope = half + 0.5 * gate * (1.0 - bend * bend) * (c0 + (3.0 * c0 * 0.044715) * square)
        hidden = (act * up).astype(bf16)
        gate_grad = (hidden_grad * up * slope).astype(bf16)
        up_grad = (hidden_grad * act).astype(bf16)
        s.ahead[...] += jnp.dot(hidden, down_w, preferred_element_type=f32)
        s.behind[...] += contract(gate_grad, gate_w, 1, 1) + contract(up_grad, up_w, 1, 1)
        s.down_wg[b] = contract(hidden, cot, 0, 0).astype(bf16)
        s.gate_wg[b] = contract(normed, gate_grad, 0, 0).astype(bf16)
        s.up_wg[b] = contract(normed, up_grad, 0, 0).astype(bf16)

    def end():
        residual = s.residual[...]
        r.output[...] = s.ahead[...].astype(bf16)
        back = s.behind[...]
        scale = mean_square_scale(residual)
        s.small_mine[1:2, :] = jnp.sum(back * residual * scale, axis=0, keepdims=True)
        g = back * r.gains[1:2, :]
        centre = jnp.mean(g * residual, axis=-1, keepdims=True)
        residual_grad = r.cot[...].astype(f32) + scale * g - (scale * scale * scale * centre) * residual
        low = residual_grad.astype(bf16)
        s.behind[...] = residual_grad
        for g_at in range(groups):
            s.grad_here[g_at] = contract(low, s.out_w[g_at], 1, 1).astype(bf16)

    def out_grad():
        low = s.behind[...].astype(bf16)
        for g_at in range(groups):
            s.out_wg[g_at] = contract(mixed_of(g_at), low, 0, 0).astype(bf16)

    return begin, block, end, out_grad


def attention_back_tasks(s, r):
    heads, length = s.dot.shape[0], s.dot.shape[1]
    count = length // BLK
    lane = lax.broadcasted_iota(jnp.int32, (BLK, 128), 1)
    low_half = lane < HEAD_DIM
    tasks = []

    def probs_copy(h, block):
        at = (h * count + block) % 2
        rows = pl.ds(block * BLK, BLK)
        return pltpu.make_async_copy(r.probs_all.at[h, rows, :], s.probs.at[at], s.probs_sem.at[at])

    def prepare():
        probs_copy(0, 0).start()
        probs_copy(0, 1).start()

        def body(step, carry):
            rows = pl.ds(pl.multiple_of(step * BLK, BLK), BLK)
            for h in range(heads):
                cols = slice(0, 128) if h < 2 else slice(128, 256)
                mine = ~low_half if h == 1 else low_half
                if h < 2:
                    grad = s.mixed_grad[step, :, 0:128].astype(f32)
                    mix = r.mixed[rows, 0:128].astype(f32)
                else:
                    fill = jnp.zeros((BLK, HEAD_DIM), f32)
                    grad = jnp.concatenate((s.mixed_grad[step, :, 128:192].astype(f32), fill), axis=1)
                    mix = jnp.concatenate((r.mixed[rows, 128:192].astype(f32), fill), axis=1)
                grad = jnp.where(mine, grad * r.inverse[rows, cols], 0.0)
                centre = -jnp.sum(grad * mix, axis=1, keepdims=True)
                high = centre.astype(bf16).astype(f32)
                base = 0 if h == 1 else HEAD_DIM
                grad = jnp.where(lane == base, high, grad)
                grad = jnp.where(lane == base + 1, centre - high, grad)
                low = grad.astype(bf16)
                s.dot[h, rows, :] = low
                s.dott[h, :, rows] = low.T
            return carry

        lax.fori_loop(0, count, body, 0)

    tasks.append(prepare)

    def block_step(h, block):
        if block == 0:
            s.near[...] = jnp.zeros_like(s.near)
            s.far[...] = jnp.zeros_like(s.far)
            s.dkt[...] = jnp.zeros_like(s.dkt)
            s.dvt[...] = jnp.zeros_like(s.dvt)
        probs_copy(h, block).wait()
        at = (h * count + block) % 2
        rows = slice(block * BLK, (block + 1) * BLK)
        d_h = s.dot[h, rows, :]
        dt_h = s.dott[h, :, rows]
        qt_h = r.qt[h, :, rows]
        query_grad = jnp.zeros((BLK, 128), f32)
        for key in key_range(block, count):
            cols = slice(key * BLK, (key + 1) * BLK)
            probs = s.probs[at, :, cols]
            slope = jnp.dot(d_h, r.vt[h, :, cols], preferred_element_type=f32)
            grad = probs.astype(f32) * slope
            low = grad.astype(bf16)
            delta = key - block
            if abs(delta) == 2:
                s.far[0 if delta < 0 else 1] += grad[:, :128] + grad[:, 128:]
            else:
                s.near[:, (delta + 1) * BLK : (delta + 2) * BLK] += grad
            query_grad = query_grad + jnp.dot(low, r.k[h, cols, :], preferred_element_type=f32)
            s.dkt[:, cols] += jnp.dot(qt_h, low, preferred_element_type=f32)
            s.dvt[:, cols] += jnp.dot(dt_h, probs, preferred_element_type=f32)
        s.grad[rows, 0:128] = query_grad * HEAD_DIM ** (-0.5)
        turn = h * count + block + 2
        if turn < heads * count:
            probs_copy(turn // count, turn % count).start()

    def head_end(h):
        def body(step, carry):
            rows = pl.ds(pl.multiple_of(step * BLK, BLK), BLK)
            s.grad[rows, 128:256] = s.dkt[:, rows].T
            s.grad[rows, 256:384] = s.dvt[:, rows].T
            for at in range(3):
                part = s.grad[rows, 128 * at : 128 * at + 128]
                if h == 0:
                    s.joined[rows, 256 * at : 256 * at + 128] = part.astype(bf16)
                elif h == 1:
                    before = s.joined[rows, 256 * at : 256 * at + 128].astype(f32)
                    s.joined[rows, 256 * at : 256 * at + 128] = jnp.where(low_half, before, part).astype(bf16)
                else:
                    s.joined[rows, 256 * at + 128 : 256 * at + 256] = jnp.where(low_half, part, 0.0).astype(bf16)
            return carry

        lax.fori_loop(0, count, body, 0)
        place = lax.broadcasted_iota(jnp.int32, (BLK, 3 * BLK), 1) - BLK
        place = place - lax.broadcasted_iota(jnp.int32, (BLK, 3 * BLK), 0)
        s.bucket[...] = bucket_of(place)
        s.table[...] = jnp.zeros_like(s.table)

        def count_bucket(b, carry):
            part = jnp.sum(jnp.where(s.bucket[...] == b, s.near[...], 0.0), axis=0, keepdims=True)
            folded = part[:, 0:128]
            for at in range(1, 6):
                folded = folded + part[:, at * 128 : (at + 1) * 128]
            s.table[pl.ds(b, 1), :] = folded
            return carry

        lax.fori_loop(0, BUCKETS, count_bucket, 0)
        for side, b in ((0, 15), (1, 31)):
            s.table[b : b + 1, :] += jnp.sum(s.far[side], axis=0, keepdims=True)
        flat = lax.dot_general(
            jnp.ones((8, 128), f32), s.table[...], (((1,), (1,)), ((), ())),
            preferred_element_type=f32, precision=lax.Precision.HIGHEST,
        )
        s.small_mine[8 + h : 9 + h, 0:BUCKETS] = flat[0:1]

    for h in range(heads):
        for block in range(count):
            tasks.append(functools.partial(block_step, h, block))
        tasks.append(functools.partial(head_end, h))

    def rows_grad(block):
        rows = slice(block * BLK, (block + 1) * BLK)
        part = jnp.dot(s.joined[rows, :], s.w[...], preferred_element_type=f32)
        s.back_acc[block] = part.astype(bf16)
        s.gain[...] += jnp.sum(part * r.normed[rows, :].astype(f32), axis=0, keepdims=True)

    def weights_grad(at):
        part = contract(s.joined[:, 256 * at : 256 * at + 256], r.normed[...], 0, 0)
        s.qkv_wg[192 * at : 192 * at + 192, :] = part[0:192].astype(bf16)

    return tasks, rows_grad, weights_grad


REST_OPERANDS = tuple(dict(
    gate_all=0, up_all=0, down_all=0, out_all=0, probs_all=0, wq=0, wk=0, wv=0, mixed_here=0, hidden_in=0,
    cot=0, gains=0, mixed=0, inverse=0, qt=0, k=0, vt=0, normed=0,
))
REST_RESULTS = tuple(dict(
    output=0, input_grad=0, small_sum=0, out_sum=0, gate_sum=0, up_sum=0, down_sum=0, qkv_sum=0,
))


def load_weights(s, r, b, slot):
    pairs = ((r.gate_all, s.gate_w), (r.up_all, s.up_w), (r.down_all, s.down_w))
    return [
        pltpu.make_async_copy(src.at[b], dst.at[slot], s.weight_sem.at[i, slot]) for i, (src, dst) in enumerate(pairs)
    ]


def load_small(s, r):
    copies = [pltpu.make_async_copy(r.out_all, s.out_w, s.first_sem.at[0])]
    for place, ref in enumerate((r.wq, r.wk, r.wv)):
        part = ref.shape[0]
        copies.append(pltpu.make_async_copy(ref, s.w.at[pl.ds(256 * place, part), :], s.first_sem.at[1 + place]))
    return copies


def start_all(s, r):
    groups = s.out_w.shape[0]
    for copy in load_small(s, r) + load_weights(s, r, 0, 0):
        copy.start()
    s.small_mine[...] = jnp.zeros_like(s.small_mine)
    s.gain[...] = jnp.zeros_like(s.gain)
    for place in range(3):
        s.w[256 * place + 192 : 256 * place + 256, :] = jnp.zeros((64, s.w.shape[1]), bf16)
    return groups


def input_grad_rows(s, r, back):
    rows = r.hidden_in[...].astype(f32)
    scale = mean_square_scale(rows)
    g = back * r.gains[0:1, :]
    centre = jnp.mean(g * rows, axis=-1, keepdims=True)
    r.input_grad[...] = (s.behind[...] + scale * g - (scale * scale * scale * centre) * rows).astype(bf16)


def add_rows(target, start, size, source):
    step = 32 if size % 32 == 0 else 16

    def body(i, carry):
        at = pl.multiple_of(i * step, step)
        rows = pl.ds(pl.multiple_of(start + at, 16), step)
        target[rows, :] = (target[rows, :].astype(f32) + source[pl.ds(at, step), :].astype(f32)).astype(bf16)
        return carry

    lax.fori_loop(0, size // step, body, 0)


def rest_kernel(names, *refs):
    r = Named(REST_OPERANDS + REST_RESULTS, refs)
    s = Named(names, refs[len(REST_OPERANDS) + len(REST_RESULTS) :])
    dp, line, core, x, y, flips = places()
    units, width = s.down_wg.shape[1:]
    part = s.out_wg.shape[1]
    items = weight_items(units, part, width)
    item_count = len(items)
    grads = (s.gate_wg, s.up_wg, s.down_wg, s.out_wg, s.qkv_wg)
    sums = (r.gate_sum, r.up_sum, r.down_sum, r.out_sum, r.qkv_sum)
    begin_unit, unit_block, end_unit, out_grad = unit_parts(s, r)
    tasks, rows_grad, weights_grad = attention_back_tasks(s, r)
    groups = start_all(s, r)
    greet(dp, line, flips)

    def item_of(i, block):
        if i < item_count - 1:
            return items[i]
        if i == item_count - 1:
            return Item(3, 0, part, block > 1, True)
        turn = i - item_count
        return Item(4, turn * part, part, turn % 2 == 0, True)

    def lead(i, block):
        return block if i < item_count else None

    def number(i, block):
        return i * groups + block if i < item_count else (item_count - 1) * groups + i - 1

    def at_block(ref, i, block):
        return ref.at[block] if i < item_count else ref

    def arrival(stage, i, block):
        return at_block(getattr(s, stage + str(i)), i, block)

    def held(i, block):
        item = item_of(i, block)
        if item.by_columns:
            return arrival("half", i, block), 0, item.rows
        return grads[item.place].at[block], item.base + core * (item.rows // 2), item.rows // 2

    def load_copy(i, block):
        item = item_of(i, block)
        window = item.window(grads[item.place], lead(i, block), 1, core, 0, 0)
        return pltpu.make_async_copy(window, arrival("half", i, block), s.load_sem.at[number(i, block)])

    def core_copy(i, block):
        item, n = item_of(i, block), number(i, block)
        window = item.window(grads[item.place], lead(i, block), 1, 1 - core, 0, 0)
        return remote(window, arrival("core", i, block), s.core_send.at[n], s.core_recv.at[n], (flips[0], line))

    def begin(i, block):
        core_copy(i, block).start()
        if item_of(i, block).by_columns:
            load_copy(i, block).start()

    def pair_copy(i, block, stage):
        ref, base, half = held(i, block)
        item, n = item_of(i, block), number(i, block)
        first, second = item.bits(x, y)
        if stage == 0:
            size, start, target = half // 2, (1 - first) * (half // 2), arrival("first", i, block)
        else:
            size = half // 4
            start, target = first * (half // 2) + (1 - second) * (half // 4), arrival("second", i, block)
        window = ref.at[pl.ds(pl.multiple_of(base + start, 16), size), :]
        partner = item.partner(1 + stage, flips)
        return remote(window, target, s.pair_send.at[stage, n], s.pair_recv.at[stage, n], (partner, line))

    def eighth(i, block):
        ref, base, half = held(i, block)
        first, second = item_of(i, block).bits(x, y)
        start = pl.multiple_of(base + first * (half // 2) + second * (half // 4), 16)
        return ref, start, half // 4

    def mine(i, block):
        ref, start, size = eighth(i, block)
        return ref.at[pl.ds(start, size), :]

    def line_copy(i, block, sender):
        target = getattr(s, "line" + str(i)).at[sender]
        return remote(
            mine(i, block), target, s.line_send.at[i, block], s.line_recv.at[i, sender], (dp, block)
        )

    def spread_copy(i, block, stage):
        item, n = item_of(i, block), number(i, block)
        first, second = item.bits(x, y)
        window = item.window(sums[item.place], None, 3 - stage, core, first, second)
        src = mine(i, block) if stage == 0 else window
        return remote(
            src, window, s.spread_send.at[stage, n], s.spread_recv.at[stage, n],
            (item.partner(2 - stage, flips), line),
        )

    def keep_copy(i, block):
        item = item_of(i, block)
        first, second = item.bits(x, y)
        window = item.window(sums[item.place], None, 3, core, first, second)
        return pltpu.make_async_copy(mine(i, block), window, s.load_sem.at[number(i, block)])

    def step_core(i, block, send=True):
        if item_of(i, block).by_columns:
            load_copy(i, block).wait()
        core_copy(i, block).wait_recv()
        ref, base, half = held(i, block)
        add_rows(ref, base, half, arrival("core", i, block))
        if send:
            pair_copy(i, block, 0).start()

    def step_first(i, block):
        pair_copy(i, block, 0).wait_recv()
        ref, base, half = held(i, block)
        first, _ = item_of(i, block).bits(x, y)
        add_rows(ref, base + first * (half // 2), half // 2, arrival("first", i, block))
        pair_copy(i, block, 1).start()

    def step_second(i, block):
        pair_copy(i, block, 1).wait_recv()
        ref, start, size = eighth(i, block)
        add_rows(ref, start, size, arrival("second", i, block))
        if i < item_count:
            pl.when(line != block)(lambda: line_copy(i, block, line).start())
        else:
            spread_copy(i, block, 0).start()
            keep_copy(i, block).start()

    def step_last(i, block):
        @pl.when(line == block)
        def _():
            ref, start, size = eighth(i, block)
            others = [o for o in range(groups) if o != block]
            for o in others:
                line_copy(i, block, o).wait_recv()
            arrived = getattr(s, "line" + str(i))
            total = ref[pl.ds(start, size), :].astype(f32)
            for o in others:
                total = total + arrived[o].astype(f32)
            ref[pl.ds(start, size), :] = total.astype(bf16)
            spread_copy(i, block, 0).start()
            keep_copy(i, block).start()

    def step_spread(i, block, stage):
        def act():
            if stage == 1:
                keep_copy(i, block).wait()
            spread_copy(i, block, stage - 1).wait_recv()
            if stage < 3:
                spread_copy(i, block, stage).start()

        if i < item_count:
            pl.when(line == block)(act)
        else:
            act()

    def swap_copy(i, sender_is_me):
        other = lax.rem(line + i, 4)
        if sender_is_me:
            return remote(
                s.grad_here.at[other], s.mixed_grad.at[line], s.swap_send.at[i - 1], s.swap_recv.at[3 - i], (dp, other)
            )
        return remote(
            s.grad_here.at[other], s.mixed_grad.at[other], s.swap_send.at[i - 1], s.swap_recv.at[i - 1], (dp, other)
        )

    def back_copy(block, at, right):
        src, send = s.back_acc.at[block], s.back_send.at[block]
        if right:
            return remote(src, s.back_left.at[block], send, s.back_left_recv.at[block], (dp, at + 1))
        return remote(src, s.back_right.at[block], send, s.back_right_recv.at[block], (dp, at - 1))

    def back_hop(hop, distance):
        @pl.when(line == hop)
        def _():
            block = hop + distance
            if block <= groups - 1:
                if hop > 0:
                    back_copy(block, hop, True).wait_recv()
                    add_rows(s.back_acc.at[block], 0, s.back_acc.shape[1], s.back_left.at[block])
                back_copy(block, hop, True).start()

        at = groups - 1 - hop

        @pl.when(line == at)
        def _():
            block = at - distance
            if block >= 0:
                if hop > 0:
                    back_copy(block, at, False).wait_recv()
                    add_rows(s.back_acc.at[block], 0, s.back_acc.shape[1], s.back_right.at[block])
                back_copy(block, at, False).start()

    def collect_rows():
        for block in range(groups):
            @pl.when(line == block)
            def _(block=block):
                total = s.back_acc[block].astype(f32)
                if block > 0:
                    back_copy(block, block, True).wait_recv()
                    total = total + s.back_left[block].astype(f32)
                if block < groups - 1:
                    back_copy(block, block, False).wait_recv()
                    total = total + s.back_right[block].astype(f32)
                input_grad_rows(s, r, total)

    def small_copy(stage):
        partner = (flips[stage], line) if stage < 3 else (dp, line + 1 - 2 * lax.rem(line, 2))
        if stage == 4:
            partner = (dp, lax.rem(line + 2, 4))
        return remote(s.small_mine, s.small_got.at[stage], s.small_send.at[stage], s.small_recv.at[stage], partner)

    def small_step(stage):
        if stage > 0:
            small_copy(stage - 1).wait()
            rows = lax.broadcasted_iota(jnp.int32, s.small_mine.shape, 0)
            got = s.small_got[stage - 1]
            if stage > 3:
                got = jnp.where(rows < 8, got, 0.0)
            s.small_mine[...] = s.small_mine[...] + got
        else:
            s.small_mine[0:1, :] = s.gain[...] / r.gains[0:1, :]
        if stage < 5:
            small_copy(stage).start()
        else:
            r.small_sum[...] = s.small_mine[...]

    outer, inner = (0, groups - 1), tuple(range(1, groups - 1))
    teams = [[(i, block) for i in (0, 1)] for block in outer + inner]
    teams += [[(i, block) for block in pair for i in (2, 3)] for pair in (outer, inner)]
    teams.append([(item_count - 1, block) for block in range(groups)])
    teams.append([(item_count + turn, 0) for turn in range(3)])
    stage_acts = (
        step_core, step_first, step_second, step_last,
        lambda i, block: step_spread(i, block, 1),
        lambda i, block: step_spread(i, block, 2),
        lambda i, block: step_spread(i, block, 3),
    )
    done = []

    def tend(moment):
        for name, team in WHEN.get(moment, ()):
            done.append((name, team))
            if name == SMALL:
                small_step(team)
            elif name == ROWS:
                collect_rows()
            elif name == HOP:
                back_hop(*team)
            else:
                for i, block in teams[team]:
                    stage_acts[name](i, block)

    for copy in load_small(s, r):
        copy.wait()
    begin_unit()

    order = outer + inner
    for turn, block in enumerate(order):
        for copy in load_weights(s, r, block, turn % 2):
            copy.wait()
        if turn + 1 < groups:
            for copy in load_weights(s, r, order[turn + 1], (turn + 1) % 2):
                copy.start()
        unit_block(block, turn % 2)
        for i in range(item_count - 1):
            begin(i, block)
        tend(UNIT + turn)
    end_unit()
    for i in (2, 1, 3):
        swap_copy(i, True).start()
    swap_keep = pltpu.make_async_copy(s.grad_here.at[line], s.mixed_grad.at[line], s.swap_keep)
    swap_keep.start()
    out_grad()
    for block in range(groups):
        begin(item_count - 1, block)
    tend(SWAP)
    for i in (1, 2, 3):
        swap_copy(i, False).wait_recv()
        swap_copy(i, True).wait_send()
    swap_keep.wait()
    for turn, task in enumerate(tasks):
        task()
        tend(turn)
    for block in range(groups):
        rows_grad(block)
    for distance in (3, 2, 1):
        back_hop(0, distance)
    for turn in range(3):
        weights_grad(turn)
        begin(item_count + turn, 0)
    small_step(0)

    for turn in range(len(WHEN)):
        tend(END + turn)
    assert len(done) == len(set(done)) == 7 * 7 + 6 + 5 + 4
    for block in range(groups):
        pl.when(line < block)(lambda block=block: back_copy(block, line, True).wait_send())
        pl.when(line > block)(lambda block=block: back_copy(block, line, False).wait_send())
    for i, block in sum(teams, []):
        core_copy(i, block).wait_send()
        pair_copy(i, block, 0).wait_send()
        pair_copy(i, block, 1).wait_send()

        def sent(i=i, block=block):
            for stage in range(3):
                spread_copy(i, block, stage).wait_send()

        if i < item_count:
            pl.when(line == block)(sent)
            pl.when(line != block)(lambda i=i, block=block: line_copy(i, block, line).wait_send())
        else:
            sent()


CORE, FIRST, SECOND, LAST, SPREAD1, SPREAD2, SPREAD3, SMALL, HOP, ROWS = range(10)
UNIT, SWAP, END = 100, 110, 120
WHEN = {
    UNIT + 1: [(CORE, 0), (CORE, 1)],
    UNIT + 3: [(FIRST, 0), (CORE, 2)],
    SWAP: [(FIRST, 1), (CORE, 3), (SECOND, 0)],
    0: [(FIRST, 2), (CORE, 4), (SECOND, 1)],
    3: [(FIRST, 3), (CORE, 5), (SECOND, 2)],
    5: [(LAST, 0)],
    7: [(FIRST, 4), (CORE, 6), (SECOND, 3), (SPREAD1, 0)],
    9: [(LAST, 1)],
    11: [(FIRST, 5), (SECOND, 4), (SPREAD2, 0), (SPREAD1, 1)],
    13: [(LAST, 2)],
    14: [(FIRST, 6), (SECOND, 5), (SPREAD2, 1), (SPREAD3, 0)],
    END + 0: [(CORE, 7), (SECOND, 6), (LAST, 3), (SPREAD1, 2), (SPREAD3, 1)],
    END + 1: [(SMALL, 1), (FIRST, 7), (HOP, (1, 2)), (LAST, 4), (SPREAD1, 3), (SPREAD2, 2)],
    END + 2: [(SMALL, 2), (SECOND, 7), (HOP, (1, 1)), (LAST, 5), (LAST, 6), (SPREAD1, 4), (SPREAD2, 3)],
    END + 3: [(SMALL, 3), (HOP, (2, 1)), (SPREAD1, 7), (SPREAD1, 5), (SPREAD1, 6), (SPREAD3, 2)],
    END + 4: [(SMALL, 4), (SPREAD2, 7), (SPREAD2, 4), (SPREAD2, 5), (SPREAD2, 6), (SPREAD3, 3)],
    END + 5: [(SMALL, 5), (SPREAD3, 7), (SPREAD3, 4), (SPREAD3, 5), (SPREAD3, 6), (ROWS, 0)],
}

def common_scratch(groups, rows, heads, length, width, units, part):
    dma = pltpu.SemaphoreType.DMA
    return dict(
        residual=pltpu.VMEM((rows, width), f32),
        normed2=pltpu.VMEM((rows, width), bf16),
        ahead=pltpu.VMEM((rows, width), f32),
        behind=pltpu.VMEM((rows, width), f32),
        out_w=pltpu.VMEM((groups, part, width), bf16),
        gate_w=pltpu.VMEM((2, width, units), bf16),
        up_w=pltpu.VMEM((2, width, units), bf16),
        down_w=pltpu.VMEM((2, units, width), bf16),
        gate_wg=pltpu.VMEM((groups, width, units), bf16),
        up_wg=pltpu.VMEM((groups, width, units), bf16),
        down_wg=pltpu.VMEM((groups, units, width), bf16),
        out_wg=pltpu.VMEM((groups, part, width), bf16),
        qkv_wg=pltpu.VMEM((3 * part, width), bf16),
        grad_here=pltpu.VMEM((groups, rows, part), bf16),
        mixed_grad=pltpu.VMEM((groups, rows, part), bf16),
        back_acc=pltpu.VMEM((groups, rows, width), bf16),
        small_mine=pltpu.VMEM((16, width), f32),
        gain=pltpu.VMEM((1, width), f32),
        probs=pltpu.VMEM((2, BLK, length), bf16),
        w=pltpu.VMEM((768, width), bf16),
        dot=pltpu.VMEM((heads, length, 128), bf16),
        dott=pltpu.VMEM((heads, 128, length), bf16),
        grad=pltpu.VMEM((length, 384), f32),
        joined=pltpu.VMEM((length, 768), bf16),
        near=pltpu.VMEM((BLK, 3 * BLK), f32),
        bucket=pltpu.VMEM((BLK, 3 * BLK), jnp.int32),
        table=pltpu.VMEM((BUCKETS, 128), f32),
        far=pltpu.VMEM((2, BLK, 128), f32),
        dkt=pltpu.VMEM((128, length), f32),
        dvt=pltpu.VMEM((128, length), f32),
        weight_sem=dma((3, 2)), first_sem=dma((4,)), probs_sem=dma((2,)),
    )


def result_shapes(rows, width, units, part):
    return (
        jax.ShapeDtypeStruct((rows, width), bf16),
        jax.ShapeDtypeStruct((rows, width), bf16),
        jax.ShapeDtypeStruct((16, width), f32),
        jax.ShapeDtypeStruct((part, width), bf16),
        jax.ShapeDtypeStruct((width, units), bf16),
        jax.ShapeDtypeStruct((width, units), bf16),
        jax.ShapeDtypeStruct((units, width), bf16),
        jax.ShapeDtypeStruct((3 * part, width), bf16),
    )


def rest_all(gate_all, up_all, down_all, out_all, probs, wq, wk, wv, mixed_here, hidden_in, cot, gains,
             mixed, inverse, qt, k, vt, normed):
    groups, part = mixed_here.shape[1], wq.shape[0]
    rows, width = hidden_in.shape
    heads, length = k.shape[0], k.shape[1]
    units = down_all.shape[1]
    items = weight_items(units, part, width)
    n = 3 + groups * len(items)
    dma = pltpu.SemaphoreType.DMA
    scratch = common_scratch(groups, rows, heads, length, width, units, part)
    for stage, divide in (("half", 1), ("core", 1), ("first", 2), ("second", 4), ("line", 4)):
        for i, item in enumerate(items):
            cols = (units, units, width, width)[item.place]
            shape = (item.rows, cols // 2) if item.by_columns else (item.rows // 2, cols)
            if stage != "half" or item.by_columns:
                scratch[stage + str(i)] = pltpu.VMEM((groups, shape[0] // divide, shape[1]), bf16)
        for turn in range(3):
            if stage != "line":
                scratch[stage + str(len(items) + turn)] = pltpu.VMEM((part // divide, width // 2), bf16)
    scratch.update(
        small_got=pltpu.VMEM((5, 16, width), f32),
        back_left=pltpu.VMEM((groups, rows, width), bf16),
        back_right=pltpu.VMEM((groups, rows, width), bf16),
        load_sem=dma((n,)), core_send=dma((n,)), core_recv=dma((n,)),
        pair_send=dma((2, n)), pair_recv=dma((2, n)),
        line_send=dma((len(items), groups)), line_recv=dma((len(items), groups)),
        spread_send=dma((3, n)), spread_recv=dma((3, n)),
        back_send=dma((groups,)), back_left_recv=dma((groups,)), back_right_recv=dma((groups,)),
        small_send=dma((5,)), small_recv=dma((5,)),
        swap_send=dma((3,)), swap_recv=dma((3,)), swap_keep=dma,
    )
    anywhere = pl.BlockSpec(memory_space=pl.ANY)
    inside = pl.BlockSpec(memory_space=pltpu.VMEM)
    return pl.pallas_call(
        functools.partial(rest_kernel, tuple(scratch)),
        name="rest_all",
        out_shape=result_shapes(rows, width, units, part),
        in_specs=[anywhere] * 8 + [inside] * 10,
        out_specs=(inside,) * 3 + (anywhere,) * 5,
        scratch_shapes=list(scratch.values()),
        compiler_params=pltpu.CompilerParams(
            collective_id=3, has_side_effects=True, vmem_limit_bytes=62 << 20
        ),
    )(gate_all, up_all, down_all, out_all, probs, wq, wk, wv, mixed_here, hidden_in, cot, gains,
      mixed, inverse, qt, k, vt, normed)


UNIT_RESULTS = tuple(dict(
    output=0, residual_grad=0, grads=0, gain2_grad=0, out_out=0, gate_out=0, up_out=0, down_out=0,
))


def unit_local_kernel(names, *refs):
    operands = tuple(dict(gate_all=0, up_all=0, down_all=0, out_all=0, mixed_here=0, hidden_in=0, cot=0, gains=0))
    r = Named(operands + UNIT_RESULTS, refs)
    s = Named(names, refs[len(operands) + len(UNIT_RESULTS) :])
    s.out_wg, s.gate_wg, s.up_wg, s.down_wg = r.out_out, r.gate_out, r.up_out, r.down_out
    s.behind, s.grad_here = r.residual_grad, r.grads
    begin, block, end, out_grad = unit_parts(s, r)
    groups = s.out_w.shape[0]
    first = [pltpu.make_async_copy(r.out_all, s.out_w, s.first_sem.at[0])] + load_weights(s, r, 0, 0)
    for copy in first:
        copy.start()
    first[0].wait()
    begin()

    def body(b, carry):
        slot = lax.rem(b, 2)
        for copy in load_weights(s, r, b, slot):
            copy.wait()

        @pl.when(b + 1 < groups)
        def _():
            for copy in load_weights(s, r, b + 1, 1 - slot):
                copy.start()

        block(b, slot)
        return carry

    lax.fori_loop(0, groups, body, 0)
    end()
    out_grad()
    r.gain2_grad[...] = s.small_mine[1:2, :]


def back_local_kernel(names, *refs):
    operands = tuple(dict(probs_all=0, mixed=0, inverse=0, qt=0, k=0, vt=0, normed=0, wq=0, wk=0, wv=0, gains=0, mixed_grad=0))
    results = tuple(dict(back_out=0, qkv_out=0, small_out=0))
    r = Named(operands + results, refs)
    s = Named(names, refs[len(operands) + len(results) :])
    s.mixed_grad, s.qkv_wg, s.small_mine, s.back_acc = r.mixed_grad, r.qkv_out, r.small_out, r.back_out
    tasks, rows_grad, weights_grad = attention_back_tasks(s, r)
    s.small_mine[...] = jnp.zeros_like(s.small_mine)
    s.gain[...] = jnp.zeros_like(s.gain)
    s.w[...] = jnp.zeros_like(s.w)
    for place, ref in enumerate((r.wq, r.wk, r.wv)):
        s.w[256 * place : 256 * place + ref.shape[0], :] = ref[...]
    for task in tasks:
        task()
    for block in range(r.back_out.shape[0]):
        rows_grad(block)
    for turn in range(3):
        weights_grad(turn)
    s.small_mine[0:1, :] = s.gain[...] / r.gains[0:1, :]


def rest_by_axis(gate_all, up_all, down_all, out_all, probs, wq, wk, wv, mixed_here, hidden_in, cot, gains,
                 mixed, inverse, qt, k, vt, normed):
    groups, part = mixed_here.shape[1], wq.shape[0]
    rows, width = hidden_in.shape
    heads, length = k.shape[0], k.shape[1]
    units = down_all.shape[1]
    anywhere = pl.BlockSpec(memory_space=pl.ANY)
    inside = pl.BlockSpec(memory_space=pltpu.VMEM)
    every = common_scratch(groups, rows, heads, length, width, units, part)
    pick = lambda names: {name: every[name] for name in names}
    shape = jax.ShapeDtypeStruct
    scratch = pick(dict(
    residual=0, normed2=0, ahead=0, out_w=0, gate_w=0, up_w=0, down_w=0, small_mine=0, weight_sem=0,
    first_sem=0,
    ))
    output, residual_grad, grads, gain2_grad, out_wg, gate_wg, up_wg, down_wg = pl.pallas_call(
        functools.partial(unit_local_kernel, tuple(scratch)),
        name="unit_local",
        out_shape=(
            shape((rows, width), bf16), shape((rows, width), f32), shape((groups, rows, part), bf16),
            shape((1, width), f32), shape((groups, part, width), bf16), shape((groups, width, units), bf16),
            shape((groups, width, units), bf16), shape((groups, units, width), bf16),
        ),
        in_specs=[anywhere] * 4 + [inside] * 4,
        out_specs=(inside,) * 8,
        scratch_shapes=list(scratch.values()),
        compiler_params=pltpu.CompilerParams(vmem_limit_bytes=56 << 20),
    )(gate_all, up_all, down_all, out_all, mixed_here, hidden_in, cot, gains)
    mixed_grad = lax.all_to_all(grads, "tensor", 0, 0)
    scratch = pick(dict(
    gain=0, probs=0, w=0, dot=0, dott=0, grad=0, joined=0, near=0, bucket=0, table=0, far=0, dkt=0, dvt=0,
    probs_sem=0,
    ))
    back, qkv_wg, small = pl.pallas_call(
        functools.partial(back_local_kernel, tuple(scratch)),
        name="back_local",
        out_shape=(
            shape((groups, rows, width), bf16), shape((3 * part, width), bf16), shape((16, width), f32),
        ),
        in_specs=[anywhere] + [inside] * 11,
        out_specs=(inside,) * 3,
        scratch_shapes=list(scratch.values()),
        compiler_params=pltpu.CompilerParams(vmem_limit_bytes=56 << 20),
    )(probs, mixed, inverse, qt, k, vt, normed, wq, wk, wv, gains, mixed_grad)
    back_sum = lax.psum_scatter(back, "tensor", scatter_dimension=0).astype(f32)
    parts = tuple(lax.psum_scatter(wg, "tensor", scatter_dimension=0) for wg in (out_wg, gate_wg, up_wg, down_wg))
    sums = lax.psum(parts + (qkv_wg,), "dp")
    small = small.at[1].set(gain2_grad[0])
    small_sum = lax.psum(small, "dp")
    gains = lax.psum(small_sum[:8], "tensor")
    input_rows = hidden_in.astype(f32)
    r1 = mean_square_scale(input_rows)
    g1 = back_sum * gains[0:1]
    centre = jnp.mean(g1 * input_rows, axis=-1, keepdims=True)
    input_grad = (residual_grad + r1 * g1 - (r1 * r1 * r1 * centre) * input_rows).astype(bf16)
    return (output, input_grad, jnp.concatenate((gains, small_sum[8:]))) + tuple(sums)


def finish_kernel(*refs):
    half = len(refs) // 2
    for source, target in zip(refs[:half], refs[half:]):
        target[...] = source[...].astype(target.dtype)


def finish(output, input_grad, qkv_sum, out_sum, gate_sum, up_sum, down_sum):
    part, width = out_sum.shape
    steps = 4
    block = lambda a, at: pl.BlockSpec((a // steps, at), lambda i: (i, 0))
    shift = lambda turn: pl.BlockSpec((part // steps, width), lambda i: (i + turn * steps, 0))
    arrays = (output, input_grad, qkv_sum, qkv_sum, qkv_sum, out_sum, gate_sum, up_sum, down_sum)
    shapes = [output.shape, input_grad.shape] + [out_sum.shape] * 4 + [gate_sum.shape, up_sum.shape, down_sum.shape]
    kinds = [bf16] * 2 + [f32] * 7
    specs = [block(*shape) for shape in shapes]
    return pl.pallas_call(
        finish_kernel,
        grid=(steps,),
        name="finish",
        out_shape=tuple(jax.ShapeDtypeStruct(s, k) for s, k in zip(shapes, kinds)),
        in_specs=specs[:2] + [shift(turn) for turn in range(3)] + specs[5:],
        out_specs=tuple(specs),
        compiler_params=pltpu.CompilerParams(dimension_semantics=("arbitrary",), vmem_limit_bytes=32 << 20),
    )(*arrays)


def gather_by_axis(hidden_in, gains, gate, up, down, out):
    rows = hidden_in.astype(f32)
    normed = (rows * mean_square_scale(rows) * gains[0:1]).astype(bf16)
    return tuple(lax.all_gather(part, "tensor", axis=0) for part in (normed, gate, up, down, out))


def shards(
    by_kernel,
    hidden_in, segment_ids, norm1_gain, query_weight, key_weight, value_weight, out_weight,
    bias_table, norm2_gain, gate_weight, up_weight, down_weight, out_cotangent,
):
    gather_parts = gather if by_kernel else gather_by_axis
    rest_parts = rest_all if by_kernel else rest_by_axis
    rows_here, width = hidden_in.shape
    length = segment_ids.shape[1]
    assert segment_ids.shape[0] == 1 and rows_here == BLK
    heads = bias_table.shape[1]
    gains = jnp.stack((norm1_gain, norm2_gain)).astype(f32)
    normed, gate_w, up_w, down_w, out_w = gather_parts(
        hidden_in, gains, gate_weight, up_weight, down_weight, out_weight
    )
    normed = normed.reshape(length, width)
    query_weight, key_weight, value_weight = query_weight.T, key_weight.T, value_weight.T
    mixed, probs, qt, k, vt, inverse, mixed_here = attend(
        by_kernel, normed, query_weight, key_weight, value_weight, segment_ids, bias_table
    )
    if not by_kernel:
        mixed_here = lax.all_to_all(mixed_here, "tensor", 1, 1)
    output, input_grad, small_sum, out_sum, gate_sum, up_sum, down_sum, qkv_sum = rest_parts(
        gate_w, up_w, down_w, out_w, probs, query_weight, key_weight, value_weight, mixed_here, hidden_in,
        out_cotangent, gains, mixed, inverse, qt, k, vt, normed,
    )
    output, input_grad, query_grad, key_grad, value_grad, out_grad, gate_grad, up_grad, down_grad = finish(
        output, input_grad, qkv_sum, out_sum, gate_sum, up_sum, down_sum
    )
    return (
        output, input_grad, small_sum[0], query_grad.T, key_grad.T, value_grad.T, out_grad,
        small_sum[8 : 8 + heads, :BUCKETS].T, small_sum[1], gate_grad, up_grad, down_grad,
    )


def solution(mesh):
    in_specs = (
        P(("dp", "tensor"), None), P("dp", None), P(),
        P(None, "tensor"), P(None, "tensor"), P(None, "tensor"), P("tensor", None),
        P(None, "tensor"), P(), P(None, "tensor"), P(None, "tensor"), P("tensor", None),
        P(("dp", "tensor"), None),
    )
    out_specs = (
        P(("dp", "tensor"), None), P(("dp", "tensor"), None), P(),
        P(None, "tensor"), P(None, "tensor"), P(None, "tensor"), P("tensor", None),
        P(None, "tensor"), P(), P(None, "tensor"), P(None, "tensor"), P("tensor", None),
    )
    by_kernel = mesh.shape["dp"] == 8 and mesh.shape["tensor"] == 4
    return jax.shard_map(
        functools.partial(shards, by_kernel), mesh=mesh, in_specs=in_specs, out_specs=out_specs, check_vma=False
    )
```

```python
import functools

import jax
import jax.numpy as jnp
from jax import lax
from jax.experimental import pallas as pl
from jax.experimental.pallas import tpu as pltpu
from jax.sharding import PartitionSpec as P

HEAD_DIM = 64
BUCKETS = 32
far_marks = (12, 16, 23, 32, 46, 64, 91)
norm_eps = 1e-06
far_score = 2.0**30
BLK = 256
f32 = jnp.float32
bf16 = jnp.bfloat16


def bucket_of(offset):
    magnitude = jnp.abs(offset)
    within = jnp.minimum(magnitude, 8)
    for far_mark in far_marks:
        within = within + (magnitude >= far_mark).astype(jnp.int32)
    return within + jnp.where(offset > 0, 16, 0).astype(jnp.int32)


def key_range(block, count):
    return range(max(0, block - 2), min(count, block + 3))


def contract(lhs, rhs, left, right):
    return lax.dot_general(
        lhs, rhs, (((left,), (right,)), ((), ())), preferred_element_type=f32
    )


def attend_kernel(
    by_kernel, normed_ref, wq_ref, wk_ref, wv_ref, seg_ref, table_ref,
    mixed_ref, probs_ref, qt_ref, k_ref, vt_ref, inv_ref, here_ref,
    w_s, kt_s, bias_s, score_s, first_s, q_s, v_s, parts_s, send_sem, recv_sem, keep_sem,
):
    head = pl.program_id(0)
    length = normed_ref.shape[0]
    count = length // BLK
    lane = lax.broadcasted_iota(jnp.int32, (BLK, 128), 1)
    low_half = lane < HEAD_DIM

    if by_kernel:
        dp, line = lax.axis_index("dp"), lax.axis_index("tensor")
        others = [lax.rem(line + i, 4) for i in (1, 2, 3)]

        @pl.when(head == 0)
        def _():
            barrier = pltpu.get_barrier_semaphore()
            for other in others:
                pl.semaphore_signal(barrier, inc=1, device_id=(dp, other), device_id_type=MESH_IDS)
            pl.semaphore_wait(barrier, 3)

        def part_copy(half, i, sender_is_me):
            place = line if sender_is_me else others[i]
            return pltpu.make_async_remote_copy(
                src_ref=parts_s.at[half, others[i]], dst_ref=here_ref.at[half, place],
                send_sem=send_sem.at[half, i], recv_sem=recv_sem.at[half, 2 - i if sender_is_me else i],
                device_id=(dp, others[i]), device_id_type=MESH_IDS,
            )

        def own_copy(half):
            return pltpu.make_async_copy(parts_s.at[half, line], here_ref.at[half, line], keep_sem.at[half])

        def send_part(half):
            for i in (1, 0, 2):
                part_copy(half, i, True).start()
            own_copy(half).start()

    @pl.when(head == 0)
    def _():
        w_s[...] = jnp.zeros_like(w_s)
        for place, ref in enumerate((wq_ref, wk_ref, wv_ref)):
            w_s[256 * place : 256 * place + 192, :] = ref[...]
        row8 = lax.broadcasted_iota(jnp.int32, (8, 128), 0)
        lane8 = lax.broadcasted_iota(jnp.int32, (8, 128), 1)
        spread = jnp.where((lane8 % HEAD_DIM) == row8, 1.0, 0.0).astype(bf16)

        def project(step, carry):
            rows = pl.ds(pl.multiple_of(step * BLK, BLK), BLK)
            seg_row = seg_ref[:, rows]
            kinds = lax.broadcasted_iota(jnp.int32, (8, BLK), 0)
            hot = jnp.where(
                jnp.broadcast_to(seg_row, (8, BLK)) == kinds, 1.0, 0.0
            ).astype(bf16)
            same = contract(hot, spread, 0, 0)
            in_aug = (lane % HEAD_DIM) < 8
            aug_q = jnp.where(in_aug, same, 0.0)
            aug_k = jnp.where(in_aug, (same - 1.0) * far_score, 0.0)
            rows_in = normed_ref[rows, :]
            q = contract(rows_in, w_s[0:256, :], 1, 1)
            k = contract(rows_in, w_s[256:512, :], 1, 1)
            v = contract(rows_in, w_s[512:768, :], 1, 1)
            scale = HEAD_DIM ** (-0.5)
            for h, (cols, mine) in enumerate(
                ((slice(0, 128), low_half), (slice(0, 128), ~low_half), (slice(128, 256), low_half))
            ):
                q_h = jnp.where(mine, q[:, cols] * scale, aug_q).astype(bf16)
                q_s[h, rows, :] = q_h
                qt_ref[h, :, rows] = q_h.T
                k_h = jnp.where(mine, k[:, cols], aug_k).astype(bf16)
                k_ref[h, rows, :] = k_h
                v_h = jnp.where(mine, v[:, cols], 1.0).astype(bf16)
                v_s[h, rows, :] = v_h
                vt_ref[h, :, rows] = v_h.T
                kt_s[h, :, rows] = k_h.T
            return carry

        lax.fori_loop(0, count, project, 0)

    offset = lax.broadcasted_iota(jnp.int32, (BUCKETS, length), 1)
    offset = jnp.where(offset >= length // 2, offset - length, offset)
    hot_bucket = jnp.where(
        bucket_of(offset) == lax.broadcasted_iota(jnp.int32, (BUCKETS, length), 0), 1.0, 0.0
    ).astype(bf16)
    by_offset = contract(table_ref[head], hot_bucket, 1, 0)[0:1]
    spread_rows = jnp.broadcast_to(by_offset, (BLK, length))
    bias_s[...] = pltpu.roll(spread_rows, 0, 1, stride=1, stride_axis=0)

    for block in range(count):
        rows = slice(block * BLK, (block + 1) * BLK)
        q_h = q_s[head, rows, :]
        top = None
        for key in key_range(block, count):
            part = jnp.dot(
                q_h, kt_s[head, :, key * BLK : (key + 1) * BLK], preferred_element_type=f32
            )
            delta = key - block
            at = (delta * BLK) % length
            part = part + bias_s[:, at : at + BLK]
            score_s[:, key * BLK : (key + 1) * BLK] = part
            top = part if top is None else jnp.maximum(top, part)
        top = jnp.max(jnp.maximum(top[:, :128], top[:, 128:]), axis=1, keepdims=True)
        total = jnp.zeros((BLK, 128), f32)
        for key in key_range(block, count):
            cols = slice(key * BLK, (key + 1) * BLK)
            part = jnp.exp(score_s[:, cols] - top).astype(bf16)
            probs_ref[0, rows, cols] = part
            total = total + jnp.dot(part, v_s[head, cols, :], preferred_element_type=f32)
        sums = pltpu.roll(total, HEAD_DIM, 1)
        inverse = 1.0 / sums
        out = total * inverse

        @pl.when(head == 0)
        def _():
            first_s[rows, 0:128] = out
            first_s[rows, 128:256] = inverse

        @pl.when(head == 1)
        def _():
            pair = jnp.where(low_half, first_s[rows, 0:128], out).astype(bf16)
            mixed_ref[rows, 0:128] = pair
            parts_s[0, block] = pair
            inv_ref[rows, 0:128] = jnp.where(low_half, first_s[rows, 128:256], inverse)

        @pl.when(head == 2)
        def _():
            mixed_ref[rows, 128:192] = out[:, 0:HEAD_DIM].astype(bf16)
            inv_ref[rows, 128:256] = inverse
            parts_s[1, block] = out.astype(bf16)

    if by_kernel:
        @pl.when(head == 1)
        def _():
            send_part(0)

        @pl.when(head == 2)
        def _():
            send_part(1)
            for half in range(2):
                own_copy(half).wait()
                for i in range(3):
                    part_copy(half, i, True).wait_send()
                    part_copy(half, i, False).wait_recv()
    else:
        @pl.when(head == 2)
        def _():
            for half in range(2):
                keep = pltpu.make_async_copy(parts_s.at[half], here_ref.at[half], keep_sem.at[half])
                keep.start()
                keep.wait()


MESH_IDS = pl.DeviceIdType.MESH


def attend(by_kernel, normed, wq, wk, wv, segments, bias_table):
    length, width = normed.shape
    heads = bias_table.shape[1]
    inner = heads * HEAD_DIM
    table = jnp.broadcast_to(bias_table.T[:, None, :], (heads, 8, BUCKETS))
    whole = lambda *dims: pl.BlockSpec(dims, lambda h: (0,) * len(dims))
    return pl.pallas_call(
        functools.partial(attend_kernel, by_kernel),
        grid=(heads,),
        name="attend",
        out_shape=(
            jax.ShapeDtypeStruct((length, inner), bf16),
            jax.ShapeDtypeStruct((heads, length, length), bf16),
            jax.ShapeDtypeStruct((heads, 128, length), bf16),
            jax.ShapeDtypeStruct((heads, length, 128), bf16),
            jax.ShapeDtypeStruct((heads, 128, length), bf16),
            jax.ShapeDtypeStruct((length, 256), f32),
            jax.ShapeDtypeStruct((2, length // BLK, BLK, 128), bf16),
        ),
        in_specs=[
            whole(length, width),
            whole(inner, width),
            whole(inner, width),
            whole(inner, width),
            whole(1, length),
            whole(heads, 8, BUCKETS),
        ],
        out_specs=(
            whole(length, inner),
            pl.BlockSpec((1, length, length), lambda h: (h, 0, 0)),
            whole(heads, 128, length),
            whole(heads, length, 128),
            whole(heads, 128, length),
            whole(length, 256),
            pl.BlockSpec(memory_space=pl.ANY),
        ),
        scratch_shapes=[
            pltpu.VMEM((768, width), bf16),
            pltpu.VMEM((heads, 128, length), bf16),
            pltpu.VMEM((BLK, length), f32),
            pltpu.VMEM((BLK, length), f32),
            pltpu.VMEM((length, 256), f32),
            pltpu.VMEM((heads, length, 128), bf16),
            pltpu.VMEM((heads, length, 128), bf16),
            pltpu.VMEM((2, length // BLK, BLK, 128), bf16),
            pltpu.SemaphoreType.DMA((2, 3)),
            pltpu.SemaphoreType.DMA((2, 3)),
            pltpu.SemaphoreType.DMA((2,)),
        ],
        compiler_params=pltpu.CompilerParams(
            dimension_semantics=("arbitrary",), vmem_limit_bytes=60 << 20,
            **(dict(collective_id=2, has_side_effects=True) if by_kernel else {}),
        ),
        cost_estimate=pl.CostEstimate(flops=3 << 30, bytes_accessed=12 << 20, transcendentals=3 << 20),
    )(normed, wq, wk, wv, segments, table)


def mean_square_scale(rows):
    return lax.rsqrt(jnp.mean(rows * rows, axis=-1, keepdims=True) + norm_eps)


def places():
    dp = lax.axis_index("dp")
    line = lax.axis_index("tensor")
    core = lax.rem(dp, 2)
    x = lax.rem(dp // 2, 2)
    y = dp // 4
    flips = (dp + 1 - 2 * core, dp + 2 - 4 * x, dp + 4 - 8 * y)
    return dp, line, core, x, y, flips


def nearest(line, k):
    upper = line // 2
    inner = line * (1 - upper) + (3 - line) * upper
    block = k + 1 - inner if k == 0 else k + 1
    block = block * (1 - upper) + (3 - block) * upper
    way = (1 if k == 0 else -1) * (1 - 2 * upper)
    return block, way


class Item:
    def __init__(self, place, base, rows, flipped, by_columns=False):
        self.place, self.base, self.rows = place, base, rows
        self.flipped, self.by_columns = flipped, by_columns

    def bits(self, x, y):
        return (y, x) if self.flipped else (x, y)

    def partner(self, level, flips):
        if level == 0:
            return flips[0]
        return flips[1 + ((level - 1) ^ int(self.flipped))]

    def window(self, ref, lead, level, core, first, second):
        width = ref.shape[-1]
        if self.by_columns:
            size = self.rows // (1, 2, 4)[level - 1]
            start = self.base + 0 * core
            if level > 1:
                start = start + first * (self.rows // 2)
            if level > 2:
                start = start + second * (self.rows // 4)
            cols = pl.ds(pl.multiple_of(core * (width // 2), 128), width // 2)
        else:
            size = self.rows // (2, 4, 8)[level - 1]
            start = self.base + core * (self.rows // 2)
            if level > 1:
                start = start + first * (self.rows // 4)
            if level > 2:
                start = start + second * (self.rows // 8)
            cols = pl.ds(0, width)
        rows = pl.ds(pl.multiple_of(start, 16), size)
        if lead is None:
            return ref.at[rows, cols]
        return ref.at[lead, rows, cols]


def weight_items(units, part, width):
    return (
        Item(0, 0, width, False),
        Item(1, 0, width, True),
        Item(2, 0, units // 2, False),
        Item(2, units // 2, units // 2, True),
        Item(3, 0, part, False, by_columns=True),
    )


def gather_kernel(
    hidden_ref, gain_ref, gate_ref, up_ref, down_ref, out_ref,
    normed_all, gate_all, up_all, down_all, out_all,
    z_send, z_recv, p_send, p_recv, own_sem,
    hold_gate, hold_up, hold_down, hold_out, hold_normed,
):
    dp, line, core, x, y, flips = places()
    upper = line // 2
    inner = line * (1 - upper) + (3 - line) * upper
    normed_ref = hold_normed
    own = (gate_ref, up_ref, down_ref, out_ref)
    full = (gate_all, up_all, down_all, out_all)
    units, width = down_ref.shape
    items = weight_items(units, out_ref.shape[0], width)
    count = len(items)

    barrier = pltpu.get_barrier_semaphore()
    for flip in flips:
        pl.semaphore_signal(barrier, inc=1, device_id=(flip, line), device_id_type=MESH_IDS)

    @pl.when(line > 0)
    def _():
        pl.semaphore_signal(barrier, inc=1, device_id=(dp, line - 1), device_id_type=MESH_IDS)

    @pl.when(line < 3)
    def _():
        pl.semaphore_signal(barrier, inc=1, device_id=(dp, line + 1), device_id_type=MESH_IDS)

    pl.semaphore_wait(barrier, 4 + inner)

    def eighth(i, ref, lead):
        item = items[i]
        first, second = item.bits(x, y)
        return item.window(ref, lead, 3, core, first, second)

    def along(i, block, target, side, first_hop):
        if i == count:
            src = normed_ref if first_hop else normed_all.at[block]
            dst = normed_all.at[block]
        else:
            dst = eighth(i, full[items[i].place], block)
            src = eighth(i, own[items[i].place], None) if first_hop else dst
        return pltpu.make_async_remote_copy(
            src_ref=src, dst_ref=dst, send_sem=z_send.at[i, block, side], recv_sem=z_recv.at[i, block],
            device_id=(dp, target), device_id_type=MESH_IDS,
        )

    def send_own(i):
        @pl.when(line > 0)
        def _():
            along(i, line, line - 1, 0, True).start()

        @pl.when(line < 3)
        def _():
            along(i, line, line + 1, 1, True).start()

    def arrive(i, k):
        block, way = nearest(line, k)
        along(i, block, line, 0, False).wait_recv()

        @pl.when(inner == 1)
        def _():
            along(i, block, line + way, 0, False).start()

    def spread(i, k, stage):
        block, _ = nearest(line, k)
        item = items[i]
        first, second = item.bits(x, y)
        window = item.window(full[item.place], block, 3 - stage, core, first, second)
        return pltpu.make_async_remote_copy(
            src_ref=window, dst_ref=window, send_sem=p_send.at[stage, i, k], recv_sem=p_recv.at[stage, i, k],
            device_id=(item.partner(2 - stage, flips), line), device_id_type=MESH_IDS,
        )

    for i in range(count):
        send_own(i)
    holds = (hold_gate, hold_up, hold_down, hold_out)
    loads = []
    stores = []
    for place, ref in enumerate(own):
        loads.append(pltpu.make_async_copy(ref, holds[place], own_sem.at[0, place]))
        stores.append(pltpu.make_async_copy(holds[place], full[place].at[line], own_sem.at[1, place]))
    for load in loads:
        load.start()
    rows = hidden_ref[...].astype(f32)
    hold_normed[...] = (rows * mean_square_scale(rows) * gain_ref[0:1, :]).astype(bf16)
    keep = pltpu.make_async_copy(hold_normed, normed_all.at[line], own_sem.at[1, 4])
    keep.start()
    for load, store in zip(loads, stores):
        load.wait()
        store.start()

    def advance(k, stage):
        for i in range(count):
            if stage > 0:
                spread(i, k, stage - 1).wait_recv()
            spread(i, k, stage).start()

    for k in range(3):
        for i in range(count):
            arrive(i, k)
            spread(i, k, 0).start()
        if k == 2:
            send_own(count)
        if k >= 1:
            advance(k - 1, 1)
        if k >= 2:
            advance(k - 2, 2)
    advance(2, 1)
    arrive(count, 0)
    advance(1, 2)
    arrive(count, 1)
    advance(2, 2)
    arrive(count, 2)

    keep.wait()
    for store in stores:
        store.wait()
    for i in range(count + 1):
        @pl.when(line > 0)
        def _(i=i):
            along(i, line, line - 1, 0, True).wait_send()

        @pl.when(line < 3)
        def _(i=i):
            along(i, line, line + 1, 1, True).wait_send()

        @pl.when(inner == 1)
        def _(i=i):
            for k in range(3):
                block, way = nearest(line, k)
                along(i, block, line + way, 0, False).wait_send()

    for k in range(3):
        for i in range(count):
            spread(i, k, 2).wait_recv()
            for stage in range(3):
                spread(i, k, stage).wait_send()


def gather(hidden_in, gains, gate, up, down, out):
    rows, width = hidden_in.shape
    units, part = gate.shape[1], out.shape[0]
    anywhere = pl.BlockSpec(memory_space=pl.ANY)
    return pl.pallas_call(
        gather_kernel,
        name="gather",
        out_shape=(
            jax.ShapeDtypeStruct((4, rows, width), bf16),
            jax.ShapeDtypeStruct((4, width, units), bf16),
            jax.ShapeDtypeStruct((4, width, units), bf16),
            jax.ShapeDtypeStruct((4, units, width), bf16),
            jax.ShapeDtypeStruct((4, part, width), bf16),
        ),
        in_specs=[pl.BlockSpec(memory_space=pltpu.VMEM)] * 2 + [anywhere] * 4,
        out_specs=(anywhere,) * 5,
        scratch_shapes=[
            pltpu.SemaphoreType.DMA((6, 4, 2)),
            pltpu.SemaphoreType.DMA((6, 4)),
            pltpu.SemaphoreType.DMA((3, 5, 3)),
            pltpu.SemaphoreType.DMA((3, 5, 3)),
            pltpu.SemaphoreType.DMA((2, 5)),
            pltpu.VMEM(gate.shape, bf16),
            pltpu.VMEM(up.shape, bf16),
            pltpu.VMEM(down.shape, bf16),
            pltpu.VMEM(out.shape, bf16),
            pltpu.VMEM(hidden_in.shape, bf16),
        ],
        compiler_params=pltpu.CompilerParams(collective_id=1, has_side_effects=True),
    )(hidden_in, gains, gate, up, down, out)


class Named:
    def __init__(self, names, refs):
        for name, ref in zip(names, refs):
            setattr(self, name, ref)


def remote(src, dst, send, recv, target):
    return pltpu.make_async_remote_copy(
        src_ref=src, dst_ref=dst, send_sem=send, recv_sem=recv, device_id=target, device_id_type=MESH_IDS
    )


def greet(dp, line, flips):
    barrier = pltpu.get_barrier_semaphore()
    for flip in flips:
        pl.semaphore_signal(barrier, inc=1, device_id=(flip, line), device_id_type=MESH_IDS)
    for i in (1, 2, 3):
        pl.semaphore_signal(
            barrier, inc=1, device_id=(dp, lax.rem(line + i, 4)), device_id_type=MESH_IDS
        )
    pl.semaphore_wait(barrier, 6)


def unit_parts(s, r):
    groups = r.mixed_here.shape[1]

    def mixed_of(g):
        return jnp.concatenate((r.mixed_here[0, g], r.mixed_here[1, g][:, 0:HEAD_DIM]), axis=1)

    def begin():
        mixed = jnp.concatenate([mixed_of(g) for g in range(groups)], axis=1)
        out_w = jnp.concatenate([s.out_w[g] for g in range(groups)], axis=0)
        residual = r.hidden_in[...].astype(f32) + jnp.dot(mixed, out_w, preferred_element_type=f32)
        s.residual[...] = residual
        s.normed2[...] = (residual * mean_square_scale(residual) * r.gains[1:2, :]).astype(bf16)
        s.ahead[...] = residual
        s.behind[...] = jnp.zeros_like(s.behind)

    def block(b, slot):
        normed = s.normed2[...]
        cot = r.cot[...]
        gate_w, up_w, down_w = s.gate_w[slot], s.up_w[slot], s.down_w[slot]
        gate = jnp.dot(normed, gate_w, preferred_element_type=f32)
        up = jnp.dot(normed, up_w, preferred_element_type=f32)
        hidden_grad = contract(cot, down_w, 1, 1)
        c0 = 0.7978845608028654
        square = gate * gate
        bend = jnp.tanh(gate * (c0 + (c0 * 0.044715) * square))
        half = 0.5 + 0.5 * bend
        act = gate * half
        slope = half + 0.5 * gate * (1.0 - bend * bend) * (c0 + (3.0 * c0 * 0.044715) * square)
        hidden = (act * up).astype(bf16)
        gate_grad = (hidden_grad * up * slope).astype(bf16)
        up_grad = (hidden_grad * act).astype(bf16)
        s.ahead[...] += jnp.dot(hidden, down_w, preferred_element_type=f32)
        s.behind[...] += contract(gate_grad, gate_w, 1, 1) + contract(up_grad, up_w, 1, 1)
        s.down_wg[b] = contract(hidden, cot, 0, 0).astype(bf16)
        s.gate_wg[b] = contract(normed, gate_grad, 0, 0).astype(bf16)
        s.up_wg[b] = contract(normed, up_grad, 0, 0).astype(bf16)

    def end():
        residual = s.residual[...]
        r.output[...] = s.ahead[...].astype(bf16)
        back = s.behind[...]
        scale = mean_square_scale(residual)
        s.small_mine[1:2, :] = jnp.sum(back * residual * scale, axis=0, keepdims=True)
        g = back * r.gains[1:2, :]
        centre = jnp.mean(g * residual, axis=-1, keepdims=True)
        residual_grad = r.cot[...].astype(f32) + scale * g - (scale * scale * scale * centre) * residual
        low = residual_grad.astype(bf16)
        s.behind[...] = residual_grad
        for g_at in range(groups):
            s.grad_here[g_at] = contract(low, s.out_w[g_at], 1, 1).astype(bf16)

    def out_grad():
        low = s.behind[...].astype(bf16)
        for g_at in range(groups):
            s.out_wg[g_at] = contract(mixed_of(g_at), low, 0, 0).astype(bf16)

    return begin, block, end, out_grad


def attention_back_tasks(s, r):
    heads, length = s.dot.shape[0], s.dot.shape[1]
    count = length // BLK
    lane = lax.broadcasted_iota(jnp.int32, (BLK, 128), 1)
    low_half = lane < HEAD_DIM
    tasks = []

    def probs_copy(h, block):
        at = (h * count + block) % 2
        rows = pl.ds(block * BLK, BLK)
        return pltpu.make_async_copy(r.probs_all.at[h, rows, :], s.probs.at[at], s.probs_sem.at[at])

    def prepare():
        probs_copy(0, 0).start()
        probs_copy(0, 1).start()

        def body(step, carry):
            rows = pl.ds(pl.multiple_of(step * BLK, BLK), BLK)
            for h in range(heads):
                cols = slice(0, 128) if h < 2 else slice(128, 256)
                mine = ~low_half if h == 1 else low_half
                if h < 2:
                    grad = s.mixed_grad[step, :, 0:128].astype(f32)
                    mix = r.mixed[rows, 0:128].astype(f32)
                else:
                    fill = jnp.zeros((BLK, HEAD_DIM), f32)
                    grad = jnp.concatenate((s.mixed_grad[step, :, 128:192].astype(f32), fill), axis=1)
                    mix = jnp.concatenate((r.mixed[rows, 128:192].astype(f32), fill), axis=1)
                grad = jnp.where(mine, grad * r.inverse[rows, cols], 0.0)
                centre = -jnp.sum(grad * mix, axis=1, keepdims=True)
                high = centre.astype(bf16).astype(f32)
                base = 0 if h == 1 else HEAD_DIM
                grad = jnp.where(lane == base, high, grad)
                grad = jnp.where(lane == base + 1, centre - high, grad)
                low = grad.astype(bf16)
                s.dot[h, rows, :] = low
                s.dott[h, :, rows] = low.T
            return carry

        lax.fori_loop(0, count, body, 0)

    tasks.append(prepare)

    def block_step(h, block):
        if block == 0:
            s.near[...] = jnp.zeros_like(s.near)
            s.far[...] = jnp.zeros_like(s.far)
            s.dkt[...] = jnp.zeros_like(s.dkt)
            s.dvt[...] = jnp.zeros_like(s.dvt)
        probs_copy(h, block).wait()
        at = (h * count + block) % 2
        rows = slice(block * BLK, (block + 1) * BLK)
        d_h = s.dot[h, rows, :]
        dt_h = s.dott[h, :, rows]
        qt_h = r.qt[h, :, rows]
        query_grad = jnp.zeros((BLK, 128), f32)
        for key in key_range(block, count):
            cols = slice(key * BLK, (key + 1) * BLK)
            probs = s.probs[at, :, cols]
            slope = jnp.dot(d_h, r.vt[h, :, cols], preferred_element_type=f32)
            grad = probs.astype(f32) * slope
            low = grad.astype(bf16)
            delta = key - block
            if abs(delta) == 2:
                s.far[0 if delta < 0 else 1] += grad[:, :128] + grad[:, 128:]
            else:
                s.near[:, (delta + 1) * BLK : (delta + 2) * BLK] += grad
            query_grad = query_grad + jnp.dot(low, r.k[h, cols, :], preferred_element_type=f32)
            s.dkt[:, cols] += jnp.dot(qt_h, low, preferred_element_type=f32)
            s.dvt[:, cols] += jnp.dot(dt_h, probs, preferred_element_type=f32)
        s.grad[rows, 0:128] = query_grad * HEAD_DIM ** (-0.5)
        turn = h * count + block + 2
        if turn < heads * count:
            probs_copy(turn // count, turn % count).start()

    def head_end(h):
        def body(step, carry):
            rows = pl.ds(pl.multiple_of(step * BLK, BLK), BLK)
            s.grad[rows, 128:256] = s.dkt[:, rows].T
            s.grad[rows, 256:384] = s.dvt[:, rows].T
            for at in range(3):
                part = s.grad[rows, 128 * at : 128 * at + 128]
                if h == 0:
                    s.joined[rows, 256 * at : 256 * at + 128] = part.astype(bf16)
                elif h == 1:
                    before = s.joined[rows, 256 * at : 256 * at + 128].astype(f32)
                    s.joined[rows, 256 * at : 256 * at + 128] = jnp.where(low_half, before, part).astype(bf16)
                else:
                    s.joined[rows, 256 * at + 128 : 256 * at + 256] = jnp.where(low_half, part, 0.0).astype(bf16)
            return carry

        lax.fori_loop(0, count, body, 0)
        place = lax.broadcasted_iota(jnp.int32, (BLK, 3 * BLK), 1) - BLK
        place = place - lax.broadcasted_iota(jnp.int32, (BLK, 3 * BLK), 0)
        s.bucket[...] = bucket_of(place)
        s.table[...] = jnp.zeros_like(s.table)

        def count_bucket(b, carry):
            part = jnp.sum(jnp.where(s.bucket[...] == b, s.near[...], 0.0), axis=0, keepdims=True)
            folded = part[:, 0:128]
            for at in range(1, 6):
                folded = folded + part[:, at * 128 : (at + 1) * 128]
            s.table[pl.ds(b, 1), :] = folded
            return carry

        lax.fori_loop(0, BUCKETS, count_bucket, 0)
        for side, b in ((0, 15), (1, 31)):
            s.table[b : b + 1, :] += jnp.sum(s.far[side], axis=0, keepdims=True)
        flat = lax.dot_general(
            jnp.ones((8, 128), f32), s.table[...], (((1,), (1,)), ((), ())),
            preferred_element_type=f32, precision=lax.Precision.HIGHEST,
        )
        s.small_mine[8 + h : 9 + h, 0:BUCKETS] = flat[0:1]

    for h in range(heads):
        for block in range(count):
            tasks.append(functools.partial(block_step, h, block))
        tasks.append(functools.partial(head_end, h))

    def rows_grad(block):
        rows = slice(block * BLK, (block + 1) * BLK)
        part = jnp.dot(s.joined[rows, :], s.w[...], preferred_element_type=f32)
        s.back_acc[block] = part.astype(bf16)
        s.gain[...] += jnp.sum(part * r.normed[rows, :].astype(f32), axis=0, keepdims=True)

    def weights_grad(at):
        part = contract(s.joined[:, 256 * at : 256 * at + 256], r.normed[...], 0, 0)
        s.qkv_wg[192 * at : 192 * at + 192, :] = part[0:192].astype(bf16)

    return tasks, rows_grad, weights_grad


REST_OPERANDS = tuple(dict(
    gate_all=0, up_all=0, down_all=0, out_all=0, probs_all=0, wq=0, wk=0, wv=0, mixed_here=0, hidden_in=0,
    cot=0, gains=0, mixed=0, inverse=0, qt=0, k=0, vt=0, normed=0,
))
REST_RESULTS = tuple(dict(
    output=0, input_grad=0, small_sum=0, out_sum=0, gate_sum=0, up_sum=0, down_sum=0, qkv_sum=0,
))


def load_weights(s, r, b, slot):
    pairs = ((r.gate_all, s.gate_w), (r.up_all, s.up_w), (r.down_all, s.down_w))
    return [
        pltpu.make_async_copy(src.at[b], dst.at[slot], s.weight_sem.at[i, slot]) for i, (src, dst) in enumerate(pairs)
    ]


def load_small(s, r):
    copies = [pltpu.make_async_copy(r.out_all, s.out_w, s.first_sem.at[0])]
    for place, ref in enumerate((r.wq, r.wk, r.wv)):
        part = ref.shape[0]
        copies.append(pltpu.make_async_copy(ref, s.w.at[pl.ds(256 * place, part), :], s.first_sem.at[1 + place]))
    return copies


def start_all(s, r):
    groups = s.out_w.shape[0]
    for copy in load_small(s, r) + load_weights(s, r, 0, 0):
        copy.start()
    s.small_mine[...] = jnp.zeros_like(s.small_mine)
    s.gain[...] = jnp.zeros_like(s.gain)
    for place in range(3):
        s.w[256 * place + 192 : 256 * place + 256, :] = jnp.zeros((64, s.w.shape[1]), bf16)
    return groups


def input_grad_rows(s, r, back):
    rows = r.hidden_in[...].astype(f32)
    scale = mean_square_scale(rows)
    g = back * r.gains[0:1, :]
    centre = jnp.mean(g * rows, axis=-1, keepdims=True)
    r.input_grad[...] = (s.behind[...] + scale * g - (scale * scale * scale * centre) * rows).astype(bf16)


def add_rows(target, start, size, source):
    step = 32 if size % 32 == 0 else 16

    def body(i, carry):
        at = pl.multiple_of(i * step, step)
        rows = pl.ds(pl.multiple_of(start + at, 16), step)
        target[rows, :] = (target[rows, :].astype(f32) + source[pl.ds(at, step), :].astype(f32)).astype(bf16)
        return carry

    lax.fori_loop(0, size // step, body, 0)


def rest_kernel(names, *refs):
    r = Named(REST_OPERANDS + REST_RESULTS, refs)
    s = Named(names, refs[len(REST_OPERANDS) + len(REST_RESULTS) :])
    dp, line, core, x, y, flips = places()
    units, width = s.down_wg.shape[1:]
    part = s.out_wg.shape[1]
    items = weight_items(units, part, width)
    item_count = len(items)
    grads = (s.gate_wg, s.up_wg, s.down_wg, s.out_wg, s.qkv_wg)
    sums = (r.gate_sum, r.up_sum, r.down_sum, r.out_sum, r.qkv_sum)
    begin_unit, unit_block, end_unit, out_grad = unit_parts(s, r)
    tasks, rows_grad, weights_grad = attention_back_tasks(s, r)
    groups = start_all(s, r)
    greet(dp, line, flips)

    def item_of(i, block):
        if i < item_count - 1:
            return items[i]
        if i == item_count - 1:
            return Item(3, 0, part, block > 1, True)
        turn = i - item_count
        return Item(4, turn * part, part, turn % 2 == 0, True)

    def lead(i, block):
        return block if i < item_count else None

    def number(i, block):
        return i * groups + block if i < item_count else (item_count - 1) * groups + i - 1

    def at_block(ref, i, block):
        return ref.at[block] if i < item_count else ref

    def arrival(stage, i, block):
        return at_block(getattr(s, stage + str(i)), i, block)

    def held(i, block):
        item = item_of(i, block)
        if item.by_columns:
            return arrival("half", i, block), 0, item.rows
        return grads[item.place].at[block], item.base + core * (item.rows // 2), item.rows // 2

    def load_copy(i, block):
        item = item_of(i, block)
        window = item.window(grads[item.place], lead(i, block), 1, core, 0, 0)
        return pltpu.make_async_copy(window, arrival("half", i, block), s.load_sem.at[number(i, block)])

    def core_copy(i, block):
        item, n = item_of(i, block), number(i, block)
        window = item.window(grads[item.place], lead(i, block), 1, 1 - core, 0, 0)
        return remote(window, arrival("core", i, block), s.core_send.at[n], s.core_recv.at[n], (flips[0], line))

    def begin(i, block):
        core_copy(i, block).start()
        if item_of(i, block).by_columns:
            load_copy(i, block).start()

    def pair_copy(i, block, stage):
        ref, base, half = held(i, block)
        item, n = item_of(i, block), number(i, block)
        first, second = item.bits(x, y)
        if stage == 0:
            size, start, target = half // 2, (1 - first) * (half // 2), arrival("first", i, block)
        else:
            size = half // 4
            start, target = first * (half // 2) + (1 - second) * (half // 4), arrival("second", i, block)
        window = ref.at[pl.ds(pl.multiple_of(base + start, 16), size), :]
        partner = item.partner(1 + stage, flips)
        return remote(window, target, s.pair_send.at[stage, n], s.pair_recv.at[stage, n], (partner, line))

    def eighth(i, block):
        ref, base, half = held(i, block)
        first, second = item_of(i, block).bits(x, y)
        start = pl.multiple_of(base + first * (half // 2) + second * (half // 4), 16)
        return ref, start, half // 4

    def mine(i, block):
        ref, start, size = eighth(i, block)
        return ref.at[pl.ds(start, size), :]

    def line_copy(i, block, sender):
        target = getattr(s, "line" + str(i)).at[sender]
        return remote(
            mine(i, block), target, s.line_send.at[i, block], s.line_recv.at[i, sender], (dp, block)
        )

    def spread_copy(i, block, stage):
        item, n = item_of(i, block), number(i, block)
        first, second = item.bits(x, y)
        window = item.window(sums[item.place], None, 3 - stage, core, first, second)
        src = mine(i, block) if stage == 0 else window
        return remote(
            src, window, s.spread_send.at[stage, n], s.spread_recv.at[stage, n],
            (item.partner(2 - stage, flips), line),
        )

    def keep_copy(i, block):
        item = item_of(i, block)
        first, second = item.bits(x, y)
        window = item.window(sums[item.place], None, 3, core, first, second)
        return pltpu.make_async_copy(mine(i, block), window, s.load_sem.at[number(i, block)])

    def step_core(i, block, send=True):
        if item_of(i, block).by_columns:
            load_copy(i, block).wait()
        core_copy(i, block).wait_recv()
        ref, base, half = held(i, block)
        add_rows(ref, base, half, arrival("core", i, block))
        if send:
            pair_copy(i, block, 0).start()

    def step_first(i, block):
        pair_copy(i, block, 0).wait_recv()
        ref, base, half = held(i, block)
        first, _ = item_of(i, block).bits(x, y)
        add_rows(ref, base + first * (half // 2), half // 2, arrival("first", i, block))
        pair_copy(i, block, 1).start()

    def step_second(i, block):
        pair_copy(i, block, 1).wait_recv()
        ref, start, size = eighth(i, block)
        add_rows(ref, start, size, arrival("second", i, block))
        if i < item_count:
            pl.when(line != block)(lambda: line_copy(i, block, line).start())
        else:
            spread_copy(i, block, 0).start()
            keep_copy(i, block).start()

    def step_last(i, block):
        @pl.when(line == block)
        def _():
            ref, start, size = eighth(i, block)
            others = [o for o in range(groups) if o != block]
            for o in others:
                line_copy(i, block, o).wait_recv()
            arrived = getattr(s, "line" + str(i))
            total = ref[pl.ds(start, size), :].astype(f32)
            for o in others:
                total = total + arrived[o].astype(f32)
            ref[pl.ds(start, size), :] = total.astype(bf16)
            spread_copy(i, block, 0).start()
            keep_copy(i, block).start()

    def step_spread(i, block, stage):
        def act():
            if stage == 1:
                keep_copy(i, block).wait()
            spread_copy(i, block, stage - 1).wait_recv()
            if stage < 3:
                spread_copy(i, block, stage).start()

        if i < item_count:
            pl.when(line == block)(act)
        else:
            act()

    def swap_copy(i, sender_is_me):
        other = lax.rem(line + i, 4)
        if sender_is_me:
            return remote(
                s.grad_here.at[other], s.mixed_grad.at[line], s.swap_send.at[i - 1], s.swap_recv.at[3 - i], (dp, other)
            )
        return remote(
            s.grad_here.at[other], s.mixed_grad.at[other], s.swap_send.at[i - 1], s.swap_recv.at[i - 1], (dp, other)
        )

    def back_copy(block, at, right):
        src, send = s.back_acc.at[block], s.back_send.at[block]
        if right:
            return remote(src, s.back_left.at[block], send, s.back_left_recv.at[block], (dp, at + 1))
        return remote(src, s.back_right.at[block], send, s.back_right_recv.at[block], (dp, at - 1))

    def back_hop(hop, distance):
        @pl.when(line == hop)
        def _():
            block = hop + distance
            if block <= groups - 1:
                if hop > 0:
                    back_copy(block, hop, True).wait_recv()
                    add_rows(s.back_acc.at[block], 0, s.back_acc.shape[1], s.back_left.at[block])
                back_copy(block, hop, True).start()

        at = groups - 1 - hop

        @pl.when(line == at)
        def _():
            block = at - distance
            if block >= 0:
                if hop > 0:
                    back_copy(block, at, False).wait_recv()
                    add_rows(s.back_acc.at[block], 0, s.back_acc.shape[1], s.back_right.at[block])
                back_copy(block, at, False).start()

    def collect_rows():
        for block in range(groups):
            @pl.when(line == block)
            def _(block=block):
                total = s.back_acc[block].astype(f32)
                if block > 0:
                    back_copy(block, block, True).wait_recv()
                    total = total + s.back_left[block].astype(f32)
                if block < groups - 1:
                    back_copy(block, block, False).wait_recv()
                    total = total + s.back_right[block].astype(f32)
                input_grad_rows(s, r, total)

    def small_copy(stage):
        partner = (flips[stage], line) if stage < 3 else (dp, line + 1 - 2 * lax.rem(line, 2))
        if stage == 4:
            partner = (dp, lax.rem(line + 2, 4))
        return remote(s.small_mine, s.small_got.at[stage], s.small_send.at[stage], s.small_recv.at[stage], partner)

    def small_step(stage):
        if stage > 0:
            small_copy(stage - 1).wait()
            rows = lax.broadcasted_iota(jnp.int32, s.small_mine.shape, 0)
            got = s.small_got[stage - 1]
            if stage > 3:
                got = jnp.where(rows < 8, got, 0.0)
            s.small_mine[...] = s.small_mine[...] + got
        else:
            s.small_mine[0:1, :] = s.gain[...] / r.gains[0:1, :]
        if stage < 5:
            small_copy(stage).start()
        else:
            r.small_sum[...] = s.small_mine[...]

    outer, inner = (0, groups - 1), tuple(range(1, groups - 1))
    teams = [[(i, block) for i in (0, 1)] for block in outer + inner]
    teams += [[(i, block) for block in pair for i in (2, 3)] for pair in (outer, inner)]
    teams.append([(item_count - 1, block) for block in range(groups)])
    teams.append([(item_count + turn, 0) for turn in range(3)])
    stage_acts = (
        step_core, step_first, step_second, step_last,
        lambda i, block: step_spread(i, block, 1),
        lambda i, block: step_spread(i, block, 2),
        lambda i, block: step_spread(i, block, 3),
    )
    done = []

    def tend(moment):
        for name, team in WHEN.get(moment, ()):
            done.append((name, team))
            if name == SMALL:
                small_step(team)
            elif name == ROWS:
                collect_rows()
            elif name == HOP:
                back_hop(*team)
            else:
                for i, block in teams[team]:
                    stage_acts[name](i, block)

    for copy in load_small(s, r):
        copy.wait()
    begin_unit()

    order = outer + inner
    for turn, block in enumerate(order):
        for copy in load_weights(s, r, block, turn % 2):
            copy.wait()
        if turn + 1 < groups:
            for copy in load_weights(s, r, order[turn + 1], (turn + 1) % 2):
                copy.start()
        unit_block(block, turn % 2)
        for i in range(item_count - 1):
            begin(i, block)
        tend(UNIT + turn)
    end_unit()
    for i in (2, 1, 3):
        swap_copy(i, True).start()
    swap_keep = pltpu.make_async_copy(s.grad_here.at[line], s.mixed_grad.at[line], s.swap_keep)
    swap_keep.start()
    out_grad()
    for block in range(groups):
        begin(item_count - 1, block)
    tend(SWAP)
    for i in (1, 2, 3):
        swap_copy(i, False).wait_recv()
        swap_copy(i, True).wait_send()
    swap_keep.wait()
    for turn, task in enumerate(tasks):
        task()
        tend(turn)
    for block in range(groups):
        rows_grad(block)
    for distance in (3, 2, 1):
        back_hop(0, distance)
    for turn in range(3):
        weights_grad(turn)
        begin(item_count + turn, 0)
    small_step(0)

    for turn in range(len(WHEN)):
        tend(END + turn)
    assert len(done) == len(set(done)) == 7 * 7 + 6 + 5 + 4
    for block in range(groups):
        pl.when(line < block)(lambda block=block: back_copy(block, line, True).wait_send())
        pl.when(line > block)(lambda block=block: back_copy(block, line, False).wait_send())
    for i, block in sum(teams, []):
        core_copy(i, block).wait_send()
        pair_copy(i, block, 0).wait_send()
        pair_copy(i, block, 1).wait_send()

        def sent(i=i, block=block):
            for stage in range(3):
                spread_copy(i, block, stage).wait_send()

        if i < item_count:
            pl.when(line == block)(sent)
            pl.when(line != block)(lambda i=i, block=block: line_copy(i, block, line).wait_send())
        else:
            sent()


CORE, FIRST, SECOND, LAST, SPREAD1, SPREAD2, SPREAD3, SMALL, HOP, ROWS = range(10)
UNIT, SWAP, END = 100, 110, 120
WHEN = {
    UNIT + 1: [(CORE, 0), (CORE, 1)],
    UNIT + 3: [(FIRST, 0), (CORE, 2), (FIRST, 1), (CORE, 3)],
    SWAP: [(SECOND, 0), (FIRST, 2), (CORE, 4), (SECOND, 1)],
    0: [(FIRST, 3), (CORE, 5), (SECOND, 2)],
    3: [(FIRST, 4), (CORE, 6), (SECOND, 3)],
    5: [(LAST, 0), (LAST, 1)],
    7: [(FIRST, 5), (SECOND, 4), (SPREAD1, 0), (SPREAD1, 1)],
    9: [(LAST, 2)],
    11: [(FIRST, 6), (SECOND, 5), (LAST, 3), (SPREAD2, 0), (SPREAD2, 1)],
    13: [(SPREAD1, 2), (SECOND, 6)],
    14: [(LAST, 4), (SPREAD1, 3), (SPREAD3, 0), (SPREAD3, 1), (SPREAD2, 2)],
    END + 0: [(CORE, 7), (LAST, 5), (SPREAD1, 4), (SPREAD2, 3)],
    END + 1: [(SMALL, 1), (HOP, (1, 2)), (FIRST, 7), (LAST, 6), (SPREAD3, 2), (SPREAD1, 5)],
    END + 2: [(SMALL, 2), (HOP, (1, 1)), (SECOND, 7), (SPREAD1, 6), (SPREAD2, 4), (SPREAD3, 3)],
    END + 3: [(SMALL, 3), (HOP, (2, 1)), (SPREAD1, 7), (SPREAD2, 5), (SPREAD2, 6)],
    END + 4: [(SMALL, 4), (SPREAD2, 7), (SPREAD3, 4), (SPREAD3, 5), (SPREAD3, 6)],
    END + 5: [(SMALL, 5), (SPREAD3, 7), (ROWS, 0)],
}

def common_scratch(groups, rows, heads, length, width, units, part):
    dma = pltpu.SemaphoreType.DMA
    return dict(
        residual=pltpu.VMEM((rows, width), f32),
        normed2=pltpu.VMEM((rows, width), bf16),
        ahead=pltpu.VMEM((rows, width), f32),
        behind=pltpu.VMEM((rows, width), f32),
        out_w=pltpu.VMEM((groups, part, width), bf16),
        gate_w=pltpu.VMEM((2, width, units), bf16),
        up_w=pltpu.VMEM((2, width, units), bf16),
        down_w=pltpu.VMEM((2, units, width), bf16),
        gate_wg=pltpu.VMEM((groups, width, units), bf16),
        up_wg=pltpu.VMEM((groups, width, units), bf16),
        down_wg=pltpu.VMEM((groups, units, width), bf16),
        out_wg=pltpu.VMEM((groups, part, width), bf16),
        qkv_wg=pltpu.VMEM((3 * part, width), bf16),
        grad_here=pltpu.VMEM((groups, rows, part), bf16),
        mixed_grad=pltpu.VMEM((groups, rows, part), bf16),
        back_acc=pltpu.VMEM((groups, rows, width), bf16),
        small_mine=pltpu.VMEM((16, width), f32),
        gain=pltpu.VMEM((1, width), f32),
        probs=pltpu.VMEM((2, BLK, length), bf16),
        w=pltpu.VMEM((768, width), bf16),
        dot=pltpu.VMEM((heads, length, 128), bf16),
        dott=pltpu.VMEM((heads, 128, length), bf16),
        grad=pltpu.VMEM((length, 384), f32),
        joined=pltpu.VMEM((length, 768), bf16),
        near=pltpu.VMEM((BLK, 3 * BLK), f32),
        bucket=pltpu.VMEM((BLK, 3 * BLK), jnp.int32),
        table=pltpu.VMEM((BUCKETS, 128), f32),
        far=pltpu.VMEM((2, BLK, 128), f32),
        dkt=pltpu.VMEM((128, length), f32),
        dvt=pltpu.VMEM((128, length), f32),
        weight_sem=dma((3, 2)), first_sem=dma((4,)), probs_sem=dma((2,)),
    )


def result_shapes(rows, width, units, part):
    return (
        jax.ShapeDtypeStruct((rows, width), bf16),
        jax.ShapeDtypeStruct((rows, width), bf16),
        jax.ShapeDtypeStruct((16, width), f32),
        jax.ShapeDtypeStruct((part, width), bf16),
        jax.ShapeDtypeStruct((width, units), bf16),
        jax.ShapeDtypeStruct((width, units), bf16),
        jax.ShapeDtypeStruct((units, width), bf16),
        jax.ShapeDtypeStruct((3 * part, width), bf16),
    )


def rest_all(gate_all, up_all, down_all, out_all, probs, wq, wk, wv, mixed_here, hidden_in, cot, gains,
             mixed, inverse, qt, k, vt, normed):
    groups, part = mixed_here.shape[1], wq.shape[0]
    rows, width = hidden_in.shape
    heads, length = k.shape[0], k.shape[1]
    units = down_all.shape[1]
    items = weight_items(units, part, width)
    n = 3 + groups * len(items)
    dma = pltpu.SemaphoreType.DMA
    scratch = common_scratch(groups, rows, heads, length, width, units, part)
    for stage, divide in (("half", 1), ("core", 1), ("first", 2), ("second", 4), ("line", 4)):
        for i, item in enumerate(items):
            cols = (units, units, width, width)[item.place]
            shape = (item.rows, cols // 2) if item.by_columns else (item.rows // 2, cols)
            if stage != "half" or item.by_columns:
                scratch[stage + str(i)] = pltpu.VMEM((groups, shape[0] // divide, shape[1]), bf16)
        for turn in range(3):
            if stage != "line":
                scratch[stage + str(len(items) + turn)] = pltpu.VMEM((part // divide, width // 2), bf16)
    scratch.update(
        small_got=pltpu.VMEM((5, 16, width), f32),
        back_left=pltpu.VMEM((groups, rows, width), bf16),
        back_right=pltpu.VMEM((groups, rows, width), bf16),
        load_sem=dma((n,)), core_send=dma((n,)), core_recv=dma((n,)),
        pair_send=dma((2, n)), pair_recv=dma((2, n)),
        line_send=dma((len(items), groups)), line_recv=dma((len(items), groups)),
        spread_send=dma((3, n)), spread_recv=dma((3, n)),
        back_send=dma((groups,)), back_left_recv=dma((groups,)), back_right_recv=dma((groups,)),
        small_send=dma((5,)), small_recv=dma((5,)),
        swap_send=dma((3,)), swap_recv=dma((3,)), swap_keep=dma,
    )
    anywhere = pl.BlockSpec(memory_space=pl.ANY)
    inside = pl.BlockSpec(memory_space=pltpu.VMEM)
    return pl.pallas_call(
        functools.partial(rest_kernel, tuple(scratch)),
        name="rest_all",
        out_shape=result_shapes(rows, width, units, part),
        in_specs=[anywhere] * 8 + [inside] * 10,
        out_specs=(inside,) * 3 + (anywhere,) * 5,
        scratch_shapes=list(scratch.values()),
        compiler_params=pltpu.CompilerParams(
            collective_id=3, has_side_effects=True, vmem_limit_bytes=62 << 20
        ),
    )(gate_all, up_all, down_all, out_all, probs, wq, wk, wv, mixed_here, hidden_in, cot, gains,
      mixed, inverse, qt, k, vt, normed)


UNIT_RESULTS = tuple(dict(
    output=0, residual_grad=0, grads=0, gain2_grad=0, out_out=0, gate_out=0, up_out=0, down_out=0,
))


def unit_local_kernel(names, *refs):
    operands = tuple(dict(gate_all=0, up_all=0, down_all=0, out_all=0, mixed_here=0, hidden_in=0, cot=0, gains=0))
    r = Named(operands + UNIT_RESULTS, refs)
    s = Named(names, refs[len(operands) + len(UNIT_RESULTS) :])
    s.out_wg, s.gate_wg, s.up_wg, s.down_wg = r.out_out, r.gate_out, r.up_out, r.down_out
    s.behind, s.grad_here = r.residual_grad, r.grads
    begin, block, end, out_grad = unit_parts(s, r)
    groups = s.out_w.shape[0]
    first = [pltpu.make_async_copy(r.out_all, s.out_w, s.first_sem.at[0])] + load_weights(s, r, 0, 0)
    for copy in first:
        copy.start()
    first[0].wait()
    begin()

    def body(b, carry):
        slot = lax.rem(b, 2)
        for copy in load_weights(s, r, b, slot):
            copy.wait()

        @pl.when(b + 1 < groups)
        def _():
            for copy in load_weights(s, r, b + 1, 1 - slot):
                copy.start()

        block(b, slot)
        return carry

    lax.fori_loop(0, groups, body, 0)
    end()
    out_grad()
    r.gain2_grad[...] = s.small_mine[1:2, :]


def back_local_kernel(names, *refs):
    operands = tuple(dict(probs_all=0, mixed=0, inverse=0, qt=0, k=0, vt=0, normed=0, wq=0, wk=0, wv=0, gains=0, mixed_grad=0))
    results = tuple(dict(back_out=0, qkv_out=0, small_out=0))
    r = Named(operands + results, refs)
    s = Named(names, refs[len(operands) + len(results) :])
    s.mixed_grad, s.qkv_wg, s.small_mine, s.back_acc = r.mixed_grad, r.qkv_out, r.small_out, r.back_out
    tasks, rows_grad, weights_grad = attention_back_tasks(s, r)
    s.small_mine[...] = jnp.zeros_like(s.small_mine)
    s.gain[...] = jnp.zeros_like(s.gain)
    s.w[...] = jnp.zeros_like(s.w)
    for place, ref in enumerate((r.wq, r.wk, r.wv)):
        s.w[256 * place : 256 * place + ref.shape[0], :] = ref[...]
    for task in tasks:
        task()
    for block in range(r.back_out.shape[0]):
        rows_grad(block)
    for turn in range(3):
        weights_grad(turn)
    s.small_mine[0:1, :] = s.gain[...] / r.gains[0:1, :]


def rest_by_axis(gate_all, up_all, down_all, out_all, probs, wq, wk, wv, mixed_here, hidden_in, cot, gains,
                 mixed, inverse, qt, k, vt, normed):
    groups, part = mixed_here.shape[1], wq.shape[0]
    rows, width = hidden_in.shape
    heads, length = k.shape[0], k.shape[1]
    units = down_all.shape[1]
    anywhere = pl.BlockSpec(memory_space=pl.ANY)
    inside = pl.BlockSpec(memory_space=pltpu.VMEM)
    every = common_scratch(groups, rows, heads, length, width, units, part)
    pick = lambda names: {name: every[name] for name in names}
    shape = jax.ShapeDtypeStruct
    scratch = pick(dict(
    residual=0, normed2=0, ahead=0, out_w=0, gate_w=0, up_w=0, down_w=0, small_mine=0, weight_sem=0,
    first_sem=0,
    ))
    output, residual_grad, grads, gain2_grad, out_wg, gate_wg, up_wg, down_wg = pl.pallas_call(
        functools.partial(unit_local_kernel, tuple(scratch)),
        name="unit_local",
        out_shape=(
            shape((rows, width), bf16), shape((rows, width), f32), shape((groups, rows, part), bf16),
            shape((1, width), f32), shape((groups, part, width), bf16), shape((groups, width, units), bf16),
            shape((groups, width, units), bf16), shape((groups, units, width), bf16),
        ),
        in_specs=[anywhere] * 4 + [inside] * 4,
        out_specs=(inside,) * 8,
        scratch_shapes=list(scratch.values()),
        compiler_params=pltpu.CompilerParams(vmem_limit_bytes=56 << 20),
    )(gate_all, up_all, down_all, out_all, mixed_here, hidden_in, cot, gains)
    mixed_grad = lax.all_to_all(grads, "tensor", 0, 0)
    scratch = pick(dict(
    gain=0, probs=0, w=0, dot=0, dott=0, grad=0, joined=0, near=0, bucket=0, table=0, far=0, dkt=0, dvt=0,
    probs_sem=0,
    ))
    back, qkv_wg, small = pl.pallas_call(
        functools.partial(back_local_kernel, tuple(scratch)),
        name="back_local",
        out_shape=(
            shape((groups, rows, width), bf16), shape((3 * part, width), bf16), shape((16, width), f32),
        ),
        in_specs=[anywhere] + [inside] * 11,
        out_specs=(inside,) * 3,
        scratch_shapes=list(scratch.values()),
        compiler_params=pltpu.CompilerParams(vmem_limit_bytes=56 << 20),
    )(probs, mixed, inverse, qt, k, vt, normed, wq, wk, wv, gains, mixed_grad)
    back_sum = lax.psum_scatter(back, "tensor", scatter_dimension=0).astype(f32)
    parts = tuple(lax.psum_scatter(wg, "tensor", scatter_dimension=0) for wg in (out_wg, gate_wg, up_wg, down_wg))
    sums = lax.psum(parts + (qkv_wg,), "dp")
    small = small.at[1].set(gain2_grad[0])
    small_sum = lax.psum(small, "dp")
    gains = lax.psum(small_sum[:8], "tensor")
    input_rows = hidden_in.astype(f32)
    r1 = mean_square_scale(input_rows)
    g1 = back_sum * gains[0:1]
    centre = jnp.mean(g1 * input_rows, axis=-1, keepdims=True)
    input_grad = (residual_grad + r1 * g1 - (r1 * r1 * r1 * centre) * input_rows).astype(bf16)
    return (output, input_grad, jnp.concatenate((gains, small_sum[8:]))) + tuple(sums)


def finish_kernel(*refs):
    half = len(refs) // 2
    for source, target in zip(refs[:half], refs[half:]):
        target[...] = source[...].astype(target.dtype)


def finish(output, input_grad, qkv_sum, out_sum, gate_sum, up_sum, down_sum):
    part, width = out_sum.shape
    steps = 4
    block = lambda a, at: pl.BlockSpec((a // steps, at), lambda i: (i, 0))
    shift = lambda turn: pl.BlockSpec((part // steps, width), lambda i: (i + turn * steps, 0))
    arrays = (output, input_grad, qkv_sum, qkv_sum, qkv_sum, out_sum, gate_sum, up_sum, down_sum)
    shapes = [output.shape, input_grad.shape] + [out_sum.shape] * 4 + [gate_sum.shape, up_sum.shape, down_sum.shape]
    kinds = [bf16] * 2 + [f32] * 7
    specs = [block(*shape) for shape in shapes]
    return pl.pallas_call(
        finish_kernel,
        grid=(steps,),
        name="finish",
        out_shape=tuple(jax.ShapeDtypeStruct(s, k) for s, k in zip(shapes, kinds)),
        in_specs=specs[:2] + [shift(turn) for turn in range(3)] + specs[5:],
        out_specs=tuple(specs),
        compiler_params=pltpu.CompilerParams(dimension_semantics=("arbitrary",), vmem_limit_bytes=62 << 20),
    )(*arrays)


def gather_by_axis(hidden_in, gains, gate, up, down, out):
    rows = hidden_in.astype(f32)
    normed = (rows * mean_square_scale(rows) * gains[0:1]).astype(bf16)
    return tuple(lax.all_gather(part, "tensor", axis=0) for part in (normed, gate, up, down, out))


def shards(
    by_kernel,
    hidden_in, segment_ids, norm1_gain, query_weight, key_weight, value_weight, out_weight,
    bias_table, norm2_gain, gate_weight, up_weight, down_weight, out_cotangent,
):
    gather_parts = gather if by_kernel else gather_by_axis
    rest_parts = rest_all if by_kernel else rest_by_axis
    rows_here, width = hidden_in.shape
    length = segment_ids.shape[1]
    assert segment_ids.shape[0] == 1 and rows_here == BLK
    heads = bias_table.shape[1]
    gains = jnp.stack((norm1_gain, norm2_gain)).astype(f32)
    normed, gate_w, up_w, down_w, out_w = gather_parts(
        hidden_in, gains, gate_weight, up_weight, down_weight, out_weight
    )
    normed = normed.reshape(length, width)
    query_weight, key_weight, value_weight = query_weight.T, key_weight.T, value_weight.T
    mixed, probs, qt, k, vt, inverse, mixed_here = attend(
        by_kernel, normed, query_weight, key_weight, value_weight, segment_ids, bias_table
    )
    if not by_kernel:
        mixed_here = lax.all_to_all(mixed_here, "tensor", 1, 1)
    output, input_grad, small_sum, out_sum, gate_sum, up_sum, down_sum, qkv_sum = rest_parts(
        gate_w, up_w, down_w, out_w, probs, query_weight, key_weight, value_weight, mixed_here, hidden_in,
        out_cotangent, gains, mixed, inverse, qt, k, vt, normed,
    )
    output, input_grad, query_grad, key_grad, value_grad, out_grad, gate_grad, up_grad, down_grad = finish(
        output, input_grad, qkv_sum, out_sum, gate_sum, up_sum, down_sum
    )
    return (
        output, input_grad, small_sum[0], query_grad.T, key_grad.T, value_grad.T, out_grad,
        small_sum[8 : 8 + heads, :BUCKETS].T, small_sum[1], gate_grad, up_grad, down_grad,
    )


def solution(mesh):
    in_specs = (
        P(("dp", "tensor"), None), P("dp", None), P(),
        P(None, "tensor"), P(None, "tensor"), P(None, "tensor"), P("tensor", None),
        P(None, "tensor"), P(), P(None, "tensor"), P(None, "tensor"), P("tensor", None),
        P(("dp", "tensor"), None),
    )
    out_specs = (
        P(("dp", "tensor"), None), P(("dp", "tensor"), None), P(),
        P(None, "tensor"), P(None, "tensor"), P(None, "tensor"), P("tensor", None),
        P(None, "tensor"), P(), P(None, "tensor"), P(None, "tensor"), P("tensor", None),
    )
    by_kernel = mesh.shape["dp"] == 8 and mesh.shape["tensor"] == 4
    return jax.shard_map(
        functools.partial(shards, by_kernel), mesh=mesh, in_specs=in_specs, out_specs=out_specs, check_vma=False
    )
```

```python
import functools

import jax
import jax.numpy as jnp
from jax import lax
from jax.experimental import pallas as pl
from jax.experimental.pallas import tpu as pltpu
from jax.sharding import PartitionSpec as P

HEAD_DIM = 64
BUCKETS = 32
far_marks = (12, 16, 23, 32, 46, 64, 91)
norm_eps = 1e-06
far_score = 2.0**30
BLK = 256
f32 = jnp.float32
bf16 = jnp.bfloat16


def bucket_of(offset):
    magnitude = jnp.abs(offset)
    within = jnp.minimum(magnitude, 8)
    for far_mark in far_marks:
        within = within + (magnitude >= far_mark).astype(jnp.int32)
    return within + jnp.where(offset > 0, 16, 0).astype(jnp.int32)


def key_range(block, count):
    return range(max(0, block - 2), min(count, block + 3))


def contract(lhs, rhs, left, right):
    return lax.dot_general(
        lhs, rhs, (((left,), (right,)), ((), ())), preferred_element_type=f32
    )


def attend_kernel(
    by_kernel, normed_ref, wq_ref, wk_ref, wv_ref, seg_ref, table_ref,
    mixed_ref, probs_ref, qt_ref, k_ref, vt_ref, inv_ref, here_ref,
    w_s, kt_s, bias_s, score_s, first_s, q_s, v_s, parts_s, send_sem, recv_sem, keep_sem,
):
    head = pl.program_id(0)
    length = normed_ref.shape[0]
    count = length // BLK
    lane = lax.broadcasted_iota(jnp.int32, (BLK, 128), 1)
    low_half = lane < HEAD_DIM

    if by_kernel:
        dp, line = lax.axis_index("dp"), lax.axis_index("tensor")
        others = [lax.rem(line + i, 4) for i in (1, 2, 3)]

        barrier = pltpu.get_barrier_semaphore()

        @pl.when(head == 0)
        def _():
            for other in others:
                pl.semaphore_signal(barrier, inc=1, device_id=(dp, other), device_id_type=MESH_IDS)

        def part_copy(half, i, sender_is_me):
            place = line if sender_is_me else others[i]
            return pltpu.make_async_remote_copy(
                src_ref=parts_s.at[half, others[i]], dst_ref=here_ref.at[half, place],
                send_sem=send_sem.at[half, i], recv_sem=recv_sem.at[half, 2 - i if sender_is_me else i],
                device_id=(dp, others[i]), device_id_type=MESH_IDS,
            )

        def own_copy(half):
            return pltpu.make_async_copy(parts_s.at[half, line], here_ref.at[half, line], keep_sem.at[half])

        def send_part(half):
            for i in (1, 0, 2):
                part_copy(half, i, True).start()
            own_copy(half).start()

    @pl.when(head == 0)
    def _():
        w_s[...] = jnp.zeros_like(w_s)
        for place, ref in enumerate((wq_ref, wk_ref, wv_ref)):
            w_s[256 * place : 256 * place + 192, :] = ref[...]
        row8 = lax.broadcasted_iota(jnp.int32, (8, 128), 0)
        lane8 = lax.broadcasted_iota(jnp.int32, (8, 128), 1)
        spread = jnp.where((lane8 % HEAD_DIM) == row8, 1.0, 0.0).astype(bf16)

        def project(step, carry):
            rows = pl.ds(pl.multiple_of(step * BLK, BLK), BLK)
            seg_row = seg_ref[:, rows]
            kinds = lax.broadcasted_iota(jnp.int32, (8, BLK), 0)
            hot = jnp.where(
                jnp.broadcast_to(seg_row, (8, BLK)) == kinds, 1.0, 0.0
            ).astype(bf16)
            same = contract(hot, spread, 0, 0)
            in_aug = (lane % HEAD_DIM) < 8
            aug_q = jnp.where(in_aug, same, 0.0)
            aug_k = jnp.where(in_aug, (same - 1.0) * far_score, 0.0)
            rows_in = normed_ref[rows, :]
            q = contract(rows_in, w_s[0:256, :], 1, 1)
            k = contract(rows_in, w_s[256:512, :], 1, 1)
            v = contract(rows_in, w_s[512:768, :], 1, 1)
            scale = HEAD_DIM ** (-0.5)
            for h, (cols, mine) in enumerate(
                ((slice(0, 128), low_half), (slice(0, 128), ~low_half), (slice(128, 256), low_half))
            ):
                q_h = jnp.where(mine, q[:, cols] * scale, aug_q).astype(bf16)
                q_s[h, rows, :] = q_h
                qt_ref[h, :, rows] = q_h.T
                k_h = jnp.where(mine, k[:, cols], aug_k).astype(bf16)
                k_ref[h, rows, :] = k_h
                v_h = jnp.where(mine, v[:, cols], 1.0).astype(bf16)
                v_s[h, rows, :] = v_h
                vt_ref[h, :, rows] = v_h.T
                kt_s[h, :, rows] = k_h.T
            return carry

        lax.fori_loop(0, count, project, 0)

    offset = lax.broadcasted_iota(jnp.int32, (BUCKETS, length), 1)
    offset = jnp.where(offset >= length // 2, offset - length, offset)
    hot_bucket = jnp.where(
        bucket_of(offset) == lax.broadcasted_iota(jnp.int32, (BUCKETS, length), 0), 1.0, 0.0
    ).astype(bf16)
    by_offset = contract(table_ref[head], hot_bucket, 1, 0)[0:1]
    spread_rows = jnp.broadcast_to(by_offset, (BLK, length))
    bias_s[...] = pltpu.roll(spread_rows, 0, 1, stride=1, stride_axis=0)

    for block in range(count):
        rows = slice(block * BLK, (block + 1) * BLK)
        q_h = q_s[head, rows, :]
        top = None
        for key in key_range(block, count):
            part = jnp.dot(
                q_h, kt_s[head, :, key * BLK : (key + 1) * BLK], preferred_element_type=f32
            )
            delta = key - block
            at = (delta * BLK) % length
            part = part + bias_s[:, at : at + BLK]
            score_s[:, key * BLK : (key + 1) * BLK] = part
            top = part if top is None else jnp.maximum(top, part)
        top = jnp.max(jnp.maximum(top[:, :128], top[:, 128:]), axis=1, keepdims=True)
        total = jnp.zeros((BLK, 128), f32)
        for key in key_range(block, count):
            cols = slice(key * BLK, (key + 1) * BLK)
            part = jnp.exp(score_s[:, cols] - top).astype(bf16)
            probs_ref[0, rows, cols] = part
            total = total + jnp.dot(part, v_s[head, cols, :], preferred_element_type=f32)
        sums = pltpu.roll(total, HEAD_DIM, 1)
        inverse = 1.0 / sums
        out = total * inverse

        @pl.when(head == 0)
        def _():
            first_s[rows, 0:128] = out
            first_s[rows, 128:256] = inverse

        @pl.when(head == 1)
        def _():
            pair = jnp.where(low_half, first_s[rows, 0:128], out).astype(bf16)
            mixed_ref[rows, 0:128] = pair
            parts_s[0, block] = pair
            inv_ref[rows, 0:128] = jnp.where(low_half, first_s[rows, 128:256], inverse)

        @pl.when(head == 2)
        def _():
            mixed_ref[rows, 128:192] = out[:, 0:HEAD_DIM].astype(bf16)
            inv_ref[rows, 128:256] = inverse
            parts_s[1, block] = out.astype(bf16)

    if by_kernel:
        @pl.when(head == 1)
        def _():
            pl.semaphore_wait(barrier, 3)
            send_part(0)

        @pl.when(head == 2)
        def _():
            send_part(1)
            for half in range(2):
                own_copy(half).wait()
                for i in range(3):
                    part_copy(half, i, True).wait_send()
                    part_copy(half, i, False).wait_recv()
    else:
        @pl.when(head == 2)
        def _():
            for half in range(2):
                keep = pltpu.make_async_copy(parts_s.at[half], here_ref.at[half], keep_sem.at[half])
                keep.start()
                keep.wait()


MESH_IDS = pl.DeviceIdType.MESH


def attend(by_kernel, normed, wq, wk, wv, segments, bias_table):
    length, width = normed.shape
    heads = bias_table.shape[1]
    inner = heads * HEAD_DIM
    table = jnp.broadcast_to(bias_table.T[:, None, :], (heads, 8, BUCKETS))
    whole = lambda *dims: pl.BlockSpec(dims, lambda h: (0,) * len(dims))
    return pl.pallas_call(
        functools.partial(attend_kernel, by_kernel),
        grid=(heads,),
        name="attend",
        out_shape=(
            jax.ShapeDtypeStruct((length, inner), bf16),
            jax.ShapeDtypeStruct((heads, length, length), bf16),
            jax.ShapeDtypeStruct((heads, 128, length), bf16),
            jax.ShapeDtypeStruct((heads, length, 128), bf16),
            jax.ShapeDtypeStruct((heads, 128, length), bf16),
            jax.ShapeDtypeStruct((length, 256), f32),
            jax.ShapeDtypeStruct((2, length // BLK, BLK, 128), bf16),
        ),
        in_specs=[
            whole(length, width),
            whole(inner, width),
            whole(inner, width),
            whole(inner, width),
            whole(1, length),
            whole(heads, 8, BUCKETS),
        ],
        out_specs=(
            whole(length, inner),
            pl.BlockSpec((1, length, length), lambda h: (h, 0, 0)),
            whole(heads, 128, length),
            whole(heads, length, 128),
            whole(heads, 128, length),
            whole(length, 256),
            pl.BlockSpec(memory_space=pl.ANY),
        ),
        scratch_shapes=[
            pltpu.VMEM((768, width), bf16),
            pltpu.VMEM((heads, 128, length), bf16),
            pltpu.VMEM((BLK, length), f32),
            pltpu.VMEM((BLK, length), f32),
            pltpu.VMEM((length, 256), f32),
            pltpu.VMEM((heads, length, 128), bf16),
            pltpu.VMEM((heads, length, 128), bf16),
            pltpu.VMEM((2, length // BLK, BLK, 128), bf16),
            pltpu.SemaphoreType.DMA((2, 3)),
            pltpu.SemaphoreType.DMA((2, 3)),
            pltpu.SemaphoreType.DMA((2,)),
        ],
        compiler_params=pltpu.CompilerParams(
            dimension_semantics=("arbitrary",), vmem_limit_bytes=60 << 20,
            **(dict(collective_id=2, has_side_effects=True) if by_kernel else {}),
        ),
        cost_estimate=pl.CostEstimate(flops=3 << 30, bytes_accessed=12 << 20, transcendentals=3 << 20),
    )(normed, wq, wk, wv, segments, table)


def mean_square_scale(rows):
    return lax.rsqrt(jnp.mean(rows * rows, axis=-1, keepdims=True) + norm_eps)


def places():
    dp = lax.axis_index("dp")
    line = lax.axis_index("tensor")
    core = lax.rem(dp, 2)
    x = lax.rem(dp // 2, 2)
    y = dp // 4
    flips = (dp + 1 - 2 * core, dp + 2 - 4 * x, dp + 4 - 8 * y)
    return dp, line, core, x, y, flips


def nearest(line, k):
    upper = line // 2
    inner = line * (1 - upper) + (3 - line) * upper
    block = k + 1 - inner if k == 0 else k + 1
    block = block * (1 - upper) + (3 - block) * upper
    way = (1 if k == 0 else -1) * (1 - 2 * upper)
    return block, way


class Item:
    def __init__(self, place, base, rows, flipped, by_columns=False):
        self.place, self.base, self.rows = place, base, rows
        self.flipped, self.by_columns = flipped, by_columns

    def bits(self, x, y):
        return (y, x) if self.flipped else (x, y)

    def partner(self, level, flips):
        if level == 0:
            return flips[0]
        return flips[1 + ((level - 1) ^ int(self.flipped))]

    def window(self, ref, lead, level, core, first, second):
        width = ref.shape[-1]
        if self.by_columns:
            size = self.rows // (1, 2, 4)[level - 1]
            start = self.base + 0 * core
            if level > 1:
                start = start + first * (self.rows // 2)
            if level > 2:
                start = start + second * (self.rows // 4)
            cols = pl.ds(pl.multiple_of(core * (width // 2), 128), width // 2)
        else:
            size = self.rows // (2, 4, 8)[level - 1]
            start = self.base + core * (self.rows // 2)
            if level > 1:
                start = start + first * (self.rows // 4)
            if level > 2:
                start = start + second * (self.rows // 8)
            cols = pl.ds(0, width)
        rows = pl.ds(pl.multiple_of(start, 16), size)
        if lead is None:
            return ref.at[rows, cols]
        return ref.at[lead, rows, cols]


def weight_items(units, part, width):
    return (
        Item(0, 0, width, False),
        Item(1, 0, width, True),
        Item(2, 0, units // 2, False),
        Item(2, units // 2, units // 2, True),
        Item(3, 0, part, False, by_columns=True),
    )


def gather_kernel(
    hidden_ref, gain_ref, gate_ref, up_ref, down_ref, out_ref,
    normed_all, gate_all, up_all, down_all, out_all,
    z_send, z_recv, p_send, p_recv, own_sem,
    hold_gate, hold_up, hold_down, hold_out, hold_normed,
):
    dp, line, core, x, y, flips = places()
    upper = line // 2
    inner = line * (1 - upper) + (3 - line) * upper
    normed_ref = hold_normed
    own = (gate_ref, up_ref, down_ref, out_ref)
    full = (gate_all, up_all, down_all, out_all)
    units, width = down_ref.shape
    items = weight_items(units, out_ref.shape[0], width)
    count = len(items)

    barrier = pltpu.get_barrier_semaphore()
    for flip in flips:
        pl.semaphore_signal(barrier, inc=1, device_id=(flip, line), device_id_type=MESH_IDS)

    @pl.when(line > 0)
    def _():
        pl.semaphore_signal(barrier, inc=1, device_id=(dp, line - 1), device_id_type=MESH_IDS)

    @pl.when(line < 3)
    def _():
        pl.semaphore_signal(barrier, inc=1, device_id=(dp, line + 1), device_id_type=MESH_IDS)

    rows = hidden_ref[...].astype(f32)
    hold_normed[...] = (rows * mean_square_scale(rows) * gain_ref[0:1, :]).astype(bf16)
    pl.semaphore_wait(barrier, 4 + inner)

    def eighth(i, ref, lead):
        item = items[i]
        first, second = item.bits(x, y)
        return item.window(ref, lead, 3, core, first, second)

    def along(i, block, target, side, first_hop):
        if i == count:
            src = normed_ref if first_hop else normed_all.at[block]
            dst = normed_all.at[block]
        else:
            dst = eighth(i, full[items[i].place], block)
            src = eighth(i, own[items[i].place], None) if first_hop else dst
        return pltpu.make_async_remote_copy(
            src_ref=src, dst_ref=dst, send_sem=z_send.at[i, block, side], recv_sem=z_recv.at[i, block],
            device_id=(dp, target), device_id_type=MESH_IDS,
        )

    def send_own(i):
        @pl.when(line > 0)
        def _():
            along(i, line, line - 1, 0, True).start()

        @pl.when(line < 3)
        def _():
            along(i, line, line + 1, 1, True).start()

    def arrive(i, k):
        block, way = nearest(line, k)
        along(i, block, line, 0, False).wait_recv()

        @pl.when(inner == 1)
        def _():
            along(i, block, line + way, 0, False).start()

    def spread(i, k, stage):
        block, _ = nearest(line, k)
        item = items[i]
        first, second = item.bits(x, y)
        window = item.window(full[item.place], block, 3 - stage, core, first, second)
        return pltpu.make_async_remote_copy(
            src_ref=window, dst_ref=window, send_sem=p_send.at[stage, i, k], recv_sem=p_recv.at[stage, i, k],
            device_id=(item.partner(2 - stage, flips), line), device_id_type=MESH_IDS,
        )

    for i in range(count):
        send_own(i)
    holds = (hold_gate, hold_up, hold_down, hold_out)
    loads = []
    stores = []
    for place, ref in enumerate(own):
        loads.append(pltpu.make_async_copy(ref, holds[place], own_sem.at[0, place]))
        stores.append(pltpu.make_async_copy(holds[place], full[place].at[line], own_sem.at[1, place]))
    for load in loads:
        load.start()
    keep = pltpu.make_async_copy(hold_normed, normed_all.at[line], own_sem.at[1, 4])
    keep.start()
    for load, store in zip(loads, stores):
        load.wait()
        store.start()

    def advance(k, stage):
        for i in range(count):
            if stage > 0:
                spread(i, k, stage - 1).wait_recv()
            spread(i, k, stage).start()

    for k in range(3):
        for i in range(count):
            arrive(i, k)
            spread(i, k, 0).start()
        if k == 2:
            send_own(count)
        if k >= 1:
            advance(k - 1, 1)
        if k >= 2:
            advance(k - 2, 2)
    advance(2, 1)
    arrive(count, 0)
    advance(1, 2)
    arrive(count, 1)
    advance(2, 2)
    arrive(count, 2)

    keep.wait()
    for store in stores:
        store.wait()
    for i in range(count + 1):
        @pl.when(line > 0)
        def _(i=i):
            along(i, line, line - 1, 0, True).wait_send()

        @pl.when(line < 3)
        def _(i=i):
            along(i, line, line + 1, 1, True).wait_send()

        @pl.when(inner == 1)
        def _(i=i):
            for k in range(3):
                block, way = nearest(line, k)
                along(i, block, line + way, 0, False).wait_send()

    for k in range(3):
        for i in range(count):
            spread(i, k, 2).wait_recv()
            for stage in range(3):
                spread(i, k, stage).wait_send()


def gather(hidden_in, gains, gate, up, down, out):
    rows, width = hidden_in.shape
    units, part = gate.shape[1], out.shape[0]
    anywhere = pl.BlockSpec(memory_space=pl.ANY)
    return pl.pallas_call(
        gather_kernel,
        name="gather",
        out_shape=(
            jax.ShapeDtypeStruct((4, rows, width), bf16),
            jax.ShapeDtypeStruct((4, width, units), bf16),
            jax.ShapeDtypeStruct((4, width, units), bf16),
            jax.ShapeDtypeStruct((4, units, width), bf16),
            jax.ShapeDtypeStruct((4, part, width), bf16),
        ),
        in_specs=[pl.BlockSpec(memory_space=pltpu.VMEM)] * 2 + [anywhere] * 4,
        out_specs=(anywhere,) * 5,
        scratch_shapes=[
            pltpu.SemaphoreType.DMA((6, 4, 2)),
            pltpu.SemaphoreType.DMA((6, 4)),
            pltpu.SemaphoreType.DMA((3, 5, 3)),
            pltpu.SemaphoreType.DMA((3, 5, 3)),
            pltpu.SemaphoreType.DMA((2, 5)),
            pltpu.VMEM(gate.shape, bf16),
            pltpu.VMEM(up.shape, bf16),
            pltpu.VMEM(down.shape, bf16),
            pltpu.VMEM(out.shape, bf16),
            pltpu.VMEM(hidden_in.shape, bf16),
        ],
        compiler_params=pltpu.CompilerParams(collective_id=1, has_side_effects=True),
    )(hidden_in, gains, gate, up, down, out)


class Named:
    def __init__(self, names, refs):
        for name, ref in zip(names, refs):
            setattr(self, name, ref)


def remote(src, dst, send, recv, target):
    return pltpu.make_async_remote_copy(
        src_ref=src, dst_ref=dst, send_sem=send, recv_sem=recv, device_id=target, device_id_type=MESH_IDS
    )


def greet(dp, line, flips):
    barrier = pltpu.get_barrier_semaphore()
    for flip in flips:
        pl.semaphore_signal(barrier, inc=1, device_id=(flip, line), device_id_type=MESH_IDS)
    for i in (1, 2, 3):
        pl.semaphore_signal(
            barrier, inc=1, device_id=(dp, lax.rem(line + i, 4)), device_id_type=MESH_IDS
        )
    return barrier


def unit_parts(s, r):
    groups = r.mixed_here.shape[1]

    def mixed_of(g):
        return jnp.concatenate((r.mixed_here[0, g], r.mixed_here[1, g][:, 0:HEAD_DIM]), axis=1)

    def begin():
        mixed = jnp.concatenate([mixed_of(g) for g in range(groups)], axis=1)
        out_w = jnp.concatenate([s.out_w[g] for g in range(groups)], axis=0)
        residual = r.hidden_in[...].astype(f32) + jnp.dot(mixed, out_w, preferred_element_type=f32)
        s.residual[...] = residual
        s.normed2[...] = (residual * mean_square_scale(residual) * r.gains[1:2, :]).astype(bf16)
        s.ahead[...] = residual
        s.behind[...] = jnp.zeros_like(s.behind)

    def block(b, slot):
        normed = s.normed2[...]
        cot = r.cot[...]
        gate_w, up_w, down_w = s.gate_w[slot], s.up_w[slot], s.down_w[slot]
        gate = jnp.dot(normed, gate_w, preferred_element_type=f32)
        up = jnp.dot(normed, up_w, preferred_element_type=f32)
        hidden_grad = contract(cot, down_w, 1, 1)
        c0 = 0.7978845608028654
        square = gate * gate
        bend = jnp.tanh(gate * (c0 + (c0 * 0.044715) * square))
        half = 0.5 + 0.5 * bend
        act = gate * half
        slope = half + 0.5 * gate * (1.0 - bend * bend) * (c0 + (3.0 * c0 * 0.044715) * square)
        hidden = (act * up).astype(bf16)
        gate_grad = (hidden_grad * up * slope).astype(bf16)
        up_grad = (hidden_grad * act).astype(bf16)
        s.ahead[...] += jnp.dot(hidden, down_w, preferred_element_type=f32)
        s.behind[...] += contract(gate_grad, gate_w, 1, 1) + contract(up_grad, up_w, 1, 1)
        s.down_wg[b] = contract(hidden, cot, 0, 0).astype(bf16)
        s.gate_wg[b] = contract(normed, gate_grad, 0, 0).astype(bf16)
        s.up_wg[b] = contract(normed, up_grad, 0, 0).astype(bf16)

    def end():
        residual = s.residual[...]
        r.output[...] = s.ahead[...].astype(bf16)
        back = s.behind[...]
        scale = mean_square_scale(residual)
        s.small_mine[1:2, :] = jnp.sum(back * residual * scale, axis=0, keepdims=True)
        g = back * r.gains[1:2, :]
        centre = jnp.mean(g * residual, axis=-1, keepdims=True)
        residual_grad = r.cot[...].astype(f32) + scale * g - (scale * scale * scale * centre) * residual
        low = residual_grad.astype(bf16)
        s.behind[...] = residual_grad
        for g_at in range(groups):
            s.grad_here[g_at] = contract(low, s.out_w[g_at], 1, 1).astype(bf16)

    def out_grad():
        low = s.behind[...].astype(bf16)
        for g_at in range(groups):
            s.out_wg[g_at] = contract(mixed_of(g_at), low, 0, 0).astype(bf16)

    return begin, block, end, out_grad


def attention_back_tasks(s, r):
    heads, length = s.dot.shape[0], s.dot.shape[1]
    count = length // BLK
    lane = lax.broadcasted_iota(jnp.int32, (BLK, 128), 1)
    low_half = lane < HEAD_DIM
    tasks = []

    def probs_copy(h, block):
        at = (h * count + block) % 2
        rows = pl.ds(block * BLK, BLK)
        return pltpu.make_async_copy(r.probs_all.at[h, rows, :], s.probs.at[at], s.probs_sem.at[at])

    def prepare():
        probs_copy(0, 0).start()
        probs_copy(0, 1).start()

        def body(step, carry):
            rows = pl.ds(pl.multiple_of(step * BLK, BLK), BLK)
            for h in range(heads):
                cols = slice(0, 128) if h < 2 else slice(128, 256)
                mine = ~low_half if h == 1 else low_half
                if h < 2:
                    grad = s.mixed_grad[step, :, 0:128].astype(f32)
                    mix = r.mixed[rows, 0:128].astype(f32)
                else:
                    fill = jnp.zeros((BLK, HEAD_DIM), f32)
                    grad = jnp.concatenate((s.mixed_grad[step, :, 128:192].astype(f32), fill), axis=1)
                    mix = jnp.concatenate((r.mixed[rows, 128:192].astype(f32), fill), axis=1)
                grad = jnp.where(mine, grad * r.inverse[rows, cols], 0.0)
                centre = -jnp.sum(grad * mix, axis=1, keepdims=True)
                high = centre.astype(bf16).astype(f32)
                base = 0 if h == 1 else HEAD_DIM
                grad = jnp.where(lane == base, high, grad)
                grad = jnp.where(lane == base + 1, centre - high, grad)
                low = grad.astype(bf16)
                s.dot[h, rows, :] = low
                s.dott[h, :, rows] = low.T
            return carry

        lax.fori_loop(0, count, body, 0)

    tasks.append(prepare)

    def block_step(h, block):
        if block == 0:
            s.near[...] = jnp.zeros_like(s.near)
            s.far[...] = jnp.zeros_like(s.far)
            s.dkt[...] = jnp.zeros_like(s.dkt)
            s.dvt[...] = jnp.zeros_like(s.dvt)
        probs_copy(h, block).wait()
        at = (h * count + block) % 2
        rows = slice(block * BLK, (block + 1) * BLK)
        d_h = s.dot[h, rows, :]
        dt_h = s.dott[h, :, rows]
        qt_h = r.qt[h, :, rows]
        query_grad = jnp.zeros((BLK, 128), f32)
        for key in key_range(block, count):
            cols = slice(key * BLK, (key + 1) * BLK)
            probs = s.probs[at, :, cols]
            slope = jnp.dot(d_h, r.vt[h, :, cols], preferred_element_type=f32)
            grad = probs.astype(f32) * slope
            low = grad.astype(bf16)
            delta = key - block
            if abs(delta) == 2:
                s.far[0 if delta < 0 else 1] += grad[:, :128] + grad[:, 128:]
            else:
                s.near[:, (delta + 1) * BLK : (delta + 2) * BLK] += grad
            query_grad = query_grad + jnp.dot(low, r.k[h, cols, :], preferred_element_type=f32)
            s.dkt[:, cols] += jnp.dot(qt_h, low, preferred_element_type=f32)
            s.dvt[:, cols] += jnp.dot(dt_h, probs, preferred_element_type=f32)
        s.grad[rows, 0:128] = query_grad * HEAD_DIM ** (-0.5)
        turn = h * count + block + 2
        if turn < heads * count:
            probs_copy(turn // count, turn % count).start()

    def head_end(h):
        def body(step, carry):
            rows = pl.ds(pl.multiple_of(step * BLK, BLK), BLK)
            s.grad[rows, 128:256] = s.dkt[:, rows].T
            s.grad[rows, 256:384] = s.dvt[:, rows].T
            for at in range(3):
                part = s.grad[rows, 128 * at : 128 * at + 128]
                if h == 0:
                    s.joined[rows, 256 * at : 256 * at + 128] = part.astype(bf16)
                elif h == 1:
                    before = s.joined[rows, 256 * at : 256 * at + 128].astype(f32)
                    s.joined[rows, 256 * at : 256 * at + 128] = jnp.where(low_half, before, part).astype(bf16)
                else:
                    s.joined[rows, 256 * at + 128 : 256 * at + 256] = jnp.where(low_half, part, 0.0).astype(bf16)
            return carry

        lax.fori_loop(0, count, body, 0)
        place = lax.broadcasted_iota(jnp.int32, (BLK, 3 * BLK), 1) - BLK
        place = place - lax.broadcasted_iota(jnp.int32, (BLK, 3 * BLK), 0)
        s.bucket[...] = bucket_of(place)
        s.table[...] = jnp.zeros_like(s.table)

        def count_bucket(b, carry):
            part = jnp.sum(jnp.where(s.bucket[...] == b, s.near[...], 0.0), axis=0, keepdims=True)
            folded = part[:, 0:128]
            for at in range(1, 6):
                folded = folded + part[:, at * 128 : (at + 1) * 128]
            s.table[pl.ds(b, 1), :] = folded
            return carry

        lax.fori_loop(0, BUCKETS, count_bucket, 0)
        for side, b in ((0, 15), (1, 31)):
            s.table[b : b + 1, :] += jnp.sum(s.far[side], axis=0, keepdims=True)
        flat = lax.dot_general(
            jnp.ones((8, 128), f32), s.table[...], (((1,), (1,)), ((), ())),
            preferred_element_type=f32, precision=lax.Precision.HIGHEST,
        )
        s.small_mine[8 + h : 9 + h, 0:BUCKETS] = flat[0:1]

    for h in range(heads):
        for block in range(count):
            tasks.append(functools.partial(block_step, h, block))
        tasks.append(functools.partial(head_end, h))

    def rows_grad(block):
        rows = slice(block * BLK, (block + 1) * BLK)
        part = jnp.dot(s.joined[rows, :], s.w[...], preferred_element_type=f32)
        s.back_acc[block] = part.astype(bf16)
        s.gain[...] += jnp.sum(part * r.normed[rows, :].astype(f32), axis=0, keepdims=True)

    def weights_grad(at):
        part = contract(s.joined[:, 256 * at : 256 * at + 256], r.normed[...], 0, 0)
        s.qkv_wg[192 * at : 192 * at + 192, :] = part[0:192].astype(bf16)

    return tasks, rows_grad, weights_grad


REST_OPERANDS = tuple(dict(
    gate_all=0, up_all=0, down_all=0, out_all=0, probs_all=0, wq=0, wk=0, wv=0, mixed_here=0, hidden_in=0,
    cot=0, gains=0, mixed=0, inverse=0, qt=0, k=0, vt=0, normed=0,
))
REST_RESULTS = tuple(dict(
    output=0, input_grad=0, small_sum=0, out_sum=0, gate_sum=0, up_sum=0, down_sum=0, qkv_sum=0,
))


def load_weights(s, r, b, slot):
    pairs = ((r.gate_all, s.gate_w), (r.up_all, s.up_w), (r.down_all, s.down_w))
    return [
        pltpu.make_async_copy(src.at[b], dst.at[slot], s.weight_sem.at[i, slot]) for i, (src, dst) in enumerate(pairs)
    ]


def load_small(s, r):
    copies = [pltpu.make_async_copy(r.out_all, s.out_w, s.first_sem.at[0])]
    for place, ref in enumerate((r.wq, r.wk, r.wv)):
        part = ref.shape[0]
        copies.append(pltpu.make_async_copy(ref, s.w.at[pl.ds(256 * place, part), :], s.first_sem.at[1 + place]))
    return copies


def start_all(s, r):
    groups = s.out_w.shape[0]
    for copy in load_small(s, r) + load_weights(s, r, 0, 0):
        copy.start()
    s.small_mine[...] = jnp.zeros_like(s.small_mine)
    s.gain[...] = jnp.zeros_like(s.gain)
    for place in range(3):
        s.w[256 * place + 192 : 256 * place + 256, :] = jnp.zeros((64, s.w.shape[1]), bf16)
    return groups


def input_grad_rows(s, r, back):
    rows = r.hidden_in[...].astype(f32)
    scale = mean_square_scale(rows)
    g = back * r.gains[0:1, :]
    centre = jnp.mean(g * rows, axis=-1, keepdims=True)
    r.input_grad[...] = (s.behind[...] + scale * g - (scale * scale * scale * centre) * rows).astype(bf16)


def add_rows(target, start, size, source):
    step = 32 if size % 32 == 0 else 16

    def body(i, carry):
        at = pl.multiple_of(i * step, step)
        rows = pl.ds(pl.multiple_of(start + at, 16), step)
        target[rows, :] = (target[rows, :].astype(f32) + source[pl.ds(at, step), :].astype(f32)).astype(bf16)
        return carry

    lax.fori_loop(0, size // step, body, 0)


def rest_kernel(names, *refs):
    r = Named(REST_OPERANDS + REST_RESULTS, refs)
    s = Named(names, refs[len(REST_OPERANDS) + len(REST_RESULTS) :])
    dp, line, core, x, y, flips = places()
    units, width = s.down_wg.shape[1:]
    part = s.out_wg.shape[1]
    items = weight_items(units, part, width)
    item_count = len(items)
    grads = (s.gate_wg, s.up_wg, s.down_wg, s.out_wg, s.qkv_wg)
    sums = (r.gate_sum, r.up_sum, r.down_sum, r.out_sum, r.qkv_sum)
    begin_unit, unit_block, end_unit, out_grad = unit_parts(s, r)
    tasks, rows_grad, weights_grad = attention_back_tasks(s, r)
    groups = start_all(s, r)
    barrier = greet(dp, line, flips)

    def item_of(i, block):
        if i < item_count - 1:
            return items[i]
        if i == item_count - 1:
            return Item(3, 0, part, block > 1, True)
        turn = i - item_count
        return Item(4, turn * part, part, turn % 2 == 0, True)

    def lead(i, block):
        return block if i < item_count else None

    def number(i, block):
        return i * groups + block if i < item_count else (item_count - 1) * groups + i - 1

    def at_block(ref, i, block):
        return ref.at[block] if i < item_count else ref

    def arrival(stage, i, block):
        return at_block(getattr(s, stage + str(i)), i, block)

    def held(i, block):
        item = item_of(i, block)
        if item.by_columns:
            return arrival("half", i, block), 0, item.rows
        return grads[item.place].at[block], item.base + core * (item.rows // 2), item.rows // 2

    def load_copy(i, block):
        item = item_of(i, block)
        window = item.window(grads[item.place], lead(i, block), 1, core, 0, 0)
        return pltpu.make_async_copy(window, arrival("half", i, block), s.load_sem.at[number(i, block)])

    def core_copy(i, block):
        item, n = item_of(i, block), number(i, block)
        window = item.window(grads[item.place], lead(i, block), 1, 1 - core, 0, 0)
        return remote(window, arrival("core", i, block), s.core_send.at[n], s.core_recv.at[n], (flips[0], line))

    def begin(i, block):
        core_copy(i, block).start()
        if item_of(i, block).by_columns:
            load_copy(i, block).start()

    def pair_copy(i, block, stage):
        ref, base, half = held(i, block)
        item, n = item_of(i, block), number(i, block)
        first, second = item.bits(x, y)
        if stage == 0:
            size, start, target = half // 2, (1 - first) * (half // 2), arrival("first", i, block)
        else:
            size = half // 4
            start, target = first * (half // 2) + (1 - second) * (half // 4), arrival("second", i, block)
        window = ref.at[pl.ds(pl.multiple_of(base + start, 16), size), :]
        partner = item.partner(1 + stage, flips)
        return remote(window, target, s.pair_send.at[stage, n], s.pair_recv.at[stage, n], (partner, line))

    def eighth(i, block):
        ref, base, half = held(i, block)
        first, second = item_of(i, block).bits(x, y)
        start = pl.multiple_of(base + first * (half // 2) + second * (half // 4), 16)
        return ref, start, half // 4

    def mine(i, block):
        ref, start, size = eighth(i, block)
        return ref.at[pl.ds(start, size), :]

    def line_copy(i, block, sender):
        target = getattr(s, "line" + str(i)).at[sender]
        return remote(
            mine(i, block), target, s.line_send.at[i, block], s.line_recv.at[i, sender], (dp, block)
        )

    def spread_copy(i, block, stage):
        item, n = item_of(i, block), number(i, block)
        first, second = item.bits(x, y)
        window = item.window(sums[item.place], None, 3 - stage, core, first, second)
        src = mine(i, block) if stage == 0 else window
        return remote(
            src, window, s.spread_send.at[stage, n], s.spread_recv.at[stage, n],
            (item.partner(2 - stage, flips), line),
        )

    def keep_copy(i, block):
        item = item_of(i, block)
        first, second = item.bits(x, y)
        window = item.window(sums[item.place], None, 3, core, first, second)
        return pltpu.make_async_copy(mine(i, block), window, s.load_sem.at[number(i, block)])

    def step_core(i, block, send=True):
        if item_of(i, block).by_columns:
            load_copy(i, block).wait()
        core_copy(i, block).wait_recv()
        ref, base, half = held(i, block)
        add_rows(ref, base, half, arrival("core", i, block))
        if send:
            pair_copy(i, block, 0).start()

    def step_first(i, block):
        pair_copy(i, block, 0).wait_recv()
        ref, base, half = held(i, block)
        first, _ = item_of(i, block).bits(x, y)
        add_rows(ref, base + first * (half // 2), half // 2, arrival("first", i, block))
        pair_copy(i, block, 1).start()

    def step_second(i, block):
        pair_copy(i, block, 1).wait_recv()
        ref, start, size = eighth(i, block)
        add_rows(ref, start, size, arrival("second", i, block))
        if i < item_count:
            pl.when(line != block)(lambda: line_copy(i, block, line).start())
        else:
            spread_copy(i, block, 0).start()
            keep_copy(i, block).start()

    def step_last(i, block):
        @pl.when(line == block)
        def _():
            ref, start, size = eighth(i, block)
            others = [o for o in range(groups) if o != block]
            for o in others:
                line_copy(i, block, o).wait_recv()
            arrived = getattr(s, "line" + str(i))
            total = ref[pl.ds(start, size), :].astype(f32)
            for o in others:
                total = total + arrived[o].astype(f32)
            ref[pl.ds(start, size), :] = total.astype(bf16)
            spread_copy(i, block, 0).start()
            keep_copy(i, block).start()

    def step_spread(i, block, stage):
        def act():
            if stage == 1:
                keep_copy(i, block).wait()
            spread_copy(i, block, stage - 1).wait_recv()
            if stage < 3:
                spread_copy(i, block, stage).start()

        if i < item_count:
            pl.when(line == block)(act)
        else:
            act()

    def swap_copy(i, sender_is_me):
        other = lax.rem(line + i, 4)
        if sender_is_me:
            return remote(
                s.grad_here.at[other], s.mixed_grad.at[line], s.swap_send.at[i - 1], s.swap_recv.at[3 - i], (dp, other)
            )
        return remote(
            s.grad_here.at[other], s.mixed_grad.at[other], s.swap_send.at[i - 1], s.swap_recv.at[i - 1], (dp, other)
        )

    def back_copy(block, at, right):
        src, send = s.back_acc.at[block], s.back_send.at[block]
        if right:
            return remote(src, s.back_left.at[block], send, s.back_left_recv.at[block], (dp, at + 1))
        return remote(src, s.back_right.at[block], send, s.back_right_recv.at[block], (dp, at - 1))

    def back_hop(hop, distance):
        @pl.when(line == hop)
        def _():
            block = hop + distance
            if block <= groups - 1:
                if hop > 0:
                    back_copy(block, hop, True).wait_recv()
                    add_rows(s.back_acc.at[block], 0, s.back_acc.shape[1], s.back_left.at[block])
                back_copy(block, hop, True).start()

        at = groups - 1 - hop

        @pl.when(line == at)
        def _():
            block = at - distance
            if block >= 0:
                if hop > 0:
                    back_copy(block, at, False).wait_recv()
                    add_rows(s.back_acc.at[block], 0, s.back_acc.shape[1], s.back_right.at[block])
                back_copy(block, at, False).start()

    def collect_rows():
        for block in range(groups):
            @pl.when(line == block)
            def _(block=block):
                total = s.back_acc[block].astype(f32)
                if block > 0:
                    back_copy(block, block, True).wait_recv()
                    total = total + s.back_left[block].astype(f32)
                if block < groups - 1:
                    back_copy(block, block, False).wait_recv()
                    total = total + s.back_right[block].astype(f32)
                input_grad_rows(s, r, total)

    def small_copy(stage):
        partner = (flips[stage], line) if stage < 3 else (dp, line + 1 - 2 * lax.rem(line, 2))
        if stage == 4:
            partner = (dp, lax.rem(line + 2, 4))
        return remote(s.small_mine, s.small_got.at[stage], s.small_send.at[stage], s.small_recv.at[stage], partner)

    def small_step(stage):
        if stage > 0:
            small_copy(stage - 1).wait()
            rows = lax.broadcasted_iota(jnp.int32, s.small_mine.shape, 0)
            got = s.small_got[stage - 1]
            if stage > 3:
                got = jnp.where(rows < 8, got, 0.0)
            s.small_mine[...] = s.small_mine[...] + got
        else:
            s.small_mine[0:1, :] = s.gain[...] / r.gains[0:1, :]
        if stage < 5:
            small_copy(stage).start()
        else:
            r.small_sum[...] = s.small_mine[...]

    outer, inner = (0, groups - 1), tuple(range(1, groups - 1))
    teams = [[(i, block) for i in (0, 1)] for block in outer + inner]
    teams += [[(i, block) for block in pair for i in (2, 3)] for pair in (outer, inner)]
    teams.append([(item_count - 1, block) for block in range(groups)])
    teams.append([(item_count + turn, 0) for turn in range(3)])
    stage_acts = (
        step_core, step_first, step_second, step_last,
        lambda i, block: step_spread(i, block, 1),
        lambda i, block: step_spread(i, block, 2),
        lambda i, block: step_spread(i, block, 3),
    )
    done = []

    def tend(moment):
        for name, team in WHEN.get(moment, ()):
            done.append((name, team))
            if name == SMALL:
                small_step(team)
            elif name == ROWS:
                collect_rows()
            elif name == HOP:
                back_hop(*team)
            else:
                for i, block in teams[team]:
                    stage_acts[name](i, block)

    for copy in load_small(s, r):
        copy.wait()
    begin_unit()

    order = outer + inner
    for turn, block in enumerate(order):
        for copy in load_weights(s, r, block, turn % 2):
            copy.wait()
        if turn + 1 < groups:
            for copy in load_weights(s, r, order[turn + 1], (turn + 1) % 2):
                copy.start()
        unit_block(block, turn % 2)
        if turn == 0:
            pl.semaphore_wait(barrier, 6)
        for i in range(item_count - 1):
            begin(i, block)
        tend(UNIT + turn)
    end_unit()
    for i in (2, 1, 3):
        swap_copy(i, True).start()
    swap_keep = pltpu.make_async_copy(s.grad_here.at[line], s.mixed_grad.at[line], s.swap_keep)
    swap_keep.start()
    out_grad()
    for block in range(groups):
        begin(item_count - 1, block)
    tend(SWAP)
    for i in (1, 2, 3):
        swap_copy(i, False).wait_recv()
        swap_copy(i, True).wait_send()
    swap_keep.wait()
    for turn, task in enumerate(tasks):
        task()
        tend(turn)
    for block in range(groups):
        rows_grad(block)
    for distance in (3, 2, 1):
        back_hop(0, distance)
    for turn in range(3):
        weights_grad(turn)
        begin(item_count + turn, 0)
    small_step(0)

    for turn in range(len(WHEN)):
        tend(END + turn)
    assert len(done) == len(set(done)) == 7 * 7 + 6 + 5 + 4
    for block in range(groups):
        pl.when(line < block)(lambda block=block: back_copy(block, line, True).wait_send())
        pl.when(line > block)(lambda block=block: back_copy(block, line, False).wait_send())
    for i, block in sum(teams, []):
        core_copy(i, block).wait_send()
        pair_copy(i, block, 0).wait_send()
        pair_copy(i, block, 1).wait_send()

        def sent(i=i, block=block):
            for stage in range(3):
                spread_copy(i, block, stage).wait_send()

        if i < item_count:
            pl.when(line == block)(sent)
            pl.when(line != block)(lambda i=i, block=block: line_copy(i, block, line).wait_send())
        else:
            sent()


CORE, FIRST, SECOND, LAST, SPREAD1, SPREAD2, SPREAD3, SMALL, HOP, ROWS = range(10)
UNIT, SWAP, END = 100, 110, 120
WHEN = {
    UNIT + 1: [(CORE, 0), (CORE, 1)],
    UNIT + 3: [(FIRST, 0), (CORE, 2), (FIRST, 1), (CORE, 3)],
    SWAP: [(SECOND, 0), (FIRST, 2), (CORE, 4), (SECOND, 1)],
    0: [(FIRST, 3), (CORE, 5), (SECOND, 2)],
    3: [(FIRST, 4), (CORE, 6), (SECOND, 3)],
    5: [(LAST, 0), (LAST, 1)],
    7: [(FIRST, 5), (SECOND, 4), (SPREAD1, 0), (SPREAD1, 1)],
    9: [(LAST, 2)],
    11: [(FIRST, 6), (SECOND, 5), (LAST, 3), (SPREAD2, 0), (SPREAD2, 1)],
    13: [(SPREAD1, 2), (SECOND, 6)],
    14: [(LAST, 4), (SPREAD1, 3), (SPREAD3, 0), (SPREAD3, 1), (SPREAD2, 2)],
    END + 0: [(CORE, 7), (LAST, 5), (SPREAD1, 4), (SPREAD2, 3)],
    END + 1: [(SMALL, 1), (HOP, (1, 2)), (FIRST, 7), (LAST, 6), (SPREAD3, 2), (SPREAD1, 5)],
    END + 2: [(SMALL, 2), (HOP, (1, 1)), (SECOND, 7), (SPREAD1, 6), (SPREAD2, 4), (SPREAD3, 3)],
    END + 3: [(SMALL, 3), (HOP, (2, 1)), (SPREAD1, 7), (SPREAD2, 5), (SPREAD2, 6)],
    END + 4: [(SMALL, 4), (SPREAD2, 7), (SPREAD3, 4), (SPREAD3, 5), (SPREAD3, 6)],
    END + 5: [(SMALL, 5), (SPREAD3, 7), (ROWS, 0)],
}

def common_scratch(groups, rows, heads, length, width, units, part):
    dma = pltpu.SemaphoreType.DMA
    return dict(
        residual=pltpu.VMEM((rows, width), f32),
        normed2=pltpu.VMEM((rows, width), bf16),
        ahead=pltpu.VMEM((rows, width), f32),
        behind=pltpu.VMEM((rows, width), f32),
        out_w=pltpu.VMEM((groups, part, width), bf16),
        gate_w=pltpu.VMEM((2, width, units), bf16),
        up_w=pltpu.VMEM((2, width, units), bf16),
        down_w=pltpu.VMEM((2, units, width), bf16),
        gate_wg=pltpu.VMEM((groups, width, units), bf16),
        up_wg=pltpu.VMEM((groups, width, units), bf16),
        down_wg=pltpu.VMEM((groups, units, width), bf16),
        out_wg=pltpu.VMEM((groups, part, width), bf16),
        qkv_wg=pltpu.VMEM((3 * part, width), bf16),
        grad_here=pltpu.VMEM((groups, rows, part), bf16),
        mixed_grad=pltpu.VMEM((groups, rows, part), bf16),
        back_acc=pltpu.VMEM((groups, rows, width), bf16),
        small_mine=pltpu.VMEM((16, width), f32),
        gain=pltpu.VMEM((1, width), f32),
        probs=pltpu.VMEM((2, BLK, length), bf16),
        w=pltpu.VMEM((768, width), bf16),
        dot=pltpu.VMEM((heads, length, 128), bf16),
        dott=pltpu.VMEM((heads, 128, length), bf16),
        grad=pltpu.VMEM((length, 384), f32),
        joined=pltpu.VMEM((length, 768), bf16),
        near=pltpu.VMEM((BLK, 3 * BLK), f32),
        bucket=pltpu.VMEM((BLK, 3 * BLK), jnp.int32),
        table=pltpu.VMEM((BUCKETS, 128), f32),
        far=pltpu.VMEM((2, BLK, 128), f32),
        dkt=pltpu.VMEM((128, length), f32),
        dvt=pltpu.VMEM((128, length), f32),
        weight_sem=dma((3, 2)), first_sem=dma((4,)), probs_sem=dma((2,)),
    )


def result_shapes(rows, width, units, part):
    return (
        jax.ShapeDtypeStruct((rows, width), bf16),
        jax.ShapeDtypeStruct((rows, width), bf16),
        jax.ShapeDtypeStruct((16, width), f32),
        jax.ShapeDtypeStruct((part, width), bf16),
        jax.ShapeDtypeStruct((width, units), bf16),
        jax.ShapeDtypeStruct((width, units), bf16),
        jax.ShapeDtypeStruct((units, width), bf16),
        jax.ShapeDtypeStruct((3 * part, width), bf16),
    )


def rest_all(gate_all, up_all, down_all, out_all, probs, wq, wk, wv, mixed_here, hidden_in, cot, gains,
             mixed, inverse, qt, k, vt, normed):
    groups, part = mixed_here.shape[1], wq.shape[0]
    rows, width = hidden_in.shape
    heads, length = k.shape[0], k.shape[1]
    units = down_all.shape[1]
    items = weight_items(units, part, width)
    n = 3 + groups * len(items)
    dma = pltpu.SemaphoreType.DMA
    scratch = common_scratch(groups, rows, heads, length, width, units, part)
    for stage, divide in (("half", 1), ("core", 1), ("first", 2), ("second", 4), ("line", 4)):
        for i, item in enumerate(items):
            cols = (units, units, width, width)[item.place]
            shape = (item.rows, cols // 2) if item.by_columns else (item.rows // 2, cols)
            if stage != "half" or item.by_columns:
                scratch[stage + str(i)] = pltpu.VMEM((groups, shape[0] // divide, shape[1]), bf16)
        for turn in range(3):
            if stage != "line":
                scratch[stage + str(len(items) + turn)] = pltpu.VMEM((part // divide, width // 2), bf16)
    scratch.update(
        small_got=pltpu.VMEM((5, 16, width), f32),
        back_left=pltpu.VMEM((groups, rows, width), bf16),
        back_right=pltpu.VMEM((groups, rows, width), bf16),
        load_sem=dma((n,)), core_send=dma((n,)), core_recv=dma((n,)),
        pair_send=dma((2, n)), pair_recv=dma((2, n)),
        line_send=dma((len(items), groups)), line_recv=dma((len(items), groups)),
        spread_send=dma((3, n)), spread_recv=dma((3, n)),
        back_send=dma((groups,)), back_left_recv=dma((groups,)), back_right_recv=dma((groups,)),
        small_send=dma((5,)), small_recv=dma((5,)),
        swap_send=dma((3,)), swap_recv=dma((3,)), swap_keep=dma,
    )
    anywhere = pl.BlockSpec(memory_space=pl.ANY)
    inside = pl.BlockSpec(memory_space=pltpu.VMEM)
    return pl.pallas_call(
        functools.partial(rest_kernel, tuple(scratch)),
        name="rest_all",
        out_shape=result_shapes(rows, width, units, part),
        in_specs=[anywhere] * 8 + [inside] * 10,
        out_specs=(inside,) * 3 + (anywhere,) * 5,
        scratch_shapes=list(scratch.values()),
        compiler_params=pltpu.CompilerParams(
            collective_id=3, has_side_effects=True, vmem_limit_bytes=62 << 20
        ),
    )(gate_all, up_all, down_all, out_all, probs, wq, wk, wv, mixed_here, hidden_in, cot, gains,
      mixed, inverse, qt, k, vt, normed)


UNIT_RESULTS = tuple(dict(
    output=0, residual_grad=0, grads=0, gain2_grad=0, out_out=0, gate_out=0, up_out=0, down_out=0,
))


def unit_local_kernel(names, *refs):
    operands = tuple(dict(gate_all=0, up_all=0, down_all=0, out_all=0, mixed_here=0, hidden_in=0, cot=0, gains=0))
    r = Named(operands + UNIT_RESULTS, refs)
    s = Named(names, refs[len(operands) + len(UNIT_RESULTS) :])
    s.out_wg, s.gate_wg, s.up_wg, s.down_wg = r.out_out, r.gate_out, r.up_out, r.down_out
    s.behind, s.grad_here = r.residual_grad, r.grads
    begin, block, end, out_grad = unit_parts(s, r)
    groups = s.out_w.shape[0]
    first = [pltpu.make_async_copy(r.out_all, s.out_w, s.first_sem.at[0])] + load_weights(s, r, 0, 0)
    for copy in first:
        copy.start()
    first[0].wait()
    begin()

    def body(b, carry):
        slot = lax.rem(b, 2)
        for copy in load_weights(s, r, b, slot):
            copy.wait()

        @pl.when(b + 1 < groups)
        def _():
            for copy in load_weights(s, r, b + 1, 1 - slot):
                copy.start()

        block(b, slot)
        return carry

    lax.fori_loop(0, groups, body, 0)
    end()
    out_grad()
    r.gain2_grad[...] = s.small_mine[1:2, :]


def back_local_kernel(names, *refs):
    operands = tuple(dict(probs_all=0, mixed=0, inverse=0, qt=0, k=0, vt=0, normed=0, wq=0, wk=0, wv=0, gains=0, mixed_grad=0))
    results = tuple(dict(back_out=0, qkv_out=0, small_out=0))
    r = Named(operands + results, refs)
    s = Named(names, refs[len(operands) + len(results) :])
    s.mixed_grad, s.qkv_wg, s.small_mine, s.back_acc = r.mixed_grad, r.qkv_out, r.small_out, r.back_out
    tasks, rows_grad, weights_grad = attention_back_tasks(s, r)
    s.small_mine[...] = jnp.zeros_like(s.small_mine)
    s.gain[...] = jnp.zeros_like(s.gain)
    s.w[...] = jnp.zeros_like(s.w)
    for place, ref in enumerate((r.wq, r.wk, r.wv)):
        s.w[256 * place : 256 * place + ref.shape[0], :] = ref[...]
    for task in tasks:
        task()
    for block in range(r.back_out.shape[0]):
        rows_grad(block)
    for turn in range(3):
        weights_grad(turn)
    s.small_mine[0:1, :] = s.gain[...] / r.gains[0:1, :]


def rest_by_axis(gate_all, up_all, down_all, out_all, probs, wq, wk, wv, mixed_here, hidden_in, cot, gains,
                 mixed, inverse, qt, k, vt, normed):
    groups, part = mixed_here.shape[1], wq.shape[0]
    rows, width = hidden_in.shape
    heads, length = k.shape[0], k.shape[1]
    units = down_all.shape[1]
    anywhere = pl.BlockSpec(memory_space=pl.ANY)
    inside = pl.BlockSpec(memory_space=pltpu.VMEM)
    every = common_scratch(groups, rows, heads, length, width, units, part)
    pick = lambda names: {name: every[name] for name in names}
    shape = jax.ShapeDtypeStruct
    scratch = pick(dict(
    residual=0, normed2=0, ahead=0, out_w=0, gate_w=0, up_w=0, down_w=0, small_mine=0, weight_sem=0,
    first_sem=0,
    ))
    output, residual_grad, grads, gain2_grad, out_wg, gate_wg, up_wg, down_wg = pl.pallas_call(
        functools.partial(unit_local_kernel, tuple(scratch)),
        name="unit_local",
        out_shape=(
            shape((rows, width), bf16), shape((rows, width), f32), shape((groups, rows, part), bf16),
            shape((1, width), f32), shape((groups, part, width), bf16), shape((groups, width, units), bf16),
            shape((groups, width, units), bf16), shape((groups, units, width), bf16),
        ),
        in_specs=[anywhere] * 4 + [inside] * 4,
        out_specs=(inside,) * 8,
        scratch_shapes=list(scratch.values()),
        compiler_params=pltpu.CompilerParams(vmem_limit_bytes=56 << 20),
    )(gate_all, up_all, down_all, out_all, mixed_here, hidden_in, cot, gains)
    mixed_grad = lax.all_to_all(grads, "tensor", 0, 0)
    scratch = pick(dict(
    gain=0, probs=0, w=0, dot=0, dott=0, grad=0, joined=0, near=0, bucket=0, table=0, far=0, dkt=0, dvt=0,
    probs_sem=0,
    ))
    back, qkv_wg, small = pl.pallas_call(
        functools.partial(back_local_kernel, tuple(scratch)),
        name="back_local",
        out_shape=(
            shape((groups, rows, width), bf16), shape((3 * part, width), bf16), shape((16, width), f32),
        ),
        in_specs=[anywhere] + [inside] * 11,
        out_specs=(inside,) * 3,
        scratch_shapes=list(scratch.values()),
        compiler_params=pltpu.CompilerParams(vmem_limit_bytes=56 << 20),
    )(probs, mixed, inverse, qt, k, vt, normed, wq, wk, wv, gains, mixed_grad)
    back_sum = lax.psum_scatter(back, "tensor", scatter_dimension=0).astype(f32)
    parts = tuple(lax.psum_scatter(wg, "tensor", scatter_dimension=0) for wg in (out_wg, gate_wg, up_wg, down_wg))
    sums = lax.psum(parts + (qkv_wg,), "dp")
    small = small.at[1].set(gain2_grad[0])
    small_sum = lax.psum(small, "dp")
    gains = lax.psum(small_sum[:8], "tensor")
    input_rows = hidden_in.astype(f32)
    r1 = mean_square_scale(input_rows)
    g1 = back_sum * gains[0:1]
    centre = jnp.mean(g1 * input_rows, axis=-1, keepdims=True)
    input_grad = (residual_grad + r1 * g1 - (r1 * r1 * r1 * centre) * input_rows).astype(bf16)
    return (output, input_grad, jnp.concatenate((gains, small_sum[8:]))) + tuple(sums)


def finish_kernel(*refs):
    half = len(refs) // 2
    for source, target in zip(refs[:half], refs[half:]):
        target[...] = source[...].astype(target.dtype)


def finish(output, input_grad, qkv_sum, out_sum, gate_sum, up_sum, down_sum):
    part, width = out_sum.shape
    steps = 4
    block = lambda a, at: pl.BlockSpec((a // steps, at), lambda i: (i, 0))
    shift = lambda turn: pl.BlockSpec((part // steps, width), lambda i: (i + turn * steps, 0))
    arrays = (output, input_grad, qkv_sum, qkv_sum, qkv_sum, out_sum, gate_sum, up_sum, down_sum)
    shapes = [output.shape, input_grad.shape] + [out_sum.shape] * 4 + [gate_sum.shape, up_sum.shape, down_sum.shape]
    kinds = [bf16] * 2 + [f32] * 7
    specs = [block(*shape) for shape in shapes]
    return pl.pallas_call(
        finish_kernel,
        grid=(steps,),
        name="finish",
        out_shape=tuple(jax.ShapeDtypeStruct(s, k) for s, k in zip(shapes, kinds)),
        in_specs=specs[:2] + [shift(turn) for turn in range(3)] + specs[5:],
        out_specs=tuple(specs),
        compiler_params=pltpu.CompilerParams(dimension_semantics=("arbitrary",), vmem_limit_bytes=62 << 20),
    )(*arrays)


def gather_by_axis(hidden_in, gains, gate, up, down, out):
    rows = hidden_in.astype(f32)
    normed = (rows * mean_square_scale(rows) * gains[0:1]).astype(bf16)
    return tuple(lax.all_gather(part, "tensor", axis=0) for part in (normed, gate, up, down, out))


def shards(
    by_kernel,
    hidden_in, segment_ids, norm1_gain, query_weight, key_weight, value_weight, out_weight,
    bias_table, norm2_gain, gate_weight, up_weight, down_weight, out_cotangent,
):
    gather_parts = gather if by_kernel else gather_by_axis
    rest_parts = rest_all if by_kernel else rest_by_axis
    rows_here, width = hidden_in.shape
    length = segment_ids.shape[1]
    assert segment_ids.shape[0] == 1 and rows_here == BLK
    heads = bias_table.shape[1]
    gains = jnp.stack((norm1_gain, norm2_gain)).astype(f32)
    normed, gate_w, up_w, down_w, out_w = gather_parts(
        hidden_in, gains, gate_weight, up_weight, down_weight, out_weight
    )
    normed = normed.reshape(length, width)
    query_weight, key_weight, value_weight = query_weight.T, key_weight.T, value_weight.T
    mixed, probs, qt, k, vt, inverse, mixed_here = attend(
        by_kernel, normed, query_weight, key_weight, value_weight, segment_ids, bias_table
    )
    if not by_kernel:
        mixed_here = lax.all_to_all(mixed_here, "tensor", 1, 1)
    output, input_grad, small_sum, out_sum, gate_sum, up_sum, down_sum, qkv_sum = rest_parts(
        gate_w, up_w, down_w, out_w, probs, query_weight, key_weight, value_weight, mixed_here, hidden_in,
        out_cotangent, gains, mixed, inverse, qt, k, vt, normed,
    )
    output, input_grad, query_grad, key_grad, value_grad, out_grad, gate_grad, up_grad, down_grad = finish(
        output, input_grad, qkv_sum, out_sum, gate_sum, up_sum, down_sum
    )
    return (
        output, input_grad, small_sum[0], query_grad.T, key_grad.T, value_grad.T, out_grad,
        small_sum[8 : 8 + heads, :BUCKETS].T, small_sum[1], gate_grad, up_grad, down_grad,
    )


def solution(mesh):
    in_specs = (
        P(("dp", "tensor"), None), P("dp", None), P(),
        P(None, "tensor"), P(None, "tensor"), P(None, "tensor"), P("tensor", None),
        P(None, "tensor"), P(), P(None, "tensor"), P(None, "tensor"), P("tensor", None),
        P(("dp", "tensor"), None),
    )
    out_specs = (
        P(("dp", "tensor"), None), P(("dp", "tensor"), None), P(),
        P(None, "tensor"), P(None, "tensor"), P(None, "tensor"), P("tensor", None),
        P(None, "tensor"), P(), P(None, "tensor"), P(None, "tensor"), P("tensor", None),
    )
    by_kernel = mesh.shape["dp"] == 8 and mesh.shape["tensor"] == 4
    return jax.shard_map(
        functools.partial(shards, by_kernel), mesh=mesh, in_specs=in_specs, out_specs=out_specs, check_vma=False
    )
```

```python
import functools

import jax
import jax.numpy as jnp
from jax import lax
from jax.experimental import pallas as pl
from jax.experimental.pallas import tpu as pltpu
from jax.sharding import PartitionSpec as P

HEAD_DIM = 64
BUCKETS = 32
far_marks = (12, 16, 23, 32, 46, 64, 91)
norm_eps = 1e-06
far_score = 2.0**30
BLK = 256
f32 = jnp.float32
bf16 = jnp.bfloat16


def bucket_of(offset):
    magnitude = jnp.abs(offset)
    within = jnp.minimum(magnitude, 8)
    for far_mark in far_marks:
        within = within + (magnitude >= far_mark).astype(jnp.int32)
    return within + jnp.where(offset > 0, 16, 0).astype(jnp.int32)


def key_range(block, count):
    return range(max(0, block - 2), min(count, block + 3))


def contract(lhs, rhs, left, right):
    return lax.dot_general(
        lhs, rhs, (((left,), (right,)), ((), ())), preferred_element_type=f32
    )


def attend_kernel(
    by_kernel, normed_ref, wq_ref, wk_ref, wv_ref, seg_ref, table_ref,
    mixed_ref, probs_ref, qt_ref, k_ref, vt_ref, inv_ref, here_ref,
    w_s, kt_s, bias_s, score_s, first_s, q_s, v_s, parts_s, send_sem, recv_sem, keep_sem,
):
    head = pl.program_id(0)
    length = normed_ref.shape[0]
    count = length // BLK
    lane = lax.broadcasted_iota(jnp.int32, (BLK, 128), 1)
    low_half = lane < HEAD_DIM

    if by_kernel:
        dp, line = lax.axis_index("dp"), lax.axis_index("tensor")
        others = [lax.rem(line + i, 4) for i in (1, 2, 3)]

        barrier = pltpu.get_barrier_semaphore()

        @pl.when(head == 0)
        def _():
            for other in others:
                pl.semaphore_signal(barrier, inc=1, device_id=(dp, other), device_id_type=MESH_IDS)

        def part_copy(half, i, sender_is_me):
            place = line if sender_is_me else others[i]
            return pltpu.make_async_remote_copy(
                src_ref=parts_s.at[half, others[i]], dst_ref=here_ref.at[half, place],
                send_sem=send_sem.at[half, i], recv_sem=recv_sem.at[half, 2 - i if sender_is_me else i],
                device_id=(dp, others[i]), device_id_type=MESH_IDS,
            )

        def own_copy(half):
            return pltpu.make_async_copy(parts_s.at[half, line], here_ref.at[half, line], keep_sem.at[half])

        def send_part(half):
            for i in (1, 0, 2):
                part_copy(half, i, True).start()
            own_copy(half).start()

    @pl.when(head == 0)
    def _():
        w_s[...] = jnp.zeros_like(w_s)
        for place, ref in enumerate((wq_ref, wk_ref, wv_ref)):
            w_s[256 * place : 256 * place + 192, :] = ref[...]
        row8 = lax.broadcasted_iota(jnp.int32, (8, 128), 0)
        lane8 = lax.broadcasted_iota(jnp.int32, (8, 128), 1)
        spread = jnp.where((lane8 % HEAD_DIM) == row8, 1.0, 0.0).astype(bf16)

        def project(step, carry):
            rows = pl.ds(pl.multiple_of(step * BLK, BLK), BLK)
            seg_row = seg_ref[:, rows]
            kinds = lax.broadcasted_iota(jnp.int32, (8, BLK), 0)
            hot = jnp.where(
                jnp.broadcast_to(seg_row, (8, BLK)) == kinds, 1.0, 0.0
            ).astype(bf16)
            same = contract(hot, spread, 0, 0)
            in_aug = (lane % HEAD_DIM) < 8
            aug_q = jnp.where(in_aug, same, 0.0)
            aug_k = jnp.where(in_aug, (same - 1.0) * far_score, 0.0)
            rows_in = normed_ref[rows, :]
            q = contract(rows_in, w_s[0:256, :], 1, 1)
            k = contract(rows_in, w_s[256:512, :], 1, 1)
            v = contract(rows_in, w_s[512:768, :], 1, 1)
            scale = HEAD_DIM ** (-0.5)
            for h, (cols, mine) in enumerate(
                ((slice(0, 128), low_half), (slice(0, 128), ~low_half), (slice(128, 256), low_half))
            ):
                q_h = jnp.where(mine, q[:, cols] * scale, aug_q).astype(bf16)
                q_s[h, rows, :] = q_h
                qt_ref[h, :, rows] = q_h.T
                k_h = jnp.where(mine, k[:, cols], aug_k).astype(bf16)
                k_ref[h, rows, :] = k_h
                v_h = jnp.where(mine, v[:, cols], 1.0).astype(bf16)
                v_s[h, rows, :] = v_h
                vt_ref[h, :, rows] = v_h.T
                kt_s[h, :, rows] = k_h.T
            return carry

        lax.fori_loop(0, count, project, 0)

    offset = lax.broadcasted_iota(jnp.int32, (BUCKETS, length), 1)
    offset = jnp.where(offset >= length // 2, offset - length, offset)
    hot_bucket = jnp.where(
        bucket_of(offset) == lax.broadcasted_iota(jnp.int32, (BUCKETS, length), 0), 1.0, 0.0
    ).astype(bf16)
    by_head = contract(table_ref[...], hot_bucket, 1, 0)
    this_head = lax.broadcasted_iota(jnp.int32, by_head.shape, 0) == head
    by_offset = jnp.sum(jnp.where(this_head, by_head, 0.0), axis=0, keepdims=True)
    spread_rows = jnp.broadcast_to(by_offset, (BLK, length))
    bias_s[...] = pltpu.roll(spread_rows, 0, 1, stride=1, stride_axis=0)

    for block in range(count):
        rows = slice(block * BLK, (block + 1) * BLK)
        q_h = q_s[head, rows, :]
        top = None
        for key in key_range(block, count):
            part = jnp.dot(
                q_h, kt_s[head, :, key * BLK : (key + 1) * BLK], preferred_element_type=f32
            )
            delta = key - block
            at = (delta * BLK) % length
            part = part + bias_s[:, at : at + BLK]
            score_s[:, key * BLK : (key + 1) * BLK] = part
            top = part if top is None else jnp.maximum(top, part)
        top = jnp.max(jnp.maximum(top[:, :128], top[:, 128:]), axis=1, keepdims=True)
        total = jnp.zeros((BLK, 128), f32)
        for key in key_range(block, count):
            cols = slice(key * BLK, (key + 1) * BLK)
            part = jnp.exp(score_s[:, cols] - top).astype(bf16)
            probs_ref[0, rows, cols] = part
            total = total + jnp.dot(part, v_s[head, cols, :], preferred_element_type=f32)
        sums = pltpu.roll(total, HEAD_DIM, 1)
        inverse = 1.0 / sums
        out = total * inverse

        @pl.when(head == 0)
        def _():
            first_s[rows, 0:128] = out
            first_s[rows, 128:256] = inverse

        @pl.when(head == 1)
        def _():
            pair = jnp.where(low_half, first_s[rows, 0:128], out).astype(bf16)
            mixed_ref[rows, 0:128] = pair
            parts_s[0, block] = pair
            inv_ref[rows, 0:128] = jnp.where(low_half, first_s[rows, 128:256], inverse)

        @pl.when(head == 2)
        def _():
            mixed_ref[rows, 128:192] = out[:, 0:HEAD_DIM].astype(bf16)
            inv_ref[rows, 128:256] = inverse
            parts_s[1, block] = out.astype(bf16)

    if by_kernel:
        @pl.when(head == 1)
        def _():
            pl.semaphore_wait(barrier, 3)
            send_part(0)

        @pl.when(head == 2)
        def _():
            send_part(1)
            for half in range(2):
                own_copy(half).wait()
                for i in range(3):
                    part_copy(half, i, True).wait_send()
                    part_copy(half, i, False).wait_recv()
    else:
        @pl.when(head == 2)
        def _():
            for half in range(2):
                keep = pltpu.make_async_copy(parts_s.at[half], here_ref.at[half], keep_sem.at[half])
                keep.start()
                keep.wait()


MESH_IDS = pl.DeviceIdType.MESH


def attend(by_kernel, normed, wq, wk, wv, segments, bias_table):
    length, width = normed.shape
    heads = bias_table.shape[1]
    inner = heads * HEAD_DIM
    table = bias_table.T
    whole = lambda *dims: pl.BlockSpec(dims, lambda h: (0,) * len(dims))
    return pl.pallas_call(
        functools.partial(attend_kernel, by_kernel),
        grid=(heads,),
        name="attend",
        out_shape=(
            jax.ShapeDtypeStruct((length, inner), bf16),
            jax.ShapeDtypeStruct((heads, length, length), bf16),
            jax.ShapeDtypeStruct((heads, 128, length), bf16),
            jax.ShapeDtypeStruct((heads, length, 128), bf16),
            jax.ShapeDtypeStruct((heads, 128, length), bf16),
            jax.ShapeDtypeStruct((length, 256), f32),
            jax.ShapeDtypeStruct((2, length // BLK, BLK, 128), bf16),
        ),
        in_specs=[
            whole(length, width),
            whole(inner, width),
            whole(inner, width),
            whole(inner, width),
            whole(1, length),
            whole(heads, BUCKETS),
        ],
        out_specs=(
            whole(length, inner),
            pl.BlockSpec((1, length, length), lambda h: (h, 0, 0)),
            whole(heads, 128, length),
            whole(heads, length, 128),
            whole(heads, 128, length),
            whole(length, 256),
            pl.BlockSpec(memory_space=pl.ANY),
        ),
        scratch_shapes=[
            pltpu.VMEM((768, width), bf16),
            pltpu.VMEM((heads, 128, length), bf16),
            pltpu.VMEM((BLK, length), f32),
            pltpu.VMEM((BLK, length), f32),
            pltpu.VMEM((length, 256), f32),
            pltpu.VMEM((heads, length, 128), bf16),
            pltpu.VMEM((heads, length, 128), bf16),
            pltpu.VMEM((2, length // BLK, BLK, 128), bf16),
            pltpu.SemaphoreType.DMA((2, 3)),
            pltpu.SemaphoreType.DMA((2, 3)),
            pltpu.SemaphoreType.DMA((2,)),
        ],
        compiler_params=pltpu.CompilerParams(
            dimension_semantics=("arbitrary",), vmem_limit_bytes=60 << 20,
            **(dict(collective_id=2, has_side_effects=True) if by_kernel else {}),
        ),
        cost_estimate=pl.CostEstimate(flops=3 << 30, bytes_accessed=12 << 20, transcendentals=3 << 20),
    )(normed, wq, wk, wv, segments, table)


def mean_square_scale(rows):
    return lax.rsqrt(jnp.mean(rows * rows, axis=-1, keepdims=True) + norm_eps)


def places():
    dp = lax.axis_index("dp")
    line = lax.axis_index("tensor")
    core = lax.rem(dp, 2)
    x = lax.rem(dp // 2, 2)
    y = dp // 4
    flips = (dp + 1 - 2 * core, dp + 2 - 4 * x, dp + 4 - 8 * y)
    return dp, line, core, x, y, flips


def nearest(line, k):
    upper = line // 2
    inner = line * (1 - upper) + (3 - line) * upper
    block = k + 1 - inner if k == 0 else k + 1
    block = block * (1 - upper) + (3 - block) * upper
    way = (1 if k == 0 else -1) * (1 - 2 * upper)
    return block, way


class Item:
    def __init__(self, place, base, rows, flipped, by_columns=False):
        self.place, self.base, self.rows = place, base, rows
        self.flipped, self.by_columns = flipped, by_columns

    def bits(self, x, y):
        return (y, x) if self.flipped else (x, y)

    def partner(self, level, flips):
        if level == 0:
            return flips[0]
        return flips[1 + ((level - 1) ^ int(self.flipped))]

    def window(self, ref, lead, level, core, first, second):
        width = ref.shape[-1]
        if self.by_columns:
            size = self.rows // (1, 2, 4)[level - 1]
            start = self.base + 0 * core
            if level > 1:
                start = start + first * (self.rows // 2)
            if level > 2:
                start = start + second * (self.rows // 4)
            cols = pl.ds(pl.multiple_of(core * (width // 2), 128), width // 2)
        else:
            size = self.rows // (2, 4, 8)[level - 1]
            start = self.base + core * (self.rows // 2)
            if level > 1:
                start = start + first * (self.rows // 4)
            if level > 2:
                start = start + second * (self.rows // 8)
            cols = pl.ds(0, width)
        rows = pl.ds(pl.multiple_of(start, 16), size)
        if lead is None:
            return ref.at[rows, cols]
        return ref.at[lead, rows, cols]


def weight_items(units, part, width):
    return (
        Item(0, 0, width, False),
        Item(1, 0, width, True),
        Item(2, 0, units // 2, False),
        Item(2, units // 2, units // 2, True),
        Item(3, 0, part, False, by_columns=True),
    )


def gather_kernel(
    hidden_ref, gain_ref, gate_ref, up_ref, down_ref, out_ref,
    normed_all, gate_all, up_all, down_all, out_all,
    z_send, z_recv, p_send, p_recv, own_sem,
    hold_gate, hold_up, hold_down, hold_out, hold_normed,
):
    dp, line, core, x, y, flips = places()
    upper = line // 2
    inner = line * (1 - upper) + (3 - line) * upper
    normed_ref = hold_normed
    own = (gate_ref, up_ref, down_ref, out_ref)
    full = (gate_all, up_all, down_all, out_all)
    units, width = down_ref.shape
    items = weight_items(units, out_ref.shape[0], width)
    count = len(items)

    barrier = pltpu.get_barrier_semaphore()
    for flip in flips:
        pl.semaphore_signal(barrier, inc=1, device_id=(flip, line), device_id_type=MESH_IDS)

    @pl.when(line > 0)
    def _():
        pl.semaphore_signal(barrier, inc=1, device_id=(dp, line - 1), device_id_type=MESH_IDS)

    @pl.when(line < 3)
    def _():
        pl.semaphore_signal(barrier, inc=1, device_id=(dp, line + 1), device_id_type=MESH_IDS)

    rows = hidden_ref[...].astype(f32)
    hold_normed[...] = (rows * mean_square_scale(rows) * gain_ref[0:1, :]).astype(bf16)
    pl.semaphore_wait(barrier, 4 + inner)

    def eighth(i, ref, lead):
        item = items[i]
        first, second = item.bits(x, y)
        return item.window(ref, lead, 3, core, first, second)

    def along(i, block, target, side, first_hop):
        if i == count:
            src = normed_ref if first_hop else normed_all.at[block]
            dst = normed_all.at[block]
        else:
            dst = eighth(i, full[items[i].place], block)
            src = eighth(i, own[items[i].place], None) if first_hop else dst
        return pltpu.make_async_remote_copy(
            src_ref=src, dst_ref=dst, send_sem=z_send.at[i, block, side], recv_sem=z_recv.at[i, block],
            device_id=(dp, target), device_id_type=MESH_IDS,
        )

    def send_own(i):
        @pl.when(line > 0)
        def _():
            along(i, line, line - 1, 0, True).start()

        @pl.when(line < 3)
        def _():
            along(i, line, line + 1, 1, True).start()

    def arrive(i, k):
        block, way = nearest(line, k)
        along(i, block, line, 0, False).wait_recv()

        @pl.when(inner == 1)
        def _():
            along(i, block, line + way, 0, False).start()

    def spread(i, k, stage):
        block, _ = nearest(line, k)
        item = items[i]
        first, second = item.bits(x, y)
        window = item.window(full[item.place], block, 3 - stage, core, first, second)
        return pltpu.make_async_remote_copy(
            src_ref=window, dst_ref=window, send_sem=p_send.at[stage, i, k], recv_sem=p_recv.at[stage, i, k],
            device_id=(item.partner(2 - stage, flips), line), device_id_type=MESH_IDS,
        )

    for i in range(count):
        send_own(i)
    holds = (hold_gate, hold_up, hold_down, hold_out)
    loads = []
    stores = []
    for place, ref in enumerate(own):
        loads.append(pltpu.make_async_copy(ref, holds[place], own_sem.at[0, place]))
        stores.append(pltpu.make_async_copy(holds[place], full[place].at[line], own_sem.at[1, place]))
    for load in loads:
        load.start()
    keep = pltpu.make_async_copy(hold_normed, normed_all.at[line], own_sem.at[1, 4])
    keep.start()
    for load, store in zip(loads, stores):
        load.wait()
        store.start()

    def advance(k, stage):
        for i in range(count):
            if stage > 0:
                spread(i, k, stage - 1).wait_recv()
            spread(i, k, stage).start()

    for k in range(3):
        for i in range(count):
            arrive(i, k)
            spread(i, k, 0).start()
        if k == 2:
            send_own(count)
        if k >= 1:
            advance(k - 1, 1)
        if k >= 2:
            advance(k - 2, 2)
    advance(2, 1)
    arrive(count, 0)
    advance(1, 2)
    arrive(count, 1)
    advance(2, 2)
    arrive(count, 2)

    keep.wait()
    for store in stores:
        store.wait()
    for i in range(count + 1):
        @pl.when(line > 0)
        def _(i=i):
            along(i, line, line - 1, 0, True).wait_send()

        @pl.when(line < 3)
        def _(i=i):
            along(i, line, line + 1, 1, True).wait_send()

        @pl.when(inner == 1)
        def _(i=i):
            for k in range(3):
                block, way = nearest(line, k)
                along(i, block, line + way, 0, False).wait_send()

    for k in range(3):
        for i in range(count):
            spread(i, k, 2).wait_recv()
            for stage in range(3):
                spread(i, k, stage).wait_send()


def gather(hidden_in, gains, gate, up, down, out):
    rows, width = hidden_in.shape
    units, part = gate.shape[1], out.shape[0]
    anywhere = pl.BlockSpec(memory_space=pl.ANY)
    return pl.pallas_call(
        gather_kernel,
        name="gather",
        out_shape=(
            jax.ShapeDtypeStruct((4, rows, width), bf16),
            jax.ShapeDtypeStruct((4, width, units), bf16),
            jax.ShapeDtypeStruct((4, width, units), bf16),
            jax.ShapeDtypeStruct((4, units, width), bf16),
            jax.ShapeDtypeStruct((4, part, width), bf16),
        ),
        in_specs=[pl.BlockSpec(memory_space=pltpu.VMEM)] * 2 + [anywhere] * 4,
        out_specs=(anywhere,) * 5,
        scratch_shapes=[
            pltpu.SemaphoreType.DMA((6, 4, 2)),
            pltpu.SemaphoreType.DMA((6, 4)),
            pltpu.SemaphoreType.DMA((3, 5, 3)),
            pltpu.SemaphoreType.DMA((3, 5, 3)),
            pltpu.SemaphoreType.DMA((2, 5)),
            pltpu.VMEM(gate.shape, bf16),
            pltpu.VMEM(up.shape, bf16),
            pltpu.VMEM(down.shape, bf16),
            pltpu.VMEM(out.shape, bf16),
            pltpu.VMEM(hidden_in.shape, bf16),
        ],
        compiler_params=pltpu.CompilerParams(collective_id=1, has_side_effects=True),
    )(hidden_in, gains, gate, up, down, out)


class Named:
    def __init__(self, names, refs):
        for name, ref in zip(names, refs):
            setattr(self, name, ref)


def remote(src, dst, send, recv, target):
    return pltpu.make_async_remote_copy(
        src_ref=src, dst_ref=dst, send_sem=send, recv_sem=recv, device_id=target, device_id_type=MESH_IDS
    )


def greet(dp, line, flips):
    barrier = pltpu.get_barrier_semaphore()
    for flip in flips:
        pl.semaphore_signal(barrier, inc=1, device_id=(flip, line), device_id_type=MESH_IDS)
    for i in (1, 2, 3):
        pl.semaphore_signal(
            barrier, inc=1, device_id=(dp, lax.rem(line + i, 4)), device_id_type=MESH_IDS
        )
    return barrier


def unit_parts(s, r):
    groups = r.mixed_here.shape[1]

    def mixed_of(g):
        return jnp.concatenate((r.mixed_here[0, g], r.mixed_here[1, g][:, 0:HEAD_DIM]), axis=1)

    def begin():
        mixed = jnp.concatenate([mixed_of(g) for g in range(groups)], axis=1)
        out_w = jnp.concatenate([s.out_w[g] for g in range(groups)], axis=0)
        residual = r.hidden_in[...].astype(f32) + jnp.dot(mixed, out_w, preferred_element_type=f32)
        s.residual[...] = residual
        s.normed2[...] = (residual * mean_square_scale(residual) * r.gains[1:2, :]).astype(bf16)
        s.ahead[...] = residual
        s.behind[...] = jnp.zeros_like(s.behind)

    def block(b, slot):
        normed = s.normed2[...]
        cot = r.cot[...]
        gate_w, up_w, down_w = s.gate_w[slot], s.up_w[slot], s.down_w[slot]
        gate = jnp.dot(normed, gate_w, preferred_element_type=f32)
        up = jnp.dot(normed, up_w, preferred_element_type=f32)
        hidden_grad = contract(cot, down_w, 1, 1)
        c0 = 0.7978845608028654
        square = gate * gate
        bend = jnp.tanh(gate * (c0 + (c0 * 0.044715) * square))
        half = 0.5 + 0.5 * bend
        act = gate * half
        slope = half + 0.5 * gate * (1.0 - bend * bend) * (c0 + (3.0 * c0 * 0.044715) * square)
        hidden = (act * up).astype(bf16)
        gate_grad = (hidden_grad * up * slope).astype(bf16)
        up_grad = (hidden_grad * act).astype(bf16)
        s.ahead[...] += jnp.dot(hidden, down_w, preferred_element_type=f32)
        s.behind[...] += contract(gate_grad, gate_w, 1, 1) + contract(up_grad, up_w, 1, 1)
        s.down_wg[b] = contract(hidden, cot, 0, 0).astype(bf16)
        s.gate_wg[b] = contract(normed, gate_grad, 0, 0).astype(bf16)
        s.up_wg[b] = contract(normed, up_grad, 0, 0).astype(bf16)

    def end():
        residual = s.residual[...]
        r.output[...] = s.ahead[...].astype(bf16)
        back = s.behind[...]
        scale = mean_square_scale(residual)
        s.small_mine[1:2, :] = jnp.sum(back * residual * scale, axis=0, keepdims=True)
        g = back * r.gains[1:2, :]
        centre = jnp.mean(g * residual, axis=-1, keepdims=True)
        residual_grad = r.cot[...].astype(f32) + scale * g - (scale * scale * scale * centre) * residual
        low = residual_grad.astype(bf16)
        s.behind[...] = residual_grad
        for g_at in range(groups):
            s.grad_here[g_at] = contract(low, s.out_w[g_at], 1, 1).astype(bf16)

    def out_grad():
        low = s.behind[...].astype(bf16)
        for g_at in range(groups):
            s.out_wg[g_at] = contract(mixed_of(g_at), low, 0, 0).astype(bf16)

    return begin, block, end, out_grad


def attention_back_tasks(s, r):
    heads, length = s.dot.shape[0], s.dot.shape[1]
    count = length // BLK
    lane = lax.broadcasted_iota(jnp.int32, (BLK, 128), 1)
    low_half = lane < HEAD_DIM
    tasks = []

    def probs_copy(h, block):
        at = (h * count + block) % 2
        rows = pl.ds(block * BLK, BLK)
        return pltpu.make_async_copy(r.probs_all.at[h, rows, :], s.probs.at[at], s.probs_sem.at[at])

    def prepare():
        probs_copy(0, 0).start()
        probs_copy(0, 1).start()

        def body(step, carry):
            rows = pl.ds(pl.multiple_of(step * BLK, BLK), BLK)
            for h in range(heads):
                cols = slice(0, 128) if h < 2 else slice(128, 256)
                mine = ~low_half if h == 1 else low_half
                if h < 2:
                    grad = s.mixed_grad[step, :, 0:128].astype(f32)
                    mix = r.mixed[rows, 0:128].astype(f32)
                else:
                    fill = jnp.zeros((BLK, HEAD_DIM), f32)
                    grad = jnp.concatenate((s.mixed_grad[step, :, 128:192].astype(f32), fill), axis=1)
                    mix = jnp.concatenate((r.mixed[rows, 128:192].astype(f32), fill), axis=1)
                grad = jnp.where(mine, grad * r.inverse[rows, cols], 0.0)
                centre = -jnp.sum(grad * mix, axis=1, keepdims=True)
                high = centre.astype(bf16).astype(f32)
                base = 0 if h == 1 else HEAD_DIM
                grad = jnp.where(lane == base, high, grad)
                grad = jnp.where(lane == base + 1, centre - high, grad)
                low = grad.astype(bf16)
                s.dot[h, rows, :] = low
                s.dott[h, :, rows] = low.T
            return carry

        lax.fori_loop(0, count, body, 0)

    tasks.append(prepare)

    def block_step(h, block):
        if block == 0:
            s.near[...] = jnp.zeros_like(s.near)
            s.far[...] = jnp.zeros_like(s.far)
            s.dkt[...] = jnp.zeros_like(s.dkt)
            s.dvt[...] = jnp.zeros_like(s.dvt)
        probs_copy(h, block).wait()
        at = (h * count + block) % 2
        rows = slice(block * BLK, (block + 1) * BLK)
        d_h = s.dot[h, rows, :]
        dt_h = s.dott[h, :, rows]
        qt_h = r.qt[h, :, rows]
        query_grad = jnp.zeros((BLK, 128), f32)
        for key in key_range(block, count):
            cols = slice(key * BLK, (key + 1) * BLK)
            probs = s.probs[at, :, cols]
            slope = jnp.dot(d_h, r.vt[h, :, cols], preferred_element_type=f32)
            grad = probs.astype(f32) * slope
            low = grad.astype(bf16)
            delta = key - block
            if abs(delta) == 2:
                s.far[0 if delta < 0 else 1] += grad[:, :128] + grad[:, 128:]
            else:
                s.near[:, (delta + 1) * BLK : (delta + 2) * BLK] += grad
            query_grad = query_grad + jnp.dot(low, r.k[h, cols, :], preferred_element_type=f32)
            s.dkt[:, cols] += jnp.dot(qt_h, low, preferred_element_type=f32)
            s.dvt[:, cols] += jnp.dot(dt_h, probs, preferred_element_type=f32)
        s.grad[rows, 0:128] = query_grad * HEAD_DIM ** (-0.5)
        turn = h * count + block + 2
        if turn < heads * count:
            probs_copy(turn // count, turn % count).start()

    def head_end(h):
        def body(step, carry):
            rows = pl.ds(pl.multiple_of(step * BLK, BLK), BLK)
            s.grad[rows, 128:256] = s.dkt[:, rows].T
            s.grad[rows, 256:384] = s.dvt[:, rows].T
            for at in range(3):
                part = s.grad[rows, 128 * at : 128 * at + 128]
                if h == 0:
                    s.joined[rows, 256 * at : 256 * at + 128] = part.astype(bf16)
                elif h == 1:
                    before = s.joined[rows, 256 * at : 256 * at + 128].astype(f32)
                    s.joined[rows, 256 * at : 256 * at + 128] = jnp.where(low_half, before, part).astype(bf16)
                else:
                    s.joined[rows, 256 * at + 128 : 256 * at + 256] = jnp.where(low_half, part, 0.0).astype(bf16)
            return carry

        lax.fori_loop(0, count, body, 0)
        place = lax.broadcasted_iota(jnp.int32, (BLK, 3 * BLK), 1) - BLK
        place = place - lax.broadcasted_iota(jnp.int32, (BLK, 3 * BLK), 0)
        s.bucket[...] = bucket_of(place)
        s.table[...] = jnp.zeros_like(s.table)

        def count_bucket(b, carry):
            part = jnp.sum(jnp.where(s.bucket[...] == b, s.near[...], 0.0), axis=0, keepdims=True)
            folded = part[:, 0:128]
            for at in range(1, 6):
                folded = folded + part[:, at * 128 : (at + 1) * 128]
            s.table[pl.ds(b, 1), :] = folded
            return carry

        lax.fori_loop(0, BUCKETS, count_bucket, 0)
        for side, b in ((0, 15), (1, 31)):
            s.table[b : b + 1, :] += jnp.sum(s.far[side], axis=0, keepdims=True)
        flat = lax.dot_general(
            jnp.ones((8, 128), f32), s.table[...], (((1,), (1,)), ((), ())),
            preferred_element_type=f32, precision=lax.Precision.HIGHEST,
        )
        s.small_mine[8 + h : 9 + h, 0:BUCKETS] = flat[0:1]

    for h in range(heads):
        for block in range(count):
            tasks.append(functools.partial(block_step, h, block))
        tasks.append(functools.partial(head_end, h))

    def rows_grad(block):
        rows = slice(block * BLK, (block + 1) * BLK)
        part = jnp.dot(s.joined[rows, :], s.w[...], preferred_element_type=f32)
        s.back_acc[block] = part.astype(bf16)
        s.gain[...] += jnp.sum(part * r.normed[rows, :].astype(f32), axis=0, keepdims=True)

    def weights_grad(at):
        part = contract(s.joined[:, 256 * at : 256 * at + 256], r.normed[...], 0, 0)
        s.qkv_wg[192 * at : 192 * at + 192, :] = part[0:192].astype(bf16)

    return tasks, rows_grad, weights_grad


REST_OPERANDS = tuple(dict(
    gate_all=0, up_all=0, down_all=0, out_all=0, probs_all=0, wq=0, wk=0, wv=0, mixed_here=0, hidden_in=0,
    cot=0, gains=0, mixed=0, inverse=0, qt=0, k=0, vt=0, normed=0,
))
REST_RESULTS = tuple(dict(
    output=0, input_grad=0, small_sum=0, out_sum=0, gate_sum=0, up_sum=0, down_sum=0, qkv_sum=0,
))


def load_weights(s, r, b, slot):
    pairs = ((r.gate_all, s.gate_w), (r.up_all, s.up_w), (r.down_all, s.down_w))
    return [
        pltpu.make_async_copy(src.at[b], dst.at[slot], s.weight_sem.at[i, slot]) for i, (src, dst) in enumerate(pairs)
    ]


def load_small(s, r):
    copies = [pltpu.make_async_copy(r.out_all, s.out_w, s.first_sem.at[0])]
    for place, ref in enumerate((r.wq, r.wk, r.wv)):
        part = ref.shape[0]
        copies.append(pltpu.make_async_copy(ref, s.w.at[pl.ds(256 * place, part), :], s.first_sem.at[1 + place]))
    return copies


def start_all(s, r):
    groups = s.out_w.shape[0]
    for copy in load_small(s, r) + load_weights(s, r, 0, 0):
        copy.start()
    s.small_mine[...] = jnp.zeros_like(s.small_mine)
    s.gain[...] = jnp.zeros_like(s.gain)
    for place in range(3):
        s.w[256 * place + 192 : 256 * place + 256, :] = jnp.zeros((64, s.w.shape[1]), bf16)
    return groups


def input_grad_rows(s, r, back):
    rows = r.hidden_in[...].astype(f32)
    scale = mean_square_scale(rows)
    g = back * r.gains[0:1, :]
    centre = jnp.mean(g * rows, axis=-1, keepdims=True)
    r.input_grad[...] = (s.behind[...] + scale * g - (scale * scale * scale * centre) * rows).astype(bf16)


def add_rows(target, start, size, source):
    step = 32 if size % 32 == 0 else 16

    def body(i, carry):
        at = pl.multiple_of(i * step, step)
        rows = pl.ds(pl.multiple_of(start + at, 16), step)
        target[rows, :] = (target[rows, :].astype(f32) + source[pl.ds(at, step), :].astype(f32)).astype(bf16)
        return carry

    lax.fori_loop(0, size // step, body, 0)


def rest_kernel(names, *refs):
    r = Named(REST_OPERANDS + REST_RESULTS, refs)
    s = Named(names, refs[len(REST_OPERANDS) + len(REST_RESULTS) :])
    dp, line, core, x, y, flips = places()
    units, width = s.down_wg.shape[1:]
    part = s.out_wg.shape[1]
    items = weight_items(units, part, width)
    item_count = len(items)
    grads = (s.gate_wg, s.up_wg, s.down_wg, s.out_wg, s.qkv_wg)
    sums = (r.gate_sum, r.up_sum, r.down_sum, r.out_sum, r.qkv_sum)
    begin_unit, unit_block, end_unit, out_grad = unit_parts(s, r)
    tasks, rows_grad, weights_grad = attention_back_tasks(s, r)
    groups = start_all(s, r)
    barrier = greet(dp, line, flips)

    def item_of(i, block):
        if i < item_count - 1:
            return items[i]
        if i == item_count - 1:
            return Item(3, 0, part, block > 1, True)
        turn = i - item_count
        return Item(4, turn * part, part, turn % 2 == 0, True)

    def lead(i, block):
        return block if i < item_count else None

    def number(i, block):
        return i * groups + block if i < item_count else (item_count - 1) * groups + i - 1

    def at_block(ref, i, block):
        return ref.at[block] if i < item_count else ref

    def arrival(stage, i, block):
        return at_block(getattr(s, stage + str(i)), i, block)

    def held(i, block):
        item = item_of(i, block)
        if item.by_columns:
            return arrival("half", i, block), 0, item.rows
        return grads[item.place].at[block], item.base + core * (item.rows // 2), item.rows // 2

    def load_copy(i, block):
        item = item_of(i, block)
        window = item.window(grads[item.place], lead(i, block), 1, core, 0, 0)
        return pltpu.make_async_copy(window, arrival("half", i, block), s.load_sem.at[number(i, block)])

    def core_copy(i, block):
        item, n = item_of(i, block), number(i, block)
        window = item.window(grads[item.place], lead(i, block), 1, 1 - core, 0, 0)
        return remote(window, arrival("core", i, block), s.core_send.at[n], s.core_recv.at[n], (flips[0], line))

    def begin(i, block):
        core_copy(i, block).start()
        if item_of(i, block).by_columns:
            load_copy(i, block).start()

    def pair_copy(i, block, stage):
        ref, base, half = held(i, block)
        item, n = item_of(i, block), number(i, block)
        first, second = item.bits(x, y)
        if stage == 0:
            size, start, target = half // 2, (1 - first) * (half // 2), arrival("first", i, block)
        else:
            size = half // 4
            start, target = first * (half // 2) + (1 - second) * (half // 4), arrival("second", i, block)
        window = ref.at[pl.ds(pl.multiple_of(base + start, 16), size), :]
        partner = item.partner(1 + stage, flips)
        return remote(window, target, s.pair_send.at[stage, n], s.pair_recv.at[stage, n], (partner, line))

    def eighth(i, block):
        ref, base, half = held(i, block)
        first, second = item_of(i, block).bits(x, y)
        start = pl.multiple_of(base + first * (half // 2) + second * (half // 4), 16)
        return ref, start, half // 4

    def mine(i, block):
        ref, start, size = eighth(i, block)
        return ref.at[pl.ds(start, size), :]

    def line_copy(i, block, sender):
        target = getattr(s, "line" + str(i)).at[sender]
        return remote(
            mine(i, block), target, s.line_send.at[i, block], s.line_recv.at[i, sender], (dp, block)
        )

    def spread_copy(i, block, stage):
        item, n = item_of(i, block), number(i, block)
        first, second = item.bits(x, y)
        window = item.window(sums[item.place], None, 3 - stage, core, first, second)
        src = mine(i, block) if stage == 0 else window
        return remote(
            src, window, s.spread_send.at[stage, n], s.spread_recv.at[stage, n],
            (item.partner(2 - stage, flips), line),
        )

    def keep_copy(i, block):
        item = item_of(i, block)
        first, second = item.bits(x, y)
        window = item.window(sums[item.place], None, 3, core, first, second)
        return pltpu.make_async_copy(mine(i, block), window, s.load_sem.at[number(i, block)])

    def step_core(i, block, send=True):
        if item_of(i, block).by_columns:
            load_copy(i, block).wait()
        core_copy(i, block).wait_recv()
        ref, base, half = held(i, block)
        add_rows(ref, base, half, arrival("core", i, block))
        if send:
            pair_copy(i, block, 0).start()

    def step_first(i, block):
        pair_copy(i, block, 0).wait_recv()
        ref, base, half = held(i, block)
        first, _ = item_of(i, block).bits(x, y)
        add_rows(ref, base + first * (half // 2), half // 2, arrival("first", i, block))
        pair_copy(i, block, 1).start()

    def step_second(i, block):
        pair_copy(i, block, 1).wait_recv()
        ref, start, size = eighth(i, block)
        add_rows(ref, start, size, arrival("second", i, block))
        if i < item_count:
            pl.when(line != block)(lambda: line_copy(i, block, line).start())
        else:
            spread_copy(i, block, 0).start()
            keep_copy(i, block).start()

    def step_last(i, block):
        @pl.when(line == block)
        def _():
            ref, start, size = eighth(i, block)
            others = [o for o in range(groups) if o != block]
            for o in others:
                line_copy(i, block, o).wait_recv()
            arrived = getattr(s, "line" + str(i))
            total = ref[pl.ds(start, size), :].astype(f32)
            for o in others:
                total = total + arrived[o].astype(f32)
            ref[pl.ds(start, size), :] = total.astype(bf16)
            spread_copy(i, block, 0).start()
            keep_copy(i, block).start()

    def step_spread(i, block, stage):
        def act():
            if stage == 1:
                keep_copy(i, block).wait()
            spread_copy(i, block, stage - 1).wait_recv()
            if stage < 3:
                spread_copy(i, block, stage).start()

        if i < item_count:
            pl.when(line == block)(act)
        else:
            act()

    def swap_copy(i, sender_is_me):
        other = lax.rem(line + i, 4)
        if sender_is_me:
            return remote(
                s.grad_here.at[other], s.mixed_grad.at[line], s.swap_send.at[i - 1], s.swap_recv.at[3 - i], (dp, other)
            )
        return remote(
            s.grad_here.at[other], s.mixed_grad.at[other], s.swap_send.at[i - 1], s.swap_recv.at[i - 1], (dp, other)
        )

    def back_copy(block, at, right):
        src, send = s.back_acc.at[block], s.back_send.at[block]
        if right:
            return remote(src, s.back_left.at[block], send, s.back_left_recv.at[block], (dp, at + 1))
        return remote(src, s.back_right.at[block], send, s.back_right_recv.at[block], (dp, at - 1))

    def back_hop(hop, distance):
        @pl.when(line == hop)
        def _():
            block = hop + distance
            if block <= groups - 1:
                if hop > 0:
                    back_copy(block, hop, True).wait_recv()
                    add_rows(s.back_acc.at[block], 0, s.back_acc.shape[1], s.back_left.at[block])
                back_copy(block, hop, True).start()

        at = groups - 1 - hop

        @pl.when(line == at)
        def _():
            block = at - distance
            if block >= 0:
                if hop > 0:
                    back_copy(block, at, False).wait_recv()
                    add_rows(s.back_acc.at[block], 0, s.back_acc.shape[1], s.back_right.at[block])
                back_copy(block, at, False).start()

    def collect_rows():
        for block in range(groups):
            @pl.when(line == block)
            def _(block=block):
                total = s.back_acc[block].astype(f32)
                if block > 0:
                    back_copy(block, block, True).wait_recv()
                    total = total + s.back_left[block].astype(f32)
                if block < groups - 1:
                    back_copy(block, block, False).wait_recv()
                    total = total + s.back_right[block].astype(f32)
                input_grad_rows(s, r, total)

    def small_copy(stage):
        partner = (flips[stage], line) if stage < 3 else (dp, line + 1 - 2 * lax.rem(line, 2))
        if stage == 4:
            partner = (dp, lax.rem(line + 2, 4))
        return remote(s.small_mine, s.small_got.at[stage], s.small_send.at[stage], s.small_recv.at[stage], partner)

    def small_step(stage):
        if stage > 0:
            small_copy(stage - 1).wait()
            rows = lax.broadcasted_iota(jnp.int32, s.small_mine.shape, 0)
            got = s.small_got[stage - 1]
            if stage > 3:
                got = jnp.where(rows < 8, got, 0.0)
            s.small_mine[...] = s.small_mine[...] + got
        else:
            s.small_mine[0:1, :] = s.gain[...] / r.gains[0:1, :]
        if stage < 5:
            small_copy(stage).start()
        else:
            r.small_sum[...] = s.small_mine[...]

    outer, inner = (0, groups - 1), tuple(range(1, groups - 1))
    teams = [[(i, block) for i in (0, 1)] for block in outer + inner]
    teams += [[(i, block) for block in pair for i in (2, 3)] for pair in (outer, inner)]
    teams.append([(item_count - 1, block) for block in range(groups)])
    teams.append([(item_count + turn, 0) for turn in range(3)])
    stage_acts = (
        step_core, step_first, step_second, step_last,
        lambda i, block: step_spread(i, block, 1),
        lambda i, block: step_spread(i, block, 2),
        lambda i, block: step_spread(i, block, 3),
    )
    done = []

    def tend(moment):
        for name, team in WHEN.get(moment, ()):
            done.append((name, team))
            if name == SMALL:
                small_step(team)
            elif name == ROWS:
                collect_rows()
            elif name == HOP:
                back_hop(*team)
            else:
                for i, block in teams[team]:
                    stage_acts[name](i, block)

    for copy in load_small(s, r):
        copy.wait()
    begin_unit()

    order = outer + inner
    for turn, block in enumerate(order):
        for copy in load_weights(s, r, block, turn % 2):
            copy.wait()
        if turn + 1 < groups:
            for copy in load_weights(s, r, order[turn + 1], (turn + 1) % 2):
                copy.start()
        unit_block(block, turn % 2)
        if turn == 0:
            pl.semaphore_wait(barrier, 6)
        for i in range(item_count - 1):
            begin(i, block)
        tend(UNIT + turn)
    end_unit()
    for i in (2, 1, 3):
        swap_copy(i, True).start()
    swap_keep = pltpu.make_async_copy(s.grad_here.at[line], s.mixed_grad.at[line], s.swap_keep)
    swap_keep.start()
    out_grad()
    for block in range(groups):
        begin(item_count - 1, block)
    tend(SWAP)
    for i in (1, 2, 3):
        swap_copy(i, False).wait_recv()
        swap_copy(i, True).wait_send()
    swap_keep.wait()
    for turn, task in enumerate(tasks):
        task()
        tend(turn)
    for block in range(groups):
        rows_grad(block)
    for distance in (3, 2, 1):
        back_hop(0, distance)
    for turn in range(3):
        weights_grad(turn)
        begin(item_count + turn, 0)
    small_step(0)

    for turn in range(len(WHEN)):
        tend(END + turn)
    assert len(done) == len(set(done)) == 7 * 7 + 6 + 5 + 4
    for block in range(groups):
        pl.when(line < block)(lambda block=block: back_copy(block, line, True).wait_send())
        pl.when(line > block)(lambda block=block: back_copy(block, line, False).wait_send())
    for i, block in sum(teams, []):
        core_copy(i, block).wait_send()
        pair_copy(i, block, 0).wait_send()
        pair_copy(i, block, 1).wait_send()

        def sent(i=i, block=block):
            for stage in range(3):
                spread_copy(i, block, stage).wait_send()

        if i < item_count:
            pl.when(line == block)(sent)
            pl.when(line != block)(lambda i=i, block=block: line_copy(i, block, line).wait_send())
        else:
            sent()


CORE, FIRST, SECOND, LAST, SPREAD1, SPREAD2, SPREAD3, SMALL, HOP, ROWS = range(10)
UNIT, SWAP, END = 100, 110, 120
WHEN = {
    UNIT + 1: [(CORE, 0), (CORE, 1)],
    UNIT + 3: [(FIRST, 0), (CORE, 2), (FIRST, 1), (CORE, 3)],
    SWAP: [(SECOND, 0), (FIRST, 2), (CORE, 4), (SECOND, 1)],
    0: [(FIRST, 3), (CORE, 5), (SECOND, 2)],
    3: [(FIRST, 4), (CORE, 6), (SECOND, 3)],
    5: [(LAST, 0), (LAST, 1)],
    7: [(FIRST, 5), (SECOND, 4), (SPREAD1, 0), (SPREAD1, 1)],
    9: [(LAST, 2)],
    11: [(FIRST, 6), (SECOND, 5), (LAST, 3), (SPREAD2, 0), (SPREAD2, 1)],
    13: [(SPREAD1, 2), (SECOND, 6)],
    14: [(LAST, 4), (SPREAD1, 3), (SPREAD3, 0), (SPREAD3, 1), (SPREAD2, 2)],
    END + 0: [(CORE, 7), (LAST, 5), (SPREAD1, 4), (SPREAD2, 3)],
    END + 1: [(SMALL, 1), (HOP, (1, 2)), (FIRST, 7), (LAST, 6), (SPREAD3, 2), (SPREAD1, 5)],
    END + 2: [(SMALL, 2), (HOP, (1, 1)), (SECOND, 7), (SPREAD1, 6), (SPREAD2, 4), (SPREAD3, 3)],
    END + 3: [(SMALL, 3), (HOP, (2, 1)), (SPREAD1, 7), (SPREAD2, 5), (SPREAD2, 6)],
    END + 4: [(SMALL, 4), (SPREAD2, 7), (SPREAD3, 4), (SPREAD3, 5), (SPREAD3, 6)],
    END + 5: [(SMALL, 5), (SPREAD3, 7), (ROWS, 0)],
}

def common_scratch(groups, rows, heads, length, width, units, part):
    dma = pltpu.SemaphoreType.DMA
    return dict(
        residual=pltpu.VMEM((rows, width), f32),
        normed2=pltpu.VMEM((rows, width), bf16),
        ahead=pltpu.VMEM((rows, width), f32),
        behind=pltpu.VMEM((rows, width), f32),
        out_w=pltpu.VMEM((groups, part, width), bf16),
        gate_w=pltpu.VMEM((2, width, units), bf16),
        up_w=pltpu.VMEM((2, width, units), bf16),
        down_w=pltpu.VMEM((2, units, width), bf16),
        gate_wg=pltpu.VMEM((groups, width, units), bf16),
        up_wg=pltpu.VMEM((groups, width, units), bf16),
        down_wg=pltpu.VMEM((groups, units, width), bf16),
        out_wg=pltpu.VMEM((groups, part, width), bf16),
        qkv_wg=pltpu.VMEM((3 * part, width), bf16),
        grad_here=pltpu.VMEM((groups, rows, part), bf16),
        mixed_grad=pltpu.VMEM((groups, rows, part), bf16),
        back_acc=pltpu.VMEM((groups, rows, width), bf16),
        small_mine=pltpu.VMEM((16, width), f32),
        gain=pltpu.VMEM((1, width), f32),
        probs=pltpu.VMEM((2, BLK, length), bf16),
        w=pltpu.VMEM((768, width), bf16),
        dot=pltpu.VMEM((heads, length, 128), bf16),
        dott=pltpu.VMEM((heads, 128, length), bf16),
        grad=pltpu.VMEM((length, 384), f32),
        joined=pltpu.VMEM((length, 768), bf16),
        near=pltpu.VMEM((BLK, 3 * BLK), f32),
        bucket=pltpu.VMEM((BLK, 3 * BLK), jnp.int32),
        table=pltpu.VMEM((BUCKETS, 128), f32),
        far=pltpu.VMEM((2, BLK, 128), f32),
        dkt=pltpu.VMEM((128, length), f32),
        dvt=pltpu.VMEM((128, length), f32),
        weight_sem=dma((3, 2)), first_sem=dma((4,)), probs_sem=dma((2,)),
    )


def result_shapes(rows, width, units, part):
    return (
        jax.ShapeDtypeStruct((rows, width), bf16),
        jax.ShapeDtypeStruct((rows, width), bf16),
        jax.ShapeDtypeStruct((16, width), f32),
        jax.ShapeDtypeStruct((part, width), bf16),
        jax.ShapeDtypeStruct((width, units), bf16),
        jax.ShapeDtypeStruct((width, units), bf16),
        jax.ShapeDtypeStruct((units, width), bf16),
        jax.ShapeDtypeStruct((3 * part, width), bf16),
    )


def rest_all(gate_all, up_all, down_all, out_all, probs, wq, wk, wv, mixed_here, hidden_in, cot, gains,
             mixed, inverse, qt, k, vt, normed):
    groups, part = mixed_here.shape[1], wq.shape[0]
    rows, width = hidden_in.shape
    heads, length = k.shape[0], k.shape[1]
    units = down_all.shape[1]
    items = weight_items(units, part, width)
    n = 3 + groups * len(items)
    dma = pltpu.SemaphoreType.DMA
    scratch = common_scratch(groups, rows, heads, length, width, units, part)
    for stage, divide in (("half", 1), ("core", 1), ("first", 2), ("second", 4), ("line", 4)):
        for i, item in enumerate(items):
            cols = (units, units, width, width)[item.place]
            shape = (item.rows, cols // 2) if item.by_columns else (item.rows // 2, cols)
            if stage != "half" or item.by_columns:
                scratch[stage + str(i)] = pltpu.VMEM((groups, shape[0] // divide, shape[1]), bf16)
        for turn in range(3):
            if stage != "line":
                scratch[stage + str(len(items) + turn)] = pltpu.VMEM((part // divide, width // 2), bf16)
    scratch.update(
        small_got=pltpu.VMEM((5, 16, width), f32),
        back_left=pltpu.VMEM((groups, rows, width), bf16),
        back_right=pltpu.VMEM((groups, rows, width), bf16),
        load_sem=dma((n,)), core_send=dma((n,)), core_recv=dma((n,)),
        pair_send=dma((2, n)), pair_recv=dma((2, n)),
        line_send=dma((len(items), groups)), line_recv=dma((len(items), groups)),
        spread_send=dma((3, n)), spread_recv=dma((3, n)),
        back_send=dma((groups,)), back_left_recv=dma((groups,)), back_right_recv=dma((groups,)),
        small_send=dma((5,)), small_recv=dma((5,)),
        swap_send=dma((3,)), swap_recv=dma((3,)), swap_keep=dma,
    )
    anywhere = pl.BlockSpec(memory_space=pl.ANY)
    inside = pl.BlockSpec(memory_space=pltpu.VMEM)
    return pl.pallas_call(
        functools.partial(rest_kernel, tuple(scratch)),
        name="rest_all",
        out_shape=result_shapes(rows, width, units, part),
        in_specs=[anywhere] * 8 + [inside] * 10,
        out_specs=(inside,) * 3 + (anywhere,) * 5,
        scratch_shapes=list(scratch.values()),
        compiler_params=pltpu.CompilerParams(
            collective_id=3, has_side_effects=True, vmem_limit_bytes=62 << 20
        ),
    )(gate_all, up_all, down_all, out_all, probs, wq, wk, wv, mixed_here, hidden_in, cot, gains,
      mixed, inverse, qt, k, vt, normed)


UNIT_RESULTS = tuple(dict(
    output=0, residual_grad=0, grads=0, gain2_grad=0, out_out=0, gate_out=0, up_out=0, down_out=0,
))


def unit_local_kernel(names, *refs):
    operands = tuple(dict(gate_all=0, up_all=0, down_all=0, out_all=0, mixed_here=0, hidden_in=0, cot=0, gains=0))
    r = Named(operands + UNIT_RESULTS, refs)
    s = Named(names, refs[len(operands) + len(UNIT_RESULTS) :])
    s.out_wg, s.gate_wg, s.up_wg, s.down_wg = r.out_out, r.gate_out, r.up_out, r.down_out
    s.behind, s.grad_here = r.residual_grad, r.grads
    begin, block, end, out_grad = unit_parts(s, r)
    groups = s.out_w.shape[0]
    first = [pltpu.make_async_copy(r.out_all, s.out_w, s.first_sem.at[0])] + load_weights(s, r, 0, 0)
    for copy in first:
        copy.start()
    first[0].wait()
    begin()

    def body(b, carry):
        slot = lax.rem(b, 2)
        for copy in load_weights(s, r, b, slot):
            copy.wait()

        @pl.when(b + 1 < groups)
        def _():
            for copy in load_weights(s, r, b + 1, 1 - slot):
                copy.start()

        block(b, slot)
        return carry

    lax.fori_loop(0, groups, body, 0)
    end()
    out_grad()
    r.gain2_grad[...] = s.small_mine[1:2, :]


def back_local_kernel(names, *refs):
    operands = tuple(dict(probs_all=0, mixed=0, inverse=0, qt=0, k=0, vt=0, normed=0, wq=0, wk=0, wv=0, gains=0, mixed_grad=0))
    results = tuple(dict(back_out=0, qkv_out=0, small_out=0))
    r = Named(operands + results, refs)
    s = Named(names, refs[len(operands) + len(results) :])
    s.mixed_grad, s.qkv_wg, s.small_mine, s.back_acc = r.mixed_grad, r.qkv_out, r.small_out, r.back_out
    tasks, rows_grad, weights_grad = attention_back_tasks(s, r)
    s.small_mine[...] = jnp.zeros_like(s.small_mine)
    s.gain[...] = jnp.zeros_like(s.gain)
    s.w[...] = jnp.zeros_like(s.w)
    for place, ref in enumerate((r.wq, r.wk, r.wv)):
        s.w[256 * place : 256 * place + ref.shape[0], :] = ref[...]
    for task in tasks:
        task()
    for block in range(r.back_out.shape[0]):
        rows_grad(block)
    for turn in range(3):
        weights_grad(turn)
    s.small_mine[0:1, :] = s.gain[...] / r.gains[0:1, :]


def rest_by_axis(gate_all, up_all, down_all, out_all, probs, wq, wk, wv, mixed_here, hidden_in, cot, gains,
                 mixed, inverse, qt, k, vt, normed):
    groups, part = mixed_here.shape[1], wq.shape[0]
    rows, width = hidden_in.shape
    heads, length = k.shape[0], k.shape[1]
    units = down_all.shape[1]
    anywhere = pl.BlockSpec(memory_space=pl.ANY)
    inside = pl.BlockSpec(memory_space=pltpu.VMEM)
    every = common_scratch(groups, rows, heads, length, width, units, part)
    pick = lambda names: {name: every[name] for name in names}
    shape = jax.ShapeDtypeStruct
    scratch = pick(dict(
    residual=0, normed2=0, ahead=0, out_w=0, gate_w=0, up_w=0, down_w=0, small_mine=0, weight_sem=0,
    first_sem=0,
    ))
    output, residual_grad, grads, gain2_grad, out_wg, gate_wg, up_wg, down_wg = pl.pallas_call(
        functools.partial(unit_local_kernel, tuple(scratch)),
        name="unit_local",
        out_shape=(
            shape((rows, width), bf16), shape((rows, width), f32), shape((groups, rows, part), bf16),
            shape((1, width), f32), shape((groups, part, width), bf16), shape((groups, width, units), bf16),
            shape((groups, width, units), bf16), shape((groups, units, width), bf16),
        ),
        in_specs=[anywhere] * 4 + [inside] * 4,
        out_specs=(inside,) * 8,
        scratch_shapes=list(scratch.values()),
        compiler_params=pltpu.CompilerParams(vmem_limit_bytes=56 << 20),
    )(gate_all, up_all, down_all, out_all, mixed_here, hidden_in, cot, gains)
    mixed_grad = lax.all_to_all(grads, "tensor", 0, 0)
    scratch = pick(dict(
    gain=0, probs=0, w=0, dot=0, dott=0, grad=0, joined=0, near=0, bucket=0, table=0, far=0, dkt=0, dvt=0,
    probs_sem=0,
    ))
    back, qkv_wg, small = pl.pallas_call(
        functools.partial(back_local_kernel, tuple(scratch)),
        name="back_local",
        out_shape=(
            shape((groups, rows, width), bf16), shape((3 * part, width), bf16), shape((16, width), f32),
        ),
        in_specs=[anywhere] + [inside] * 11,
        out_specs=(inside,) * 3,
        scratch_shapes=list(scratch.values()),
        compiler_params=pltpu.CompilerParams(vmem_limit_bytes=56 << 20),
    )(probs, mixed, inverse, qt, k, vt, normed, wq, wk, wv, gains, mixed_grad)
    back_sum = lax.psum_scatter(back, "tensor", scatter_dimension=0).astype(f32)
    parts = tuple(lax.psum_scatter(wg, "tensor", scatter_dimension=0) for wg in (out_wg, gate_wg, up_wg, down_wg))
    sums = lax.psum(parts + (qkv_wg,), "dp")
    small = small.at[1].set(gain2_grad[0])
    small_sum = lax.psum(small, "dp")
    gains = lax.psum(small_sum[:8], "tensor")
    input_rows = hidden_in.astype(f32)
    r1 = mean_square_scale(input_rows)
    g1 = back_sum * gains[0:1]
    centre = jnp.mean(g1 * input_rows, axis=-1, keepdims=True)
    input_grad = (residual_grad + r1 * g1 - (r1 * r1 * r1 * centre) * input_rows).astype(bf16)
    return (output, input_grad, jnp.concatenate((gains, small_sum[8:]))) + tuple(sums)


def finish_kernel(*refs):
    half = len(refs) // 2
    for source, target in zip(refs[:half], refs[half:]):
        target[...] = source[...].astype(target.dtype)


def finish(output, input_grad, qkv_sum, out_sum, gate_sum, up_sum, down_sum):
    part, width = out_sum.shape
    steps = 4
    block = lambda a, at: pl.BlockSpec((a // steps, at), lambda i: (i, 0))
    shift = lambda turn: pl.BlockSpec((part // steps, width), lambda i: (i + turn * steps, 0))
    arrays = (output, input_grad, qkv_sum, qkv_sum, qkv_sum, out_sum, gate_sum, up_sum, down_sum)
    shapes = [output.shape, input_grad.shape] + [out_sum.shape] * 4 + [gate_sum.shape, up_sum.shape, down_sum.shape]
    kinds = [bf16] * 2 + [f32] * 7
    specs = [block(*shape) for shape in shapes]
    return pl.pallas_call(
        finish_kernel,
        grid=(steps,),
        name="finish",
        out_shape=tuple(jax.ShapeDtypeStruct(s, k) for s, k in zip(shapes, kinds)),
        in_specs=specs[:2] + [shift(turn) for turn in range(3)] + specs[5:],
        out_specs=tuple(specs),
        compiler_params=pltpu.CompilerParams(dimension_semantics=("arbitrary",), vmem_limit_bytes=62 << 20),
    )(*arrays)


def gather_by_axis(hidden_in, gains, gate, up, down, out):
    rows = hidden_in.astype(f32)
    normed = (rows * mean_square_scale(rows) * gains[0:1]).astype(bf16)
    return tuple(lax.all_gather(part, "tensor", axis=0) for part in (normed, gate, up, down, out))


def shards(
    by_kernel,
    hidden_in, segment_ids, norm1_gain, query_weight, key_weight, value_weight, out_weight,
    bias_table, norm2_gain, gate_weight, up_weight, down_weight, out_cotangent,
):
    gather_parts = gather if by_kernel else gather_by_axis
    rest_parts = rest_all if by_kernel else rest_by_axis
    rows_here, width = hidden_in.shape
    length = segment_ids.shape[1]
    assert segment_ids.shape[0] == 1 and rows_here == BLK
    heads = bias_table.shape[1]
    gains = jnp.stack((norm1_gain, norm2_gain)).astype(f32)
    normed, gate_w, up_w, down_w, out_w = gather_parts(
        hidden_in, gains, gate_weight, up_weight, down_weight, out_weight
    )
    normed = normed.reshape(length, width)
    query_weight, key_weight, value_weight = query_weight.T, key_weight.T, value_weight.T
    mixed, probs, qt, k, vt, inverse, mixed_here = attend(
        by_kernel, normed, query_weight, key_weight, value_weight, segment_ids, bias_table
    )
    if not by_kernel:
        mixed_here = lax.all_to_all(mixed_here, "tensor", 1, 1)
    output, input_grad, small_sum, out_sum, gate_sum, up_sum, down_sum, qkv_sum = rest_parts(
        gate_w, up_w, down_w, out_w, probs, query_weight, key_weight, value_weight, mixed_here, hidden_in,
        out_cotangent, gains, mixed, inverse, qt, k, vt, normed,
    )
    output, input_grad, query_grad, key_grad, value_grad, out_grad, gate_grad, up_grad, down_grad = finish(
        output, input_grad, qkv_sum, out_sum, gate_sum, up_sum, down_sum
    )
    return (
        output, input_grad, small_sum[0], query_grad.T, key_grad.T, value_grad.T, out_grad,
        small_sum[8 : 8 + heads, :BUCKETS].T, small_sum[1], gate_grad, up_grad, down_grad,
    )


def solution(mesh):
    in_specs = (
        P(("dp", "tensor"), None), P("dp", None), P(),
        P(None, "tensor"), P(None, "tensor"), P(None, "tensor"), P("tensor", None),
        P(None, "tensor"), P(), P(None, "tensor"), P(None, "tensor"), P("tensor", None),
        P(("dp", "tensor"), None),
    )
    out_specs = (
        P(("dp", "tensor"), None), P(("dp", "tensor"), None), P(),
        P(None, "tensor"), P(None, "tensor"), P(None, "tensor"), P("tensor", None),
        P(None, "tensor"), P(), P(None, "tensor"), P(None, "tensor"), P("tensor", None),
    )
    by_kernel = mesh.shape["dp"] == 8 and mesh.shape["tensor"] == 4
    return jax.shard_map(
        functools.partial(shards, by_kernel), mesh=mesh, in_specs=in_specs, out_specs=out_specs, check_vma=False
    )
```
